32 devices in a mesh: section: 2 (over x), dp: 16 (over z, y, core).
Axes of the slice: x: 2, y: 2, z: 4, core: 2. Of those that a mesh axis runs over, the one named last changes fastest.
Arguments:
- inputs: bfloat16 [2, 16, 256, 768], P(None, 'dp'), may hold values from -6 to 6
- clip_lengths: int32 [2, 16, 4], P(None, 'dp'), may hold values from 1 to 128, 256 in all within a row
- anchor_offsets: int32 [2, 16, 4], P(None, 'dp'), may hold values from 0 to 63
- cotangent: bfloat16 [2, 16, 256, 768], P(None, 'dp'), may hold values from -6 to 6
- inward_weight: bfloat16 [2, 768, 2304], P('section'), may hold values from -0.3125 to 0.3125
- outward_weight: bfloat16 [2, 768, 768], P('section'), may hold values from -0.625 to 0.625
- up_weight: bfloat16 [2, 768, 3072], P('section'), may hold values from -0.21875 to 0.21875
- down_weight: bfloat16 [2, 3072, 768], P('section'), may hold values from -0.15625 to 0.15625
- norm_gain: float32 [2, 2, 768], P('section'), may hold values from 0.1 to 1.9
- norm_bias: float32 [2, 2, 768], P('section'), may hold values from -3 to 3
Outputs:
- layer_outputs: bfloat16 [2, 2, 16, 256, 768], P('section', None, 'dp')
- input_grads: float32 [2, 2, 16, 256, 768], P('section', None, 'dp')
- inward_grad: float32 [2, 768, 2304], P('section', 'dp')
- outward_grad: float32 [2, 768, 768], P('section', 'dp')
- up_grad: float32 [2, 768, 3072], P('section', 'dp')
- down_grad: float32 [2, 3072, 768], P('section', 'dp')
- gain_grad: float32 [2, 2, 768], P('section', None, 'dp')
- bias_grad: float32 [2, 2, 768], P('section', None, 'dp')
The draws below stay inside these ranges and needn't reach their ends.
Inputs may be any that keep to these rules, and one draw needn't show every extreme that they name: `clip_lengths`: in each sequence the 4 clip lengths sum to 256, and the longest is half of 256.
All inputs are finite; a program needn't handle non-finite values.
Results may differ from the reference program's by a relative error of at most 0.025.
Values may be sent and summed in bfloat16 or wider, within the bound.
A program may use at most 320 MiB of HBM per device.

```python
import math
import jax
import jax.numpy as jnp
import numpy as np
from jax import lax

D = 768
HEADS = 12
HEAD = 64
FF = 3072
SEQ_LEN = 256
CLIPS = 4
MICRO = 2
SEQS = 16
N_SECTION = 2


def set_ends(array, own_key, low, largest):
    dims = array.shape
    spot = [jax.random.randint(jax.random.fold_in(own_key, axis), (), 0, dims[axis]) for axis in range(len(dims))]
    array = array.at[tuple(spot)].set(low)
    longest = dims.index(max(dims))
    spot[longest] = (spot[longest] + 1) % dims[longest]
    return array.at[tuple(spot)].set(largest)


def steps_of(key, dims, cuts, smallest, largest):
    gain = 1.0
    for position, parts in cuts:
        heights = jax.random.uniform(jax.random.fold_in(jax.random.fold_in(key, 6), position), (parts,), jnp.float32, smallest / len(cuts), largest / len(cuts))
        gain = gain * jnp.repeat(jnp.exp(heights), dims[position] // parts).reshape((-1,) + (1,) * (len(dims) - 1 - position))
    return gain


def profile(number_of, total, most, skew):
    portions = [(1 << 20) // math.isqrt(grade ** skew) + 1 for grade in range(2, number_of + 1)]
    surplus, counts = total - most - (number_of - 1), [1] * (number_of - 1)
    while surplus > 0:
        free = [i for i in range(number_of - 1) if counts[i] < most]
        whole, budget = sum([portions[i] for i in free]), surplus
        for i in free:
            more = min(most - counts[i], max(1, budget * portions[i] // whole), surplus)
            counts[i] = counts[i] + more
            surplus = surplus - more
    return np.array([most] + counts)


def ragged_sizes(key, amount, total, bound, skew):
    if amount == 2:
        one = jax.random.randint(key, (), max(1, total - bound), min(bound, total - 1) + 1)
        return jnp.stack([one, total - one])
    tallies = jnp.asarray(profile(amount, total, bound, skew), jnp.int32)
    couples = (amount - 1) // 2
    giver, receiver = tallies[1:1 + 2 * couples:2], tallies[2:2 + 2 * couples:2]
    room = jnp.minimum(giver - 1, bound - receiver)
    moved = jax.random.randint(jax.random.fold_in(key, 1), (couples,), 0, 1 << 20) % (room + 1)
    tallies = tallies.at[1:1 + 2 * couples:2].set(giver - moved).at[2:2 + 2 * couples:2].set(receiver + moved)
    return tallies[jax.random.permutation(jax.random.fold_in(key, 2), amount)]


def noise(rng, shape, scale, reach, split=(), kind=jnp.bfloat16):
    level = steps_of(rng, shape, split, -0.22, 0.18) if split else 1.0
    array = jax.random.normal(rng, shape, jnp.float32) * scale * level
    return jnp.minimum(jnp.maximum(array, -reach), reach).astype(kind)


def setup_inputs(seed: int = 0) -> dict:
    seeds = jax.random.split(jax.random.key(seed), 11)
    inputs = noise(seeds[0], (MICRO, SEQS, SEQ_LEN, D), 1.0, 6.0, ((1, 16),))
    clip_lengths = jax.vmap(lambda own: ragged_sizes(own, CLIPS, SEQ_LEN, SEQ_LEN // 2, 2))(jax.random.split(seeds[1], MICRO * SEQS)).reshape((MICRO, SEQS, CLIPS)).astype(jnp.int32)
    anchor_offsets = set_ends(jax.random.randint(seeds[2], (MICRO, SEQS, CLIPS), 0, 64), jax.random.fold_in(seeds[2], 1), 0, 63).astype(jnp.int32)
    cotangent = noise(seeds[3], (MICRO, SEQS, SEQ_LEN, D), 1.0, 6.0, ((1, 16),))
    inward_weight = noise(seeds[4], (N_SECTION, D, 3 * D), (D // 2) ** -0.5, 0.3125, ((0, 2),))
    outward_weight = noise(seeds[5], (N_SECTION, D, D), (D // 8) ** -0.5, 0.625, ((0, 2),))
    up_weight = noise(seeds[6], (N_SECTION, D, FF), D ** -0.5, 0.21875, ((0, 2),))
    down_weight = noise(seeds[7], (N_SECTION, FF, D), (FF // 2) ** -0.5, 0.15625, ((0, 2),))
    norm_gain = jnp.clip(1.0 + 0.18 * jax.random.normal(seeds[8], (N_SECTION, 2, D), jnp.float32), 0.1, 1.9)
    norm_bias = noise(seeds[9], (N_SECTION, 2, D), 0.3, 3.0, ((0, 2),), jnp.float32)
    return {"inputs": inputs, "clip_lengths": clip_lengths, "anchor_offsets": anchor_offsets, "cotangent": cotangent, "inward_weight": inward_weight, "outward_weight": outward_weight, "up_weight": up_weight, "down_weight": down_weight, "norm_gain": norm_gain, "norm_bias": norm_bias}


@jax.custom_vjp
def low(v):
    return lax.optimization_barrier(v.astype(jnp.bfloat16)).astype(jnp.float32)

@jax.custom_vjp
def low_back(v):
    return v

def low_keep(v):
    return (low(v), None)

def low_pass(kept, grad):
    return (grad,)

def back_keep(v):
    return (v, None)

def back_low(kept, grad):
    return (low(grad),)
low.defvjp(low_keep, low_pass)
low_back.defvjp(back_keep, back_low)
EPSILON = 1e-06
HIGHEST = lax.Precision.HIGHEST

def norm_rows(values, norm_gain, norm_bias):
    average = lax.optimization_barrier(jnp.mean(values, -1, keepdims=True))
    centred = values - average
    inverse = lax.rsqrt(lax.optimization_barrier(jnp.mean(centred * centred, -1, keepdims=True)) + EPSILON)
    return centred * inverse * norm_gain + norm_bias

def clip_marks(lengths, offsets):
    positions = jnp.arange(SEQ_LEN, dtype=jnp.int32)
    clip_ends = jnp.cumsum(lengths).astype(jnp.int32)
    clip_starts = clip_ends - lengths
    anchor_at = clip_starts + offsets % lengths
    clip_ids = lax.optimization_barrier(jnp.sum((positions[:, None] >= clip_ends[None, :]).astype(jnp.int32), 1))
    anchors = jnp.any(positions[:, None] == anchor_at[None, :], 1)
    return (clip_ids, anchors)

def attend(queries, key_rows, values, clip_ids, anchors):
    block_rows = min(512, SEQ_LEN)
    count_blocks = SEQ_LEN // block_rows
    query_blocks = queries.reshape(count_blocks, block_rows, HEADS, HEAD)
    id_blocks = clip_ids.reshape(count_blocks, block_rows)
    scaling = HEAD ** (-0.5)

    def attend_block(item):
        query_block, id_block = item
        scores = low_back(jnp.einsum('qhd,khd->hqk', query_block, key_rows, precision=HIGHEST) * scaling)
        seen = (id_block[:, None] == clip_ids[None, :]) | anchors[None, :]
        scores = jnp.where(seen[None], scores, -1000000000.0)
        row_max = lax.optimization_barrier(jnp.max(scores, -1, keepdims=True))
        raised = jnp.exp(scores - row_max)
        weights = raised / lax.optimization_barrier(jnp.sum(raised, -1, keepdims=True))
        return jnp.einsum('hqk,khd->qhd', low(weights), values, precision=HIGHEST)
    pieces = lax.map(jax.checkpoint(attend_block), (query_blocks, id_blocks))
    return pieces.reshape(SEQ_LEN, HEADS * HEAD)

def layer(residual, inward, outward, upward, downward, norm_gain, norm_bias, clip_ids, anchors):
    first_norm = low(norm_rows(residual, norm_gain[0], norm_bias[0]))
    joined = low(low_back(jnp.dot(first_norm, inward, precision=HIGHEST)))
    heads_view = joined.reshape(SEQ_LEN, 3, HEADS, HEAD)
    attended = attend(heads_view[:, 0], heads_view[:, 1], heads_view[:, 2], clip_ids, anchors)
    attended = low(low_back(attended))
    middle = residual + low_back(jnp.dot(attended, outward, precision=HIGHEST))
    second_norm = low(norm_rows(middle, norm_gain[1], norm_bias[1]))
    lifted = low_back(jnp.dot(second_norm, upward, precision=HIGHEST))
    active = low(jax.nn.gelu(lifted, approximate=False))
    return middle + low_back(jnp.dot(active, downward, precision=HIGHEST))

def two_layers(weights, residual, zero_in, clip_ids, anchors):
    inward, outward, upward, downward, norm_gain, norm_bias = weights
    first_out = layer(residual, inward[0], outward[0], upward[0], downward[0], norm_gain[0], norm_bias[0], clip_ids, anchors)
    sent = low(low_back(first_out)) + zero_in
    second_out = layer(sent, inward[1], outward[1], upward[1], downward[1], norm_gain[1], norm_bias[1], clip_ids, anchors)
    return (second_out, sent)

def reference(inputs, clip_lengths, anchor_offsets, cotangent, inward_weight, outward_weight, up_weight, down_weight, norm_gain, norm_bias):
    weights = (inward_weight.astype(jnp.float32), outward_weight.astype(jnp.float32), up_weight.astype(jnp.float32), down_weight.astype(jnp.float32), norm_gain.astype(jnp.float32), norm_bias.astype(jnp.float32))
    count_seqs = MICRO * SEQS
    seq_inputs = inputs.astype(jnp.float32).reshape(count_seqs, SEQ_LEN, D)
    seq_cots = cotangent.astype(jnp.float32).reshape(count_seqs, SEQ_LEN, D)
    seq_lengths = clip_lengths.reshape(count_seqs, CLIPS).astype(jnp.int32)
    seq_offsets = anchor_offsets.reshape(count_seqs, CLIPS).astype(jnp.int32)

    def visit(totals, item):
        residual, cot_rows, lengths, offsets = item
        clip_ids, anchors = clip_marks(lengths, offsets)
        zero_in = jnp.zeros_like(residual)

        def forward(weight_set, first_in, extra_in):
            return two_layers(weight_set, first_in, extra_in, clip_ids, anchors)
        (second_out, sent), pull = jax.vjp(forward, weights, residual, zero_in)
        weight_grads, first_grad, second_grad = pull((cot_rows, jnp.zeros_like(sent)))
        totals = jax.tree.map(jnp.add, totals, weight_grads)
        return (totals, (sent, second_out, first_grad, second_grad))
    start_totals = jax.tree.map(jnp.zeros_like, weights)
    totals, (sent, second_out, first_grad, second_grad) = lax.scan(visit, start_totals, (seq_inputs, seq_cots, seq_lengths, seq_offsets))
    shape_out = (MICRO, SEQS, SEQ_LEN, D)
    layer_outputs = jnp.stack([sent.reshape(shape_out), second_out.reshape(shape_out)]).astype(jnp.bfloat16)
    input_grads = jnp.stack([first_grad.reshape(shape_out), second_grad.reshape(shape_out)])
    return (layer_outputs, input_grads, totals[0], totals[1], totals[2], totals[3], totals[4], totals[5])
```

```python
import functools
import types

import jax
import jax.numpy as jnp
from jax import lax
from jax.experimental import pallas as pl
from jax.experimental.pallas import tpu as pltpu
from jax.sharding import PartitionSpec as P

HEAD = 64
EPSILON = 1e-06
MESH = pl.DeviceIdType.MESH
WIDE = jnp.float32
SLIM = jnp.bfloat16
VMEM_BYTES = 67043328

UNITS = 12
BLOCK = 48


def times(left, right):
    return jnp.dot(left, right, preferred_element_type=WIDE)


def times_turned(left, right):
    return lax.dot_general(left, right, (((1,), (1,)), ((), ())), preferred_element_type=WIDE)


def unit_rows(values):
    centred = values - jnp.mean(values, -1, keepdims=True)
    inverse = lax.rsqrt(jnp.mean(centred * centred, -1, keepdims=True) + EPSILON)
    return centred * inverse, inverse


def norm_rows_bf16(r, values, which):
    unit, _ = unit_rows(values)
    return (unit * r.gain[0, which : which + 1, :] + r.bias[0, which : which + 1, :]).astype(SLIM)


def norm_backward(r, values, norm_grad, which):
    unit, inverse = unit_rows(values)
    width = values.shape[1]
    r.sums[which] += jnp.sum((norm_grad * unit).reshape(-1, 8, width), 0)
    r.sums[2 + which] += jnp.sum(norm_grad.reshape(-1, 8, width), 0)
    inner = norm_grad * r.gain[0, which : which + 1, :]
    return inverse * (
        inner
        - jnp.mean(inner, -1, keepdims=True)
        - unit * jnp.mean(inner * unit, -1, keepdims=True)
    )


def head_lanes():
    lane = lax.broadcasted_iota(jnp.int32, (1, 2 * HEAD), 1)
    first = jnp.where(lane < HEAD, 1.0, 0.0).astype(WIDE)
    return first, 1.0 - first


def mask_bias(r, micro):
    length = r.bias_mask.shape[0]

    def marks(positions):
        end = jnp.int32(0)
        ids = jnp.zeros(positions.shape, jnp.int32)
        anchors = jnp.zeros(positions.shape, jnp.int32)
        for clip in range(r.lengths.shape[2]):
            size = r.lengths[micro, 0, clip]
            anchor = end + lax.rem(r.offsets[micro, 0, clip], size)
            end = end + size
            ids = ids + jnp.where(positions >= end, 1, 0)
            anchors = anchors + jnp.where(positions == anchor, 1, 0)
        return ids, anchors

    key_ids, anchors = marks(lax.broadcasted_iota(jnp.int32, (length, 1), 0))
    query_ids, _ = marks(lax.broadcasted_iota(jnp.int32, (1, length), 1))
    seen = (key_ids == query_ids) | (jnp.broadcast_to(anchors, (length, length)) > 0)
    r.bias_mask[...] = jnp.where(seen, 0.0, -1000000000.0).astype(WIDE)


def place(r, slab, tokens):
    for line in range(8):
        z, y = line // 2, line % 2
        rows = pl.ds(y * 192 + z * BLOCK, BLOCK)
        own = pl.ds(pl.multiple_of(2 * BLOCK * line + r.c * BLOCK, 16), BLOCK)
        other = pl.ds(pl.multiple_of(2 * BLOCK * line + (1 - r.c) * BLOCK, 16), BLOCK)
        r.acts[slab, rows, tokens] = r.turned[own, :]
        r.acts_out[slab, rows, :] = r.turned[other, :]


def forward(r, micro, tok, first):
    length, width = r.normed.shape
    tokens = pl.ds(tok, length)
    mask_bias(r, micro)
    r.normed[...] = norm_rows_bf16(r, r.stream[micro].astype(WIDE), 0)

    @pl.when(first)
    def _():
        r.load_inward.wait()

    for part in range(3):
        r.grads[6 + part, tokens, :] = times(
            r.normed[...], r.inward[:, part * width : (part + 1) * width]
        ).astype(SLIM)

    @pl.when(micro > 0)
    def _():
        r.share_acts(0).wait_send()

    r.turned[...] = r.normed[...].T
    place(r, 6, tokens)
    one, two = (lanes.astype(SLIM) for lanes in head_lanes())
    for pair in range(width // (2 * HEAD)):
        cols = pl.ds(pair * 2 * HEAD, 2 * HEAD)
        queries = r.grads[6, tokens, cols] * jnp.asarray(HEAD**-0.5, SLIM)
        keys = r.grads[7, tokens, cols]
        values_turned = r.grads[8, tokens, cols].T
        scores = times_turned(jnp.concatenate([keys * one, keys * two], 0), queries)
        pieces = []
        for head in range(2):
            masked = scores[length * head : length * (head + 1)] + r.bias_mask[...]
            raised = jnp.exp(masked - jnp.max(masked, 0, keepdims=True))
            weights = (raised * (1.0 / jnp.sum(raised, 0, keepdims=True))).astype(SLIM)
            r.weights[micro, 2 * pair + head] = weights
            pieces.append(times(values_turned[HEAD * head : HEAD * (head + 1)], weights).astype(SLIM))
        attended_turned = jnp.concatenate(pieces, 0)
        r.turned[cols, :] = attended_turned
        r.held[:, cols] = attended_turned.T
    place(r, 5, tokens)

    @pl.when(first)
    def _():
        r.load_outward.wait()
        r.load_up.wait()
        r.load_down.wait()

    r.middle[micro] = r.stream[micro].astype(WIDE) + times(r.held[...], r.outward[...])
    r.normed[...] = norm_rows_bf16(r, r.middle[micro], 1)
    r.turned[...] = r.normed[...].T
    place(r, 4, tokens)
    r.total[...] = r.middle[micro]
    for part in range(4):
        cols = slice(part * width, (part + 1) * width)
        lifted = times(r.normed[...], r.up[:, cols])
        cumulative = 0.5 * (1.0 + lax.erf(lifted * 0.7071067811865476))
        density = jnp.exp(-0.5 * lifted * lifted) * 0.3989422804014327
        r.grads[1 + part, tokens, :] = (cumulative + lifted * density).astype(SLIM)
        active = (lifted * cumulative).astype(SLIM)
        r.total[...] += times(active, r.down[cols, :])
        r.turned[...] = active.T
        for y in range(2):
            for piece in range(4):
                rows = pl.ds(y * 192 + part * BLOCK, BLOCK)
                start = 384 * y + BLOCK * piece
                own = pl.ds(pl.multiple_of(start + r.c * 192, 16), BLOCK)
                other = pl.ds(pl.multiple_of(start + (1 - r.c) * 192, 16), BLOCK)
                r.acts[piece, rows, tokens] = r.turned[own, :]
                r.acts_out[piece, rows, :] = r.turned[other, :]
    r.result[micro] = r.total[...].astype(SLIM)


def backward(r, micro, tok):
    length, width = r.normed.shape
    tokens = pl.ds(tok, length)
    r.total[...] = jnp.zeros((length, width), WIDE)
    for part in range(4):
        cols = slice(part * width, (part + 1) * width)
        hidden = times_turned(r.grads[0, tokens, :], r.down[cols, :])
        lifted_grad = (hidden * r.grads[1 + part, tokens, :].astype(WIDE)).astype(SLIM)
        r.grads[1 + part, tokens, :] = lifted_grad
        r.total[...] += times_turned(lifted_grad, r.up[:, cols])
    middle_grad = r.grads[0, tokens, :].astype(WIDE) + norm_backward(
        r, r.middle[micro], r.total[...], 1
    )
    r.middle[micro] = middle_grad
    r.grads[5, tokens, :] = middle_grad.astype(SLIM)
    r.held[...] = times_turned(r.grads[5, tokens, :], r.outward[...]).astype(SLIM)
    first, second = head_lanes()
    one, two = first.astype(SLIM), second.astype(SLIM)
    scaling = HEAD**-0.5
    for pair in range(width // (2 * HEAD)):
        cols = pl.ds(pair * 2 * HEAD, 2 * HEAD)
        queries = r.grads[6, tokens, cols] * jnp.asarray(scaling, SLIM)
        values = r.grads[8, tokens, cols]
        keys_turned = r.grads[7, tokens, cols].T
        incoming = r.held[:, cols]
        weight_grads = times_turned(jnp.concatenate([values * one, values * two], 0), incoming)
        score_grads, query_grads, weights = [], [], []
        for head in range(2):
            kept = r.weights[micro, 2 * pair + head]
            wide = kept.astype(WIDE)
            own = weight_grads[length * head : length * (head + 1)]
            score_grad = (wide * (own - jnp.sum(wide * own, 0, keepdims=True))).astype(SLIM)
            score_grads.append(score_grad)
            weights.append(kept)
            query_grads.append(
                (times(keys_turned[HEAD * head : HEAD * (head + 1)], score_grad) * scaling).astype(SLIM)
            )
        key_grad = times(jnp.concatenate(score_grads, 0), queries)
        value_grad = times(jnp.concatenate(weights, 0), incoming)
        r.grads[6, tokens, cols] = jnp.concatenate(query_grads, 0).T
        r.grads[7, tokens, cols] = (key_grad[:length] * first + key_grad[length:] * second).astype(SLIM)
        r.grads[8, tokens, cols] = (value_grad[:length] * first + value_grad[length:] * second).astype(SLIM)
    norm_grad = times_turned(r.grads[6, tokens, :], r.inward[:, 0:width])
    for part in range(1, 3):
        norm_grad += times_turned(r.grads[6 + part, tokens, :], r.inward[:, part * width : (part + 1) * width])
    r.total[...] = norm_grad
    input_grad = r.middle[micro] + norm_backward(r, r.stream[micro].astype(WIDE), r.total[...], 0)
    r.middle[micro] = input_grad
    r.passed[micro] = input_grad.astype(SLIM)


NAMES = (
    "x_in", "cot_in", "inward_in", "outward_in", "up_in", "down_in", "gain", "bias", "lengths", "offsets",
    "out_result", "out_grad", "out_weights", "out_norms",
    "stream", "inward", "outward", "up", "down", "grads", "acts", "acts_out", "weights", "middle", "normed", "held",
    "turned", "total", "result", "passed", "sums", "bias_mask",
    "partial", "y_in", "z_in", "staged", "norms",
    "load_sem", "source_sem", "store_sem", "unit_sem",
    "relay_send", "relay_recv", "acts_send", "acts_recv", "branch_send", "branch_recv", "grads_send", "grads_recv",
    "y_send", "y_recv", "z_send", "z_recv", "norm_send", "norm_recv",
)


def step_kernel(*refs):
    r = types.SimpleNamespace(**dict(zip(NAMES, refs)))
    section, dp = lax.axis_index("section"), lax.axis_index("dp")
    c, y, z = lax.rem(dp, 2), lax.rem(lax.div(dp, 2), 2), lax.div(dp, 4)
    r.c = c
    length = r.normed.shape[0]
    leading = section == 0
    pair_dp, y_dp = dp + 1 - 2 * c, dp + 2 - 4 * y

    def slot_of(core, micro):
        return pl.ds(pl.multiple_of((core * 2 + micro) * length, length), length)

    def remote(src, dst, send, recv, to_section, to_dp):
        return pltpu.make_async_remote_copy(
            src_ref=src, dst_ref=dst, send_sem=send, recv_sem=recv,
            device_id=(to_section, to_dp), device_id_type=MESH,
        )

    def local(src, dst, sem):
        return pltpu.make_async_copy(src, dst, sem)

    r.load_inward = local(r.inward_in.at[0], r.inward, r.load_sem.at[0])
    r.load_outward = local(r.outward_in.at[0], r.outward, r.load_sem.at[1])
    r.load_up = local(r.up_in.at[0], r.up, r.load_sem.at[2])
    r.load_down = local(r.down_in.at[0], r.down, r.load_sem.at[3])

    def load_x(micro):
        return local(r.x_in.at[micro, 0], r.stream.at[micro], r.source_sem.at[micro])

    def load_cot(micro):
        return local(r.cot_in.at[micro, 0], r.grads.at[0, slot_of(c, micro)], r.source_sem.at[micro])

    def relay_up(micro):
        return remote(r.result.at[micro], r.stream.at[micro], r.relay_send.at[micro], r.relay_recv.at[micro], 1 - section, dp)

    def relay_back(micro):
        return remote(
            r.passed.at[micro], r.grads.at[0, slot_of(c, micro)], r.relay_send.at[micro], r.relay_recv.at[micro], 1 - section, dp
        )

    def share_acts(micro, core=c):
        return remote(
            r.acts_out, r.acts.at[:, :, slot_of(core, micro)], r.acts_send.at[micro], r.acts_recv.at[micro], section, pair_dp
        )

    def share_branch(micro, core=c):
        rows = slot_of(core, micro)
        return remote(r.grads.at[0, rows], r.grads.at[0, rows], r.branch_send.at[micro], r.branch_recv.at[micro], section, pair_dp)

    def share_grads(micro, core=c):
        rows = slot_of(core, micro)
        return remote(
            r.grads.at[1:9, rows], r.grads.at[1:9, rows], r.grads_send.at[micro], r.grads_recv.at[micro], section, pair_dp
        )

    r.share_acts = share_acts

    def store_result(micro):
        return local(r.result.at[micro], r.out_result.at[micro], r.store_sem.at[0, micro])

    def store_grad(micro):
        return local(r.middle.at[micro], r.out_grad.at[micro], r.store_sem.at[1, micro])

    def to_y(unit):
        return remote(r.partial.at[unit, 0:192], r.y_in.at[unit], r.y_send.at[unit], r.y_recv.at[unit], section, y_dp)

    def kept(place):
        return pl.ds(192 + BLOCK * place, BLOCK)

    def to_right(unit, place):
        return remote(
            r.partial.at[unit, kept(place)], r.z_in.at[unit, place + 1],
            r.z_send.at[unit, place - 1], r.z_recv.at[unit, place + 1], section, dp + 4,
        )

    def to_left(unit, place):
        return remote(
            r.partial.at[unit, kept(place)], r.z_in.at[unit, place],
            r.z_send.at[unit, place], r.z_recv.at[unit, place], section, dp - 4,
        )

    def store_unit(unit):
        return local(r.staged.at[unit], r.out_weights.at[unit], r.unit_sem.at[unit])

    r.load_inward.start()

    @pl.when(leading)
    def _():
        load_x(0).start()
        load_x(1).start()

    @pl.when(jnp.logical_not(leading))
    def _():
        load_cot(0).start()
        load_cot(1).start()

    r.load_outward.start()
    r.load_up.start()
    r.load_down.start()
    r.sums[...] = jnp.zeros_like(r.sums)

    barrier = pltpu.get_barrier_semaphore()
    peers = [(1 - section, dp), (section, pair_dp), (section, y_dp)]
    peers += [(section, lax.rem(dp + 4 * hop, 16)) for hop in (1, 2, 3)]
    for peer in peers:
        pl.semaphore_signal(barrier, inc=1, device_id=peer, device_id_type=MESH)
    pl.semaphore_wait(barrier, len(peers))

    def arrive(micro):
        relay_back(micro).wait_recv()
        share_branch(micro).start()

    def weight_unit(unit):
        slab = jnp.minimum(unit, 4) + jnp.where(unit >= 8, 1, 0) + jnp.where(unit >= 9, 1, 0)
        column = jnp.maximum(unit - 3, 0)
        other = pl.ds(pl.multiple_of((1 - y) * 192, 64), 192)
        own = pl.ds(pl.multiple_of(y * 192, 64), 192)
        r.partial[unit, 0:192, :] = times(r.acts[slab, other, :], r.grads[column]).astype(SLIM)
        to_y(unit).start()
        r.partial[unit, 192:384, :] = times(r.acts[slab, own, :], r.grads[column]).astype(SLIM)

    def weight_units(low, high):
        def body(unit, carry):
            weight_unit(unit)
            return carry

        lax.fori_loop(low, high, body, 0)

    def slot(t, carry):
        trailing = jnp.logical_not(leading)
        half = lax.div(t, 2)
        is_forward = (leading & (t < 2)) | (trailing & ((t == 1) | (t == 3)))
        is_backward = (leading & ((t == 3) | (t == 5))) | (trailing & ((t == 2) | (t == 4)))
        is_weights = (leading & (t == 4)) | (trailing & (t == 5))

        @pl.when(trailing & (t == 0))
        def _():
            for micro in range(2):
                load_cot(micro).wait()
                share_branch(micro).start()

        @pl.when(is_forward)
        def _():
            micro = jnp.where(leading, jnp.minimum(t, 1), jnp.minimum(half, 1))

            @pl.when(leading)
            def _():
                load_x(micro).wait()

            @pl.when(trailing)
            def _():
                relay_up(micro).wait_recv()

            forward(r, micro, pl.multiple_of((c * 2 + micro) * length, length), t == section)

            @pl.when(leading)
            def _():
                relay_up(micro).start()

            share_acts(micro).start()
            store_result(micro).start()

        @pl.when(leading & (t == 3))
        def _():
            arrive(0)

        @pl.when(is_backward)
        def _():
            micro = jnp.clip(half - 1, 0, 1)
            backward(r, micro, pl.multiple_of((c * 2 + micro) * length, length))

            @pl.when(trailing)
            def _():
                relay_back(micro).start()

            share_grads(micro).start()
            store_grad(micro).start()

        @pl.when(leading & (t == 4))
        def _():
            arrive(1)

        @pl.when(is_weights)
        def _():
            for micro in range(2):
                share_branch(micro, 1 - c).wait_recv()
                share_acts(micro, 1 - c).wait_recv()
            weight_units(0, 4)

        return carry

    lax.fori_loop(0, 6, slot, 0)

    def norm_copy(src, dst, index, to_dp):
        return remote(r.norms.at[src], r.norms.at[dst], r.norm_send.at[index], r.norm_recv.at[index], section, to_dp)

    def norm_to_pair():
        return norm_copy(0, 1, 0, pair_dp)

    def norm_to_y():
        return norm_copy(2, 3, 1, y_dp)

    def norm_to_z(hop):
        return norm_copy(4, 4 + hop, 1 + hop, lax.rem(dp + 4 * hop, 16))

    r.norms[0] = jnp.concatenate([jnp.sum(r.sums[...], 1), jnp.zeros((4, r.sums.shape[2]), WIDE)], 0)
    norm_to_pair().start()
    norm_to_pair().wait_recv()
    r.norms[2] = r.norms[0] + r.norms[1]
    norm_to_y().start()
    for micro in range(2):
        share_grads(micro, 1 - c).wait_recv()
    weight_units(4, UNITS)

    def sum_y(unit):
        to_y(unit).wait_recv()
        r.partial[unit, 192:384, :] = (
            r.partial[unit, 192:384, :].astype(WIDE) + r.y_in[unit].astype(WIDE)
        ).astype(SLIM)

    def arrived(unit, index):
        remote(
            r.partial.at[unit, kept(0)], r.z_in.at[unit, index], r.z_send.at[unit, 0], r.z_recv.at[unit, index], section, dp
        ).wait_recv()
        return r.z_in[unit, index].astype(WIDE)

    def go_right(unit, here):
        for place in range(3, here, -1):
            if here > 0:
                value = r.partial[unit, kept(place), :].astype(WIDE) + arrived(unit, place + 1)
                r.partial[unit, kept(place), :] = value.astype(SLIM)
            to_right(unit, place).start()

    def go_left(unit, here):
        for place in range(here):
            if here < 3:
                value = r.partial[unit, kept(place), :].astype(WIDE) + arrived(unit, place)
                r.partial[unit, kept(place), :] = value.astype(SLIM)
            to_left(unit, place).start()

    def finish(unit, here):
        value = r.partial[unit, kept(here), :].astype(WIDE)
        if here > 0:
            value = value + arrived(unit, here + 1)
        if here < 3:
            value = value + arrived(unit, here)
        r.staged[unit] = value
        store_unit(unit).start()

    def advance(i, carry):
        @pl.when(i < UNITS)
        def _():
            sum_y(i)

            @pl.when(z == 0)
            def _():
                go_right(i, 0)

            @pl.when(z == 3)
            def _():
                go_left(i, 3)

        @pl.when((i >= 1) & (i < UNITS + 1))
        def _():
            @pl.when(z == 1)
            def _():
                go_right(i - 1, 1)

            @pl.when(z == 2)
            def _():
                go_left(i - 1, 2)

        @pl.when((i >= 2) & (i < UNITS + 2))
        def _():
            @pl.when(z == 1)
            def _():
                go_left(i - 2, 1)

            @pl.when(z == 2)
            def _():
                go_right(i - 2, 2)

        @pl.when(i >= 3)
        def _():
            for here in range(4):

                @pl.when(z == here)
                def _():
                    finish(i - 3, here)

        @pl.when(i == 5)
        def _():
            norm_to_y().wait_recv()
            r.norms[4] = r.norms[2] + r.norms[3]
            for hop in (1, 2, 3):
                norm_to_z(hop).start()

        @pl.when(i == 11)
        def _():
            for hop in (1, 2, 3):
                norm_to_z(hop).wait_recv()
            r.norms[0] = (r.norms[4] + r.norms[5]) + (r.norms[6] + r.norms[7])

        return carry

    norm_to_pair().wait_send()
    lax.fori_loop(0, UNITS + 3, advance, 0)
    store_norms = local(r.norms.at[0], r.out_norms, r.store_sem.at[2, 0])
    store_norms.start()

    norm_to_y().wait_send()
    for hop in (1, 2, 3):
        norm_to_z(hop).wait_send()
    share_acts(1).wait_send()
    for micro in range(2):
        share_branch(micro).wait_send()
        share_grads(micro).wait_send()
        store_result(micro).wait()
        store_grad(micro).wait()

        @pl.when(leading)
        def _():
            relay_up(micro).wait_send()

        @pl.when(jnp.logical_not(leading))
        def _():
            relay_back(micro).wait_send()

    def drain(unit, carry):
        to_y(unit).wait_send()
        for index in range(3):
            remote(
                r.partial.at[unit, kept(0)], r.z_in.at[unit, 0], r.z_send.at[unit, index], r.z_recv.at[unit, 0], section, dp
            ).wait_send()
        store_unit(unit).wait()
        return carry

    lax.fori_loop(0, UNITS, drain, 0)
    store_norms.wait()


def step_on_device(
    inputs, clip_lengths, anchor_offsets, cotangent, inward_weight, outward_weight, up_weight, down_weight, norm_gain, norm_bias
):
    _, _, length, width = inputs.shape
    wide_ff = up_weight.shape[2]
    anywhere = pl.BlockSpec(memory_space=pl.ANY)
    in_vmem = pl.BlockSpec(memory_space=pltpu.VMEM)
    in_smem = pl.BlockSpec(memory_space=pltpu.SMEM)
    dma = pltpu.SemaphoreType.DMA
    results, grads, units, norms = pl.pallas_call(
        step_kernel,
        out_shape=(
            jax.ShapeDtypeStruct((2, length, width), SLIM),
            jax.ShapeDtypeStruct((2, length, width), WIDE),
            jax.ShapeDtypeStruct((UNITS, BLOCK, width), WIDE),
            jax.ShapeDtypeStruct((8, width), WIDE),
        ),
        in_specs=[anywhere] * 6 + [in_vmem] * 2 + [in_smem] * 2,
        out_specs=[anywhere] * 4,
        scratch_shapes=[
            pltpu.VMEM((2, length, width), SLIM),
            pltpu.VMEM((width, 3 * width), SLIM),
            pltpu.VMEM((width, width), SLIM),
            pltpu.VMEM((width, wide_ff), SLIM),
            pltpu.VMEM((wide_ff, width), SLIM),
            pltpu.VMEM((9, 4 * length, width), SLIM),
            pltpu.VMEM((7, 8 * BLOCK, 4 * length), SLIM),
            pltpu.VMEM((7, 8 * BLOCK, length), SLIM),
            pltpu.VMEM((2, width // HEAD, length, length), SLIM),
            pltpu.VMEM((2, length, width), WIDE),
            pltpu.VMEM((length, width), SLIM),
            pltpu.VMEM((length, width), SLIM),
            pltpu.VMEM((width, length), SLIM),
            pltpu.VMEM((length, width), WIDE),
            pltpu.VMEM((2, length, width), SLIM),
            pltpu.VMEM((2, length, width), SLIM),
            pltpu.VMEM((4, 8, width), WIDE),
            pltpu.VMEM((length, length), WIDE),
            pltpu.VMEM((UNITS, 8 * BLOCK, width), SLIM),
            pltpu.VMEM((UNITS, 4 * BLOCK, width), SLIM),
            pltpu.VMEM((UNITS, 5, BLOCK, width), SLIM),
            pltpu.VMEM((UNITS, BLOCK, width), WIDE),
            pltpu.VMEM((8, 8, width), WIDE),
            dma((4,)), dma((2,)), dma((3, 2)), dma((UNITS,)),
            dma((2,)), dma((2,)), dma((2,)), dma((2,)), dma((2,)), dma((2,)), dma((2,)), dma((2,)),
            dma((UNITS,)), dma((UNITS,)), dma((UNITS, 3)), dma((UNITS, 5)), dma((5,)), dma((5,)),
        ],
        compiler_params=pltpu.CompilerParams(
            collective_id=0, has_side_effects=True, vmem_limit_bytes=VMEM_BYTES
        ),
    )(
        inputs, cotangent, inward_weight, outward_weight, up_weight, down_weight,
        norm_gain, norm_bias, clip_lengths, anchor_offsets,
    )
    share = width // lax.axis_size("dp")
    mine = lax.dynamic_slice(norms, (0, lax.axis_index("dp") * share), (4, share))

    def side_by_side(some):
        return some.transpose(1, 0, 2).reshape(1, BLOCK, -1)

    return (
        results[None, :, None],
        grads[None, :, None],
        side_by_side(units[9:12]),
        units[8:9],
        side_by_side(units[4:8]),
        units[0:4].reshape(1, 4 * BLOCK, width),
        mine[None, 0:2],
        mine[None, 2:4],
    )


def shifted(x, axis, by):
    size = lax.axis_size(axis)
    pairs = [(i, i + by) for i in range(size) if 0 <= i + by < size]
    return lax.ppermute(x, axis, pairs)


def norm_rows(values, norm_gain, norm_bias):
    average = jnp.mean(values, -1, keepdims=True)
    centred = values - average
    inverse = lax.rsqrt(jnp.mean(centred * centred, -1, keepdims=True) + EPSILON)
    normed = centred * inverse
    return (normed * norm_gain + norm_bias, normed, inverse)


def norm_back(norm_grad, normed, inverse, norm_gain):
    inner = norm_grad * norm_gain
    through = inverse * (
        inner
        - jnp.mean(inner, -1, keepdims=True)
        - normed * jnp.mean(inner * normed, -1, keepdims=True)
    )
    return (through, jnp.sum(norm_grad * normed, 0), jnp.sum(norm_grad, 0))


def gelu_slope(lifted):
    cumulative = 0.5 * (1.0 + lax.erf(lifted * 0.7071067811865476))
    density = jnp.exp(-0.5 * lifted * lifted) * 0.3989422804014327
    return cumulative + lifted * density


def clip_marks(lengths, offsets, length):
    positions = jnp.arange(length, dtype=jnp.int32)
    clip_ends = jnp.cumsum(lengths)
    clip_starts = clip_ends - lengths
    anchor_at = clip_starts + offsets % lengths
    clip_ids = jnp.sum((positions[:, None] >= clip_ends[None, :]).astype(jnp.int32), 1)
    anchors = jnp.any(positions[:, None] == anchor_at[None, :], 1)
    return (clip_ids, anchors)


def masked_scores(query_block, key_rows, id_block, clip_ids, anchors, scaling):
    scores = (
        jnp.einsum("qhd,khd->hqk", query_block, key_rows, preferred_element_type=jnp.float32)
        * scaling
    )
    seen = (id_block[:, None] == clip_ids[None, :]) | anchors[None, :]
    return jnp.where(seen[None], scores, -1000000000.0)


def forward_layer(source, clip_ids, anchors, params):
    inward, outward, upward, downward, norm_gain, norm_bias = params
    length, model_width = source.shape
    head_count = model_width // HEAD
    scaling = HEAD ** (-0.5)
    residual = source.astype(jnp.float32)
    first_norm, unit_one, scale_one = norm_rows(residual, norm_gain[0], norm_bias[0])
    joined = jnp.dot(
        first_norm.astype(jnp.bfloat16), inward, preferred_element_type=jnp.float32
    ).astype(jnp.bfloat16)
    heads_view = joined.reshape(length, 3, head_count, HEAD)
    queries = heads_view[:, 0]
    key_rows = heads_view[:, 1]
    values = heads_view[:, 2]
    scores = masked_scores(queries, key_rows, clip_ids, clip_ids, anchors, scaling)
    row_max = jnp.max(scores, -1, keepdims=True)
    raised = jnp.exp(scores - row_max)
    row_sum = jnp.sum(raised, -1, keepdims=True)
    weights = (raised / row_sum).astype(jnp.bfloat16)
    pieces = [jnp.einsum("hqk,khd->qhd", weights, values, preferred_element_type=jnp.float32)]
    log_sums = [(row_max + jnp.log(row_sum))[..., 0]]
    attended = jnp.concatenate(pieces, 0).reshape(length, model_width).astype(jnp.bfloat16)
    logsum = jnp.concatenate(log_sums, 1)
    middle = residual + jnp.dot(attended, outward, preferred_element_type=jnp.float32)
    second_norm, unit_two, scale_two = norm_rows(middle, norm_gain[1], norm_bias[1])
    lifted = jnp.dot(second_norm.astype(jnp.bfloat16), upward, preferred_element_type=jnp.float32)
    active = jax.nn.gelu(lifted, approximate=False).astype(jnp.bfloat16)
    result = middle + jnp.dot(active, downward, preferred_element_type=jnp.float32)
    stored = (unit_one, scale_one, joined, logsum, attended, unit_two, scale_two, lifted, active)
    return (result, stored)


def contract_rows(left, right):
    return lax.dot_general(
        left, right, (((0,), (0,)), ((), ())), preferred_element_type=jnp.float32
    )


def contract_cols(left, right):
    return lax.dot_general(
        left, right, (((1,), (1,)), ((), ())), preferred_element_type=jnp.float32
    )


def feed_backward(incoming, stored, params):
    inward, outward, upward, downward, norm_gain, norm_bias = params
    unit_one, scale_one, joined, logsum, attended, unit_two, scale_two, lifted, active = stored
    branch = incoming.astype(jnp.bfloat16)
    down_part = contract_rows(active, branch)
    hidden_grad = contract_cols(branch, downward)
    lifted_grad = (hidden_grad * gelu_slope(lifted)).astype(jnp.bfloat16)
    second_in = (unit_two * norm_gain[1] + norm_bias[1]).astype(jnp.bfloat16)
    up_part = contract_rows(second_in, lifted_grad)
    normed_grad = contract_cols(lifted_grad, upward)
    through, gain_two, bias_two = norm_back(normed_grad, unit_two, scale_two, norm_gain[1])
    return (incoming + through, (up_part, down_part, gain_two, bias_two))


def attend_backward(middle_grad, stored, clip_ids, anchors, params):
    inward, outward, upward, downward, norm_gain, norm_bias = params
    unit_one, scale_one, joined, logsum, attended, unit_two, scale_two, lifted, active = stored
    length, model_width = attended.shape
    head_count = model_width // HEAD
    scaling = HEAD ** (-0.5)
    branch = middle_grad.astype(jnp.bfloat16)
    outward_part = contract_rows(attended, branch)
    attended_grad = (
        contract_cols(branch, outward).astype(jnp.bfloat16).reshape(length, head_count, HEAD)
    )
    heads_view = joined.reshape(length, 3, head_count, HEAD)
    queries = heads_view[:, 0]
    key_rows = heads_view[:, 1]
    values = heads_view[:, 2]
    key_grad = jnp.zeros((length, head_count, HEAD), jnp.float32)
    value_grad = jnp.zeros((length, head_count, HEAD), jnp.float32)
    block_rows = min(512, length)
    scores = masked_scores(queries, key_rows, clip_ids, clip_ids, anchors, scaling)
    weights = jnp.exp(scores - logsum[:, 0:block_rows, None])
    weight_grad = jnp.einsum(
        "qhd,khd->hqk", attended_grad, values, preferred_element_type=jnp.float32
    )
    score_grad = (
        weights * (weight_grad - jnp.sum(weights * weight_grad, -1, keepdims=True))
    ).astype(jnp.bfloat16)
    query_pieces = [
        scaling
        * jnp.einsum("hqk,khd->qhd", score_grad, key_rows, preferred_element_type=jnp.float32)
    ]
    key_grad = key_grad + scaling * jnp.einsum(
        "hqk,qhd->khd", score_grad, queries, preferred_element_type=jnp.float32
    )
    value_grad = value_grad + jnp.einsum(
        "hqk,qhd->khd",
        weights.astype(jnp.bfloat16),
        attended_grad,
        preferred_element_type=jnp.float32,
    )
    query_grad = jnp.concatenate(query_pieces, 0)
    joined_grad = (
        jnp.stack([query_grad, key_grad, value_grad], 1)
        .reshape(length, 3 * model_width)
        .astype(jnp.bfloat16)
    )
    first_in = (unit_one * norm_gain[0] + norm_bias[0]).astype(jnp.bfloat16)
    inward_part = contract_rows(first_in, joined_grad)
    normed_grad = contract_cols(joined_grad, inward)
    through, gain_one, bias_one = norm_back(normed_grad, unit_one, scale_one, norm_gain[0])
    return (middle_grad + through, (inward_part, outward_part, gain_one, bias_one))


def resting(function):

    def blank(*operands):
        return jax.tree.map(jnp.zeros_like, function(*operands))

    return blank


def take_slot(holder, buffer_slot):
    return jax.tree.map(
        lambda element: lax.dynamic_index_in_dim(element, buffer_slot, 0, False), holder
    )


def place_slot(holder, item, buffer_slot, working):

    def update(element, fresh):
        former = lax.dynamic_index_in_dim(element, buffer_slot, 0, False)
        return lax.dynamic_update_index_in_dim(
            element, jnp.where(working, fresh, former), buffer_slot, 0
        )

    return jax.tree.map(update, holder, item)


def per_device(
    inputs,
    clip_lengths,
    anchor_offsets,
    cotangent,
    inward_weight,
    outward_weight,
    up_weight,
    down_weight,
    norm_gain,
    norm_bias,
):
    params = (
        inward_weight[0],
        outward_weight[0],
        up_weight[0],
        down_weight[0],
        norm_gain[0],
        norm_bias[0],
    )
    stream = inputs[:, 0]
    cot_rows = cotangent[:, 0]
    lengths_all = clip_lengths[:, 0]
    offsets_all = anchor_offsets[:, 0]
    micro_count = stream.shape[0]
    length = stream.shape[1]
    section_index = lax.axis_index("section")
    section_count = lax.axis_size("section")
    leading = section_index == 0
    trailing = section_index == section_count - 1
    periods = micro_count + section_count - 1
    arriving = jnp.zeros_like(stream[0])
    produced = jnp.zeros_like(stream)
    archive = None
    for period in range(periods):
        micro_index = period - section_index
        working = (micro_index >= 0) & (micro_index < micro_count)
        buffer_slot = jnp.clip(micro_index, 0, micro_count - 1)
        source = jnp.where(leading, stream[min(period, micro_count - 1)], arriving)
        clip_ids, anchors = clip_marks(
            take_slot(lengths_all, buffer_slot), take_slot(offsets_all, buffer_slot), length
        )
        result, stored = lax.cond(
            working, forward_layer, resting(forward_layer), source, clip_ids, anchors, params
        )
        if archive is None:
            archive = jax.tree.map(
                lambda element: jnp.zeros((micro_count,) + element.shape, element.dtype), stored
            )
        archive = place_slot(archive, stored, buffer_slot, working)
        sending = result.astype(jnp.bfloat16)
        produced = place_slot(produced, sending, buffer_slot, working)
        if period < micro_count:
            arriving = shifted(sending, "section", 1)
    inward, outward, upward, downward, gains, biases = params
    up_sum = jnp.zeros(upward.shape, jnp.float32)
    down_sum = jnp.zeros(downward.shape, jnp.float32)
    gain_two = jnp.zeros(gains.shape[1:], jnp.float32)
    bias_two = jnp.zeros(biases.shape[1:], jnp.float32)
    inward_sum = jnp.zeros(inward.shape, jnp.float32)
    outward_sum = jnp.zeros(outward.shape, jnp.float32)
    gain_one = jnp.zeros(gains.shape[1:], jnp.float32)
    bias_one = jnp.zeros(biases.shape[1:], jnp.float32)
    upstream = jnp.zeros_like(stream[0])
    returned = jnp.zeros(stream.shape, jnp.float32)
    for period in range(periods):
        micro_index = micro_count - 1 - period + (section_count - 1 - section_index)
        working = (micro_index >= 0) & (micro_index < micro_count)
        buffer_slot = jnp.clip(micro_index, 0, micro_count - 1)
        incoming = jnp.where(trailing, take_slot(cot_rows, buffer_slot), upstream).astype(
            jnp.float32
        )
        clip_ids, anchors = clip_marks(
            take_slot(lengths_all, buffer_slot), take_slot(offsets_all, buffer_slot), length
        )
        stored = take_slot(archive, buffer_slot)
        middle_grad, feed_part = lax.cond(
            working, feed_backward, resting(feed_backward), incoming, stored, params
        )
        up_sum = up_sum + feed_part[0]
        down_sum = down_sum + feed_part[1]
        gain_two = gain_two + feed_part[2]
        bias_two = bias_two + feed_part[3]
        input_grad, attend_part = lax.cond(
            working,
            attend_backward,
            resting(attend_backward),
            middle_grad,
            stored,
            clip_ids,
            anchors,
            params,
        )
        inward_sum = inward_sum + attend_part[0]
        outward_sum = outward_sum + attend_part[1]
        gain_one = gain_one + attend_part[2]
        bias_one = bias_one + attend_part[3]
        returned = place_slot(returned, input_grad, buffer_slot, working)
        if period < periods - 1:
            upstream = shifted(input_grad.astype(jnp.bfloat16), "section", -1)
    inward_sum, outward_sum, up_sum, down_sum, gain_one, gain_two, bias_one, bias_two = (
        lax.psum_scatter(inward_sum, "dp", scatter_dimension=0, tiled=True),
        lax.psum_scatter(outward_sum, "dp", scatter_dimension=0, tiled=True),
        lax.psum_scatter(up_sum, "dp", scatter_dimension=0, tiled=True),
        lax.psum_scatter(down_sum, "dp", scatter_dimension=0, tiled=True),
        lax.psum_scatter(gain_one, "dp", scatter_dimension=0, tiled=True),
        lax.psum_scatter(gain_two, "dp", scatter_dimension=0, tiled=True),
        lax.psum_scatter(bias_one, "dp", scatter_dimension=0, tiled=True),
        lax.psum_scatter(bias_two, "dp", scatter_dimension=0, tiled=True),
    )
    layer_outputs = produced[None, :, None]
    input_grads = returned[None, :, None]
    gain_grad = jnp.stack([gain_one, gain_two])[None]
    bias_grad = jnp.stack([bias_one, bias_two])[None]
    return (
        layer_outputs,
        input_grads,
        inward_sum[None],
        outward_sum[None],
        up_sum[None],
        down_sum[None],
        gain_grad,
        bias_grad,
    )


def solution(mesh):
    local = step_on_device if mesh.shape["dp"] == 16 and mesh.shape["section"] == 2 else per_device
    return jax.shard_map(
        local,
        mesh=mesh,
        in_specs=(
            P(None, "dp", None, None),
            P(None, "dp", None),
            P(None, "dp", None),
            P(None, "dp", None, None),
            P("section", None, None),
            P("section", None, None),
            P("section", None, None),
            P("section", None, None),
            P("section", None, None),
            P("section", None, None),
        ),
        out_specs=(
            P("section", None, "dp", None, None),
            P("section", None, "dp", None, None),
            P("section", "dp", None),
            P("section", "dp", None),
            P("section", "dp", None),
            P("section", "dp", None),
            P("section", None, "dp"),
            P("section", None, "dp"),
        ),
        check_vma=False,
    )
```

```python
import functools
import types

import jax
import jax.numpy as jnp
from jax import lax
from jax.experimental import pallas as pl
from jax.experimental.pallas import tpu as pltpu
from jax.sharding import PartitionSpec as P

HEAD = 64
EPSILON = 1e-06
MESH = pl.DeviceIdType.MESH
WIDE = jnp.float32
SLIM = jnp.bfloat16
VMEM_BYTES = 67043328

UNITS = 24
FAR = 4
NEAR = UNITS - FAR
EARLY = 8
BLOCK = 48
COLUMNS = 384


def times(left, right):
    return jnp.dot(left, right, preferred_element_type=WIDE)


def times_turned(left, right):
    return lax.dot_general(left, right, (((1,), (1,)), ((), ())), preferred_element_type=WIDE)


def unit_rows(values):
    centred = values - jnp.mean(values, -1, keepdims=True)
    inverse = lax.rsqrt(jnp.mean(centred * centred, -1, keepdims=True) + EPSILON)
    return centred * inverse, inverse


def norm_rows_bf16(r, values, which):
    unit, _ = unit_rows(values)
    return (unit * r.gain[0, which : which + 1, :] + r.bias[0, which : which + 1, :]).astype(SLIM)


def norm_backward(r, values, norm_grad, which):
    unit, inverse = unit_rows(values)
    width = values.shape[1]
    r.sums[which] += jnp.sum((norm_grad * unit).reshape(-1, 8, width), 0)
    r.sums[2 + which] += jnp.sum(norm_grad.reshape(-1, 8, width), 0)
    inner = norm_grad * r.gain[0, which : which + 1, :]
    return inverse * (
        inner
        - jnp.mean(inner, -1, keepdims=True)
        - unit * jnp.mean(inner * unit, -1, keepdims=True)
    )


def head_lanes():
    lane = lax.broadcasted_iota(jnp.int32, (1, 2 * HEAD), 1)
    first = jnp.where(lane < HEAD, 1.0, 0.0).astype(WIDE)
    return first, 1.0 - first


def mask_bias(r, micro):
    length = r.bias_mask.shape[0]

    def marks(positions):
        end = jnp.int32(0)
        ids = jnp.zeros(positions.shape, jnp.int32)
        anchors = jnp.zeros(positions.shape, jnp.int32)
        for clip in range(r.lengths.shape[2]):
            size = r.lengths[micro, 0, clip]
            anchor = end + lax.rem(r.offsets[micro, 0, clip], size)
            end = end + size
            ids = ids + jnp.where(positions >= end, 1, 0)
            anchors = anchors + jnp.where(positions == anchor, 1, 0)
        return ids, anchors

    key_ids, anchors = marks(lax.broadcasted_iota(jnp.int32, (length, 1), 0))
    query_ids, _ = marks(lax.broadcasted_iota(jnp.int32, (1, length), 1))
    seen = (key_ids == query_ids) | (jnp.broadcast_to(anchors, (length, length)) > 0)
    r.bias_mask[...] = jnp.where(seen, 0.0, -1000000000.0).astype(WIDE)


def place(r, slab, tokens):
    for line in range(8):
        z, y = line // 2, line % 2
        rows = pl.ds(y * 192 + z * BLOCK, BLOCK)
        own = pl.ds(pl.multiple_of(2 * BLOCK * line + r.c * BLOCK, 16), BLOCK)
        other = pl.ds(pl.multiple_of(2 * BLOCK * line + (1 - r.c) * BLOCK, 16), BLOCK)
        r.acts[slab, rows, tokens] = r.turned[own, :]
        r.acts_out[slab, rows, :] = r.turned[other, :]


def forward(r, micro, tok, first):
    length, width = r.normed.shape
    tokens = pl.ds(tok, length)
    mask_bias(r, micro)
    r.normed[...] = norm_rows_bf16(r, r.stream[micro].astype(WIDE), 0)

    @pl.when(first)
    def _():
        r.load_inward.wait()

    for part in range(3):
        r.grads[6 + part, tokens, :] = times(
            r.normed[...], r.inward[:, part * width : (part + 1) * width]
        ).astype(SLIM)

    @pl.when(micro > 0)
    def _():
        r.share_acts(0).wait_send()

    r.turned[...] = r.normed[...].T
    place(r, 6, tokens)
    one, two = (lanes.astype(SLIM) for lanes in head_lanes())
    for pair in range(width // (2 * HEAD)):
        cols = pl.ds(pair * 2 * HEAD, 2 * HEAD)
        queries = r.grads[6, tokens, cols] * jnp.asarray(HEAD**-0.5, SLIM)
        keys = r.grads[7, tokens, cols]
        values_turned = r.grads[8, tokens, cols].T
        scores = times_turned(jnp.concatenate([keys * one, keys * two], 0), queries)
        pieces = []
        for head in range(2):
            masked = scores[length * head : length * (head + 1)] + r.bias_mask[...]
            raised = jnp.exp(masked - jnp.max(masked, 0, keepdims=True))
            weights = (raised * (1.0 / jnp.sum(raised, 0, keepdims=True))).astype(SLIM)
            r.weights[micro, 2 * pair + head] = weights
            pieces.append(times(values_turned[HEAD * head : HEAD * (head + 1)], weights).astype(SLIM))
        attended_turned = jnp.concatenate(pieces, 0)
        r.turned[cols, :] = attended_turned
        r.held[:, cols] = attended_turned.T
    place(r, 5, tokens)

    @pl.when(first)
    def _():
        r.load_outward.wait()
        r.load_up.wait()
        r.load_down.wait()

    r.middle[micro] = r.stream[micro].astype(WIDE) + times(r.held[...], r.outward[...])
    r.normed[...] = norm_rows_bf16(r, r.middle[micro], 1)
    r.turned[...] = r.normed[...].T
    place(r, 4, tokens)
    r.total[...] = r.middle[micro]
    for part in range(4):
        cols = slice(part * width, (part + 1) * width)
        lifted = times(r.normed[...], r.up[:, cols])
        cumulative = 0.5 * (1.0 + lax.erf(lifted * 0.7071067811865476))
        density = jnp.exp(-0.5 * lifted * lifted) * 0.3989422804014327
        r.grads[1 + part, tokens, :] = (cumulative + lifted * density).astype(SLIM)
        active = (lifted * cumulative).astype(SLIM)
        r.total[...] += times(active, r.down[cols, :])
        r.turned[...] = active.T
        for y in range(2):
            for piece in range(4):
                rows = pl.ds(y * 192 + part * BLOCK, BLOCK)
                start = 384 * y + BLOCK * piece
                own = pl.ds(pl.multiple_of(start + r.c * 192, 16), BLOCK)
                other = pl.ds(pl.multiple_of(start + (1 - r.c) * 192, 16), BLOCK)
                r.acts[piece, rows, tokens] = r.turned[own, :]
                r.acts_out[piece, rows, :] = r.turned[other, :]
    r.result[micro] = r.total[...].astype(SLIM)


def backward(r, micro, tok):
    length, width = r.normed.shape
    tokens = pl.ds(tok, length)
    r.total[...] = jnp.zeros((length, width), WIDE)
    for part in range(4):
        cols = slice(part * width, (part + 1) * width)
        hidden = times_turned(r.grads[0, tokens, :], r.down[cols, :])
        lifted_grad = (hidden * r.grads[1 + part, tokens, :].astype(WIDE)).astype(SLIM)
        r.grads[1 + part, tokens, :] = lifted_grad
        r.total[...] += times_turned(lifted_grad, r.up[:, cols])
    middle_grad = r.grads[0, tokens, :].astype(WIDE) + norm_backward(
        r, r.middle[micro], r.total[...], 1
    )
    r.middle[micro] = middle_grad
    r.grads[5, tokens, :] = middle_grad.astype(SLIM)
    r.held[...] = times_turned(r.grads[5, tokens, :], r.outward[...]).astype(SLIM)
    first, second = head_lanes()
    one, two = first.astype(SLIM), second.astype(SLIM)
    scaling = HEAD**-0.5
    for pair in range(width // (2 * HEAD)):
        cols = pl.ds(pair * 2 * HEAD, 2 * HEAD)
        queries = r.grads[6, tokens, cols] * jnp.asarray(scaling, SLIM)
        values = r.grads[8, tokens, cols]
        keys_turned = r.grads[7, tokens, cols].T
        incoming = r.held[:, cols]
        weight_grads = times_turned(jnp.concatenate([values * one, values * two], 0), incoming)
        score_grads, query_grads, weights = [], [], []
        for head in range(2):
            kept = r.weights[micro, 2 * pair + head]
            wide = kept.astype(WIDE)
            own = weight_grads[length * head : length * (head + 1)]
            score_grad = (wide * (own - jnp.sum(wide * own, 0, keepdims=True))).astype(SLIM)
            score_grads.append(score_grad)
            weights.append(kept)
            query_grads.append(
                (times(keys_turned[HEAD * head : HEAD * (head + 1)], score_grad) * scaling).astype(SLIM)
            )
        key_grad = times(jnp.concatenate(score_grads, 0), queries)
        value_grad = times(jnp.concatenate(weights, 0), incoming)
        r.grads[6, tokens, cols] = jnp.concatenate(query_grads, 0).T
        r.grads[7, tokens, cols] = (key_grad[:length] * first + key_grad[length:] * second).astype(SLIM)
        r.grads[8, tokens, cols] = (value_grad[:length] * first + value_grad[length:] * second).astype(SLIM)
    norm_grad = times_turned(r.grads[6, tokens, :], r.inward[:, 0:width])
    for part in range(1, 3):
        norm_grad += times_turned(r.grads[6 + part, tokens, :], r.inward[:, part * width : (part + 1) * width])
    r.total[...] = norm_grad
    input_grad = r.middle[micro] + norm_backward(r, r.stream[micro].astype(WIDE), r.total[...], 0)
    r.middle[micro] = input_grad
    r.passed[micro] = input_grad.astype(SLIM)


NAMES = (
    "x_in", "cot_in", "inward_in", "outward_in", "up_in", "down_in", "gain", "bias", "lengths", "offsets",
    "out_result", "out_grad", "out_down", "out_up", "out_outward", "out_inward", "out_norms",
    "stream", "inward", "outward", "up", "down", "grads", "acts", "acts_out", "weights", "middle", "normed", "held",
    "turned", "total", "result", "passed", "sums", "bias_mask",
    "partial", "y_in", "z_in", "far_y_in", "far_z_in", "staged", "norms",
    "load_sem", "source_sem", "store_sem", "unit_sem",
    "relay_send", "relay_recv", "acts_send", "acts_recv", "branch_send", "branch_recv", "grads_send", "grads_recv",
    "y_send", "y_recv", "z_send", "z_recv", "far_y_send", "far_y_recv", "far_z_send", "far_z_recv", "norm_send", "norm_recv",
)


def step_kernel(*refs):
    r = types.SimpleNamespace(**dict(zip(NAMES, refs)))
    section, dp = lax.axis_index("section"), lax.axis_index("dp")
    c, y, z = lax.rem(dp, 2), lax.rem(lax.div(dp, 2), 2), lax.div(dp, 4)
    r.c = c
    length = r.normed.shape[0]
    leading = section == 0
    pair_dp, y_dp = dp + 1 - 2 * c, dp + 2 - 4 * y

    def slot_of(core, micro):
        return pl.ds(pl.multiple_of((core * 2 + micro) * length, length), length)

    def remote(src, dst, send, recv, to_section, to_dp):
        return pltpu.make_async_remote_copy(
            src_ref=src, dst_ref=dst, send_sem=send, recv_sem=recv,
            device_id=(to_section, to_dp), device_id_type=MESH,
        )

    def local(src, dst, sem):
        return pltpu.make_async_copy(src, dst, sem)

    r.load_inward = local(r.inward_in.at[0], r.inward, r.load_sem.at[0])
    r.load_outward = local(r.outward_in.at[0], r.outward, r.load_sem.at[1])
    r.load_up = local(r.up_in.at[0], r.up, r.load_sem.at[2])
    r.load_down = local(r.down_in.at[0], r.down, r.load_sem.at[3])

    def load_x(micro):
        return local(r.x_in.at[micro, 0], r.stream.at[micro], r.source_sem.at[micro])

    def load_cot(micro):
        return local(r.cot_in.at[micro, 0], r.grads.at[0, slot_of(c, micro)], r.source_sem.at[micro])

    def relay_up(micro):
        return remote(r.result.at[micro], r.stream.at[micro], r.relay_send.at[micro], r.relay_recv.at[micro], 1 - section, dp)

    def relay_back(micro):
        return remote(
            r.passed.at[micro], r.grads.at[0, slot_of(c, micro)], r.relay_send.at[micro], r.relay_recv.at[micro], 1 - section, dp
        )

    def share_acts(micro, core=c):
        return remote(
            r.acts_out, r.acts.at[:, :, slot_of(core, micro)], r.acts_send.at[micro], r.acts_recv.at[micro], section, pair_dp
        )

    def share_branch(micro, core=c):
        rows = slot_of(core, micro)
        return remote(r.grads.at[0, rows], r.grads.at[0, rows], r.branch_send.at[micro], r.branch_recv.at[micro], section, pair_dp)

    def share_grads(micro, core=c):
        rows = slot_of(core, micro)
        return remote(
            r.grads.at[1:9, rows], r.grads.at[1:9, rows], r.grads_send.at[micro], r.grads_recv.at[micro], section, pair_dp
        )

    r.share_acts = share_acts

    def store_result(micro):
        return local(r.result.at[micro], r.out_result.at[micro], r.store_sem.at[0, micro])

    def store_grad(micro):
        return local(r.middle.at[micro], r.out_grad.at[micro], r.store_sem.at[1, micro])

    def to_y(unit):
        return remote(
            r.partial.at[unit, 0], r.y_in.at[unit - FAR], r.y_send.at[unit - FAR], r.y_recv.at[unit - FAR], section, y_dp
        )

    def rows_of(place):
        return pl.ds(BLOCK * place, BLOCK)

    def near_z(unit, place, index, lane, to_dp):
        near = unit - FAR
        return remote(
            r.partial.at[unit, 1, rows_of(place)], r.z_in.at[near, index],
            r.z_send.at[near, lane], r.z_recv.at[near, index], section, to_dp,
        )

    def far_z(unit, place, index, lane, to_dp):
        return remote(
            r.partial.at[unit, :, rows_of(place)], r.far_z_in.at[unit, index],
            r.far_z_send.at[unit, lane], r.far_z_recv.at[unit, index], section, to_dp,
        )

    def far_to_y(unit, place):
        return remote(
            r.partial.at[unit, 0, rows_of(place)], r.far_y_in.at[unit], r.far_y_send.at[unit], r.far_y_recv.at[unit], section, y_dp
        )

    def store_unit(unit):
        source, sem = r.staged.at[unit], r.unit_sem.at[unit]

        def part(out, base):
            return local(source, out.at[:, pl.ds(pl.multiple_of((unit - base) * COLUMNS, 128), COLUMNS)], sem)

        @pl.when(unit < 8)
        def _():
            rows = pl.ds(pl.multiple_of(lax.div(unit, 2) * BLOCK, 16), BLOCK)
            cols = pl.ds(pl.multiple_of(lax.rem(unit, 2) * COLUMNS, 128), COLUMNS)
            local(source, r.out_down.at[rows, cols], sem).start()

        @pl.when((unit >= 8) & (unit < 16))
        def _():
            part(r.out_up, 8).start()

        @pl.when((unit >= 16) & (unit < 18))
        def _():
            part(r.out_outward, 16).start()

        @pl.when(unit >= 18)
        def _():
            part(r.out_inward, 18).start()

    r.load_inward.start()

    @pl.when(leading)
    def _():
        load_x(0).start()
        load_x(1).start()

    @pl.when(jnp.logical_not(leading))
    def _():
        load_cot(0).start()
        load_cot(1).start()

    r.load_outward.start()
    r.load_up.start()
    r.load_down.start()
    r.sums[...] = jnp.zeros_like(r.sums)

    barrier = pltpu.get_barrier_semaphore()
    peers = [(1 - section, dp), (section, pair_dp), (section, y_dp)]
    peers += [(section, lax.rem(dp + 4 * hop, 16)) for hop in (1, 2, 3)]
    for peer in peers:
        pl.semaphore_signal(barrier, inc=1, device_id=peer, device_id_type=MESH)

    def everyone_in():
        pl.semaphore_wait(barrier, len(peers))

    def arrive(micro):
        relay_back(micro).wait_recv()
        share_branch(micro).start()

    def weight_operands(unit):
        whole = lax.div(unit, 2)
        slab = jnp.minimum(whole, 4) + jnp.where(whole >= 8, 1, 0) + jnp.where(whole >= 9, 1, 0)
        cols = pl.ds(pl.multiple_of(lax.rem(unit, 2) * COLUMNS, 128), COLUMNS)
        other = pl.ds(pl.multiple_of((1 - y) * 192, 64), 192)
        own = pl.ds(pl.multiple_of(y * 192, 64), 192)
        return slab, other, own, r.grads[jnp.maximum(whole - 3, 0), :, cols]

    def near_unit(unit):
        slab, other, own, grads = weight_operands(unit)
        r.partial[unit, 0] = times(r.acts[slab, other, :], grads).astype(SLIM)
        to_y(unit).start()
        r.partial[unit, 1] = times(r.acts[slab, own, :], grads).astype(SLIM)

    def far_unit(unit):
        slab, other, own, grads = weight_operands(unit)
        r.partial[unit, 0] = times(r.acts[slab, other, :], grads).astype(SLIM)
        r.partial[unit, 1] = times(r.acts[slab, own, :], grads).astype(SLIM)
        at_ends(unit, far_z, r.far_z_in)

    def arrived(unit, index, copy, into):
        copy(unit, 0, index, 0, dp).wait_recv()
        return into[unit if into is r.far_z_in else unit - FAR, index].astype(WIDE)

    def pick(unit, place, copy):
        return (unit, slice(None) if copy is far_z else 1, rows_of(place))

    def go_right(unit, here, copy, into):
        for place in range(3, here, -1):
            at = pick(unit, place, copy)
            if here > 0:
                r.partial[at] = (r.partial[at].astype(WIDE) + arrived(unit, place + 1, copy, into)).astype(SLIM)
            copy(unit, place, place + 1, place - 1, dp + 4).start()

    def go_left(unit, here, copy, into):
        for place in range(here):
            at = pick(unit, place, copy)
            if here < 3:
                r.partial[at] = (r.partial[at].astype(WIDE) + arrived(unit, place, copy, into)).astype(SLIM)
            copy(unit, place, place, place, dp - 4).start()

    def at_ends(unit, copy, into):
        @pl.when(z == 0)
        def _():
            go_right(unit, 0, copy, into)

        @pl.when(z == 3)
        def _():
            go_left(unit, 3, copy, into)

    def at_middle_first(unit, copy, into):
        @pl.when(z == 1)
        def _():
            go_right(unit, 1, copy, into)

        @pl.when(z == 2)
        def _():
            go_left(unit, 2, copy, into)

    def at_middle_second(unit, copy, into):
        @pl.when(z == 1)
        def _():
            go_left(unit, 1, copy, into)

        @pl.when(z == 2)
        def _():
            go_right(unit, 2, copy, into)

    def gathered(unit, here, copy, into):
        value = r.partial[pick(unit, here, copy)].astype(WIDE)
        if here > 0:
            value = value + arrived(unit, here + 1, copy, into)
        if here < 3:
            value = value + arrived(unit, here, copy, into)
        return value

    def everywhere(action):
        for here in range(4):

            @pl.when(z == here)
            def _():
                action(here)

    def slot(t, carry):
        trailing = jnp.logical_not(leading)
        half = lax.div(t, 2)
        is_forward = (leading & (t < 2)) | (trailing & ((t == 1) | (t == 3)))
        is_backward = (leading & ((t == 3) | (t == 5))) | (trailing & ((t == 2) | (t == 4)))
        is_weights = (leading & (t == 4)) | (trailing & (t == 5))

        @pl.when(trailing & (t == 0))
        def _():
            everyone_in()
            for micro in range(2):
                load_cot(micro).wait()
                share_branch(micro).start()

        @pl.when(is_forward)
        def _():
            micro = jnp.where(leading, jnp.minimum(t, 1), jnp.minimum(half, 1))

            @pl.when(leading)
            def _():
                load_x(micro).wait()

            @pl.when(trailing)
            def _():
                relay_up(micro).wait_recv()

            forward(r, micro, pl.multiple_of((c * 2 + micro) * length, length), t == section)

            @pl.when(leading & (t == 0))
            def _():
                everyone_in()

            @pl.when(leading)
            def _():
                relay_up(micro).start()

            share_acts(micro).start()
            store_result(micro).start()

        @pl.when(leading & (t == 3))
        def _():
            arrive(0)

        @pl.when(is_backward)
        def _():
            micro = jnp.clip(half - 1, 0, 1)
            backward(r, micro, pl.multiple_of((c * 2 + micro) * length, length))

            @pl.when(trailing)
            def _():
                relay_back(micro).start()

            share_grads(micro).start()
            store_grad(micro).start()

        @pl.when(leading & (t == 4))
        def _():
            arrive(1)

        @pl.when(is_weights)
        def _():
            for micro in range(2):
                share_branch(micro, 1 - c).wait_recv()
                share_acts(micro, 1 - c).wait_recv()

            def body(i, carry):
                near_unit(FAR + i)
                far_unit(i)
                return carry

            lax.fori_loop(0, FAR, body, 0)

        return carry

    lax.fori_loop(0, 6, slot, 0)

    def norm_copy(src, dst, index, to_dp):
        return remote(r.norms.at[src], r.norms.at[dst], r.norm_send.at[index], r.norm_recv.at[index], section, to_dp)

    def norm_to_pair():
        return norm_copy(0, 1, 0, pair_dp)

    def norm_to_y():
        return norm_copy(2, 3, 1, y_dp)

    def norm_to_z(hop):
        return norm_copy(4, 4 + hop, 1 + hop, lax.rem(dp + 4 * hop, 16))

    r.norms[0] = jnp.concatenate([jnp.sum(r.sums[...], 1), jnp.zeros((4, r.sums.shape[2]), WIDE)], 0)
    norm_to_pair().start()
    norm_to_pair().wait_recv()
    r.norms[2] = r.norms[0] + r.norms[1]
    norm_to_y().start()
    for micro in range(2):
        share_grads(micro, 1 - c).wait_recv()

    def sum_y(unit):
        to_y(unit).wait_recv()
        r.partial[unit, 1] = (r.partial[unit, 1].astype(WIDE) + r.y_in[unit - FAR].astype(WIDE)).astype(SLIM)

    def advance(i, carry):
        @pl.when(i < UNITS - EARLY)
        def _():
            near_unit(EARLY + i)

        @pl.when(i < NEAR)
        def _():
            sum_y(FAR + i)
            at_ends(FAR + i, near_z, r.z_in)

        half = lax.div(i, 2)
        odd = lax.rem(i, 2) == 1

        @pl.when(odd & (i < 2 * FAR))
        def _():
            at_middle_first(half, far_z, r.far_z_in)

        @pl.when(jnp.logical_not(odd) & (i >= 4) & (i < 4 + 2 * FAR))
        def _():
            at_middle_second(half - 2, far_z, r.far_z_in)

        @pl.when(odd & (i >= 7) & (i < 7 + 2 * FAR))
        def _():
            def action(here):
                unit = half - 3
                value = gathered(unit, here, far_z, r.far_z_in)
                r.partial[unit, 0, rows_of(here)] = value[0].astype(SLIM)
                far_to_y(unit, here).start()
                r.staged[unit] = value[1]

            everywhere(action)

        @pl.when(jnp.logical_not(odd) & (i >= 10) & (i < 10 + 2 * FAR))
        def _():
            unit = half - 5
            far_to_y(unit, 0).wait_recv()
            r.staged[unit] += r.far_y_in[unit].astype(WIDE)
            store_unit(unit)

        @pl.when((i >= 1) & (i < NEAR + 1))
        def _():
            at_middle_first(FAR + i - 1, near_z, r.z_in)

        @pl.when((i >= 2) & (i < NEAR + 2))
        def _():
            at_middle_second(FAR + i - 2, near_z, r.z_in)

        @pl.when(i >= 3)
        def _():
            def action(here):
                r.staged[FAR + i - 3] = gathered(FAR + i - 3, here, near_z, r.z_in)

            everywhere(action)
            store_unit(FAR + i - 3)

        @pl.when(i == 4)
        def _():
            norm_to_y().wait_recv()
            r.norms[4] = r.norms[2] + r.norms[3]
            for hop in (1, 2, 3):
                norm_to_z(hop).start()

        @pl.when(i == 18)
        def _():
            for hop in (1, 2, 3):
                norm_to_z(hop).wait_recv()
            r.norms[0] = (r.norms[4] + r.norms[5]) + (r.norms[6] + r.norms[7])
            local(r.norms.at[0], r.out_norms, r.store_sem.at[2, 0]).start()

        return carry

    norm_to_pair().wait_send()
    lax.fori_loop(0, NEAR + 3, advance, 0)

    norm_to_y().wait_send()
    for hop in (1, 2, 3):
        norm_to_z(hop).wait_send()
    share_acts(1).wait_send()
    for micro in range(2):
        share_branch(micro).wait_send()
        share_grads(micro).wait_send()
        store_result(micro).wait()
        store_grad(micro).wait()

        @pl.when(leading)
        def _():
            relay_up(micro).wait_send()

        @pl.when(jnp.logical_not(leading))
        def _():
            relay_back(micro).wait_send()

    def drain_near(near, carry):
        to_y(FAR + near).wait_send()
        for lane in range(3):
            near_z(FAR + near, 0, 0, lane, dp).wait_send()
        return carry

    lax.fori_loop(0, NEAR, drain_near, 0)

    def drain_far(unit, carry):
        far_to_y(unit, 0).wait_send()
        for lane in range(3):
            far_z(unit, 0, 0, lane, dp).wait_send()
        return carry

    lax.fori_loop(0, FAR, drain_far, 0)

    def drain_store(unit, carry):
        local(r.staged.at[unit], r.out_outward.at[:, 0:COLUMNS], r.unit_sem.at[unit]).wait()
        return carry

    lax.fori_loop(0, UNITS, drain_store, 0)
    local(r.norms.at[0], r.out_norms, r.store_sem.at[2, 0]).wait()


def hand_over_kernel(*refs):
    sources, norms, targets = refs[:6], refs[6], refs[7:13]
    gain_grad, bias_grad, held, in_sem, out_sem = refs[13], refs[14], refs[15:21], refs[21], refs[22]
    loads = [pltpu.make_async_copy(a, b, in_sem.at[k]) for k, (a, b) in enumerate(zip(sources, held))]
    stores = [pltpu.make_async_copy(a, b, out_sem.at[k]) for k, (a, b) in enumerate(zip(held, targets))]
    for load in loads:
        load.start()
    share = gain_grad.shape[2]
    for index in range(norms.shape[1] // share):

        @pl.when(lax.axis_index("dp") == index)
        def _():
            gain_grad[0] = norms[0:2, index * share : (index + 1) * share]
            bias_grad[0] = norms[2:4, index * share : (index + 1) * share]

    for load, store in zip(loads, stores):
        load.wait()
        store.start()
    for store in stores:
        store.wait()


def step_on_device(
    inputs, clip_lengths, anchor_offsets, cotangent, inward_weight, outward_weight, up_weight, down_weight, norm_gain, norm_bias
):
    _, _, length, width = inputs.shape
    wide_ff = up_weight.shape[2]
    anywhere = pl.BlockSpec(memory_space=pl.ANY)
    in_vmem = pl.BlockSpec(memory_space=pltpu.VMEM)
    in_smem = pl.BlockSpec(memory_space=pltpu.SMEM)
    dma = pltpu.SemaphoreType.DMA
    share = width // lax.axis_size("dp")
    shapes = [
        jax.ShapeDtypeStruct((2, length, width), SLIM),
        jax.ShapeDtypeStruct((2, length, width), WIDE),
        jax.ShapeDtypeStruct((4 * BLOCK, width), WIDE),
        jax.ShapeDtypeStruct((BLOCK, wide_ff), WIDE),
        jax.ShapeDtypeStruct((BLOCK, width), WIDE),
        jax.ShapeDtypeStruct((BLOCK, 3 * width), WIDE),
    ]
    made = pl.pallas_call(
        step_kernel,
        out_shape=(*shapes, jax.ShapeDtypeStruct((8, width), WIDE)),
        in_specs=[anywhere] * 6 + [in_vmem] * 2 + [in_smem] * 2,
        out_specs=[anywhere] * 7,
        scratch_shapes=[
            pltpu.VMEM((2, length, width), SLIM),
            pltpu.VMEM((width, 3 * width), SLIM),
            pltpu.VMEM((width, width), SLIM),
            pltpu.VMEM((width, wide_ff), SLIM),
            pltpu.VMEM((wide_ff, width), SLIM),
            pltpu.VMEM((9, 4 * length, width), SLIM),
            pltpu.VMEM((7, 8 * BLOCK, 4 * length), SLIM),
            pltpu.VMEM((7, 8 * BLOCK, length), SLIM),
            pltpu.VMEM((2, width // HEAD, length, length), SLIM),
            pltpu.VMEM((2, length, width), WIDE),
            pltpu.VMEM((length, width), SLIM),
            pltpu.VMEM((length, width), SLIM),
            pltpu.VMEM((width, length), SLIM),
            pltpu.VMEM((length, width), WIDE),
            pltpu.VMEM((2, length, width), SLIM),
            pltpu.VMEM((2, length, width), SLIM),
            pltpu.VMEM((4, 8, width), WIDE),
            pltpu.VMEM((length, length), WIDE),
            pltpu.VMEM((UNITS, 2, 4 * BLOCK, COLUMNS), SLIM),
            pltpu.VMEM((NEAR, 4 * BLOCK, COLUMNS), SLIM),
            pltpu.VMEM((NEAR, 5, BLOCK, COLUMNS), SLIM),
            pltpu.VMEM((FAR, BLOCK, COLUMNS), SLIM),
            pltpu.VMEM((FAR, 5, 2, BLOCK, COLUMNS), SLIM),
            pltpu.VMEM((UNITS, BLOCK, COLUMNS), WIDE),
            pltpu.VMEM((8, 8, width), WIDE),
            dma((4,)), dma((2,)), dma((3, 2)), dma((UNITS,)),
            dma((2,)), dma((2,)), dma((2,)), dma((2,)), dma((2,)), dma((2,)), dma((2,)), dma((2,)),
            dma((NEAR,)), dma((NEAR,)), dma((NEAR, 3)), dma((NEAR, 5)),
            dma((FAR,)), dma((FAR,)), dma((FAR, 3)), dma((FAR, 5)), dma((5,)), dma((5,)),
        ],
        compiler_params=pltpu.CompilerParams(
            collective_id=0, has_side_effects=True, vmem_limit_bytes=VMEM_BYTES
        ),
    )(
        inputs, cotangent, inward_weight, outward_weight, up_weight, down_weight,
        norm_gain, norm_bias, clip_lengths, anchor_offsets,
    )
    result, grad, down, up, outward, inward, gain_grad, bias_grad = pl.pallas_call(
        hand_over_kernel,
        out_shape=(*shapes, *[jax.ShapeDtypeStruct((1, 2, share), WIDE)] * 2),
        in_specs=[anywhere] * 6 + [in_vmem],
        out_specs=[anywhere] * 6 + [in_vmem] * 2,
        scratch_shapes=[pltpu.VMEM(shape.shape, shape.dtype) for shape in shapes] + [dma((6,)), dma((6,))],
    )(*made)
    return (
        result[None, :, None],
        grad[None, :, None],
        inward[None],
        outward[None],
        up[None],
        down[None],
        gain_grad,
        bias_grad,
    )


def shifted(x, axis, by):
    size = lax.axis_size(axis)
    pairs = [(i, i + by) for i in range(size) if 0 <= i + by < size]
    return lax.ppermute(x, axis, pairs)


def norm_rows(values, norm_gain, norm_bias):
    average = jnp.mean(values, -1, keepdims=True)
    centred = values - average
    inverse = lax.rsqrt(jnp.mean(centred * centred, -1, keepdims=True) + EPSILON)
    normed = centred * inverse
    return (normed * norm_gain + norm_bias, normed, inverse)


def norm_back(norm_grad, normed, inverse, norm_gain):
    inner = norm_grad * norm_gain
    through = inverse * (
        inner
        - jnp.mean(inner, -1, keepdims=True)
        - normed * jnp.mean(inner * normed, -1, keepdims=True)
    )
    return (through, jnp.sum(norm_grad * normed, 0), jnp.sum(norm_grad, 0))


def gelu_slope(lifted):
    cumulative = 0.5 * (1.0 + lax.erf(lifted * 0.7071067811865476))
    density = jnp.exp(-0.5 * lifted * lifted) * 0.3989422804014327
    return cumulative + lifted * density


def clip_marks(lengths, offsets, length):
    positions = jnp.arange(length, dtype=jnp.int32)
    clip_ends = jnp.cumsum(lengths)
    clip_starts = clip_ends - lengths
    anchor_at = clip_starts + offsets % lengths
    clip_ids = jnp.sum((positions[:, None] >= clip_ends[None, :]).astype(jnp.int32), 1)
    anchors = jnp.any(positions[:, None] == anchor_at[None, :], 1)
    return (clip_ids, anchors)


def masked_scores(query_block, key_rows, id_block, clip_ids, anchors, scaling):
    scores = (
        jnp.einsum("qhd,khd->hqk", query_block, key_rows, preferred_element_type=jnp.float32)
        * scaling
    )
    seen = (id_block[:, None] == clip_ids[None, :]) | anchors[None, :]
    return jnp.where(seen[None], scores, -1000000000.0)


def forward_layer(source, clip_ids, anchors, params):
    inward, outward, upward, downward, norm_gain, norm_bias = params
    length, model_width = source.shape
    head_count = model_width // HEAD
    scaling = HEAD ** (-0.5)
    residual = source.astype(jnp.float32)
    first_norm, unit_one, scale_one = norm_rows(residual, norm_gain[0], norm_bias[0])
    joined = jnp.dot(
        first_norm.astype(jnp.bfloat16), inward, preferred_element_type=jnp.float32
    ).astype(jnp.bfloat16)
    heads_view = joined.reshape(length, 3, head_count, HEAD)
    queries = heads_view[:, 0]
    key_rows = heads_view[:, 1]
    values = heads_view[:, 2]
    scores = masked_scores(queries, key_rows, clip_ids, clip_ids, anchors, scaling)
    row_max = jnp.max(scores, -1, keepdims=True)
    raised = jnp.exp(scores - row_max)
    row_sum = jnp.sum(raised, -1, keepdims=True)
    weights = (raised / row_sum).astype(jnp.bfloat16)
    pieces = [jnp.einsum("hqk,khd->qhd", weights, values, preferred_element_type=jnp.float32)]
    log_sums = [(row_max + jnp.log(row_sum))[..., 0]]
    attended = jnp.concatenate(pieces, 0).reshape(length, model_width).astype(jnp.bfloat16)
    logsum = jnp.concatenate(log_sums, 1)
    middle = residual + jnp.dot(attended, outward, preferred_element_type=jnp.float32)
    second_norm, unit_two, scale_two = norm_rows(middle, norm_gain[1], norm_bias[1])
    lifted = jnp.dot(second_norm.astype(jnp.bfloat16), upward, preferred_element_type=jnp.float32)
    active = jax.nn.gelu(lifted, approximate=False).astype(jnp.bfloat16)
    result = middle + jnp.dot(active, downward, preferred_element_type=jnp.float32)
    stored = (unit_one, scale_one, joined, logsum, attended, unit_two, scale_two, lifted, active)
    return (result, stored)


def contract_rows(left, right):
    return lax.dot_general(
        left, right, (((0,), (0,)), ((), ())), preferred_element_type=jnp.float32
    )


def contract_cols(left, right):
    return lax.dot_general(
        left, right, (((1,), (1,)), ((), ())), preferred_element_type=jnp.float32
    )


def feed_backward(incoming, stored, params):
    inward, outward, upward, downward, norm_gain, norm_bias = params
    unit_one, scale_one, joined, logsum, attended, unit_two, scale_two, lifted, active = stored
    branch = incoming.astype(jnp.bfloat16)
    down_part = contract_rows(active, branch)
    hidden_grad = contract_cols(branch, downward)
    lifted_grad = (hidden_grad * gelu_slope(lifted)).astype(jnp.bfloat16)
    second_in = (unit_two * norm_gain[1] + norm_bias[1]).astype(jnp.bfloat16)
    up_part = contract_rows(second_in, lifted_grad)
    normed_grad = contract_cols(lifted_grad, upward)
    through, gain_two, bias_two = norm_back(normed_grad, unit_two, scale_two, norm_gain[1])
    return (incoming + through, (up_part, down_part, gain_two, bias_two))


def attend_backward(middle_grad, stored, clip_ids, anchors, params):
    inward, outward, upward, downward, norm_gain, norm_bias = params
    unit_one, scale_one, joined, logsum, attended, unit_two, scale_two, lifted, active = stored
    length, model_width = attended.shape
    head_count = model_width // HEAD
    scaling = HEAD ** (-0.5)
    branch = middle_grad.astype(jnp.bfloat16)
    outward_part = contract_rows(attended, branch)
    attended_grad = (
        contract_cols(branch, outward).astype(jnp.bfloat16).reshape(length, head_count, HEAD)
    )
    heads_view = joined.reshape(length, 3, head_count, HEAD)
    queries = heads_view[:, 0]
    key_rows = heads_view[:, 1]
    values = heads_view[:, 2]
    key_grad = jnp.zeros((length, head_count, HEAD), jnp.float32)
    value_grad = jnp.zeros((length, head_count, HEAD), jnp.float32)
    block_rows = min(512, length)
    scores = masked_scores(queries, key_rows, clip_ids, clip_ids, anchors, scaling)
    weights = jnp.exp(scores - logsum[:, 0:block_rows, None])
    weight_grad = jnp.einsum(
        "qhd,khd->hqk", attended_grad, values, preferred_element_type=jnp.float32
    )
    score_grad = (
        weights * (weight_grad - jnp.sum(weights * weight_grad, -1, keepdims=True))
    ).astype(jnp.bfloat16)
    query_pieces = [
        scaling
        * jnp.einsum("hqk,khd->qhd", score_grad, key_rows, preferred_element_type=jnp.float32)
    ]
    key_grad = key_grad + scaling * jnp.einsum(
        "hqk,qhd->khd", score_grad, queries, preferred_element_type=jnp.float32
    )
    value_grad = value_grad + jnp.einsum(
        "hqk,qhd->khd",
        weights.astype(jnp.bfloat16),
        attended_grad,
        preferred_element_type=jnp.float32,
    )
    query_grad = jnp.concatenate(query_pieces, 0)
    joined_grad = (
        jnp.stack([query_grad, key_grad, value_grad], 1)
        .reshape(length, 3 * model_width)
        .astype(jnp.bfloat16)
    )
    first_in = (unit_one * norm_gain[0] + norm_bias[0]).astype(jnp.bfloat16)
    inward_part = contract_rows(first_in, joined_grad)
    normed_grad = contract_cols(joined_grad, inward)
    through, gain_one, bias_one = norm_back(normed_grad, unit_one, scale_one, norm_gain[0])
    return (middle_grad + through, (inward_part, outward_part, gain_one, bias_one))


def resting(function):

    def blank(*operands):
        return jax.tree.map(jnp.zeros_like, function(*operands))

    return blank


def take_slot(holder, buffer_slot):
    return jax.tree.map(
        lambda element: lax.dynamic_index_in_dim(element, buffer_slot, 0, False), holder
    )


def place_slot(holder, item, buffer_slot, working):

    def update(element, fresh):
        former = lax.dynamic_index_in_dim(element, buffer_slot, 0, False)
        return lax.dynamic_update_index_in_dim(
            element, jnp.where(working, fresh, former), buffer_slot, 0
        )

    return jax.tree.map(update, holder, item)


def per_device(
    inputs,
    clip_lengths,
    anchor_offsets,
    cotangent,
    inward_weight,
    outward_weight,
    up_weight,
    down_weight,
    norm_gain,
    norm_bias,
):
    params = (
        inward_weight[0],
        outward_weight[0],
        up_weight[0],
        down_weight[0],
        norm_gain[0],
        norm_bias[0],
    )
    stream = inputs[:, 0]
    cot_rows = cotangent[:, 0]
    lengths_all = clip_lengths[:, 0]
    offsets_all = anchor_offsets[:, 0]
    micro_count = stream.shape[0]
    length = stream.shape[1]
    section_index = lax.axis_index("section")
    section_count = lax.axis_size("section")
    leading = section_index == 0
    trailing = section_index == section_count - 1
    periods = micro_count + section_count - 1
    arriving = jnp.zeros_like(stream[0])
    produced = jnp.zeros_like(stream)
    archive = None
    for period in range(periods):
        micro_index = period - section_index
        working = (micro_index >= 0) & (micro_index < micro_count)
        buffer_slot = jnp.clip(micro_index, 0, micro_count - 1)
        source = jnp.where(leading, stream[min(period, micro_count - 1)], arriving)
        clip_ids, anchors = clip_marks(
            take_slot(lengths_all, buffer_slot), take_slot(offsets_all, buffer_slot), length
        )
        result, stored = lax.cond(
            working, forward_layer, resting(forward_layer), source, clip_ids, anchors, params
        )
        if archive is None:
            archive = jax.tree.map(
                lambda element: jnp.zeros((micro_count,) + element.shape, element.dtype), stored
            )
        archive = place_slot(archive, stored, buffer_slot, working)
        sending = result.astype(jnp.bfloat16)
        produced = place_slot(produced, sending, buffer_slot, working)
        if period < micro_count:
            arriving = shifted(sending, "section", 1)
    inward, outward, upward, downward, gains, biases = params
    up_sum = jnp.zeros(upward.shape, jnp.float32)
    down_sum = jnp.zeros(downward.shape, jnp.float32)
    gain_two = jnp.zeros(gains.shape[1:], jnp.float32)
    bias_two = jnp.zeros(biases.shape[1:], jnp.float32)
    inward_sum = jnp.zeros(inward.shape, jnp.float32)
    outward_sum = jnp.zeros(outward.shape, jnp.float32)
    gain_one = jnp.zeros(gains.shape[1:], jnp.float32)
    bias_one = jnp.zeros(biases.shape[1:], jnp.float32)
    upstream = jnp.zeros_like(stream[0])
    returned = jnp.zeros(stream.shape, jnp.float32)
    for period in range(periods):
        micro_index = micro_count - 1 - period + (section_count - 1 - section_index)
        working = (micro_index >= 0) & (micro_index < micro_count)
        buffer_slot = jnp.clip(micro_index, 0, micro_count - 1)
        incoming = jnp.where(trailing, take_slot(cot_rows, buffer_slot), upstream).astype(
            jnp.float32
        )
        clip_ids, anchors = clip_marks(
            take_slot(lengths_all, buffer_slot), take_slot(offsets_all, buffer_slot), length
        )
        stored = take_slot(archive, buffer_slot)
        middle_grad, feed_part = lax.cond(
            working, feed_backward, resting(feed_backward), incoming, stored, params
        )
        up_sum = up_sum + feed_part[0]
        down_sum = down_sum + feed_part[1]
        gain_two = gain_two + feed_part[2]
        bias_two = bias_two + feed_part[3]
        input_grad, attend_part = lax.cond(
            working,
            attend_backward,
            resting(attend_backward),
            middle_grad,
            stored,
            clip_ids,
            anchors,
            params,
        )
        inward_sum = inward_sum + attend_part[0]
        outward_sum = outward_sum + attend_part[1]
        gain_one = gain_one + attend_part[2]
        bias_one = bias_one + attend_part[3]
        returned = place_slot(returned, input_grad, buffer_slot, working)
        if period < periods - 1:
            upstream = shifted(input_grad.astype(jnp.bfloat16), "section", -1)
    inward_sum, outward_sum, up_sum, down_sum, gain_one, gain_two, bias_one, bias_two = (
        lax.psum_scatter(inward_sum, "dp", scatter_dimension=0, tiled=True),
        lax.psum_scatter(outward_sum, "dp", scatter_dimension=0, tiled=True),
        lax.psum_scatter(up_sum, "dp", scatter_dimension=0, tiled=True),
        lax.psum_scatter(down_sum, "dp", scatter_dimension=0, tiled=True),
        lax.psum_scatter(gain_one, "dp", scatter_dimension=0, tiled=True),
        lax.psum_scatter(gain_two, "dp", scatter_dimension=0, tiled=True),
        lax.psum_scatter(bias_one, "dp", scatter_dimension=0, tiled=True),
        lax.psum_scatter(bias_two, "dp", scatter_dimension=0, tiled=True),
    )
    layer_outputs = produced[None, :, None]
    input_grads = returned[None, :, None]
    gain_grad = jnp.stack([gain_one, gain_two])[None]
    bias_grad = jnp.stack([bias_one, bias_two])[None]
    return (
        layer_outputs,
        input_grads,
        inward_sum[None],
        outward_sum[None],
        up_sum[None],
        down_sum[None],
        gain_grad,
        bias_grad,
    )


def solution(mesh):
    local = step_on_device if mesh.shape["dp"] == 16 and mesh.shape["section"] == 2 else per_device
    return jax.shard_map(
        local,
        mesh=mesh,
        in_specs=(
            P(None, "dp", None, None),
            P(None, "dp", None),
            P(None, "dp", None),
            P(None, "dp", None, None),
            P("section", None, None),
            P("section", None, None),
            P("section", None, None),
            P("section", None, None),
            P("section", None, None),
            P("section", None, None),
        ),
        out_specs=(
            P("section", None, "dp", None, None),
            P("section", None, "dp", None, None),
            P("section", "dp", None),
            P("section", "dp", None),
            P("section", "dp", None),
            P("section", "dp", None),
            P("section", None, "dp"),
            P("section", None, "dp"),
        ),
        check_vma=False,
    )
```

```python
import functools
import types

import jax
import jax.numpy as jnp
from jax import lax
from jax.experimental import pallas as pl
from jax.experimental.pallas import tpu as pltpu
from jax.sharding import PartitionSpec as P

HEAD = 64
EPSILON = 1e-06
MESH = pl.DeviceIdType.MESH
WIDE = jnp.float32
SLIM = jnp.bfloat16
VMEM_BYTES = 67043328

UNITS = 24
FAR = 4
NEAR = UNITS - FAR
BLOCK = 48
COLUMNS = 384
EARLY_NEAR = 4
HOLD = 1
LAGS = (2, 3, 4)
FAR_AT = (-1, -1, 3, 8)
FAR_FIRST = (2, 4, 10, 15)
FAR_SECOND = (5, 15, 14, 20)
FAR_ARRIVED = (17, 18, 20, 21)
FAR_DONE = (20, 21, 22, 23)


def times(left, right):
    return jnp.dot(left, right, preferred_element_type=WIDE)


def times_turned(left, right):
    return lax.dot_general(left, right, (((1,), (1,)), ((), ())), preferred_element_type=WIDE)


def unit_rows(values):
    centred = values - jnp.mean(values, -1, keepdims=True)
    inverse = lax.rsqrt(jnp.mean(centred * centred, -1, keepdims=True) + EPSILON)
    return centred * inverse, inverse


def norm_rows_bf16(r, values, which):
    unit, _ = unit_rows(values)
    return (unit * r.gain[0, which : which + 1, :] + r.bias[0, which : which + 1, :]).astype(SLIM)


def norm_backward(r, values, norm_grad, which):
    unit, inverse = unit_rows(values)
    width = values.shape[1]
    r.sums[which] += jnp.sum((norm_grad * unit).reshape(-1, 8, width), 0)
    r.sums[2 + which] += jnp.sum(norm_grad.reshape(-1, 8, width), 0)
    inner = norm_grad * r.gain[0, which : which + 1, :]
    return inverse * (
        inner
        - jnp.mean(inner, -1, keepdims=True)
        - unit * jnp.mean(inner * unit, -1, keepdims=True)
    )


def head_lanes():
    lane = lax.broadcasted_iota(jnp.int32, (1, 2 * HEAD), 1)
    first = jnp.where(lane < HEAD, 1.0, 0.0).astype(WIDE)
    return first, 1.0 - first


def mask_bias(r, micro):
    length = r.bias_mask.shape[0]

    def marks(positions):
        end = jnp.int32(0)
        ids = jnp.zeros(positions.shape, jnp.int32)
        anchors = jnp.zeros(positions.shape, jnp.int32)
        for clip in range(r.lengths.shape[2]):
            size = r.lengths[micro, 0, clip]
            anchor = end + lax.rem(r.offsets[micro, 0, clip], size)
            end = end + size
            ids = ids + jnp.where(positions >= end, 1, 0)
            anchors = anchors + jnp.where(positions == anchor, 1, 0)
        return ids, anchors

    key_ids, anchors = marks(lax.broadcasted_iota(jnp.int32, (length, 1), 0))
    query_ids, _ = marks(lax.broadcasted_iota(jnp.int32, (1, length), 1))
    seen = (key_ids == query_ids) | (jnp.broadcast_to(anchors, (length, length)) > 0)
    r.bias_mask[...] = jnp.where(seen, 0.0, -1000000000.0).astype(WIDE)


def place(r, slab, tokens):
    for line in range(8):
        z, y = line // 2, line % 2
        rows = pl.ds(y * 192 + z * BLOCK, BLOCK)
        own = pl.ds(pl.multiple_of(2 * BLOCK * line + r.c * BLOCK, 16), BLOCK)
        other = pl.ds(pl.multiple_of(2 * BLOCK * line + (1 - r.c) * BLOCK, 16), BLOCK)
        r.acts[slab, rows, tokens] = r.turned[own, :]
        r.acts_out[slab, rows, :] = r.turned[other, :]


def forward(r, micro, tok, first, leading):
    length, width = r.normed.shape
    tokens = pl.ds(tok, length)
    mask_bias(r, micro)
    r.normed[...] = norm_rows_bf16(r, r.stream[micro].astype(WIDE), 0)

    @pl.when(first)
    def _():
        r.load_inward.wait()

        @pl.when(leading)
        def _():
            r.load_rest()

    for part in range(3):
        r.grads[6 + part, tokens, :] = times(
            r.normed[...], r.inward[:, part * width : (part + 1) * width]
        ).astype(SLIM)

    @pl.when(micro > 0)
    def _():
        r.share_acts(0).wait_send()

    r.turned[...] = r.normed[...].T
    place(r, 6, tokens)
    one, two = (lanes.astype(SLIM) for lanes in head_lanes())
    for pair in range(width // (2 * HEAD)):
        cols = pl.ds(pair * 2 * HEAD, 2 * HEAD)
        queries = r.grads[6, tokens, cols] * jnp.asarray(HEAD**-0.5, SLIM)
        keys = r.grads[7, tokens, cols]
        values_turned = r.grads[8, tokens, cols].T
        scores = times_turned(jnp.concatenate([keys * one, keys * two], 0), queries)
        pieces = []
        for head in range(2):
            masked = scores[length * head : length * (head + 1)] + r.bias_mask[...]
            raised = jnp.exp(masked - jnp.max(masked, 0, keepdims=True))
            weights = (raised * (1.0 / jnp.sum(raised, 0, keepdims=True))).astype(SLIM)
            r.weights[micro, 2 * pair + head] = weights
            pieces.append(times(values_turned[HEAD * head : HEAD * (head + 1)], weights).astype(SLIM))
        attended_turned = jnp.concatenate(pieces, 0)
        r.turned[cols, :] = attended_turned
        r.held[:, cols] = attended_turned.T
    place(r, 5, tokens)

    @pl.when(first)
    def _():
        r.load_outward.wait()

    r.middle[micro] = r.stream[micro].astype(WIDE) + times(r.held[...], r.outward[...])
    r.normed[...] = norm_rows_bf16(r, r.middle[micro], 1)
    r.turned[...] = r.normed[...].T
    place(r, 4, tokens)
    r.total[...] = r.middle[micro]

    @pl.when(first)
    def _():
        r.load_up.wait()
        r.load_down.wait()

    for part in range(4):
        cols = slice(part * width, (part + 1) * width)
        lifted = times(r.normed[...], r.up[:, cols])
        cumulative = 0.5 * (1.0 + lax.erf(lifted * 0.7071067811865476))
        density = jnp.exp(-0.5 * lifted * lifted) * 0.3989422804014327
        r.grads[1 + part, tokens, :] = (cumulative + lifted * density).astype(SLIM)
        active = (lifted * cumulative).astype(SLIM)
        r.total[...] += times(active, r.down[cols, :])
        r.turned[...] = active.T
        for y in range(2):
            for piece in range(4):
                rows = pl.ds(y * 192 + part * BLOCK, BLOCK)
                start = 384 * y + BLOCK * piece
                own = pl.ds(pl.multiple_of(start + r.c * 192, 16), BLOCK)
                other = pl.ds(pl.multiple_of(start + (1 - r.c) * 192, 16), BLOCK)
                r.acts[piece, rows, tokens] = r.turned[own, :]
                r.acts_out[piece, rows, :] = r.turned[other, :]
    r.result[micro] = r.total[...].astype(SLIM)


def backward(r, micro, tok):
    length, width = r.normed.shape
    tokens = pl.ds(tok, length)
    r.total[...] = jnp.zeros((length, width), WIDE)
    for part in range(4):
        cols = slice(part * width, (part + 1) * width)
        hidden = times_turned(r.grads[0, tokens, :], r.down[cols, :])
        lifted_grad = (hidden * r.grads[1 + part, tokens, :].astype(WIDE)).astype(SLIM)
        r.grads[1 + part, tokens, :] = lifted_grad
        r.total[...] += times_turned(lifted_grad, r.up[:, cols])
    r.share_lifted(micro).start()
    middle_grad = r.grads[0, tokens, :].astype(WIDE) + norm_backward(
        r, r.middle[micro], r.total[...], 1
    )
    r.middle[micro] = middle_grad
    r.grads[5, tokens, :] = middle_grad.astype(SLIM)
    r.held[...] = times_turned(r.grads[5, tokens, :], r.outward[...]).astype(SLIM)
    first, second = head_lanes()
    one, two = first.astype(SLIM), second.astype(SLIM)
    scaling = HEAD**-0.5
    for pair in range(width // (2 * HEAD)):
        cols = pl.ds(pair * 2 * HEAD, 2 * HEAD)
        queries = r.grads[6, tokens, cols] * jnp.asarray(scaling, SLIM)
        values = r.grads[8, tokens, cols]
        keys_turned = r.grads[7, tokens, cols].T
        incoming = r.held[:, cols]
        weight_grads = times_turned(jnp.concatenate([values * one, values * two], 0), incoming)
        score_grads, query_grads, weights = [], [], []
        for head in range(2):
            kept = r.weights[micro, 2 * pair + head]
            wide = kept.astype(WIDE)
            own = weight_grads[length * head : length * (head + 1)]
            score_grad = (wide * (own - jnp.sum(wide * own, 0, keepdims=True))).astype(SLIM)
            score_grads.append(score_grad)
            weights.append(kept)
            query_grads.append(
                (times(keys_turned[HEAD * head : HEAD * (head + 1)], score_grad) * scaling).astype(SLIM)
            )
        key_grad = times(jnp.concatenate(score_grads, 0), queries)
        value_grad = times(jnp.concatenate(weights, 0), incoming)
        r.grads[6, tokens, cols] = jnp.concatenate(query_grads, 0).T
        r.grads[7, tokens, cols] = (key_grad[:length] * first + key_grad[length:] * second).astype(SLIM)
        r.grads[8, tokens, cols] = (value_grad[:length] * first + value_grad[length:] * second).astype(SLIM)
    norm_grad = times_turned(r.grads[6, tokens, :], r.inward[:, 0:width])
    for part in range(1, 3):
        norm_grad += times_turned(r.grads[6 + part, tokens, :], r.inward[:, part * width : (part + 1) * width])
    r.total[...] = norm_grad
    input_grad = r.middle[micro] + norm_backward(r, r.stream[micro].astype(WIDE), r.total[...], 0)
    r.middle[micro] = input_grad
    r.passed[micro] = input_grad.astype(SLIM)


NAMES = (
    "x_in", "cot_in", "inward_in", "outward_in", "up_in", "down_in", "gain", "bias", "lengths", "offsets",
    "out_result", "out_grad", "out_down", "out_up", "out_outward", "out_inward", "out_norms",
    "stream", "inward", "outward", "up", "down", "grads", "acts", "acts_out", "weights", "middle", "normed", "held",
    "turned", "total", "result", "passed", "sums", "bias_mask",
    "partial", "y_in", "z_in", "far_y_in", "far_z_in", "staged", "norms",
    "load_sem", "source_sem", "store_sem", "unit_sem",
    "relay_send", "relay_recv", "acts_send", "acts_recv", "branch_send", "branch_recv", "lifted_send", "lifted_recv",
    "rest_send", "rest_recv", "turn",
    "y_send", "y_recv", "z_send", "z_recv", "far_y_send", "far_y_recv", "far_z_send", "far_z_recv", "norm_send", "norm_recv",
)


def step_kernel(*refs):
    r = types.SimpleNamespace(**dict(zip(NAMES, refs)))
    section, dp = lax.axis_index("section"), lax.axis_index("dp")
    c, y, z = lax.rem(dp, 2), lax.rem(lax.div(dp, 2), 2), lax.div(dp, 4)
    r.c = c
    length = r.normed.shape[0]
    leading = section == 0
    pair_dp, y_dp = dp + 1 - 2 * c, dp + 2 - 4 * y

    def slot_of(core, micro):
        return pl.ds(pl.multiple_of((core * 2 + micro) * length, length), length)

    def remote(src, dst, send, recv, to_section, to_dp):
        return pltpu.make_async_remote_copy(
            src_ref=src, dst_ref=dst, send_sem=send, recv_sem=recv,
            device_id=(to_section, to_dp), device_id_type=MESH,
        )

    def local(src, dst, sem):
        return pltpu.make_async_copy(src, dst, sem)

    r.load_inward = local(r.inward_in.at[0], r.inward, r.load_sem.at[0])
    r.load_outward = local(r.outward_in.at[0], r.outward, r.load_sem.at[1])
    r.load_up = local(r.up_in.at[0], r.up, r.load_sem.at[2])
    r.load_down = local(r.down_in.at[0], r.down, r.load_sem.at[3])

    def load_rest():
        r.load_outward.start()
        r.load_up.start()
        r.load_down.start()

    r.load_rest = load_rest

    def load_x(micro):
        return local(r.x_in.at[micro, 0], r.stream.at[micro], r.source_sem.at[micro])

    def load_cot(micro):
        return local(r.cot_in.at[micro, 0], r.grads.at[0, slot_of(c, micro)], r.source_sem.at[micro])

    def relay_up(micro):
        return remote(r.result.at[micro], r.stream.at[micro], r.relay_send.at[micro], r.relay_recv.at[micro], 1 - section, dp)

    def relay_back(micro):
        return remote(
            r.passed.at[micro], r.grads.at[0, slot_of(c, micro)], r.relay_send.at[micro], r.relay_recv.at[micro], 1 - section, dp
        )

    def share_acts(micro, core=c):
        return remote(
            r.acts_out, r.acts.at[:, :, slot_of(core, micro)], r.acts_send.at[micro], r.acts_recv.at[micro], section, pair_dp
        )

    def share_branch(micro, core=c):
        rows = slot_of(core, micro)
        return remote(r.grads.at[0, rows], r.grads.at[0, rows], r.branch_send.at[micro], r.branch_recv.at[micro], section, pair_dp)

    def share_lifted(micro, core=c):
        rows = slot_of(core, micro)
        return remote(
            r.grads.at[1:5, rows], r.grads.at[1:5, rows], r.lifted_send.at[micro], r.lifted_recv.at[micro], section, pair_dp
        )

    def share_rest(micro, core=c):
        rows = slot_of(core, micro)
        return remote(
            r.grads.at[5:9, rows], r.grads.at[5:9, rows], r.rest_send.at[micro], r.rest_recv.at[micro], section, pair_dp
        )

    r.share_lifted = share_lifted
    r.share_acts = share_acts

    def store_result(micro):
        return local(r.result.at[micro], r.out_result.at[micro], r.store_sem.at[0, micro])

    def store_grad(micro):
        return local(r.middle.at[micro], r.out_grad.at[micro], r.store_sem.at[1, micro])

    def to_y(unit):
        return remote(
            r.partial.at[unit, 0], r.y_in.at[unit - FAR], r.y_send.at[unit - FAR], r.y_recv.at[unit - FAR], section, y_dp
        )

    def rows_of(place):
        return pl.ds(BLOCK * place, BLOCK)

    def near_z(unit, place, index, lane, to_dp):
        near = unit - FAR
        return remote(
            r.partial.at[unit, 1, rows_of(place)], r.z_in.at[near, index],
            r.z_send.at[near, lane], r.z_recv.at[near, index], section, to_dp,
        )

    def far_z(unit, place, index, lane, to_dp):
        return remote(
            r.partial.at[unit, :, rows_of(place)], r.far_z_in.at[unit, index],
            r.far_z_send.at[unit, lane], r.far_z_recv.at[unit, index], section, to_dp,
        )

    def far_to_y(unit, place):
        return remote(
            r.partial.at[unit, 0, rows_of(place)], r.far_y_in.at[unit], r.far_y_send.at[unit], r.far_y_recv.at[unit], section, y_dp
        )

    def store_unit(unit):
        source, sem = r.staged.at[unit], r.unit_sem.at[unit]

        def part(out, base):
            return local(source, out.at[:, pl.ds(pl.multiple_of((unit - base) * COLUMNS, 128), COLUMNS)], sem)

        @pl.when(unit < 8)
        def _():
            rows = pl.ds(pl.multiple_of(lax.div(unit, 2) * BLOCK, 16), BLOCK)
            cols = pl.ds(pl.multiple_of(lax.rem(unit, 2) * COLUMNS, 128), COLUMNS)
            local(source, r.out_down.at[rows, cols], sem).start()

        @pl.when((unit >= 8) & (unit < 16))
        def _():
            part(r.out_up, 8).start()

        @pl.when((unit >= 16) & (unit < 18))
        def _():
            part(r.out_outward, 16).start()

        @pl.when(unit >= 18)
        def _():
            part(r.out_inward, 18).start()

    r.load_inward.start()

    @pl.when(leading)
    def _():
        load_x(0).start()
        load_x(1).start()

    @pl.when(jnp.logical_not(leading))
    def _():
        load_cot(0).start()
        load_cot(1).start()

    @pl.when(jnp.logical_not(leading))
    def _():
        r.load_rest()

    r.sums[...] = jnp.zeros_like(r.sums)

    barrier = pltpu.get_barrier_semaphore()
    peers = [(1 - section, dp), (section, pair_dp), (section, y_dp)]
    peers += [(section, lax.rem(dp + 4 * hop, 16)) for hop in (1, 2, 3)]
    for peer in peers:
        pl.semaphore_signal(barrier, inc=1, device_id=peer, device_id_type=MESH)

    def everyone_in():
        pl.semaphore_wait(barrier, len(peers))

    def arrive(micro):
        relay_back(micro).wait_recv()
        share_branch(micro).start()

    def weight_operands(unit):
        whole = lax.div(unit, 2)
        slab = jnp.minimum(whole, 4) + jnp.where(whole >= 8, 1, 0) + jnp.where(whole >= 9, 1, 0)
        cols = pl.ds(pl.multiple_of(lax.rem(unit, 2) * COLUMNS, 128), COLUMNS)
        other = pl.ds(pl.multiple_of((1 - y) * 192, 64), 192)
        own = pl.ds(pl.multiple_of(y * 192, 64), 192)
        return slab, other, own, r.grads[jnp.maximum(whole - 3, 0), :, cols]

    def near_unit(unit):
        slab, other, own, grads = weight_operands(unit)
        r.partial[unit, 0] = times(r.acts[slab, other, :], grads).astype(SLIM)
        to_y(unit).start()
        r.partial[unit, 1] = times(r.acts[slab, own, :], grads).astype(SLIM)

    def far_unit(unit):
        slab, other, own, grads = weight_operands(unit)
        r.partial[unit, 0] = times(r.acts[slab, other, :], grads).astype(SLIM)
        r.partial[unit, 1] = times(r.acts[slab, own, :], grads).astype(SLIM)
        at_ends(unit, far_z, r.far_z_in)

    def arrived(unit, index, copy, into):
        copy(unit, 0, index, 0, dp).wait_recv()
        return into[unit if into is r.far_z_in else unit - FAR, index].astype(WIDE)

    def pick(unit, place, copy):
        return (unit, slice(None) if copy is far_z else 1, rows_of(place))

    def go_right(unit, here, copy, into):
        for place in range(3, here, -1):
            at = pick(unit, place, copy)
            if here > 0:
                r.partial[at] = (r.partial[at].astype(WIDE) + arrived(unit, place + 1, copy, into)).astype(SLIM)
            copy(unit, place, place + 1, place - 1, dp + 4).start()

    def go_left(unit, here, copy, into):
        for place in range(here):
            at = pick(unit, place, copy)
            if here < 3:
                r.partial[at] = (r.partial[at].astype(WIDE) + arrived(unit, place, copy, into)).astype(SLIM)
            copy(unit, place, place, place, dp - 4).start()

    def at_ends(unit, copy, into):
        @pl.when(z == 0)
        def _():
            go_right(unit, 0, copy, into)

        @pl.when(z == 3)
        def _():
            go_left(unit, 3, copy, into)

    def at_middle_first(unit, copy, into):
        @pl.when(z == 1)
        def _():
            go_right(unit, 1, copy, into)

        @pl.when(z == 2)
        def _():
            go_left(unit, 2, copy, into)

    def at_middle_second(unit, copy, into):
        @pl.when(z == 1)
        def _():
            go_left(unit, 1, copy, into)

        @pl.when(z == 2)
        def _():
            go_right(unit, 2, copy, into)

    def gathered(unit, here, copy, into):
        value = r.partial[pick(unit, here, copy)].astype(WIDE)
        if here > 0:
            value = value + arrived(unit, here + 1, copy, into)
        if here < 3:
            value = value + arrived(unit, here, copy, into)
        return value

    def everywhere(action):
        for here in range(4):

            @pl.when(z == here)
            def _():
                action(here)

    def slot(t, carry):
        trailing = jnp.logical_not(leading)
        half = lax.div(t, 2)
        is_forward = (leading & (t < 2)) | (trailing & ((t == 1) | (t == 3)))
        is_backward = (leading & ((t == 3) | (t == 5))) | (trailing & ((t == 2) | (t == 4)))
        is_weights = (leading & (t == 4)) | (trailing & (t == 5))

        @pl.when(trailing & (t == 0))
        def _():
            everyone_in()
            for micro in range(2):
                load_cot(micro).wait()
                share_branch(micro).start()

        @pl.when(is_forward)
        def _():
            micro = jnp.where(leading, jnp.minimum(t, 1), jnp.minimum(half, 1))

            @pl.when(leading)
            def _():
                load_x(micro).wait()

            @pl.when(trailing)
            def _():
                relay_up(micro).wait_recv()

            forward(r, micro, pl.multiple_of((c * 2 + micro) * length, length), t == section, leading)

            @pl.when(leading & (t == 0))
            def _():
                everyone_in()

            share_acts(micro).start()
            store_result(micro).start()
            ahead = leading & (c == 0) & (t == 0)

            @pl.when(leading & (c == 1) & (t == 0))
            def _():
                pl.semaphore_wait(r.turn, 1)

            @pl.when(leading)
            def _():
                relay_up(micro).start()

            @pl.when(ahead)
            def _():
                relay_up(0).wait_send()
                pl.semaphore_signal(r.turn, inc=1, device_id=(section, pair_dp), device_id_type=MESH)

        @pl.when(leading & (t == 3))
        def _():
            arrive(0)

        @pl.when(is_backward)
        def _():
            micro = jnp.clip(half - 1, 0, 1)
            backward(r, micro, pl.multiple_of((c * 2 + micro) * length, length))

            @pl.when(trailing)
            def _():
                relay_back(micro).start()

            share_rest(micro).start()
            store_grad(micro).start()

        @pl.when(leading & (t == 4))
        def _():
            arrive(1)

        @pl.when(is_weights)
        def _():
            for micro in range(2):
                share_branch(micro, 1 - c).wait_recv()
                share_acts(micro, 1 - c).wait_recv()

            early_far = sum(at < 0 for at in FAR_AT)

            def body(i, carry):
                @pl.when(i < EARLY_NEAR)
                def _():
                    near_unit(FAR + i)

                @pl.when(i < early_far)
                def _():
                    far_unit(i)

                return carry

            lax.fori_loop(0, max(EARLY_NEAR, early_far), body, 0)

        return carry

    lax.fori_loop(0, 6, slot, 0)

    def norm_copy(src, dst, index, to_dp):
        return remote(r.norms.at[src], r.norms.at[dst], r.norm_send.at[index], r.norm_recv.at[index], section, to_dp)

    def norm_to_pair():
        return norm_copy(0, 1, 0, pair_dp)

    def norm_to_y():
        return norm_copy(2, 3, 1, y_dp)

    def norm_to_z(hop):
        return norm_copy(4, 4 + hop, 1 + hop, lax.rem(dp + 4 * hop, 16))

    r.norms[0] = jnp.concatenate([jnp.sum(r.sums[...], 1), jnp.zeros((4, r.sums.shape[2]), WIDE)], 0)
    norm_to_pair().start()
    for micro in range(2):
        share_lifted(micro, 1 - c).wait_recv()

    def sum_y(unit):
        to_y(unit).wait_recv()
        r.partial[unit, 1] = (r.partial[unit, 1].astype(WIDE) + r.y_in[unit - FAR].astype(WIDE)).astype(SLIM)

    def far_turn(i, steps):
        turn, unit = i < 0, jnp.int32(0)
        for index, step in enumerate(steps):
            if step >= 0:
                turn = turn | (i == step)
                unit = jnp.where(i == step, index, unit)
        return turn, unit

    def near_turn(i, lag):
        return (i >= lag) & (i < NEAR + lag), jnp.clip(i - lag, 0, NEAR - 1) + FAR

    def advance(i, carry):
        issued = FAR + EARLY_NEAR + i - HOLD

        @pl.when(issued == 16)
        def _():
            for micro in range(2):
                share_rest(micro, 1 - c).wait_recv()

        @pl.when((issued >= FAR + EARLY_NEAR) & (issued < UNITS))
        def _():
            near_unit(issued)

        turn, unit = far_turn(i, FAR_AT)

        @pl.when(turn)
        def _(unit=unit):
            far_unit(unit)

        @pl.when(i < NEAR)
        def _():
            sum_y(FAR + i)
            at_ends(FAR + i, near_z, r.z_in)

        turn, unit = near_turn(i, LAGS[0])

        @pl.when(turn)
        def _(unit=unit):
            at_middle_first(unit, near_z, r.z_in)

        turn, unit = far_turn(i, FAR_FIRST)

        @pl.when(turn)
        def _(unit=unit):
            at_middle_first(unit, far_z, r.far_z_in)

        turn, unit = far_turn(i, FAR_SECOND)

        @pl.when(turn)
        def _(unit=unit):
            at_middle_second(unit, far_z, r.far_z_in)

        turn, unit = far_turn(i, FAR_ARRIVED)

        @pl.when(turn)
        def _(unit=unit):
            def action(here):
                value = gathered(unit, here, far_z, r.far_z_in)
                r.partial[unit, 0, rows_of(here)] = value[0].astype(SLIM)
                far_to_y(unit, here).start()
                r.staged[unit] = value[1]

            everywhere(action)

        turn, unit = far_turn(i, FAR_DONE)

        @pl.when(turn)
        def _(unit=unit):
            far_to_y(unit, 0).wait_recv()
            r.staged[unit] += r.far_y_in[unit].astype(WIDE)
            store_unit(unit)

        turn, unit = near_turn(i, LAGS[1])

        @pl.when(turn)
        def _(unit=unit):
            at_middle_second(unit, near_z, r.z_in)

        turn, unit = near_turn(i, LAGS[2])

        @pl.when(turn)
        def _(unit=unit):
            def action(here):
                r.staged[unit] = gathered(unit, here, near_z, r.z_in)

            everywhere(action)
            store_unit(unit)

        @pl.when(i == 1)
        def _():
            norm_to_pair().wait()
            r.norms[2] = r.norms[0] + r.norms[1]
            norm_to_y().start()

        @pl.when(i == 9)
        def _():
            norm_to_y().wait_recv()
            r.norms[4] = r.norms[2] + r.norms[3]
            for hop in (1, 2, 3):
                norm_to_z(hop).start()

        @pl.when(i == 18)
        def _():
            for hop in (1, 2, 3):
                norm_to_z(hop).wait_recv()
            r.norms[0] = (r.norms[4] + r.norms[5]) + (r.norms[6] + r.norms[7])
            local(r.norms.at[0], r.out_norms, r.store_sem.at[2, 0]).start()

        return carry

    lax.fori_loop(0, max(NEAR + LAGS[2], FAR_DONE[-1] + 1), advance, 0)

    norm_to_y().wait_send()
    for hop in (1, 2, 3):
        norm_to_z(hop).wait_send()
    share_acts(1).wait_send()
    for micro in range(2):
        share_branch(micro).wait_send()
        share_lifted(micro).wait_send()
        share_rest(micro).wait_send()
        store_result(micro).wait()
        store_grad(micro).wait()

        @pl.when(leading if micro else leading & (c == 1))
        def _():
            relay_up(micro).wait_send()

        @pl.when(jnp.logical_not(leading))
        def _():
            relay_back(micro).wait_send()

    def drain_near(near, carry):
        to_y(FAR + near).wait_send()
        for lane in range(3):
            near_z(FAR + near, 0, 0, lane, dp).wait_send()
        return carry

    lax.fori_loop(0, NEAR, drain_near, 0)

    def drain_far(unit, carry):
        far_to_y(unit, 0).wait_send()
        for lane in range(3):
            far_z(unit, 0, 0, lane, dp).wait_send()
        return carry

    lax.fori_loop(0, FAR, drain_far, 0)

    def drain_store(unit, carry):
        local(r.staged.at[unit], r.out_outward.at[:, 0:COLUMNS], r.unit_sem.at[unit]).wait()
        return carry

    lax.fori_loop(0, UNITS, drain_store, 0)
    local(r.norms.at[0], r.out_norms, r.store_sem.at[2, 0]).wait()


def hand_over_kernel(*refs):
    sources, norms, targets = refs[:6], refs[6], refs[7:13]
    gain_grad, bias_grad, held, in_sem, out_sem = refs[13], refs[14], refs[15:21], refs[21], refs[22]
    loads = [pltpu.make_async_copy(a, b, in_sem.at[k]) for k, (a, b) in enumerate(zip(sources, held))]
    stores = [pltpu.make_async_copy(a, b, out_sem.at[k]) for k, (a, b) in enumerate(zip(held, targets))]
    for load in loads:
        load.start()
    share = gain_grad.shape[2]
    for index in range(norms.shape[1] // share):

        @pl.when(lax.axis_index("dp") == index)
        def _():
            gain_grad[0] = norms[0:2, index * share : (index + 1) * share]
            bias_grad[0] = norms[2:4, index * share : (index + 1) * share]

    for load, store in zip(loads, stores):
        load.wait()
        store.start()
    for store in stores:
        store.wait()


def step_on_device(
    inputs, clip_lengths, anchor_offsets, cotangent, inward_weight, outward_weight, up_weight, down_weight, norm_gain, norm_bias
):
    _, _, length, width = inputs.shape
    wide_ff = up_weight.shape[2]
    anywhere = pl.BlockSpec(memory_space=pl.ANY)
    in_vmem = pl.BlockSpec(memory_space=pltpu.VMEM)
    in_smem = pl.BlockSpec(memory_space=pltpu.SMEM)
    dma = pltpu.SemaphoreType.DMA
    share = width // lax.axis_size("dp")
    shapes = [
        jax.ShapeDtypeStruct((2, length, width), SLIM),
        jax.ShapeDtypeStruct((2, length, width), WIDE),
        jax.ShapeDtypeStruct((4 * BLOCK, width), WIDE),
        jax.ShapeDtypeStruct((BLOCK, wide_ff), WIDE),
        jax.ShapeDtypeStruct((BLOCK, width), WIDE),
        jax.ShapeDtypeStruct((BLOCK, 3 * width), WIDE),
    ]
    made = pl.pallas_call(
        step_kernel,
        out_shape=(*shapes, jax.ShapeDtypeStruct((8, width), WIDE)),
        in_specs=[anywhere] * 6 + [in_vmem] * 2 + [in_smem] * 2,
        out_specs=[anywhere] * 7,
        scratch_shapes=[
            pltpu.VMEM((2, length, width), SLIM),
            pltpu.VMEM((width, 3 * width), SLIM),
            pltpu.VMEM((width, width), SLIM),
            pltpu.VMEM((width, wide_ff), SLIM),
            pltpu.VMEM((wide_ff, width), SLIM),
            pltpu.VMEM((9, 4 * length, width), SLIM),
            pltpu.VMEM((7, 8 * BLOCK, 4 * length), SLIM),
            pltpu.VMEM((7, 8 * BLOCK, length), SLIM),
            pltpu.VMEM((2, width // HEAD, length, length), SLIM),
            pltpu.VMEM((2, length, width), WIDE),
            pltpu.VMEM((length, width), SLIM),
            pltpu.VMEM((length, width), SLIM),
            pltpu.VMEM((width, length), SLIM),
            pltpu.VMEM((length, width), WIDE),
            pltpu.VMEM((2, length, width), SLIM),
            pltpu.VMEM((2, length, width), SLIM),
            pltpu.VMEM((4, 8, width), WIDE),
            pltpu.VMEM((length, length), WIDE),
            pltpu.VMEM((UNITS, 2, 4 * BLOCK, COLUMNS), SLIM),
            pltpu.VMEM((NEAR, 4 * BLOCK, COLUMNS), SLIM),
            pltpu.VMEM((NEAR, 5, BLOCK, COLUMNS), SLIM),
            pltpu.VMEM((FAR, BLOCK, COLUMNS), SLIM),
            pltpu.VMEM((FAR, 5, 2, BLOCK, COLUMNS), SLIM),
            pltpu.VMEM((UNITS, BLOCK, COLUMNS), WIDE),
            pltpu.VMEM((8, 8, width), WIDE),
            dma((4,)), dma((2,)), dma((3, 2)), dma((UNITS,)),
            *[dma((2,))] * 10, pltpu.SemaphoreType.REGULAR,
            dma((NEAR,)), dma((NEAR,)), dma((NEAR, 3)), dma((NEAR, 5)),
            dma((FAR,)), dma((FAR,)), dma((FAR, 3)), dma((FAR, 5)), dma((5,)), dma((5,)),
        ],
        compiler_params=pltpu.CompilerParams(
            collective_id=0, has_side_effects=True, vmem_limit_bytes=VMEM_BYTES
        ),
    )(
        inputs, cotangent, inward_weight, outward_weight, up_weight, down_weight,
        norm_gain, norm_bias, clip_lengths, anchor_offsets,
    )
    result, grad, down, up, outward, inward, gain_grad, bias_grad = pl.pallas_call(
        hand_over_kernel,
        out_shape=(*shapes, *[jax.ShapeDtypeStruct((1, 2, share), WIDE)] * 2),
        in_specs=[anywhere] * 6 + [in_vmem],
        out_specs=[anywhere] * 6 + [in_vmem] * 2,
        scratch_shapes=[pltpu.VMEM(shape.shape, shape.dtype) for shape in shapes] + [dma((6,)), dma((6,))],
    )(*made)
    return (
        result[None, :, None],
        grad[None, :, None],
        inward[None],
        outward[None],
        up[None],
        down[None],
        gain_grad,
        bias_grad,
    )


def shifted(x, axis, by):
    size = lax.axis_size(axis)
    pairs = [(i, i + by) for i in range(size) if 0 <= i + by < size]
    return lax.ppermute(x, axis, pairs)


def norm_rows(values, norm_gain, norm_bias):
    average = jnp.mean(values, -1, keepdims=True)
    centred = values - average
    inverse = lax.rsqrt(jnp.mean(centred * centred, -1, keepdims=True) + EPSILON)
    normed = centred * inverse
    return (normed * norm_gain + norm_bias, normed, inverse)


def norm_back(norm_grad, normed, inverse, norm_gain):
    inner = norm_grad * norm_gain
    through = inverse * (
        inner
        - jnp.mean(inner, -1, keepdims=True)
        - normed * jnp.mean(inner * normed, -1, keepdims=True)
    )
    return (through, jnp.sum(norm_grad * normed, 0), jnp.sum(norm_grad, 0))


def gelu_slope(lifted):
    cumulative = 0.5 * (1.0 + lax.erf(lifted * 0.7071067811865476))
    density = jnp.exp(-0.5 * lifted * lifted) * 0.3989422804014327
    return cumulative + lifted * density


def clip_marks(lengths, offsets, length):
    positions = jnp.arange(length, dtype=jnp.int32)
    clip_ends = jnp.cumsum(lengths)
    clip_starts = clip_ends - lengths
    anchor_at = clip_starts + offsets % lengths
    clip_ids = jnp.sum((positions[:, None] >= clip_ends[None, :]).astype(jnp.int32), 1)
    anchors = jnp.any(positions[:, None] == anchor_at[None, :], 1)
    return (clip_ids, anchors)


def masked_scores(query_block, key_rows, id_block, clip_ids, anchors, scaling):
    scores = (
        jnp.einsum("qhd,khd->hqk", query_block, key_rows, preferred_element_type=jnp.float32)
        * scaling
    )
    seen = (id_block[:, None] == clip_ids[None, :]) | anchors[None, :]
    return jnp.where(seen[None], scores, -1000000000.0)


def forward_layer(source, clip_ids, anchors, params):
    inward, outward, upward, downward, norm_gain, norm_bias = params
    length, model_width = source.shape
    head_count = model_width // HEAD
    scaling = HEAD ** (-0.5)
    residual = source.astype(jnp.float32)
    first_norm, unit_one, scale_one = norm_rows(residual, norm_gain[0], norm_bias[0])
    joined = jnp.dot(
        first_norm.astype(jnp.bfloat16), inward, preferred_element_type=jnp.float32
    ).astype(jnp.bfloat16)
    heads_view = joined.reshape(length, 3, head_count, HEAD)
    queries = heads_view[:, 0]
    key_rows = heads_view[:, 1]
    values = heads_view[:, 2]
    scores = masked_scores(queries, key_rows, clip_ids, clip_ids, anchors, scaling)
    row_max = jnp.max(scores, -1, keepdims=True)
    raised = jnp.exp(scores - row_max)
    row_sum = jnp.sum(raised, -1, keepdims=True)
    weights = (raised / row_sum).astype(jnp.bfloat16)
    pieces = [jnp.einsum("hqk,khd->qhd", weights, values, preferred_element_type=jnp.float32)]
    log_sums = [(row_max + jnp.log(row_sum))[..., 0]]
    attended = jnp.concatenate(pieces, 0).reshape(length, model_width).astype(jnp.bfloat16)
    logsum = jnp.concatenate(log_sums, 1)
    middle = residual + jnp.dot(attended, outward, preferred_element_type=jnp.float32)
    second_norm, unit_two, scale_two = norm_rows(middle, norm_gain[1], norm_bias[1])
    lifted = jnp.dot(second_norm.astype(jnp.bfloat16), upward, preferred_element_type=jnp.float32)
    active = jax.nn.gelu(lifted, approximate=False).astype(jnp.bfloat16)
    result = middle + jnp.dot(active, downward, preferred_element_type=jnp.float32)
    stored = (unit_one, scale_one, joined, logsum, attended, unit_two, scale_two, lifted, active)
    return (result, stored)


def contract_rows(left, right):
    return lax.dot_general(
        left, right, (((0,), (0,)), ((), ())), preferred_element_type=jnp.float32
    )


def contract_cols(left, right):
    return lax.dot_general(
        left, right, (((1,), (1,)), ((), ())), preferred_element_type=jnp.float32
    )


def feed_backward(incoming, stored, params):
    inward, outward, upward, downward, norm_gain, norm_bias = params
    unit_one, scale_one, joined, logsum, attended, unit_two, scale_two, lifted, active = stored
    branch = incoming.astype(jnp.bfloat16)
    down_part = contract_rows(active, branch)
    hidden_grad = contract_cols(branch, downward)
    lifted_grad = (hidden_grad * gelu_slope(lifted)).astype(jnp.bfloat16)
    second_in = (unit_two * norm_gain[1] + norm_bias[1]).astype(jnp.bfloat16)
    up_part = contract_rows(second_in, lifted_grad)
    normed_grad = contract_cols(lifted_grad, upward)
    through, gain_two, bias_two = norm_back(normed_grad, unit_two, scale_two, norm_gain[1])
    return (incoming + through, (up_part, down_part, gain_two, bias_two))


def attend_backward(middle_grad, stored, clip_ids, anchors, params):
    inward, outward, upward, downward, norm_gain, norm_bias = params
    unit_one, scale_one, joined, logsum, attended, unit_two, scale_two, lifted, active = stored
    length, model_width = attended.shape
    head_count = model_width // HEAD
    scaling = HEAD ** (-0.5)
    branch = middle_grad.astype(jnp.bfloat16)
    outward_part = contract_rows(attended, branch)
    attended_grad = (
        contract_cols(branch, outward).astype(jnp.bfloat16).reshape(length, head_count, HEAD)
    )
    heads_view = joined.reshape(length, 3, head_count, HEAD)
    queries = heads_view[:, 0]
    key_rows = heads_view[:, 1]
    values = heads_view[:, 2]
    key_grad = jnp.zeros((length, head_count, HEAD), jnp.float32)
    value_grad = jnp.zeros((length, head_count, HEAD), jnp.float32)
    block_rows = min(512, length)
    scores = masked_scores(queries, key_rows, clip_ids, clip_ids, anchors, scaling)
    weights = jnp.exp(scores - logsum[:, 0:block_rows, None])
    weight_grad = jnp.einsum(
        "qhd,khd->hqk", attended_grad, values, preferred_element_type=jnp.float32
    )
    score_grad = (
        weights * (weight_grad - jnp.sum(weights * weight_grad, -1, keepdims=True))
    ).astype(jnp.bfloat16)
    query_pieces = [
        scaling
        * jnp.einsum("hqk,khd->qhd", score_grad, key_rows, preferred_element_type=jnp.float32)
    ]
    key_grad = key_grad + scaling * jnp.einsum(
        "hqk,qhd->khd", score_grad, queries, preferred_element_type=jnp.float32
    )
    value_grad = value_grad + jnp.einsum(
        "hqk,qhd->khd",
        weights.astype(jnp.bfloat16),
        attended_grad,
        preferred_element_type=jnp.float32,
    )
    query_grad = jnp.concatenate(query_pieces, 0)
    joined_grad = (
        jnp.stack([query_grad, key_grad, value_grad], 1)
        .reshape(length, 3 * model_width)
        .astype(jnp.bfloat16)
    )
    first_in = (unit_one * norm_gain[0] + norm_bias[0]).astype(jnp.bfloat16)
    inward_part = contract_rows(first_in, joined_grad)
    normed_grad = contract_cols(joined_grad, inward)
    through, gain_one, bias_one = norm_back(normed_grad, unit_one, scale_one, norm_gain[0])
    return (middle_grad + through, (inward_part, outward_part, gain_one, bias_one))


def resting(function):

    def blank(*operands):
        return jax.tree.map(jnp.zeros_like, function(*operands))

    return blank


def take_slot(holder, buffer_slot):
    return jax.tree.map(
        lambda element: lax.dynamic_index_in_dim(element, buffer_slot, 0, False), holder
    )


def place_slot(holder, item, buffer_slot, working):

    def update(element, fresh):
        former = lax.dynamic_index_in_dim(element, buffer_slot, 0, False)
        return lax.dynamic_update_index_in_dim(
            element, jnp.where(working, fresh, former), buffer_slot, 0
        )

    return jax.tree.map(update, holder, item)


def per_device(
    inputs,
    clip_lengths,
    anchor_offsets,
    cotangent,
    inward_weight,
    outward_weight,
    up_weight,
    down_weight,
    norm_gain,
    norm_bias,
):
    params = (
        inward_weight[0],
        outward_weight[0],
        up_weight[0],
        down_weight[0],
        norm_gain[0],
        norm_bias[0],
    )
    stream = inputs[:, 0]
    cot_rows = cotangent[:, 0]
    lengths_all = clip_lengths[:, 0]
    offsets_all = anchor_offsets[:, 0]
    micro_count = stream.shape[0]
    length = stream.shape[1]
    section_index = lax.axis_index("section")
    section_count = lax.axis_size("section")
    leading = section_index == 0
    trailing = section_index == section_count - 1
    periods = micro_count + section_count - 1
    arriving = jnp.zeros_like(stream[0])
    produced = jnp.zeros_like(stream)
    archive = None
    for period in range(periods):
        micro_index = period - section_index
        working = (micro_index >= 0) & (micro_index < micro_count)
        buffer_slot = jnp.clip(micro_index, 0, micro_count - 1)
        source = jnp.where(leading, stream[min(period, micro_count - 1)], arriving)
        clip_ids, anchors = clip_marks(
            take_slot(lengths_all, buffer_slot), take_slot(offsets_all, buffer_slot), length
        )
        result, stored = lax.cond(
            working, forward_layer, resting(forward_layer), source, clip_ids, anchors, params
        )
        if archive is None:
            archive = jax.tree.map(
                lambda element: jnp.zeros((micro_count,) + element.shape, element.dtype), stored
            )
        archive = place_slot(archive, stored, buffer_slot, working)
        sending = result.astype(jnp.bfloat16)
        produced = place_slot(produced, sending, buffer_slot, working)
        if period < micro_count:
            arriving = shifted(sending, "section", 1)
    inward, outward, upward, downward, gains, biases = params
    up_sum = jnp.zeros(upward.shape, jnp.float32)
    down_sum = jnp.zeros(downward.shape, jnp.float32)
    gain_two = jnp.zeros(gains.shape[1:], jnp.float32)
    bias_two = jnp.zeros(biases.shape[1:], jnp.float32)
    inward_sum = jnp.zeros(inward.shape, jnp.float32)
    outward_sum = jnp.zeros(outward.shape, jnp.float32)
    gain_one = jnp.zeros(gains.shape[1:], jnp.float32)
    bias_one = jnp.zeros(biases.shape[1:], jnp.float32)
    upstream = jnp.zeros_like(stream[0])
    returned = jnp.zeros(stream.shape, jnp.float32)
    for period in range(periods):
        micro_index = micro_count - 1 - period + (section_count - 1 - section_index)
        working = (micro_index >= 0) & (micro_index < micro_count)
        buffer_slot = jnp.clip(micro_index, 0, micro_count - 1)
        incoming = jnp.where(trailing, take_slot(cot_rows, buffer_slot), upstream).astype(
            jnp.float32
        )
        clip_ids, anchors = clip_marks(
            take_slot(lengths_all, buffer_slot), take_slot(offsets_all, buffer_slot), length
        )
        stored = take_slot(archive, buffer_slot)
        middle_grad, feed_part = lax.cond(
            working, feed_backward, resting(feed_backward), incoming, stored, params
        )
        up_sum = up_sum + feed_part[0]
        down_sum = down_sum + feed_part[1]
        gain_two = gain_two + feed_part[2]
        bias_two = bias_two + feed_part[3]
        input_grad, attend_part = lax.cond(
            working,
            attend_backward,
            resting(attend_backward),
            middle_grad,
            stored,
            clip_ids,
            anchors,
            params,
        )
        inward_sum = inward_sum + attend_part[0]
        outward_sum = outward_sum + attend_part[1]
        gain_one = gain_one + attend_part[2]
        bias_one = bias_one + attend_part[3]
        returned = place_slot(returned, input_grad, buffer_slot, working)
        if period < periods - 1:
            upstream = shifted(input_grad.astype(jnp.bfloat16), "section", -1)
    inward_sum, outward_sum, up_sum, down_sum, gain_one, gain_two, bias_one, bias_two = (
        lax.psum_scatter(inward_sum, "dp", scatter_dimension=0, tiled=True),
        lax.psum_scatter(outward_sum, "dp", scatter_dimension=0, tiled=True),
        lax.psum_scatter(up_sum, "dp", scatter_dimension=0, tiled=True),
        lax.psum_scatter(down_sum, "dp", scatter_dimension=0, tiled=True),
        lax.psum_scatter(gain_one, "dp", scatter_dimension=0, tiled=True),
        lax.psum_scatter(gain_two, "dp", scatter_dimension=0, tiled=True),
        lax.psum_scatter(bias_one, "dp", scatter_dimension=0, tiled=True),
        lax.psum_scatter(bias_two, "dp", scatter_dimension=0, tiled=True),
    )
    layer_outputs = produced[None, :, None]
    input_grads = returned[None, :, None]
    gain_grad = jnp.stack([gain_one, gain_two])[None]
    bias_grad = jnp.stack([bias_one, bias_two])[None]
    return (
        layer_outputs,
        input_grads,
        inward_sum[None],
        outward_sum[None],
        up_sum[None],
        down_sum[None],
        gain_grad,
        bias_grad,
    )


def solution(mesh):
    local = step_on_device if mesh.shape["dp"] == 16 and mesh.shape["section"] == 2 else per_device
    return jax.shard_map(
        local,
        mesh=mesh,
        in_specs=(
            P(None, "dp", None, None),
            P(None, "dp", None),
            P(None, "dp", None),
            P(None, "dp", None, None),
            P("section", None, None),
            P("section", None, None),
            P("section", None, None),
            P("section", None, None),
            P("section", None, None),
            P("section", None, None),
        ),
        out_specs=(
            P("section", None, "dp", None, None),
            P("section", None, "dp", None, None),
            P("section", "dp", None),
            P("section", "dp", None),
            P("section", "dp", None),
            P("section", "dp", None),
            P("section", None, "dp"),
            P("section", None, "dp"),
        ),
        check_vma=False,
    )
```

```python
import functools
import types

import jax
import jax.numpy as jnp
from jax import lax
from jax.experimental import pallas as pl
from jax.experimental.pallas import tpu as pltpu
from jax.sharding import PartitionSpec as P

HEAD = 64
EPSILON = 1e-06
MESH = pl.DeviceIdType.MESH
WIDE = jnp.float32
SLIM = jnp.bfloat16
VMEM_BYTES = 67043328

UNITS = 24
FAR = 4
NEAR = UNITS - FAR
BLOCK = 48
COLUMNS = 384
EARLY_NEAR = 4
HOLD = 1
LAGS = (2, 3, 4)
FAR_AT = (-1, -1, 3, 8)
FAR_FIRST = (2, 4, 10, 15)
FAR_SECOND = (5, 15, 14, 20)
FAR_ARRIVED = (17, 18, 20, 21)
FAR_DONE = (20, 21, 22, 23)


def times(left, right):
    return jnp.dot(left, right, preferred_element_type=WIDE)


def times_turned(left, right):
    return lax.dot_general(left, right, (((1,), (1,)), ((), ())), preferred_element_type=WIDE)


def unit_rows(values):
    centred = values - jnp.mean(values, -1, keepdims=True)
    inverse = lax.rsqrt(jnp.mean(centred * centred, -1, keepdims=True) + EPSILON)
    return centred * inverse, inverse


def norm_rows_bf16(r, values, which):
    unit, _ = unit_rows(values)
    return (unit * r.gain[0, which : which + 1, :] + r.bias[0, which : which + 1, :]).astype(SLIM)


def norm_backward(r, values, norm_grad, which):
    unit, inverse = unit_rows(values)
    width = values.shape[1]
    r.sums[which] += jnp.sum((norm_grad * unit).reshape(-1, 8, width), 0)
    r.sums[2 + which] += jnp.sum(norm_grad.reshape(-1, 8, width), 0)
    inner = norm_grad * r.gain[0, which : which + 1, :]
    return inverse * (
        inner
        - jnp.mean(inner, -1, keepdims=True)
        - unit * jnp.mean(inner * unit, -1, keepdims=True)
    )


def head_lanes():
    lane = lax.broadcasted_iota(jnp.int32, (1, 2 * HEAD), 1)
    first = jnp.where(lane < HEAD, 1.0, 0.0).astype(WIDE)
    return first, 1.0 - first


def mask_bias(r, micro):
    length = r.bias_mask.shape[0]

    def marks(positions):
        end = jnp.int32(0)
        ids = jnp.zeros(positions.shape, jnp.int32)
        anchors = jnp.zeros(positions.shape, jnp.int32)
        for clip in range(r.lengths.shape[2]):
            size = r.lengths[micro, 0, clip]
            anchor = end + lax.rem(r.offsets[micro, 0, clip], size)
            end = end + size
            ids = ids + jnp.where(positions >= end, 1, 0)
            anchors = anchors + jnp.where(positions == anchor, 1, 0)
        return ids, anchors

    key_ids, anchors = marks(lax.broadcasted_iota(jnp.int32, (length, 1), 0))
    query_ids, _ = marks(lax.broadcasted_iota(jnp.int32, (1, length), 1))
    seen = (key_ids == query_ids) | (jnp.broadcast_to(anchors, (length, length)) > 0)
    r.bias_mask[...] = jnp.where(seen, 0.0, -1000000000.0).astype(WIDE)


def place(r, slab, tokens):
    for line in range(8):
        z, y = line // 2, line % 2
        rows = pl.ds(y * 192 + z * BLOCK, BLOCK)
        own = pl.ds(pl.multiple_of(2 * BLOCK * line + r.c * BLOCK, 16), BLOCK)
        other = pl.ds(pl.multiple_of(2 * BLOCK * line + (1 - r.c) * BLOCK, 16), BLOCK)
        r.acts[slab, rows, tokens] = r.turned[own, :]
        r.acts_out[slab, rows, :] = r.turned[other, :]


def forward(r, micro, tok, first, leading):
    length, width = r.normed.shape
    tokens = pl.ds(tok, length)
    mask_bias(r, micro)
    r.normed[...] = norm_rows_bf16(r, r.stream[micro].astype(WIDE), 0)

    @pl.when(first)
    def _():
        r.load_inward.wait()

        @pl.when(leading)
        def _():
            r.load_rest()

    for part in range(3):
        r.grads[6 + part, tokens, :] = times(
            r.normed[...], r.inward[:, part * width : (part + 1) * width]
        ).astype(SLIM)

    @pl.when(micro > 0)
    def _():
        r.share_acts(0).wait_send()

    r.turned[...] = r.normed[...].T
    place(r, 6, tokens)
    one, two = (lanes.astype(SLIM) for lanes in head_lanes())
    for pair in range(width // (2 * HEAD)):
        cols = pl.ds(pair * 2 * HEAD, 2 * HEAD)
        queries = r.grads[6, tokens, cols] * jnp.asarray(HEAD**-0.5, SLIM)
        keys = r.grads[7, tokens, cols]
        values_turned = r.grads[8, tokens, cols].T
        scores = times_turned(jnp.concatenate([keys * one, keys * two], 0), queries)
        pieces = []
        for head in range(2):
            masked = scores[length * head : length * (head + 1)] + r.bias_mask[...]
            raised = jnp.exp(masked - jnp.max(masked, 0, keepdims=True))
            weights = (raised * (1.0 / jnp.sum(raised, 0, keepdims=True))).astype(SLIM)
            r.weights[micro, 2 * pair + head] = weights
            pieces.append(times(values_turned[HEAD * head : HEAD * (head + 1)], weights).astype(SLIM))
        attended_turned = jnp.concatenate(pieces, 0)
        r.turned[cols, :] = attended_turned
        r.held[:, cols] = attended_turned.T
    place(r, 5, tokens)

    @pl.when(first)
    def _():
        r.load_outward.wait()

    r.middle[micro] = r.stream[micro].astype(WIDE) + times(r.held[...], r.outward[...])
    r.normed[...] = norm_rows_bf16(r, r.middle[micro], 1)
    r.turned[...] = r.normed[...].T
    place(r, 4, tokens)
    r.total[...] = r.middle[micro]

    @pl.when(first)
    def _():
        r.load_up.wait()
        r.load_down.wait()

    for part in range(4):
        cols = slice(part * width, (part + 1) * width)
        lifted = times(r.normed[...], r.up[:, cols])
        cumulative = 0.5 * (1.0 + lax.erf(lifted * 0.7071067811865476))
        density = jnp.exp(-0.5 * lifted * lifted) * 0.3989422804014327
        r.grads[1 + part, tokens, :] = (cumulative + lifted * density).astype(SLIM)
        active = (lifted * cumulative).astype(SLIM)
        r.total[...] += times(active, r.down[cols, :])
        r.turned[...] = active.T
        for y in range(2):
            for piece in range(4):
                rows = pl.ds(y * 192 + part * BLOCK, BLOCK)
                start = 384 * y + BLOCK * piece
                own = pl.ds(pl.multiple_of(start + r.c * 192, 16), BLOCK)
                other = pl.ds(pl.multiple_of(start + (1 - r.c) * 192, 16), BLOCK)
                r.acts[piece, rows, tokens] = r.turned[own, :]
                r.acts_out[piece, rows, :] = r.turned[other, :]
    r.result[micro] = r.total[...].astype(SLIM)


def backward(r, micro, tok):
    length, width = r.normed.shape
    tokens = pl.ds(tok, length)
    r.total[...] = jnp.zeros((length, width), WIDE)
    for part in range(4):
        cols = slice(part * width, (part + 1) * width)
        hidden = times_turned(r.grads[0, tokens, :], r.down[cols, :])
        lifted_grad = (hidden * r.grads[1 + part, tokens, :].astype(WIDE)).astype(SLIM)
        r.grads[1 + part, tokens, :] = lifted_grad
        r.total[...] += times_turned(lifted_grad, r.up[:, cols])
    r.share_lifted(micro).start()
    middle_grad = r.grads[0, tokens, :].astype(WIDE) + norm_backward(
        r, r.middle[micro], r.total[...], 1
    )
    r.middle[micro] = middle_grad
    r.grads[5, tokens, :] = middle_grad.astype(SLIM)
    r.held[...] = times_turned(r.grads[5, tokens, :], r.outward[...]).astype(SLIM)
    first, second = head_lanes()
    one, two = first.astype(SLIM), second.astype(SLIM)
    scaling = HEAD**-0.5
    for pair in range(width // (2 * HEAD)):
        cols = pl.ds(pair * 2 * HEAD, 2 * HEAD)
        queries = r.grads[6, tokens, cols] * jnp.asarray(scaling, SLIM)
        values = r.grads[8, tokens, cols]
        keys_turned = r.grads[7, tokens, cols].T
        incoming = r.held[:, cols]
        weight_grads = times_turned(jnp.concatenate([values * one, values * two], 0), incoming)
        score_grads, query_grads, weights = [], [], []
        for head in range(2):
            kept = r.weights[micro, 2 * pair + head]
            wide = kept.astype(WIDE)
            own = weight_grads[length * head : length * (head + 1)]
            score_grad = (wide * (own - jnp.sum(wide * own, 0, keepdims=True))).astype(SLIM)
            score_grads.append(score_grad)
            weights.append(kept)
            query_grads.append(
                (times(keys_turned[HEAD * head : HEAD * (head + 1)], score_grad) * scaling).astype(SLIM)
            )
        key_grad = times(jnp.concatenate(score_grads, 0), queries)
        value_grad = times(jnp.concatenate(weights, 0), incoming)
        r.grads[6, tokens, cols] = jnp.concatenate(query_grads, 0).T
        r.grads[7, tokens, cols] = (key_grad[:length] * first + key_grad[length:] * second).astype(SLIM)
        r.grads[8, tokens, cols] = (value_grad[:length] * first + value_grad[length:] * second).astype(SLIM)
    norm_grad = times_turned(r.grads[6, tokens, :], r.inward[:, 0:width])
    for part in range(1, 3):
        norm_grad += times_turned(r.grads[6 + part, tokens, :], r.inward[:, part * width : (part + 1) * width])
    r.total[...] = norm_grad
    input_grad = r.middle[micro] + norm_backward(r, r.stream[micro].astype(WIDE), r.total[...], 0)
    r.middle[micro] = input_grad
    r.passed[micro] = input_grad.astype(SLIM)


NAMES = (
    "x_in", "cot_in", "inward_in", "outward_in", "up_in", "down_in", "gain", "bias", "lengths", "offsets",
    "result", "middle", "staged", "out_norms",
    "stream", "inward", "outward", "up", "down", "grads", "acts", "acts_out", "weights", "normed", "held",
    "turned", "total", "passed", "sums", "bias_mask",
    "partial", "y_in", "z_in", "far_y_in", "far_z_in", "norms",
    "load_sem", "source_sem",
    "relay_send", "relay_recv", "acts_send", "acts_recv", "branch_send", "branch_recv", "lifted_send", "lifted_recv",
    "rest_send", "rest_recv", "turn",
    "y_send", "y_recv", "z_send", "z_recv", "far_y_send", "far_y_recv", "far_z_send", "far_z_recv", "norm_send", "norm_recv",
)


def step_kernel(*refs):
    r = types.SimpleNamespace(**dict(zip(NAMES, refs)))
    section, dp = lax.axis_index("section"), lax.axis_index("dp")
    c, y, z = lax.rem(dp, 2), lax.rem(lax.div(dp, 2), 2), lax.div(dp, 4)
    r.c = c
    length = r.normed.shape[0]
    leading = section == 0
    pair_dp, y_dp = dp + 1 - 2 * c, dp + 2 - 4 * y

    def slot_of(core, micro):
        return pl.ds(pl.multiple_of((core * 2 + micro) * length, length), length)

    def remote(src, dst, send, recv, to_section, to_dp):
        return pltpu.make_async_remote_copy(
            src_ref=src, dst_ref=dst, send_sem=send, recv_sem=recv,
            device_id=(to_section, to_dp), device_id_type=MESH,
        )

    def local(src, dst, sem):
        return pltpu.make_async_copy(src, dst, sem)

    r.load_inward = local(r.inward_in.at[0], r.inward, r.load_sem.at[0])
    r.load_outward = local(r.outward_in.at[0], r.outward, r.load_sem.at[1])
    r.load_up = local(r.up_in.at[0], r.up, r.load_sem.at[2])
    r.load_down = local(r.down_in.at[0], r.down, r.load_sem.at[3])

    def load_rest():
        r.load_outward.start()
        r.load_up.start()
        r.load_down.start()

    r.load_rest = load_rest

    def load_x(micro):
        return local(r.x_in.at[micro, 0], r.stream.at[micro], r.source_sem.at[micro])

    def load_cot(micro):
        return local(r.cot_in.at[micro, 0], r.grads.at[0, slot_of(c, micro)], r.source_sem.at[micro])

    def relay_up(micro):
        return remote(r.result.at[micro], r.stream.at[micro], r.relay_send.at[micro], r.relay_recv.at[micro], 1 - section, dp)

    def relay_back(micro):
        return remote(
            r.passed.at[micro], r.grads.at[0, slot_of(c, micro)], r.relay_send.at[micro], r.relay_recv.at[micro], 1 - section, dp
        )

    def share_acts(micro, core=c):
        return remote(
            r.acts_out, r.acts.at[:, :, slot_of(core, micro)], r.acts_send.at[micro], r.acts_recv.at[micro], section, pair_dp
        )

    def share_branch(micro, core=c):
        rows = slot_of(core, micro)
        return remote(r.grads.at[0, rows], r.grads.at[0, rows], r.branch_send.at[micro], r.branch_recv.at[micro], section, pair_dp)

    def share_lifted(micro, core=c):
        rows = slot_of(core, micro)
        return remote(
            r.grads.at[1:5, rows], r.grads.at[1:5, rows], r.lifted_send.at[micro], r.lifted_recv.at[micro], section, pair_dp
        )

    def share_rest(micro, core=c):
        rows = slot_of(core, micro)
        return remote(
            r.grads.at[5:9, rows], r.grads.at[5:9, rows], r.rest_send.at[micro], r.rest_recv.at[micro], section, pair_dp
        )

    r.share_lifted = share_lifted
    r.share_acts = share_acts

    def to_y(unit):
        return remote(
            r.partial.at[unit, 0], r.y_in.at[unit - FAR], r.y_send.at[unit - FAR], r.y_recv.at[unit - FAR], section, y_dp
        )

    def rows_of(place):
        return pl.ds(BLOCK * place, BLOCK)

    def near_z(unit, place, index, lane, to_dp):
        near = unit - FAR
        return remote(
            r.partial.at[unit, 1, rows_of(place)], r.z_in.at[near, index],
            r.z_send.at[near, lane], r.z_recv.at[near, index], section, to_dp,
        )

    def far_z(unit, place, index, lane, to_dp):
        return remote(
            r.partial.at[unit, :, rows_of(place)], r.far_z_in.at[unit, index],
            r.far_z_send.at[unit, lane], r.far_z_recv.at[unit, index], section, to_dp,
        )

    def far_to_y(unit, place):
        return remote(
            r.partial.at[unit, 0, rows_of(place)], r.far_y_in.at[unit], r.far_y_send.at[unit], r.far_y_recv.at[unit], section, y_dp
        )

    r.load_inward.start()

    @pl.when(leading)
    def _():
        load_x(0).start()
        load_x(1).start()

    @pl.when(jnp.logical_not(leading))
    def _():
        load_cot(0).start()
        load_cot(1).start()

    @pl.when(jnp.logical_not(leading))
    def _():
        r.load_rest()

    r.sums[...] = jnp.zeros_like(r.sums)

    barrier = pltpu.get_barrier_semaphore()
    peers = [(1 - section, dp), (section, pair_dp), (section, y_dp)]
    peers += [(section, lax.rem(dp + 4 * hop, 16)) for hop in (1, 2, 3)]
    for peer in peers:
        pl.semaphore_signal(barrier, inc=1, device_id=peer, device_id_type=MESH)

    def everyone_in():
        pl.semaphore_wait(barrier, len(peers))

    def arrive(micro):
        relay_back(micro).wait_recv()
        share_branch(micro).start()

    def weight_operands(unit):
        whole = lax.div(unit, 2)
        slab = jnp.minimum(whole, 4) + jnp.where(whole >= 8, 1, 0) + jnp.where(whole >= 9, 1, 0)
        cols = pl.ds(pl.multiple_of(lax.rem(unit, 2) * COLUMNS, 128), COLUMNS)
        other = pl.ds(pl.multiple_of((1 - y) * 192, 64), 192)
        own = pl.ds(pl.multiple_of(y * 192, 64), 192)
        return slab, other, own, r.grads[jnp.maximum(whole - 3, 0), :, cols]

    def near_unit(unit):
        slab, other, own, grads = weight_operands(unit)
        r.partial[unit, 0] = times(r.acts[slab, other, :], grads).astype(SLIM)
        to_y(unit).start()
        r.partial[unit, 1] = times(r.acts[slab, own, :], grads).astype(SLIM)

    def far_unit(unit):
        slab, other, own, grads = weight_operands(unit)
        r.partial[unit, 0] = times(r.acts[slab, other, :], grads).astype(SLIM)
        r.partial[unit, 1] = times(r.acts[slab, own, :], grads).astype(SLIM)
        at_ends(unit, far_z, r.far_z_in)

    def arrived(unit, index, copy, into):
        copy(unit, 0, index, 0, dp).wait_recv()
        return into[unit if into is r.far_z_in else unit - FAR, index].astype(WIDE)

    def pick(unit, place, copy):
        return (unit, slice(None) if copy is far_z else 1, rows_of(place))

    def go_right(unit, here, copy, into):
        for place in range(3, here, -1):
            at = pick(unit, place, copy)
            if here > 0:
                r.partial[at] = (r.partial[at].astype(WIDE) + arrived(unit, place + 1, copy, into)).astype(SLIM)
            copy(unit, place, place + 1, place - 1, dp + 4).start()

    def go_left(unit, here, copy, into):
        for place in range(here):
            at = pick(unit, place, copy)
            if here < 3:
                r.partial[at] = (r.partial[at].astype(WIDE) + arrived(unit, place, copy, into)).astype(SLIM)
            copy(unit, place, place, place, dp - 4).start()

    def at_ends(unit, copy, into):
        @pl.when(z == 0)
        def _():
            go_right(unit, 0, copy, into)

        @pl.when(z == 3)
        def _():
            go_left(unit, 3, copy, into)

    def at_middle_first(unit, copy, into):
        @pl.when(z == 1)
        def _():
            go_right(unit, 1, copy, into)

        @pl.when(z == 2)
        def _():
            go_left(unit, 2, copy, into)

    def at_middle_second(unit, copy, into):
        @pl.when(z == 1)
        def _():
            go_left(unit, 1, copy, into)

        @pl.when(z == 2)
        def _():
            go_right(unit, 2, copy, into)

    def gathered(unit, here, copy, into):
        value = r.partial[pick(unit, here, copy)].astype(WIDE)
        if here > 0:
            value = value + arrived(unit, here + 1, copy, into)
        if here < 3:
            value = value + arrived(unit, here, copy, into)
        return value

    def everywhere(action):
        for here in range(4):

            @pl.when(z == here)
            def _():
                action(here)

    def slot(t, carry):
        trailing = jnp.logical_not(leading)
        half = lax.div(t, 2)
        is_forward = (leading & (t < 2)) | (trailing & ((t == 1) | (t == 3)))
        is_backward = (leading & ((t == 3) | (t == 5))) | (trailing & ((t == 2) | (t == 4)))
        is_weights = (leading & (t == 4)) | (trailing & (t == 5))

        @pl.when(trailing & (t == 0))
        def _():
            everyone_in()
            for micro in range(2):
                load_cot(micro).wait()
                share_branch(micro).start()

        @pl.when(is_forward)
        def _():
            micro = jnp.where(leading, jnp.minimum(t, 1), jnp.minimum(half, 1))

            @pl.when(leading)
            def _():
                load_x(micro).wait()

            @pl.when(trailing)
            def _():
                relay_up(micro).wait_recv()

            forward(r, micro, pl.multiple_of((c * 2 + micro) * length, length), t == section, leading)

            @pl.when(leading & (t == 0))
            def _():
                everyone_in()

            share_acts(micro).start()
            ahead = leading & (c == 0) & (t == 0)

            @pl.when(leading & (c == 1) & (t == 0))
            def _():
                pl.semaphore_wait(r.turn, 1)

            @pl.when(leading)
            def _():
                relay_up(micro).start()

            @pl.when(ahead)
            def _():
                relay_up(0).wait_send()
                pl.semaphore_signal(r.turn, inc=1, device_id=(section, pair_dp), device_id_type=MESH)

        @pl.when(leading & (t == 3))
        def _():
            arrive(0)

        @pl.when(is_backward)
        def _():
            micro = jnp.clip(half - 1, 0, 1)
            backward(r, micro, pl.multiple_of((c * 2 + micro) * length, length))

            @pl.when(trailing)
            def _():
                relay_back(micro).start()

            share_rest(micro).start()

        @pl.when(leading & (t == 4))
        def _():
            arrive(1)

        @pl.when(is_weights)
        def _():
            for micro in range(2):
                share_branch(micro, 1 - c).wait_recv()
                share_acts(micro, 1 - c).wait_recv()

            early_far = sum(at < 0 for at in FAR_AT)

            def body(i, carry):
                @pl.when(i < EARLY_NEAR)
                def _():
                    near_unit(FAR + i)

                @pl.when(i < early_far)
                def _():
                    far_unit(i)

                return carry

            lax.fori_loop(0, max(EARLY_NEAR, early_far), body, 0)

        return carry

    lax.fori_loop(0, 6, slot, 0)

    def norm_copy(src, dst, index, to_dp):
        return remote(r.norms.at[src], r.norms.at[dst], r.norm_send.at[index], r.norm_recv.at[index], section, to_dp)

    def norm_to_pair():
        return norm_copy(0, 1, 0, pair_dp)

    def norm_to_y():
        return norm_copy(2, 3, 1, y_dp)

    def norm_to_z(hop):
        return norm_copy(4, 4 + hop, 1 + hop, lax.rem(dp + 4 * hop, 16))

    r.norms[0] = jnp.concatenate([jnp.sum(r.sums[...], 1), jnp.zeros((4, r.sums.shape[2]), WIDE)], 0)
    norm_to_pair().start()
    for micro in range(2):
        share_lifted(micro, 1 - c).wait_recv()

    def sum_y(unit):
        to_y(unit).wait_recv()
        r.partial[unit, 1] = (r.partial[unit, 1].astype(WIDE) + r.y_in[unit - FAR].astype(WIDE)).astype(SLIM)

    def far_turn(i, steps):
        turn, unit = i < 0, jnp.int32(0)
        for index, step in enumerate(steps):
            if step >= 0:
                turn = turn | (i == step)
                unit = jnp.where(i == step, index, unit)
        return turn, unit

    def near_turn(i, lag):
        return (i >= lag) & (i < NEAR + lag), jnp.clip(i - lag, 0, NEAR - 1) + FAR

    def advance(i, carry):
        issued = FAR + EARLY_NEAR + i - HOLD

        @pl.when(issued == 16)
        def _():
            for micro in range(2):
                share_rest(micro, 1 - c).wait_recv()

        @pl.when((issued >= FAR + EARLY_NEAR) & (issued < UNITS))
        def _():
            near_unit(issued)

        turn, unit = far_turn(i, FAR_AT)

        @pl.when(turn)
        def _(unit=unit):
            far_unit(unit)

        @pl.when(i < NEAR)
        def _():
            sum_y(FAR + i)
            at_ends(FAR + i, near_z, r.z_in)

        turn, unit = near_turn(i, LAGS[0])

        @pl.when(turn)
        def _(unit=unit):
            at_middle_first(unit, near_z, r.z_in)

        turn, unit = far_turn(i, FAR_FIRST)

        @pl.when(turn)
        def _(unit=unit):
            at_middle_first(unit, far_z, r.far_z_in)

        turn, unit = far_turn(i, FAR_SECOND)

        @pl.when(turn)
        def _(unit=unit):
            at_middle_second(unit, far_z, r.far_z_in)

        turn, unit = far_turn(i, FAR_ARRIVED)

        @pl.when(turn)
        def _(unit=unit):
            def action(here):
                value = gathered(unit, here, far_z, r.far_z_in)
                r.partial[unit, 0, rows_of(here)] = value[0].astype(SLIM)
                far_to_y(unit, here).start()
                r.staged[unit] = value[1]

            everywhere(action)

        turn, unit = far_turn(i, FAR_DONE)

        @pl.when(turn)
        def _(unit=unit):
            far_to_y(unit, 0).wait_recv()
            r.staged[unit] += r.far_y_in[unit].astype(WIDE)

        turn, unit = near_turn(i, LAGS[1])

        @pl.when(turn)
        def _(unit=unit):
            at_middle_second(unit, near_z, r.z_in)

        turn, unit = near_turn(i, LAGS[2])

        @pl.when(turn)
        def _(unit=unit):
            def action(here):
                r.staged[unit] = gathered(unit, here, near_z, r.z_in)

            everywhere(action)

        @pl.when(i == 1)
        def _():
            norm_to_pair().wait()
            r.norms[2] = r.norms[0] + r.norms[1]
            norm_to_y().start()

        @pl.when(i == 9)
        def _():
            norm_to_y().wait_recv()
            r.norms[4] = r.norms[2] + r.norms[3]
            for hop in (1, 2, 3):
                norm_to_z(hop).start()

        @pl.when(i == 18)
        def _():
            for hop in (1, 2, 3):
                norm_to_z(hop).wait_recv()
            r.out_norms[...] = (r.norms[4] + r.norms[5]) + (r.norms[6] + r.norms[7])

        return carry

    lax.fori_loop(0, max(NEAR + LAGS[2], FAR_DONE[-1] + 1), advance, 0)

    norm_to_y().wait_send()
    for hop in (1, 2, 3):
        norm_to_z(hop).wait_send()
    share_acts(1).wait_send()
    for micro in range(2):
        share_branch(micro).wait_send()
        share_lifted(micro).wait_send()
        share_rest(micro).wait_send()

        @pl.when(leading if micro else leading & (c == 1))
        def _():
            relay_up(micro).wait_send()

        @pl.when(jnp.logical_not(leading))
        def _():
            relay_back(micro).wait_send()

    def drain_near(near, carry):
        to_y(FAR + near).wait_send()
        for lane in range(3):
            near_z(FAR + near, 0, 0, lane, dp).wait_send()
        return carry

    lax.fori_loop(0, NEAR, drain_near, 0)

    def drain_far(unit, carry):
        far_to_y(unit, 0).wait_send()
        for lane in range(3):
            far_z(unit, 0, 0, lane, dp).wait_send()
        return carry

    lax.fori_loop(0, FAR, drain_far, 0)


def hand_over_kernel(result, grad, staged, norms, *refs):
    out_result, out_grad, out_inward, out_outward, out_up, out_down, gain_grad, bias_grad, sem = refs
    width = result.shape[2]

    def start(source, target):
        copy = pltpu.make_async_copy(source, target, sem)
        copy.start()
        return copy

    copies = [start(result, out_result.at[0, :, 0]), start(grad, out_grad.at[0, :, 0])]
    for unit in range(UNITS):
        half = pl.ds(unit % 2 * COLUMNS, COLUMNS)
        if unit < 8:
            target = out_down.at[0, pl.ds(unit // 2 * BLOCK, BLOCK), half]
        elif unit < 16:
            target = out_up.at[0, :, pl.ds((unit - 8) * COLUMNS, COLUMNS)]
        elif unit < 18:
            target = out_outward.at[0, :, half]
        else:
            target = out_inward.at[0, :, pl.ds((unit - 18) * COLUMNS, COLUMNS)]
        copies.append(start(staged.at[unit], target))
    share = gain_grad.shape[2]
    for index in range(width // share):

        @pl.when(lax.axis_index("dp") == index)
        def _():
            gain_grad[0] = norms[0:2, index * share : (index + 1) * share]
            bias_grad[0] = norms[2:4, index * share : (index + 1) * share]

    for copy in copies:
        copy.wait()


def step_on_device(
    inputs, clip_lengths, anchor_offsets, cotangent, inward_weight, outward_weight, up_weight, down_weight, norm_gain, norm_bias
):
    _, _, length, width = inputs.shape
    wide_ff = up_weight.shape[2]
    anywhere = pl.BlockSpec(memory_space=pl.ANY)
    in_vmem = pl.BlockSpec(memory_space=pltpu.VMEM)
    in_smem = pl.BlockSpec(memory_space=pltpu.SMEM)
    dma = pltpu.SemaphoreType.DMA
    share = width // lax.axis_size("dp")
    made = pl.pallas_call(
        step_kernel,
        out_shape=(
            pltpu.VMEM((2, length, width), SLIM),
            pltpu.VMEM((2, length, width), WIDE),
            pltpu.VMEM((UNITS, BLOCK, COLUMNS), WIDE),
            pltpu.VMEM((8, width), WIDE),
        ),
        in_specs=[anywhere] * 6 + [in_vmem] * 2 + [in_smem] * 2,
        out_specs=[in_vmem] * 4,
        scratch_shapes=[
            pltpu.VMEM((2, length, width), SLIM),
            pltpu.VMEM((width, 3 * width), SLIM),
            pltpu.VMEM((width, width), SLIM),
            pltpu.VMEM((width, wide_ff), SLIM),
            pltpu.VMEM((wide_ff, width), SLIM),
            pltpu.VMEM((9, 4 * length, width), SLIM),
            pltpu.VMEM((7, 8 * BLOCK, 4 * length), SLIM),
            pltpu.VMEM((7, 8 * BLOCK, length), SLIM),
            pltpu.VMEM((2, width // HEAD, length, length), SLIM),
            pltpu.VMEM((length, width), SLIM),
            pltpu.VMEM((length, width), SLIM),
            pltpu.VMEM((width, length), SLIM),
            pltpu.VMEM((length, width), WIDE),
            pltpu.VMEM((2, length, width), SLIM),
            pltpu.VMEM((4, 8, width), WIDE),
            pltpu.VMEM((length, length), WIDE),
            pltpu.VMEM((UNITS, 2, 4 * BLOCK, COLUMNS), SLIM),
            pltpu.VMEM((NEAR, 4 * BLOCK, COLUMNS), SLIM),
            pltpu.VMEM((NEAR, 5, BLOCK, COLUMNS), SLIM),
            pltpu.VMEM((FAR, BLOCK, COLUMNS), SLIM),
            pltpu.VMEM((FAR, 5, 2, BLOCK, COLUMNS), SLIM),
            pltpu.VMEM((8, 8, width), WIDE),
            dma((4,)), dma((2,)),
            *[dma((2,))] * 10, pltpu.SemaphoreType.REGULAR,
            dma((NEAR,)), dma((NEAR,)), dma((NEAR, 3)), dma((NEAR, 5)),
            dma((FAR,)), dma((FAR,)), dma((FAR, 3)), dma((FAR, 5)), dma((5,)), dma((5,)),
        ],
        compiler_params=pltpu.CompilerParams(
            collective_id=0, has_side_effects=True, vmem_limit_bytes=VMEM_BYTES - 4500000
        ),
    )(
        inputs, cotangent, inward_weight, outward_weight, up_weight, down_weight,
        norm_gain, norm_bias, clip_lengths, anchor_offsets,
    )
    sections = 1
    return pl.pallas_call(
        hand_over_kernel,
        out_shape=(
            jax.ShapeDtypeStruct((sections, 2, 1, length, width), SLIM),
            jax.ShapeDtypeStruct((sections, 2, 1, length, width), WIDE),
            jax.ShapeDtypeStruct((sections, BLOCK, 3 * width), WIDE),
            jax.ShapeDtypeStruct((sections, BLOCK, width), WIDE),
            jax.ShapeDtypeStruct((sections, BLOCK, wide_ff), WIDE),
            jax.ShapeDtypeStruct((sections, 4 * BLOCK, width), WIDE),
            jax.ShapeDtypeStruct((sections, 2, share), WIDE),
            jax.ShapeDtypeStruct((sections, 2, share), WIDE),
        ),
        in_specs=[in_vmem] * 4,
        out_specs=[anywhere] * 6 + [in_vmem] * 2,
        scratch_shapes=[dma],
        compiler_params=pltpu.CompilerParams(vmem_limit_bytes=1 << 20),
    )(*[pltpu.with_memory_space_constraint(one, pltpu.VMEM) for one in made])


def shifted(x, axis, by):
    size = lax.axis_size(axis)
    pairs = [(i, i + by) for i in range(size) if 0 <= i + by < size]
    return lax.ppermute(x, axis, pairs)


def norm_rows(values, norm_gain, norm_bias):
    average = jnp.mean(values, -1, keepdims=True)
    centred = values - average
    inverse = lax.rsqrt(jnp.mean(centred * centred, -1, keepdims=True) + EPSILON)
    normed = centred * inverse
    return (normed * norm_gain + norm_bias, normed, inverse)


def norm_back(norm_grad, normed, inverse, norm_gain):
    inner = norm_grad * norm_gain
    through = inverse * (
        inner
        - jnp.mean(inner, -1, keepdims=True)
        - normed * jnp.mean(inner * normed, -1, keepdims=True)
    )
    return (through, jnp.sum(norm_grad * normed, 0), jnp.sum(norm_grad, 0))


def gelu_slope(lifted):
    cumulative = 0.5 * (1.0 + lax.erf(lifted * 0.7071067811865476))
    density = jnp.exp(-0.5 * lifted * lifted) * 0.3989422804014327
    return cumulative + lifted * density


def clip_marks(lengths, offsets, length):
    positions = jnp.arange(length, dtype=jnp.int32)
    clip_ends = jnp.cumsum(lengths)
    clip_starts = clip_ends - lengths
    anchor_at = clip_starts + offsets % lengths
    clip_ids = jnp.sum((positions[:, None] >= clip_ends[None, :]).astype(jnp.int32), 1)
    anchors = jnp.any(positions[:, None] == anchor_at[None, :], 1)
    return (clip_ids, anchors)


def masked_scores(query_block, key_rows, id_block, clip_ids, anchors, scaling):
    scores = (
        jnp.einsum("qhd,khd->hqk", query_block, key_rows, preferred_element_type=jnp.float32)
        * scaling
    )
    seen = (id_block[:, None] == clip_ids[None, :]) | anchors[None, :]
    return jnp.where(seen[None], scores, -1000000000.0)


def forward_layer(source, clip_ids, anchors, params):
    inward, outward, upward, downward, norm_gain, norm_bias = params
    length, model_width = source.shape
    head_count = model_width // HEAD
    scaling = HEAD ** (-0.5)
    residual = source.astype(jnp.float32)
    first_norm, unit_one, scale_one = norm_rows(residual, norm_gain[0], norm_bias[0])
    joined = jnp.dot(
        first_norm.astype(jnp.bfloat16), inward, preferred_element_type=jnp.float32
    ).astype(jnp.bfloat16)
    heads_view = joined.reshape(length, 3, head_count, HEAD)
    queries = heads_view[:, 0]
    key_rows = heads_view[:, 1]
    values = heads_view[:, 2]
    scores = masked_scores(queries, key_rows, clip_ids, clip_ids, anchors, scaling)
    row_max = jnp.max(scores, -1, keepdims=True)
    raised = jnp.exp(scores - row_max)
    row_sum = jnp.sum(raised, -1, keepdims=True)
    weights = (raised / row_sum).astype(jnp.bfloat16)
    pieces = [jnp.einsum("hqk,khd->qhd", weights, values, preferred_element_type=jnp.float32)]
    log_sums = [(row_max + jnp.log(row_sum))[..., 0]]
    attended = jnp.concatenate(pieces, 0).reshape(length, model_width).astype(jnp.bfloat16)
    logsum = jnp.concatenate(log_sums, 1)
    middle = residual + jnp.dot(attended, outward, preferred_element_type=jnp.float32)
    second_norm, unit_two, scale_two = norm_rows(middle, norm_gain[1], norm_bias[1])
    lifted = jnp.dot(second_norm.astype(jnp.bfloat16), upward, preferred_element_type=jnp.float32)
    active = jax.nn.gelu(lifted, approximate=False).astype(jnp.bfloat16)
    result = middle + jnp.dot(active, downward, preferred_element_type=jnp.float32)
    stored = (unit_one, scale_one, joined, logsum, attended, unit_two, scale_two, lifted, active)
    return (result, stored)


def contract_rows(left, right):
    return lax.dot_general(
        left, right, (((0,), (0,)), ((), ())), preferred_element_type=jnp.float32
    )


def contract_cols(left, right):
    return lax.dot_general(
        left, right, (((1,), (1,)), ((), ())), preferred_element_type=jnp.float32
    )


def feed_backward(incoming, stored, params):
    inward, outward, upward, downward, norm_gain, norm_bias = params
    unit_one, scale_one, joined, logsum, attended, unit_two, scale_two, lifted, active = stored
    branch = incoming.astype(jnp.bfloat16)
    down_part = contract_rows(active, branch)
    hidden_grad = contract_cols(branch, downward)
    lifted_grad = (hidden_grad * gelu_slope(lifted)).astype(jnp.bfloat16)
    second_in = (unit_two * norm_gain[1] + norm_bias[1]).astype(jnp.bfloat16)
    up_part = contract_rows(second_in, lifted_grad)
    normed_grad = contract_cols(lifted_grad, upward)
    through, gain_two, bias_two = norm_back(normed_grad, unit_two, scale_two, norm_gain[1])
    return (incoming + through, (up_part, down_part, gain_two, bias_two))


def attend_backward(middle_grad, stored, clip_ids, anchors, params):
    inward, outward, upward, downward, norm_gain, norm_bias = params
    unit_one, scale_one, joined, logsum, attended, unit_two, scale_two, lifted, active = stored
    length, model_width = attended.shape
    head_count = model_width // HEAD
    scaling = HEAD ** (-0.5)
    branch = middle_grad.astype(jnp.bfloat16)
    outward_part = contract_rows(attended, branch)
    attended_grad = (
        contract_cols(branch, outward).astype(jnp.bfloat16).reshape(length, head_count, HEAD)
    )
    heads_view = joined.reshape(length, 3, head_count, HEAD)
    queries = heads_view[:, 0]
    key_rows = heads_view[:, 1]
    values = heads_view[:, 2]
    key_grad = jnp.zeros((length, head_count, HEAD), jnp.float32)
    value_grad = jnp.zeros((length, head_count, HEAD), jnp.float32)
    block_rows = min(512, length)
    scores = masked_scores(queries, key_rows, clip_ids, clip_ids, anchors, scaling)
    weights = jnp.exp(scores - logsum[:, 0:block_rows, None])
    weight_grad = jnp.einsum(
        "qhd,khd->hqk", attended_grad, values, preferred_element_type=jnp.float32
    )
    score_grad = (
        weights * (weight_grad - jnp.sum(weights * weight_grad, -1, keepdims=True))
    ).astype(jnp.bfloat16)
    query_pieces = [
        scaling
        * jnp.einsum("hqk,khd->qhd", score_grad, key_rows, preferred_element_type=jnp.float32)
    ]
    key_grad = key_grad + scaling * jnp.einsum(
        "hqk,qhd->khd", score_grad, queries, preferred_element_type=jnp.float32
    )
    value_grad = value_grad + jnp.einsum(
        "hqk,qhd->khd",
        weights.astype(jnp.bfloat16),
        attended_grad,
        preferred_element_type=jnp.float32,
    )
    query_grad = jnp.concatenate(query_pieces, 0)
    joined_grad = (
        jnp.stack([query_grad, key_grad, value_grad], 1)
        .reshape(length, 3 * model_width)
        .astype(jnp.bfloat16)
    )
    first_in = (unit_one * norm_gain[0] + norm_bias[0]).astype(jnp.bfloat16)
    inward_part = contract_rows(first_in, joined_grad)
    normed_grad = contract_cols(joined_grad, inward)
    through, gain_one, bias_one = norm_back(normed_grad, unit_one, scale_one, norm_gain[0])
    return (middle_grad + through, (inward_part, outward_part, gain_one, bias_one))


def resting(function):

    def blank(*operands):
        return jax.tree.map(jnp.zeros_like, function(*operands))

    return blank


def take_slot(holder, buffer_slot):
    return jax.tree.map(
        lambda element: lax.dynamic_index_in_dim(element, buffer_slot, 0, False), holder
    )


def place_slot(holder, item, buffer_slot, working):

    def update(element, fresh):
        former = lax.dynamic_index_in_dim(element, buffer_slot, 0, False)
        return lax.dynamic_update_index_in_dim(
            element, jnp.where(working, fresh, former), buffer_slot, 0
        )

    return jax.tree.map(update, holder, item)


def per_device(
    inputs,
    clip_lengths,
    anchor_offsets,
    cotangent,
    inward_weight,
    outward_weight,
    up_weight,
    down_weight,
    norm_gain,
    norm_bias,
):
    params = (
        inward_weight[0],
        outward_weight[0],
        up_weight[0],
        down_weight[0],
        norm_gain[0],
        norm_bias[0],
    )
    stream = inputs[:, 0]
    cot_rows = cotangent[:, 0]
    lengths_all = clip_lengths[:, 0]
    offsets_all = anchor_offsets[:, 0]
    micro_count = stream.shape[0]
    length = stream.shape[1]
    section_index = lax.axis_index("section")
    section_count = lax.axis_size("section")
    leading = section_index == 0
    trailing = section_index == section_count - 1
    periods = micro_count + section_count - 1
    arriving = jnp.zeros_like(stream[0])
    produced = jnp.zeros_like(stream)
    archive = None
    for period in range(periods):
        micro_index = period - section_index
        working = (micro_index >= 0) & (micro_index < micro_count)
        buffer_slot = jnp.clip(micro_index, 0, micro_count - 1)
        source = jnp.where(leading, stream[min(period, micro_count - 1)], arriving)
        clip_ids, anchors = clip_marks(
            take_slot(lengths_all, buffer_slot), take_slot(offsets_all, buffer_slot), length
        )
        result, stored = lax.cond(
            working, forward_layer, resting(forward_layer), source, clip_ids, anchors, params
        )
        if archive is None:
            archive = jax.tree.map(
                lambda element: jnp.zeros((micro_count,) + element.shape, element.dtype), stored
            )
        archive = place_slot(archive, stored, buffer_slot, working)
        sending = result.astype(jnp.bfloat16)
        produced = place_slot(produced, sending, buffer_slot, working)
        if period < micro_count:
            arriving = shifted(sending, "section", 1)
    inward, outward, upward, downward, gains, biases = params
    up_sum = jnp.zeros(upward.shape, jnp.float32)
    down_sum = jnp.zeros(downward.shape, jnp.float32)
    gain_two = jnp.zeros(gains.shape[1:], jnp.float32)
    bias_two = jnp.zeros(biases.shape[1:], jnp.float32)
    inward_sum = jnp.zeros(inward.shape, jnp.float32)
    outward_sum = jnp.zeros(outward.shape, jnp.float32)
    gain_one = jnp.zeros(gains.shape[1:], jnp.float32)
    bias_one = jnp.zeros(biases.shape[1:], jnp.float32)
    upstream = jnp.zeros_like(stream[0])
    returned = jnp.zeros(stream.shape, jnp.float32)
    for period in range(periods):
        micro_index = micro_count - 1 - period + (section_count - 1 - section_index)
        working = (micro_index >= 0) & (micro_index < micro_count)
        buffer_slot = jnp.clip(micro_index, 0, micro_count - 1)
        incoming = jnp.where(trailing, take_slot(cot_rows, buffer_slot), upstream).astype(
            jnp.float32
        )
        clip_ids, anchors = clip_marks(
            take_slot(lengths_all, buffer_slot), take_slot(offsets_all, buffer_slot), length
        )
        stored = take_slot(archive, buffer_slot)
        middle_grad, feed_part = lax.cond(
            working, feed_backward, resting(feed_backward), incoming, stored, params
        )
        up_sum = up_sum + feed_part[0]
        down_sum = down_sum + feed_part[1]
        gain_two = gain_two + feed_part[2]
        bias_two = bias_two + feed_part[3]
        input_grad, attend_part = lax.cond(
            working,
            attend_backward,
            resting(attend_backward),
            middle_grad,
            stored,
            clip_ids,
            anchors,
            params,
        )
        inward_sum = inward_sum + attend_part[0]
        outward_sum = outward_sum + attend_part[1]
        gain_one = gain_one + attend_part[2]
        bias_one = bias_one + attend_part[3]
        returned = place_slot(returned, input_grad, buffer_slot, working)
        if period < periods - 1:
            upstream = shifted(input_grad.astype(jnp.bfloat16), "section", -1)
    inward_sum, outward_sum, up_sum, down_sum, gain_one, gain_two, bias_one, bias_two = (
        lax.psum_scatter(inward_sum, "dp", scatter_dimension=0, tiled=True),
        lax.psum_scatter(outward_sum, "dp", scatter_dimension=0, tiled=True),
        lax.psum_scatter(up_sum, "dp", scatter_dimension=0, tiled=True),
        lax.psum_scatter(down_sum, "dp", scatter_dimension=0, tiled=True),
        lax.psum_scatter(gain_one, "dp", scatter_dimension=0, tiled=True),
        lax.psum_scatter(gain_two, "dp", scatter_dimension=0, tiled=True),
        lax.psum_scatter(bias_one, "dp", scatter_dimension=0, tiled=True),
        lax.psum_scatter(bias_two, "dp", scatter_dimension=0, tiled=True),
    )
    layer_outputs = produced[None, :, None]
    input_grads = returned[None, :, None]
    gain_grad = jnp.stack([gain_one, gain_two])[None]
    bias_grad = jnp.stack([bias_one, bias_two])[None]
    return (
        layer_outputs,
        input_grads,
        inward_sum[None],
        outward_sum[None],
        up_sum[None],
        down_sum[None],
        gain_grad,
        bias_grad,
    )


def solution(mesh):
    local = step_on_device if mesh.shape["dp"] == 16 and mesh.shape["section"] == 2 else per_device
    return jax.shard_map(
        local,
        mesh=mesh,
        in_specs=(
            P(None, "dp", None, None),
            P(None, "dp", None),
            P(None, "dp", None),
            P(None, "dp", None, None),
            P("section", None, None),
            P("section", None, None),
            P("section", None, None),
            P("section", None, None),
            P("section", None, None),
            P("section", None, None),
        ),
        out_specs=(
            P("section", None, "dp", None, None),
            P("section", None, "dp", None, None),
            P("section", "dp", None),
            P("section", "dp", None),
            P("section", "dp", None),
            P("section", "dp", None),
            P("section", None, "dp"),
            P("section", None, "dp"),
        ),
        check_vma=False,
    )
```

```python
import functools
import types

import jax
import jax.numpy as jnp
from jax import lax
from jax.experimental import pallas as pl
from jax.experimental.pallas import tpu as pltpu
from jax.sharding import PartitionSpec as P

HEAD = 64
EPSILON = 1e-06
MESH = pl.DeviceIdType.MESH
WIDE = jnp.float32
SLIM = jnp.bfloat16
VMEM_BYTES = 67043328

UNITS = 24
FAR = 4
NEAR = UNITS - FAR
BLOCK = 48
COLUMNS = 384
EARLY_NEAR = 5
HOLD = 1
LAGS = (3, 6, 8)
FAR_AT = (-1, -1, -1, 6)
FAR_FIRST = (2, 5, 10, 11)
FAR_SECOND = (6, 11, 16, 14)
FAR_ARRIVED = (17, 20, 21, 19)
FAR_DONE = (22, 27, 24, 21)
EARLY_FAR = sum(step < 0 for step in FAR_AT)


PIECES = [s if s < EARLY_FAR else 8 + s - EARLY_FAR for s in range(FAR)]
PIECES += [s - FAR + EARLY_FAR if s - FAR < 8 - EARLY_FAR else s for s in range(FAR, UNITS)]


def piece_of(slot):
    near = slot - FAR
    far_piece = jnp.where(slot < EARLY_FAR, slot, 8 + slot - EARLY_FAR)
    return jnp.where(slot < FAR, far_piece, jnp.where(near < 8 - EARLY_FAR, near + EARLY_FAR, slot))


def times(left, right):
    return jnp.dot(left, right, preferred_element_type=WIDE)


def times_turned(left, right):
    return lax.dot_general(left, right, (((1,), (1,)), ((), ())), preferred_element_type=WIDE)


def unit_rows(values):
    centred = values - jnp.mean(values, -1, keepdims=True)
    inverse = lax.rsqrt(jnp.mean(centred * centred, -1, keepdims=True) + EPSILON)
    return centred * inverse, inverse


def norm_rows_bf16(r, values, which):
    unit, _ = unit_rows(values)
    return (unit * r.gain[0, which : which + 1, :] + r.bias[0, which : which + 1, :]).astype(SLIM)


def norm_backward(r, values, norm_grad, which):
    unit, inverse = unit_rows(values)
    width = values.shape[1]
    r.sums[which] += jnp.sum((norm_grad * unit).reshape(-1, 8, width), 0)
    r.sums[2 + which] += jnp.sum(norm_grad.reshape(-1, 8, width), 0)
    inner = norm_grad * r.gain[0, which : which + 1, :]
    return inverse * (
        inner
        - jnp.mean(inner, -1, keepdims=True)
        - unit * jnp.mean(inner * unit, -1, keepdims=True)
    )


def head_lanes():
    lane = lax.broadcasted_iota(jnp.int32, (1, 2 * HEAD), 1)
    first = jnp.where(lane < HEAD, 1.0, 0.0).astype(WIDE)
    return first, 1.0 - first


def mask_bias(r, micro):
    length = r.bias_mask.shape[0]

    def marks(positions):
        end = jnp.int32(0)
        ids = jnp.zeros(positions.shape, jnp.int32)
        anchors = jnp.zeros(positions.shape, jnp.int32)
        for clip in range(r.lengths.shape[2]):
            size = r.lengths[micro, 0, clip]
            anchor = end + lax.rem(r.offsets[micro, 0, clip], size)
            end = end + size
            ids = ids + jnp.where(positions >= end, 1, 0)
            anchors = anchors + jnp.where(positions == anchor, 1, 0)
        return ids, anchors

    key_ids, anchors = marks(lax.broadcasted_iota(jnp.int32, (length, 1), 0))
    query_ids, _ = marks(lax.broadcasted_iota(jnp.int32, (1, length), 1))
    seen = (key_ids == query_ids) | (jnp.broadcast_to(anchors, (length, length)) > 0)
    r.bias_mask[...] = jnp.where(seen, 0.0, -1000000000.0).astype(WIDE)


def place(r, slab, tokens):
    for line in range(8):
        z, y = line // 2, line % 2
        rows = pl.ds(y * 192 + z * BLOCK, BLOCK)
        own = pl.ds(pl.multiple_of(2 * BLOCK * line + r.c * BLOCK, 16), BLOCK)
        other = pl.ds(pl.multiple_of(2 * BLOCK * line + (1 - r.c) * BLOCK, 16), BLOCK)
        r.acts[slab, rows, tokens] = r.turned[own, :]
        r.acts_out[slab, rows, :] = r.turned[other, :]


def forward(r, micro, tok, first, leading):
    length, width = r.normed.shape
    tokens = pl.ds(tok, length)
    mask_bias(r, micro)
    r.normed[...] = norm_rows_bf16(r, r.stream[micro].astype(WIDE), 0)

    @pl.when(first)
    def _():
        r.load_inward.wait()

        @pl.when(leading)
        def _():
            r.load_rest()

    for part in range(3):
        r.grads[6 + part, tokens, :] = times(
            r.normed[...], r.inward[:, part * width : (part + 1) * width]
        ).astype(SLIM)

    @pl.when(micro > 0)
    def _():
        r.share_acts(0).wait_send()

    r.turned[...] = r.normed[...].T
    place(r, 6, tokens)
    one, two = (lanes.astype(SLIM) for lanes in head_lanes())
    for pair in range(width // (2 * HEAD)):
        cols = pl.ds(pair * 2 * HEAD, 2 * HEAD)
        queries = r.grads[6, tokens, cols] * jnp.asarray(HEAD**-0.5, SLIM)
        keys = r.grads[7, tokens, cols]
        values_turned = r.grads[8, tokens, cols].T
        scores = times_turned(jnp.concatenate([keys * one, keys * two], 0), queries)
        pieces = []
        for head in range(2):
            masked = scores[length * head : length * (head + 1)] + r.bias_mask[...]
            raised = jnp.exp(masked - jnp.max(masked, 0, keepdims=True))
            weights = (raised * (1.0 / jnp.sum(raised, 0, keepdims=True))).astype(SLIM)
            r.weights[micro, 2 * pair + head] = weights
            pieces.append(times(values_turned[HEAD * head : HEAD * (head + 1)], weights).astype(SLIM))
        attended_turned = jnp.concatenate(pieces, 0)
        r.turned[cols, :] = attended_turned
        r.held[:, cols] = attended_turned.T
    place(r, 5, tokens)

    @pl.when(first)
    def _():
        r.load_outward.wait()

    r.middle[micro] = r.stream[micro].astype(WIDE) + times(r.held[...], r.outward[...])
    r.normed[...] = norm_rows_bf16(r, r.middle[micro], 1)
    r.turned[...] = r.normed[...].T
    place(r, 4, tokens)

    @pl.when(first)
    def _():
        r.load_up.wait()
        r.load_down.wait()

    def activate(part):
        lifted = times(r.normed[...], r.up[:, part * width : (part + 1) * width])
        cumulative = 0.5 * (1.0 + lax.erf(lifted * 0.7071067811865476))
        density = jnp.exp(-0.5 * lifted * lifted) * 0.3989422804014327
        r.grads[1 + part, tokens, :] = (cumulative + lifted * density).astype(SLIM)
        active = (lifted * cumulative).astype(SLIM)
        r.turned[...] = active.T
        for y in range(2):
            for piece in range(4):
                rows = pl.ds(y * 192 + part * BLOCK, BLOCK)
                start = 384 * y + BLOCK * piece
                own = pl.ds(pl.multiple_of(start + r.c * 192, 16), BLOCK)
                other = pl.ds(pl.multiple_of(start + (1 - r.c) * 192, 16), BLOCK)
                r.acts[piece, rows, tokens] = r.turned[own, :]
                r.acts_out[piece, rows, :] = r.turned[other, :]
        return active

    @pl.when(leading)
    def _():
        r.total[...] = r.middle[micro]
        for part in range(4):
            r.total[...] += times(activate(part), r.down[part * width : (part + 1) * width, :])
        r.result[micro] = r.total[...].astype(SLIM)

    @pl.when(jnp.logical_not(leading))
    def _():
        for part in range(4):
            set_aside(r, micro * 12 + 2 * part, activate(part))
        middle = r.middle[micro]
        upper = middle.astype(SLIM)
        set_aside(r, micro * 12 + 8, upper)
        set_aside(r, micro * 12 + 10, (middle - upper.astype(WIDE)).astype(SLIM))


def set_aside(r, slot, values):
    for half in range(2):
        columns = values[:, half * COLUMNS : (half + 1) * COLUMNS]
        r.partial[slot + half, 0] = columns[:192]
        r.partial[slot + half, 1, 0:64] = columns[192:]


def set_back(r, slot):
    halves = [
        jnp.concatenate([r.partial[slot + half, 0], r.partial[slot + half, 1, 0:64]], 0) for half in range(2)
    ]
    return jnp.concatenate(halves, 1)


def last_output(r, micro):
    width = r.normed.shape[1]
    r.total[...] = set_back(r, micro * 12 + 8).astype(WIDE) + set_back(r, micro * 12 + 10).astype(WIDE)
    for part in range(4):
        r.total[...] += times(set_back(r, micro * 12 + 2 * part), r.down[part * width : (part + 1) * width, :])
    r.result[micro] = r.total[...].astype(SLIM)


def backward(r, micro, tok):
    length, width = r.normed.shape
    tokens = pl.ds(tok, length)
    r.total[...] = jnp.zeros((length, width), WIDE)
    for part in range(4):
        cols = slice(part * width, (part + 1) * width)
        hidden = times_turned(r.grads[0, tokens, :], r.down[cols, :])
        lifted_grad = (hidden * r.grads[1 + part, tokens, :].astype(WIDE)).astype(SLIM)
        r.grads[1 + part, tokens, :] = lifted_grad
        r.total[...] += times_turned(lifted_grad, r.up[:, cols])
    r.share_lifted(micro).start()
    middle_grad = r.grads[0, tokens, :].astype(WIDE) + norm_backward(
        r, r.middle[micro], r.total[...], 1
    )
    r.middle[micro] = middle_grad
    r.grads[5, tokens, :] = middle_grad.astype(SLIM)
    r.held[...] = times_turned(r.grads[5, tokens, :], r.outward[...]).astype(SLIM)
    first, second = head_lanes()
    one, two = first.astype(SLIM), second.astype(SLIM)
    scaling = HEAD**-0.5
    for pair in range(width // (2 * HEAD)):
        cols = pl.ds(pair * 2 * HEAD, 2 * HEAD)
        queries = r.grads[6, tokens, cols] * jnp.asarray(scaling, SLIM)
        values = r.grads[8, tokens, cols]
        keys_turned = r.grads[7, tokens, cols].T
        incoming = r.held[:, cols]
        weight_grads = times_turned(jnp.concatenate([values * one, values * two], 0), incoming)
        score_grads, query_grads, weights = [], [], []
        for head in range(2):
            kept = r.weights[micro, 2 * pair + head]
            wide = kept.astype(WIDE)
            own = weight_grads[length * head : length * (head + 1)]
            score_grad = (wide * (own - jnp.sum(wide * own, 0, keepdims=True))).astype(SLIM)
            score_grads.append(score_grad)
            weights.append(kept)
            query_grads.append(
                (times(keys_turned[HEAD * head : HEAD * (head + 1)], score_grad) * scaling).astype(SLIM)
            )
        key_grad = times(jnp.concatenate(score_grads, 0), queries)
        value_grad = times(jnp.concatenate(weights, 0), incoming)
        r.grads[6, tokens, cols] = jnp.concatenate(query_grads, 0).T
        r.grads[7, tokens, cols] = (key_grad[:length] * first + key_grad[length:] * second).astype(SLIM)
        r.grads[8, tokens, cols] = (value_grad[:length] * first + value_grad[length:] * second).astype(SLIM)
    norm_grad = times_turned(r.grads[6, tokens, :], r.inward[:, 0:width])
    for part in range(1, 3):
        norm_grad += times_turned(r.grads[6 + part, tokens, :], r.inward[:, part * width : (part + 1) * width])
    r.total[...] = norm_grad
    input_grad = r.middle[micro] + norm_backward(r, r.stream[micro].astype(WIDE), r.total[...], 0)
    r.middle[micro] = input_grad
    r.passed[micro] = input_grad.astype(SLIM)


NAMES = (
    "x_in", "cot_in", "inward_in", "outward_in", "up_in", "down_in", "gain", "bias", "lengths", "offsets",
    "result", "middle", "staged", "out_norms",
    "stream", "inward", "outward", "up", "down", "grads", "acts", "acts_out", "weights", "normed", "held",
    "turned", "total", "passed", "sums", "bias_mask",
    "partial", "y_in", "z_in", "far_y_in", "far_z_in", "norms",
    "load_sem", "source_sem",
    "relay_send", "relay_recv", "acts_send", "acts_recv", "branch_send", "branch_recv", "lifted_send", "lifted_recv",
    "rest_send", "rest_recv", "turn",
    "y_send", "y_recv", "z_send", "z_recv", "far_y_send", "far_y_recv", "far_z_send", "far_z_recv", "norm_send", "norm_recv",
)


def step_kernel(*refs):
    r = types.SimpleNamespace(**dict(zip(NAMES, refs)))
    section, dp = lax.axis_index("section"), lax.axis_index("dp")
    c, y, z = lax.rem(dp, 2), lax.rem(lax.div(dp, 2), 2), lax.div(dp, 4)
    r.c = c
    length = r.normed.shape[0]
    leading = section == 0
    pair_dp, y_dp = dp + 1 - 2 * c, dp + 2 - 4 * y

    def slot_of(core, micro):
        return pl.ds(pl.multiple_of((core * 2 + micro) * length, length), length)

    def remote(src, dst, send, recv, to_section, to_dp):
        return pltpu.make_async_remote_copy(
            src_ref=src, dst_ref=dst, send_sem=send, recv_sem=recv,
            device_id=(to_section, to_dp), device_id_type=MESH,
        )

    def local(src, dst, sem):
        return pltpu.make_async_copy(src, dst, sem)

    r.load_inward = local(r.inward_in.at[0], r.inward, r.load_sem.at[0])
    r.load_outward = local(r.outward_in.at[0], r.outward, r.load_sem.at[1])
    r.load_up = local(r.up_in.at[0], r.up, r.load_sem.at[2])
    r.load_down = local(r.down_in.at[0], r.down, r.load_sem.at[3])

    def load_rest():
        r.load_outward.start()
        r.load_up.start()
        r.load_down.start()

    r.load_rest = load_rest

    def load_x(micro):
        return local(r.x_in.at[micro, 0], r.stream.at[micro], r.source_sem.at[micro])

    def load_cot(micro):
        return local(r.cot_in.at[micro, 0], r.grads.at[0, slot_of(c, micro)], r.source_sem.at[micro])

    def relay_up(micro):
        return remote(r.result.at[micro], r.stream.at[micro], r.relay_send.at[micro], r.relay_recv.at[micro], 1 - section, dp)

    def relay_back(micro):
        return remote(
            r.passed.at[micro], r.grads.at[0, slot_of(c, micro)], r.relay_send.at[micro], r.relay_recv.at[micro], 1 - section, dp
        )

    def share_acts(micro, core=c):
        return remote(
            r.acts_out, r.acts.at[:, :, slot_of(core, micro)], r.acts_send.at[micro], r.acts_recv.at[micro], section, pair_dp
        )

    def share_branch(micro, core=c):
        rows = slot_of(core, micro)
        return remote(r.grads.at[0, rows], r.grads.at[0, rows], r.branch_send.at[micro], r.branch_recv.at[micro], section, pair_dp)

    def share_lifted(micro, core=c):
        rows = slot_of(core, micro)
        return remote(
            r.grads.at[1:5, rows], r.grads.at[1:5, rows], r.lifted_send.at[micro], r.lifted_recv.at[micro], section, pair_dp
        )

    def share_rest(micro, core=c):
        rows = slot_of(core, micro)
        return remote(
            r.grads.at[5:9, rows], r.grads.at[5:9, rows], r.rest_send.at[micro], r.rest_recv.at[micro], section, pair_dp
        )

    r.share_lifted = share_lifted
    r.share_acts = share_acts

    def to_y(unit):
        return remote(
            r.partial.at[unit, 0], r.y_in.at[unit - FAR], r.y_send.at[unit - FAR], r.y_recv.at[unit - FAR], section, y_dp
        )

    def rows_of(place):
        return pl.ds(BLOCK * place, BLOCK)

    def near_z(unit, place, index, lane, to_dp):
        near = unit - FAR
        return remote(
            r.partial.at[unit, 1, rows_of(place)], r.z_in.at[near, index],
            r.z_send.at[near, lane], r.z_recv.at[near, index], section, to_dp,
        )

    def far_z(unit, place, index, lane, to_dp):
        return remote(
            r.partial.at[unit, :, rows_of(place)], r.far_z_in.at[unit, index],
            r.far_z_send.at[unit, lane], r.far_z_recv.at[unit, index], section, to_dp,
        )

    def far_to_y(unit, place):
        return remote(
            r.partial.at[unit, 0, rows_of(place)], r.far_y_in.at[unit], r.far_y_send.at[unit], r.far_y_recv.at[unit], section, y_dp
        )

    r.load_inward.start()

    @pl.when(leading)
    def _():
        load_x(0).start()
        load_x(1).start()

    @pl.when(jnp.logical_not(leading))
    def _():
        load_cot(0).start()
        load_cot(1).start()

    @pl.when(jnp.logical_not(leading))
    def _():
        r.load_rest()

    r.sums[...] = jnp.zeros_like(r.sums)

    barrier = pltpu.get_barrier_semaphore()
    peers = [(1 - section, dp), (section, pair_dp), (section, y_dp)]
    peers += [(section, lax.rem(dp + 4 * hop, 16)) for hop in (1, 2, 3)]
    for peer in peers:
        pl.semaphore_signal(barrier, inc=1, device_id=peer, device_id_type=MESH)

    def everyone_in():
        pl.semaphore_wait(barrier, len(peers))

    def arrive(micro):
        relay_back(micro).wait_recv()
        share_branch(micro).start()

    def weight_operands(unit):
        piece = piece_of(unit)
        whole = lax.div(piece, 2)
        slab = jnp.minimum(whole, 4) + jnp.where(whole >= 8, 1, 0) + jnp.where(whole >= 9, 1, 0)
        cols = pl.ds(pl.multiple_of(lax.rem(piece, 2) * COLUMNS, 128), COLUMNS)
        other = pl.ds(pl.multiple_of((1 - y) * 192, 64), 192)
        own = pl.ds(pl.multiple_of(y * 192, 64), 192)
        return slab, other, own, r.grads[jnp.maximum(whole - 3, 0), :, cols]

    def near_unit(unit):
        slab, other, own, grads = weight_operands(unit)
        r.partial[unit, 0] = times(r.acts[slab, other, :], grads).astype(SLIM)
        to_y(unit).start()
        r.partial[unit, 1] = times(r.acts[slab, own, :], grads).astype(SLIM)

    def far_unit(unit):
        slab, other, own, grads = weight_operands(unit)
        r.partial[unit, 0] = times(r.acts[slab, other, :], grads).astype(SLIM)
        r.partial[unit, 1] = times(r.acts[slab, own, :], grads).astype(SLIM)
        at_ends(unit, far_z, r.far_z_in)

    def arrived(unit, index, copy, into):
        copy(unit, 0, index, 0, dp).wait_recv()
        return into[unit if into is r.far_z_in else unit - FAR, index].astype(WIDE)

    def pick(unit, place, copy):
        return (unit, slice(None) if copy is far_z else 1, rows_of(place))

    def go_right(unit, here, copy, into):
        for place in range(3, here, -1):
            at = pick(unit, place, copy)
            if here > 0:
                r.partial[at] = (r.partial[at].astype(WIDE) + arrived(unit, place + 1, copy, into)).astype(SLIM)
            copy(unit, place, place + 1, place - 1, dp + 4).start()

    def go_left(unit, here, copy, into):
        for place in range(here):
            at = pick(unit, place, copy)
            if here < 3:
                r.partial[at] = (r.partial[at].astype(WIDE) + arrived(unit, place, copy, into)).astype(SLIM)
            copy(unit, place, place, place, dp - 4).start()

    def at_ends(unit, copy, into):
        @pl.when(z == 0)
        def _():
            go_right(unit, 0, copy, into)

        @pl.when(z == 3)
        def _():
            go_left(unit, 3, copy, into)

    def at_middle_first(unit, copy, into):
        @pl.when(z == 1)
        def _():
            go_right(unit, 1, copy, into)

        @pl.when(z == 2)
        def _():
            go_left(unit, 2, copy, into)

    def at_middle_second(unit, copy, into):
        @pl.when(z == 1)
        def _():
            go_left(unit, 1, copy, into)

        @pl.when(z == 2)
        def _():
            go_right(unit, 2, copy, into)

    def gathered(unit, here, copy, into):
        value = r.partial[pick(unit, here, copy)].astype(WIDE)
        if here > 0:
            value = value + arrived(unit, here + 1, copy, into)
        if here < 3:
            value = value + arrived(unit, here, copy, into)
        return value

    def everywhere(action):
        for here in range(4):

            @pl.when(z == here)
            def _():
                action(here)

    def slot(t, carry):
        trailing = jnp.logical_not(leading)
        half = lax.div(t, 2)
        is_forward = (leading & (t < 2)) | (trailing & ((t == 1) | (t == 3)))
        is_backward = (leading & ((t == 3) | (t == 5))) | (trailing & ((t == 2) | (t == 4)))
        is_weights = (leading & (t == 4)) | (trailing & (t == 5))

        @pl.when(trailing & (t == 0))
        def _():
            everyone_in()
            for micro in range(2):
                load_cot(micro).wait()
                share_branch(micro).start()

        @pl.when(is_forward)
        def _():
            micro = jnp.where(leading, jnp.minimum(t, 1), jnp.minimum(half, 1))

            @pl.when(leading)
            def _():
                load_x(micro).wait()

            @pl.when(trailing)
            def _():
                relay_up(micro).wait_recv()

            forward(r, micro, pl.multiple_of((c * 2 + micro) * length, length), t == section, leading)

            @pl.when(leading & (t == 0))
            def _():
                everyone_in()

            ahead = leading & (c == 0) & (t == 0)

            @pl.when(ahead)
            def _():
                relay_up(0).start()
                relay_up(0).wait_send()
                pl.semaphore_signal(r.turn, inc=1, device_id=(section, pair_dp), device_id_type=MESH)

            @pl.when(leading & (t == 1))
            def _():
                relay_up(1).start()

            share_acts(micro).start()

            @pl.when(leading & (c == 1) & (t == 0))
            def _():
                pl.semaphore_wait(r.turn, 1)
                relay_up(0).start()

        @pl.when(leading & (t == 3))
        def _():
            arrive(0)

        @pl.when(is_backward)
        def _():
            micro = jnp.clip(half - 1, 0, 1)
            backward(r, micro, pl.multiple_of((c * 2 + micro) * length, length))

            @pl.when(trailing)
            def _():
                relay_back(micro).start()

            share_rest(micro).start()

            @pl.when(trailing & (t == 4))
            def _():
                def body(done, carry):
                    last_output(r, done)
                    return carry

                lax.fori_loop(0, 2, body, 0)

        @pl.when(leading & (t == 4))
        def _():
            arrive(1)

        @pl.when(is_weights)
        def _():
            for micro in range(2):
                share_branch(micro, 1 - c).wait_recv()
                share_acts(micro, 1 - c).wait_recv()

            def body(i, carry):
                @pl.when(i < EARLY_NEAR)
                def _():
                    near_unit(FAR + i)

                @pl.when(i < EARLY_FAR)
                def _():
                    far_unit(i)

                return carry

            lax.fori_loop(0, max(EARLY_NEAR, EARLY_FAR), body, 0)

        return carry

    lax.fori_loop(0, 6, slot, 0)

    def norm_copy(src, dst, index, to_dp):
        return remote(r.norms.at[src], r.norms.at[dst], r.norm_send.at[index], r.norm_recv.at[index], section, to_dp)

    def norm_to_pair():
        return norm_copy(0, 1, 0, pair_dp)

    def norm_to_y():
        return norm_copy(2, 3, 1, y_dp)

    def norm_to_z(hop):
        return norm_copy(4, 4 + hop, 1 + hop, lax.rem(dp + 4 * hop, 16))

    r.norms[0] = jnp.concatenate([jnp.sum(r.sums[...], 1), jnp.zeros((4, r.sums.shape[2]), WIDE)], 0)
    norm_to_pair().start()
    for micro in range(2):
        share_lifted(micro, 1 - c).wait_recv()

    def sum_y(unit):
        to_y(unit).wait_recv()
        r.partial[unit, 1] = (r.partial[unit, 1].astype(WIDE) + r.y_in[unit - FAR].astype(WIDE)).astype(SLIM)

    def far_turn(i, steps):
        turn, unit = i < 0, jnp.int32(0)
        for index, step in enumerate(steps):
            if step >= 0:
                turn = turn | (i == step)
                unit = jnp.where(i == step, index, unit)
        return turn, unit

    def near_turn(i, lag):
        return (i >= lag) & (i < NEAR + lag), jnp.clip(i - lag, 0, NEAR - 1) + FAR

    def advance(i, carry):
        @pl.when(i < NEAR)
        def _():
            sum_y(FAR + i)
            at_ends(FAR + i, near_z, r.z_in)

        issued = FAR + EARLY_NEAR + i - HOLD

        @pl.when(issued == 16)
        def _():
            for micro in range(2):
                share_rest(micro, 1 - c).wait_recv()

        @pl.when((issued >= FAR + EARLY_NEAR) & (issued < UNITS))
        def _():
            near_unit(issued)

        turn, unit = far_turn(i, FAR_AT)

        @pl.when(turn)
        def _(unit=unit):
            far_unit(unit)

        turn, unit = near_turn(i, LAGS[0])

        @pl.when(turn)
        def _(unit=unit):
            at_middle_first(unit, near_z, r.z_in)

        turn, unit = far_turn(i, FAR_FIRST)

        @pl.when(turn)
        def _(unit=unit):
            at_middle_first(unit, far_z, r.far_z_in)

        turn, unit = far_turn(i, FAR_SECOND)

        @pl.when(turn)
        def _(unit=unit):
            at_middle_second(unit, far_z, r.far_z_in)

        turn, unit = far_turn(i, FAR_ARRIVED)

        @pl.when(turn)
        def _(unit=unit):
            def action(here):
                value = gathered(unit, here, far_z, r.far_z_in)
                r.partial[unit, 0, rows_of(here)] = value[0].astype(SLIM)
                far_to_y(unit, here).start()
                r.staged[unit] = value[1]

            everywhere(action)

        turn, unit = far_turn(i, FAR_DONE)

        @pl.when(turn)
        def _(unit=unit):
            far_to_y(unit, 0).wait_recv()
            r.staged[unit] += r.far_y_in[unit].astype(WIDE)

        turn, unit = near_turn(i, LAGS[1])

        @pl.when(turn)
        def _(unit=unit):
            at_middle_second(unit, near_z, r.z_in)

        turn, unit = near_turn(i, LAGS[2])

        @pl.when(turn)
        def _(unit=unit):
            def action(here):
                r.staged[unit] = gathered(unit, here, near_z, r.z_in)

            everywhere(action)

        @pl.when(i == 1)
        def _():
            norm_to_pair().wait()
            r.norms[2] = r.norms[0] + r.norms[1]
            norm_to_y().start()

        @pl.when(i == 9)
        def _():
            norm_to_y().wait_recv()
            r.norms[4] = r.norms[2] + r.norms[3]
            for hop in (1, 2, 3):
                norm_to_z(hop).start()

        @pl.when(i == 18)
        def _():
            for hop in (1, 2, 3):
                norm_to_z(hop).wait_recv()
            r.out_norms[...] = (r.norms[4] + r.norms[5]) + (r.norms[6] + r.norms[7])

        return carry

    lax.fori_loop(0, max(NEAR + LAGS[2], *(step + 1 for step in FAR_DONE)), advance, 0)

    norm_to_y().wait_send()
    for hop in (1, 2, 3):
        norm_to_z(hop).wait_send()
    share_acts(1).wait_send()
    for micro in range(2):
        share_branch(micro).wait_send()
        share_lifted(micro).wait_send()
        share_rest(micro).wait_send()

        @pl.when(leading if micro else leading & (c == 1))
        def _():
            relay_up(micro).wait_send()

        @pl.when(jnp.logical_not(leading))
        def _():
            relay_back(micro).wait_send()

    def drain_near(near, carry):
        to_y(FAR + near).wait_send()
        for lane in range(3):
            near_z(FAR + near, 0, 0, lane, dp).wait_send()
        return carry

    lax.fori_loop(0, NEAR, drain_near, 0)

    def drain_far(unit, carry):
        far_to_y(unit, 0).wait_send()
        for lane in range(3):
            far_z(unit, 0, 0, lane, dp).wait_send()
        return carry

    lax.fori_loop(0, FAR, drain_far, 0)


def hand_over_kernel(result, grad, staged, norms, *refs):
    out_result, out_grad, out_inward, out_outward, out_up, out_down, gain_grad, bias_grad, sem = refs
    width = result.shape[2]

    def start(source, target):
        copy = pltpu.make_async_copy(source, target, sem)
        copy.start()
        return copy

    copies = [start(result, out_result.at[0, :, 0]), start(grad, out_grad.at[0, :, 0])]
    for slot, piece in enumerate(PIECES):
        half = pl.ds(piece % 2 * COLUMNS, COLUMNS)
        if piece < 8:
            target = out_down.at[0, pl.ds(piece // 2 * BLOCK, BLOCK), half]
        elif piece < 16:
            target = out_up.at[0, :, pl.ds((piece - 8) * COLUMNS, COLUMNS)]
        elif piece < 18:
            target = out_outward.at[0, :, half]
        else:
            target = out_inward.at[0, :, pl.ds((piece - 18) * COLUMNS, COLUMNS)]
        copies.append(start(staged.at[slot], target))
    share = gain_grad.shape[2]
    for index in range(width // share):

        @pl.when(lax.axis_index("dp") == index)
        def _():
            gain_grad[0] = norms[0:2, index * share : (index + 1) * share]
            bias_grad[0] = norms[2:4, index * share : (index + 1) * share]

    for copy in copies:
        copy.wait()


def step_on_device(
    inputs, clip_lengths, anchor_offsets, cotangent, inward_weight, outward_weight, up_weight, down_weight, norm_gain, norm_bias
):
    _, _, length, width = inputs.shape
    wide_ff = up_weight.shape[2]
    anywhere = pl.BlockSpec(memory_space=pl.ANY)
    in_vmem = pl.BlockSpec(memory_space=pltpu.VMEM)
    in_smem = pl.BlockSpec(memory_space=pltpu.SMEM)
    dma = pltpu.SemaphoreType.DMA
    share = width // lax.axis_size("dp")
    made = pl.pallas_call(
        step_kernel,
        out_shape=(
            pltpu.VMEM((2, length, width), SLIM),
            pltpu.VMEM((2, length, width), WIDE),
            pltpu.VMEM((UNITS, BLOCK, COLUMNS), WIDE),
            pltpu.VMEM((8, width), WIDE),
        ),
        in_specs=[anywhere] * 6 + [in_vmem] * 2 + [in_smem] * 2,
        out_specs=[in_vmem] * 4,
        scratch_shapes=[
            pltpu.VMEM((2, length, width), SLIM),
            pltpu.VMEM((width, 3 * width), SLIM),
            pltpu.VMEM((width, width), SLIM),
            pltpu.VMEM((width, wide_ff), SLIM),
            pltpu.VMEM((wide_ff, width), SLIM),
            pltpu.VMEM((9, 4 * length, width), SLIM),
            pltpu.VMEM((7, 8 * BLOCK, 4 * length), SLIM),
            pltpu.VMEM((7, 8 * BLOCK, length), SLIM),
            pltpu.VMEM((2, width // HEAD, length, length), SLIM),
            pltpu.VMEM((length, width), SLIM),
            pltpu.VMEM((length, width), SLIM),
            pltpu.VMEM((width, length), SLIM),
            pltpu.VMEM((length, width), WIDE),
            pltpu.VMEM((2, length, width), SLIM),
            pltpu.VMEM((4, 8, width), WIDE),
            pltpu.VMEM((length, length), WIDE),
            pltpu.VMEM((UNITS, 2, 4 * BLOCK, COLUMNS), SLIM),
            pltpu.VMEM((NEAR, 4 * BLOCK, COLUMNS), SLIM),
            pltpu.VMEM((NEAR, 5, BLOCK, COLUMNS), SLIM),
            pltpu.VMEM((FAR, BLOCK, COLUMNS), SLIM),
            pltpu.VMEM((FAR, 5, 2, BLOCK, COLUMNS), SLIM),
            pltpu.VMEM((8, 8, width), WIDE),
            dma((4,)), dma((2,)),
            *[dma((2,))] * 10, pltpu.SemaphoreType.REGULAR,
            dma((NEAR,)), dma((NEAR,)), dma((NEAR, 3)), dma((NEAR, 5)),
            dma((FAR,)), dma((FAR,)), dma((FAR, 3)), dma((FAR, 5)), dma((5,)), dma((5,)),
        ],
        compiler_params=pltpu.CompilerParams(
            collective_id=0, has_side_effects=True, vmem_limit_bytes=VMEM_BYTES - 4500000
        ),
    )(
        inputs, cotangent, inward_weight, outward_weight, up_weight, down_weight,
        norm_gain, norm_bias, clip_lengths, anchor_offsets,
    )
    sections = 1
    return pl.pallas_call(
        hand_over_kernel,
        out_shape=(
            jax.ShapeDtypeStruct((sections, 2, 1, length, width), SLIM),
            jax.ShapeDtypeStruct((sections, 2, 1, length, width), WIDE),
            jax.ShapeDtypeStruct((sections, BLOCK, 3 * width), WIDE),
            jax.ShapeDtypeStruct((sections, BLOCK, width), WIDE),
            jax.ShapeDtypeStruct((sections, BLOCK, wide_ff), WIDE),
            jax.ShapeDtypeStruct((sections, 4 * BLOCK, width), WIDE),
            jax.ShapeDtypeStruct((sections, 2, share), WIDE),
            jax.ShapeDtypeStruct((sections, 2, share), WIDE),
        ),
        in_specs=[in_vmem] * 4,
        out_specs=[anywhere] * 6 + [in_vmem] * 2,
        scratch_shapes=[dma],
        compiler_params=pltpu.CompilerParams(vmem_limit_bytes=1 << 20),
    )(*[pltpu.with_memory_space_constraint(one, pltpu.VMEM) for one in made])


def shifted(x, axis, by):
    size = lax.axis_size(axis)
    pairs = [(i, i + by) for i in range(size) if 0 <= i + by < size]
    return lax.ppermute(x, axis, pairs)


def norm_rows(values, norm_gain, norm_bias):
    average = jnp.mean(values, -1, keepdims=True)
    centred = values - average
    inverse = lax.rsqrt(jnp.mean(centred * centred, -1, keepdims=True) + EPSILON)
    normed = centred * inverse
    return (normed * norm_gain + norm_bias, normed, inverse)


def norm_back(norm_grad, normed, inverse, norm_gain):
    inner = norm_grad * norm_gain
    through = inverse * (
        inner
        - jnp.mean(inner, -1, keepdims=True)
        - normed * jnp.mean(inner * normed, -1, keepdims=True)
    )
    return (through, jnp.sum(norm_grad * normed, 0), jnp.sum(norm_grad, 0))


def gelu_slope(lifted):
    cumulative = 0.5 * (1.0 + lax.erf(lifted * 0.7071067811865476))
    density = jnp.exp(-0.5 * lifted * lifted) * 0.3989422804014327
    return cumulative + lifted * density


def clip_marks(lengths, offsets, length):
    positions = jnp.arange(length, dtype=jnp.int32)
    clip_ends = jnp.cumsum(lengths)
    clip_starts = clip_ends - lengths
    anchor_at = clip_starts + offsets % lengths
    clip_ids = jnp.sum((positions[:, None] >= clip_ends[None, :]).astype(jnp.int32), 1)
    anchors = jnp.any(positions[:, None] == anchor_at[None, :], 1)
    return (clip_ids, anchors)


def masked_scores(query_block, key_rows, id_block, clip_ids, anchors, scaling):
    scores = (
        jnp.einsum("qhd,khd->hqk", query_block, key_rows, preferred_element_type=jnp.float32)
        * scaling
    )
    seen = (id_block[:, None] == clip_ids[None, :]) | anchors[None, :]
    return jnp.where(seen[None], scores, -1000000000.0)


def forward_layer(source, clip_ids, anchors, params):
    inward, outward, upward, downward, norm_gain, norm_bias = params
    length, model_width = source.shape
    head_count = model_width // HEAD
    scaling = HEAD ** (-0.5)
    residual = source.astype(jnp.float32)
    first_norm, unit_one, scale_one = norm_rows(residual, norm_gain[0], norm_bias[0])
    joined = jnp.dot(
        first_norm.astype(jnp.bfloat16), inward, preferred_element_type=jnp.float32
    ).astype(jnp.bfloat16)
    heads_view = joined.reshape(length, 3, head_count, HEAD)
    queries = heads_view[:, 0]
    key_rows = heads_view[:, 1]
    values = heads_view[:, 2]
    scores = masked_scores(queries, key_rows, clip_ids, clip_ids, anchors, scaling)
    row_max = jnp.max(scores, -1, keepdims=True)
    raised = jnp.exp(scores - row_max)
    row_sum = jnp.sum(raised, -1, keepdims=True)
    weights = (raised / row_sum).astype(jnp.bfloat16)
    pieces = [jnp.einsum("hqk,khd->qhd", weights, values, preferred_element_type=jnp.float32)]
    log_sums = [(row_max + jnp.log(row_sum))[..., 0]]
    attended = jnp.concatenate(pieces, 0).reshape(length, model_width).astype(jnp.bfloat16)
    logsum = jnp.concatenate(log_sums, 1)
    middle = residual + jnp.dot(attended, outward, preferred_element_type=jnp.float32)
    second_norm, unit_two, scale_two = norm_rows(middle, norm_gain[1], norm_bias[1])
    lifted = jnp.dot(second_norm.astype(jnp.bfloat16), upward, preferred_element_type=jnp.float32)
    active = jax.nn.gelu(lifted, approximate=False).astype(jnp.bfloat16)
    result = middle + jnp.dot(active, downward, preferred_element_type=jnp.float32)
    stored = (unit_one, scale_one, joined, logsum, attended, unit_two, scale_two, lifted, active)
    return (result, stored)


def contract_rows(left, right):
    return lax.dot_general(
        left, right, (((0,), (0,)), ((), ())), preferred_element_type=jnp.float32
    )


def contract_cols(left, right):
    return lax.dot_general(
        left, right, (((1,), (1,)), ((), ())), preferred_element_type=jnp.float32
    )


def feed_backward(incoming, stored, params):
    inward, outward, upward, downward, norm_gain, norm_bias = params
    unit_one, scale_one, joined, logsum, attended, unit_two, scale_two, lifted, active = stored
    branch = incoming.astype(jnp.bfloat16)
    down_part = contract_rows(active, branch)
    hidden_grad = contract_cols(branch, downward)
    lifted_grad = (hidden_grad * gelu_slope(lifted)).astype(jnp.bfloat16)
    second_in = (unit_two * norm_gain[1] + norm_bias[1]).astype(jnp.bfloat16)
    up_part = contract_rows(second_in, lifted_grad)
    normed_grad = contract_cols(lifted_grad, upward)
    through, gain_two, bias_two = norm_back(normed_grad, unit_two, scale_two, norm_gain[1])
    return (incoming + through, (up_part, down_part, gain_two, bias_two))


def attend_backward(middle_grad, stored, clip_ids, anchors, params):
    inward, outward, upward, downward, norm_gain, norm_bias = params
    unit_one, scale_one, joined, logsum, attended, unit_two, scale_two, lifted, active = stored
    length, model_width = attended.shape
    head_count = model_width // HEAD
    scaling = HEAD ** (-0.5)
    branch = middle_grad.astype(jnp.bfloat16)
    outward_part = contract_rows(attended, branch)
    attended_grad = (
        contract_cols(branch, outward).astype(jnp.bfloat16).reshape(length, head_count, HEAD)
    )
    heads_view = joined.reshape(length, 3, head_count, HEAD)
    queries = heads_view[:, 0]
    key_rows = heads_view[:, 1]
    values = heads_view[:, 2]
    key_grad = jnp.zeros((length, head_count, HEAD), jnp.float32)
    value_grad = jnp.zeros((length, head_count, HEAD), jnp.float32)
    block_rows = min(512, length)
    scores = masked_scores(queries, key_rows, clip_ids, clip_ids, anchors, scaling)
    weights = jnp.exp(scores - logsum[:, 0:block_rows, None])
    weight_grad = jnp.einsum(
        "qhd,khd->hqk", attended_grad, values, preferred_element_type=jnp.float32
    )
    score_grad = (
        weights * (weight_grad - jnp.sum(weights * weight_grad, -1, keepdims=True))
    ).astype(jnp.bfloat16)
    query_pieces = [
        scaling
        * jnp.einsum("hqk,khd->qhd", score_grad, key_rows, preferred_element_type=jnp.float32)
    ]
    key_grad = key_grad + scaling * jnp.einsum(
        "hqk,qhd->khd", score_grad, queries, preferred_element_type=jnp.float32
    )
    value_grad = value_grad + jnp.einsum(
        "hqk,qhd->khd",
        weights.astype(jnp.bfloat16),
        attended_grad,
        preferred_element_type=jnp.float32,
    )
    query_grad = jnp.concatenate(query_pieces, 0)
    joined_grad = (
        jnp.stack([query_grad, key_grad, value_grad], 1)
        .reshape(length, 3 * model_width)
        .astype(jnp.bfloat16)
    )
    first_in = (unit_one * norm_gain[0] + norm_bias[0]).astype(jnp.bfloat16)
    inward_part = contract_rows(first_in, joined_grad)
    normed_grad = contract_cols(joined_grad, inward)
    through, gain_one, bias_one = norm_back(normed_grad, unit_one, scale_one, norm_gain[0])
    return (middle_grad + through, (inward_part, outward_part, gain_one, bias_one))


def resting(function):

    def blank(*operands):
        return jax.tree.map(jnp.zeros_like, function(*operands))

    return blank


def take_slot(holder, buffer_slot):
    return jax.tree.map(
        lambda element: lax.dynamic_index_in_dim(element, buffer_slot, 0, False), holder
    )


def place_slot(holder, item, buffer_slot, working):

    def update(element, fresh):
        former = lax.dynamic_index_in_dim(element, buffer_slot, 0, False)
        return lax.dynamic_update_index_in_dim(
            element, jnp.where(working, fresh, former), buffer_slot, 0
        )

    return jax.tree.map(update, holder, item)


def per_device(
    inputs,
    clip_lengths,
    anchor_offsets,
    cotangent,
    inward_weight,
    outward_weight,
    up_weight,
    down_weight,
    norm_gain,
    norm_bias,
):
    params = (
        inward_weight[0],
        outward_weight[0],
        up_weight[0],
        down_weight[0],
        norm_gain[0],
        norm_bias[0],
    )
    stream = inputs[:, 0]
    cot_rows = cotangent[:, 0]
    lengths_all = clip_lengths[:, 0]
    offsets_all = anchor_offsets[:, 0]
    micro_count = stream.shape[0]
    length = stream.shape[1]
    section_index = lax.axis_index("section")
    section_count = lax.axis_size("section")
    leading = section_index == 0
    trailing = section_index == section_count - 1
    periods = micro_count + section_count - 1
    arriving = jnp.zeros_like(stream[0])
    produced = jnp.zeros_like(stream)
    archive = None
    for period in range(periods):
        micro_index = period - section_index
        working = (micro_index >= 0) & (micro_index < micro_count)
        buffer_slot = jnp.clip(micro_index, 0, micro_count - 1)
        source = jnp.where(leading, stream[min(period, micro_count - 1)], arriving)
        clip_ids, anchors = clip_marks(
            take_slot(lengths_all, buffer_slot), take_slot(offsets_all, buffer_slot), length
        )
        result, stored = lax.cond(
            working, forward_layer, resting(forward_layer), source, clip_ids, anchors, params
        )
        if archive is None:
            archive = jax.tree.map(
                lambda element: jnp.zeros((micro_count,) + element.shape, element.dtype), stored
            )
        archive = place_slot(archive, stored, buffer_slot, working)
        sending = result.astype(jnp.bfloat16)
        produced = place_slot(produced, sending, buffer_slot, working)
        if period < micro_count:
            arriving = shifted(sending, "section", 1)
    inward, outward, upward, downward, gains, biases = params
    up_sum = jnp.zeros(upward.shape, jnp.float32)
    down_sum = jnp.zeros(downward.shape, jnp.float32)
    gain_two = jnp.zeros(gains.shape[1:], jnp.float32)
    bias_two = jnp.zeros(biases.shape[1:], jnp.float32)
    inward_sum = jnp.zeros(inward.shape, jnp.float32)
    outward_sum = jnp.zeros(outward.shape, jnp.float32)
    gain_one = jnp.zeros(gains.shape[1:], jnp.float32)
    bias_one = jnp.zeros(biases.shape[1:], jnp.float32)
    upstream = jnp.zeros_like(stream[0])
    returned = jnp.zeros(stream.shape, jnp.float32)
    for period in range(periods):
        micro_index = micro_count - 1 - period + (section_count - 1 - section_index)
        working = (micro_index >= 0) & (micro_index < micro_count)
        buffer_slot = jnp.clip(micro_index, 0, micro_count - 1)
        incoming = jnp.where(trailing, take_slot(cot_rows, buffer_slot), upstream).astype(
            jnp.float32
        )
        clip_ids, anchors = clip_marks(
            take_slot(lengths_all, buffer_slot), take_slot(offsets_all, buffer_slot), length
        )
        stored = take_slot(archive, buffer_slot)
        middle_grad, feed_part = lax.cond(
            working, feed_backward, resting(feed_backward), incoming, stored, params
        )
        up_sum = up_sum + feed_part[0]
        down_sum = down_sum + feed_part[1]
        gain_two = gain_two + feed_part[2]
        bias_two = bias_two + feed_part[3]
        input_grad, attend_part = lax.cond(
            working,
            attend_backward,
            resting(attend_backward),
            middle_grad,
            stored,
            clip_ids,
            anchors,
            params,
        )
        inward_sum = inward_sum + attend_part[0]
        outward_sum = outward_sum + attend_part[1]
        gain_one = gain_one + attend_part[2]
        bias_one = bias_one + attend_part[3]
        returned = place_slot(returned, input_grad, buffer_slot, working)
        if period < periods - 1:
            upstream = shifted(input_grad.astype(jnp.bfloat16), "section", -1)
    inward_sum, outward_sum, up_sum, down_sum, gain_one, gain_two, bias_one, bias_two = (
        lax.psum_scatter(inward_sum, "dp", scatter_dimension=0, tiled=True),
        lax.psum_scatter(outward_sum, "dp", scatter_dimension=0, tiled=True),
        lax.psum_scatter(up_sum, "dp", scatter_dimension=0, tiled=True),
        lax.psum_scatter(down_sum, "dp", scatter_dimension=0, tiled=True),
        lax.psum_scatter(gain_one, "dp", scatter_dimension=0, tiled=True),
        lax.psum_scatter(gain_two, "dp", scatter_dimension=0, tiled=True),
        lax.psum_scatter(bias_one, "dp", scatter_dimension=0, tiled=True),
        lax.psum_scatter(bias_two, "dp", scatter_dimension=0, tiled=True),
    )
    layer_outputs = produced[None, :, None]
    input_grads = returned[None, :, None]
    gain_grad = jnp.stack([gain_one, gain_two])[None]
    bias_grad = jnp.stack([bias_one, bias_two])[None]
    return (
        layer_outputs,
        input_grads,
        inward_sum[None],
        outward_sum[None],
        up_sum[None],
        down_sum[None],
        gain_grad,
        bias_grad,
    )


def solution(mesh):
    local = step_on_device if mesh.shape["dp"] == 16 and mesh.shape["section"] == 2 else per_device
    return jax.shard_map(
        local,
        mesh=mesh,
        in_specs=(
            P(None, "dp", None, None),
            P(None, "dp", None),
            P(None, "dp", None),
            P(None, "dp", None, None),
            P("section", None, None),
            P("section", None, None),
            P("section", None, None),
            P("section", None, None),
            P("section", None, None),
            P("section", None, None),
        ),
        out_specs=(
            P("section", None, "dp", None, None),
            P("section", None, "dp", None, None),
            P("section", "dp", None),
            P("section", "dp", None),
            P("section", "dp", None),
            P("section", "dp", None),
            P("section", None, "dp"),
            P("section", None, "dp"),
        ),
        check_vma=False,
    )
```

```python
import functools
import types

import jax
import jax.numpy as jnp
from jax import lax
from jax.experimental import pallas as pl
from jax.experimental.pallas import tpu as pltpu
from jax.sharding import PartitionSpec as P

HEAD = 64
EPSILON = 1e-06
MESH = pl.DeviceIdType.MESH
WIDE = jnp.float32
SLIM = jnp.bfloat16
VMEM_BYTES = 67043328

UNITS = 24
FAR = 2
QUAD = 8
NEAR = UNITS - QUAD
BLOCK = 48
COLUMNS = 384
EARLY_NEAR = 2
HOLD = 0
LAGS = (2, 4, 6)
FAR_FIRST = (0, 5)
FAR_SECOND = (2, 9)
FAR_ARRIVED = (3, 18)
FAR_DONE = (7, 21)
QUAD_AT = (-1, -1, 2, 4, 6, 12)
QUAD_FIRST = (3, 2, 6, 7, 9, 13)
QUAD_SECOND = (5, 7, 15, 13, 11, 16)
QUAD_DONE = (18, 13, 19, 21, 12, 20)


def times(left, right):
    return jnp.dot(left, right, preferred_element_type=WIDE)


def times_turned(left, right):
    return lax.dot_general(left, right, (((1,), (1,)), ((), ())), preferred_element_type=WIDE)


def unit_rows(values):
    centred = values - jnp.mean(values, -1, keepdims=True)
    inverse = lax.rsqrt(jnp.mean(centred * centred, -1, keepdims=True) + EPSILON)
    return centred * inverse, inverse


def norm_rows_bf16(r, values, which):
    unit, _ = unit_rows(values)
    return (unit * r.gain[0, which : which + 1, :] + r.bias[0, which : which + 1, :]).astype(SLIM)


def norm_backward(r, values, norm_grad, which):
    unit, inverse = unit_rows(values)
    width = values.shape[1]
    r.sums[which] += jnp.sum((norm_grad * unit).reshape(-1, 8, width), 0)
    r.sums[2 + which] += jnp.sum(norm_grad.reshape(-1, 8, width), 0)
    inner = norm_grad * r.gain[0, which : which + 1, :]
    return inverse * (
        inner
        - jnp.mean(inner, -1, keepdims=True)
        - unit * jnp.mean(inner * unit, -1, keepdims=True)
    )


def head_lanes():
    lane = lax.broadcasted_iota(jnp.int32, (1, 2 * HEAD), 1)
    first = jnp.where(lane < HEAD, 1.0, 0.0).astype(WIDE)
    return first, 1.0 - first


def mask_bias(r, micro):
    length = r.bias_mask.shape[0]

    def marks(positions):
        end = jnp.int32(0)
        ids = jnp.zeros(positions.shape, jnp.int32)
        anchors = jnp.zeros(positions.shape, jnp.int32)
        for clip in range(r.lengths.shape[2]):
            size = r.lengths[micro, 0, clip]
            anchor = end + lax.rem(r.offsets[micro, 0, clip], size)
            end = end + size
            ids = ids + jnp.where(positions >= end, 1, 0)
            anchors = anchors + jnp.where(positions == anchor, 1, 0)
        return ids, anchors

    key_ids, anchors = marks(lax.broadcasted_iota(jnp.int32, (length, 1), 0))
    query_ids, _ = marks(lax.broadcasted_iota(jnp.int32, (1, length), 1))
    seen = (key_ids == query_ids) | (jnp.broadcast_to(anchors, (length, length)) > 0)
    r.bias_mask[...] = jnp.where(seen, 0.0, -1000000000.0).astype(WIDE)


def place(r, slab, tokens):
    for line in range(8):
        z, y = line // 2, line % 2
        rows = pl.ds(y * 192 + z * BLOCK, BLOCK)
        own = pl.ds(pl.multiple_of(2 * BLOCK * line + r.c * BLOCK, 16), BLOCK)
        other = pl.ds(pl.multiple_of(2 * BLOCK * line + (1 - r.c) * BLOCK, 16), BLOCK)
        r.acts[slab, rows, tokens] = r.turned[own, :]
        r.acts_out[slab, rows, :] = r.turned[other, :]


def forward(r, micro, tok, first, leading):
    length, width = r.normed.shape
    tokens = pl.ds(tok, length)
    mask_bias(r, micro)
    r.normed[...] = norm_rows_bf16(r, r.stream[micro].astype(WIDE), 0)

    @pl.when(first)
    def _():
        r.load_inward.wait()

        @pl.when(leading)
        def _():
            r.load_rest()

    for part in range(3):
        r.grads[5 + part, tokens, :] = times(
            r.normed[...], r.inward[:, part * width : (part + 1) * width]
        ).astype(SLIM)

    @pl.when(micro > 0)
    def _():
        r.share_acts(0).wait_send()

    r.turned[...] = r.normed[...].T
    place(r, 3, tokens)
    one, two = (lanes.astype(SLIM) for lanes in head_lanes())
    for pair in range(width // (2 * HEAD)):
        cols = pl.ds(pair * 2 * HEAD, 2 * HEAD)
        queries = r.grads[5, tokens, cols] * jnp.asarray(HEAD**-0.5, SLIM)
        keys = r.grads[6, tokens, cols]
        values_turned = r.grads[7, tokens, cols].T
        scores = times_turned(jnp.concatenate([keys * one, keys * two], 0), queries)
        pieces = []
        for head in range(2):
            masked = scores[length * head : length * (head + 1)] + r.bias_mask[...]
            raised = jnp.exp(masked - jnp.max(masked, 0, keepdims=True))
            weights = (raised * (1.0 / jnp.sum(raised, 0, keepdims=True))).astype(SLIM)
            r.weights[micro, 2 * pair + head] = weights
            pieces.append(times(values_turned[HEAD * head : HEAD * (head + 1)], weights).astype(SLIM))
        attended_turned = jnp.concatenate(pieces, 0)
        r.turned[cols, :] = attended_turned
        r.held[:, cols] = attended_turned.T
    place(r, 2, tokens)

    @pl.when(first)
    def _():
        r.load_outward.wait()

    r.middle[micro] = r.stream[micro].astype(WIDE) + times(r.held[...], r.outward[...])
    r.normed[...] = norm_rows_bf16(r, r.middle[micro], 1)
    r.turned[...] = r.normed[...].T
    place(r, 1, tokens)

    @pl.when(first)
    def _():
        r.load_up.wait()
        r.load_down.wait()

    def activate(part):
        lifted = times(r.normed[...], r.up[:, part * width : (part + 1) * width])
        cumulative = 0.5 * (1.0 + lax.erf(lifted * 0.7071067811865476))
        density = jnp.exp(-0.5 * lifted * lifted) * 0.3989422804014327
        r.grads[part, tokens, :] = (cumulative + lifted * density).astype(SLIM)
        active = (lifted * cumulative).astype(SLIM)
        r.turned[...] = active.T
        rows = pl.ds(part * BLOCK, BLOCK)
        for y in range(2):
            placed = pl.ds(y * 192 + part * BLOCK, BLOCK)
            own = pl.ds(pl.multiple_of(384 * y + r.c * 192, 16), BLOCK)
            other = pl.ds(pl.multiple_of(384 * y + (1 - r.c) * 192, 16), BLOCK)
            r.acts[0, placed, tokens] = r.turned[own, :]
            r.acts_out[0, placed, :] = r.turned[other, :]
        for piece in range(3):

            def rows_for(core, side):
                start = 384 * side + 192 * core + BLOCK * (piece + 1)
                return r.turned[pl.ds(pl.multiple_of(start, 16), BLOCK), :]

            r.quad_acts[piece, rows, r.quad_rows(micro)] = rows_for(r.c, r.y)
            r.quad_out[micro, 0, piece, rows, :] = rows_for(1 - r.c, r.y)
            r.quad_out[micro, 1, piece, rows, :] = rows_for(r.c, 1 - r.y)
            r.quad_out[micro, 2, piece, rows, :] = rows_for(1 - r.c, 1 - r.y)
        return active

    @pl.when(leading)
    def _():
        r.total[...] = r.middle[micro]
        for part in range(4):
            r.total[...] += times(activate(part), r.down[part * width : (part + 1) * width, :])
        r.result[micro] = r.total[...].astype(SLIM)

    @pl.when(jnp.logical_not(leading))
    def _():
        for part in range(4):
            set_aside(r, micro * 12 + 2 * part, activate(part))
        middle = r.middle[micro]
        upper = middle.astype(SLIM)
        set_aside(r, micro * 12 + 8, upper)
        set_aside(r, micro * 12 + 10, (middle - upper.astype(WIDE)).astype(SLIM))


def set_aside(r, slot, values):
    for half in range(2):
        columns = values[:, half * COLUMNS : (half + 1) * COLUMNS]
        r.partial[slot + half, 0] = columns[:192]
        r.partial[slot + half, 1, 0:64] = columns[192:]


def set_back(r, slot):
    halves = [
        jnp.concatenate([r.partial[slot + half, 0], r.partial[slot + half, 1, 0:64]], 0) for half in range(2)
    ]
    return jnp.concatenate(halves, 1)


def last_output(r, micro):
    width = r.normed.shape[1]
    r.total[...] = set_back(r, micro * 12 + 8).astype(WIDE) + set_back(r, micro * 12 + 10).astype(WIDE)
    for part in range(4):
        r.total[...] += times(set_back(r, micro * 12 + 2 * part), r.down[part * width : (part + 1) * width, :])
    r.result[micro] = r.total[...].astype(SLIM)


def backward(r, micro, tok):
    length, width = r.normed.shape
    tokens = pl.ds(tok, length)
    r.total[...] = jnp.zeros((length, width), WIDE)
    for part in range(4):
        cols = slice(part * width, (part + 1) * width)
        hidden = times_turned(r.branch[r.quad_rows(micro), :], r.down[cols, :])
        lifted_grad = (hidden * r.grads[part, tokens, :].astype(WIDE)).astype(SLIM)
        r.grads[part, tokens, :] = lifted_grad
        r.total[...] += times_turned(lifted_grad, r.up[:, cols])
    r.share_lifted(micro).start()
    middle_grad = r.branch[r.quad_rows(micro), :].astype(WIDE) + norm_backward(
        r, r.middle[micro], r.total[...], 1
    )
    r.middle[micro] = middle_grad
    r.grads[4, tokens, :] = middle_grad.astype(SLIM)
    r.held[...] = times_turned(r.grads[4, tokens, :], r.outward[...]).astype(SLIM)
    first, second = head_lanes()
    one, two = first.astype(SLIM), second.astype(SLIM)
    scaling = HEAD**-0.5
    for pair in range(width // (2 * HEAD)):
        cols = pl.ds(pair * 2 * HEAD, 2 * HEAD)
        queries = r.grads[5, tokens, cols] * jnp.asarray(scaling, SLIM)
        values = r.grads[7, tokens, cols]
        keys_turned = r.grads[6, tokens, cols].T
        incoming = r.held[:, cols]
        weight_grads = times_turned(jnp.concatenate([values * one, values * two], 0), incoming)
        score_grads, query_grads, weights = [], [], []
        for head in range(2):
            kept = r.weights[micro, 2 * pair + head]
            wide = kept.astype(WIDE)
            own = weight_grads[length * head : length * (head + 1)]
            score_grad = (wide * (own - jnp.sum(wide * own, 0, keepdims=True))).astype(SLIM)
            score_grads.append(score_grad)
            weights.append(kept)
            query_grads.append(
                (times(keys_turned[HEAD * head : HEAD * (head + 1)], score_grad) * scaling).astype(SLIM)
            )
        key_grad = times(jnp.concatenate(score_grads, 0), queries)
        value_grad = times(jnp.concatenate(weights, 0), incoming)
        r.grads[5, tokens, cols] = jnp.concatenate(query_grads, 0).T
        r.grads[6, tokens, cols] = (key_grad[:length] * first + key_grad[length:] * second).astype(SLIM)
        r.grads[7, tokens, cols] = (value_grad[:length] * first + value_grad[length:] * second).astype(SLIM)
    norm_grad = times_turned(r.grads[5, tokens, :], r.inward[:, 0:width])
    for part in range(1, 3):
        norm_grad += times_turned(r.grads[5 + part, tokens, :], r.inward[:, part * width : (part + 1) * width])
    r.total[...] = norm_grad
    input_grad = r.middle[micro] + norm_backward(r, r.stream[micro].astype(WIDE), r.total[...], 0)
    r.middle[micro] = input_grad
    r.stream[micro] = input_grad.astype(SLIM)


NAMES = (
    "x_in", "cot_in", "inward_in", "outward_in", "up_in", "down_in", "gain", "bias", "lengths", "offsets",
    "result", "middle", "staged", "out_norms",
    "stream", "inward", "outward", "up", "down", "grads", "branch", "acts", "acts_out", "quad_acts", "quad_out", "weights", "normed", "held",
    "turned", "total", "sums", "bias_mask",
    "partial", "y_in", "z_in", "far_y_in", "far_z_in", "norms",
    "load_sem", "source_sem",
    "relay_send", "relay_recv", "acts_send", "acts_recv", "branch_send", "branch_recv", "lifted_send", "lifted_recv",
    "across_send", "across_recv", "onward_send", "onward_recv", "quad_send", "quad_recv",
    "rest_send", "rest_recv", "turn",
    "y_send", "y_recv", "z_send", "z_recv", "far_y_send", "far_y_recv", "far_z_send", "far_z_recv", "norm_send", "norm_recv",
)


def step_kernel(*refs):
    r = types.SimpleNamespace(**dict(zip(NAMES, refs)))
    section, dp = lax.axis_index("section"), lax.axis_index("dp")
    c, y, z = lax.rem(dp, 2), lax.rem(lax.div(dp, 2), 2), lax.div(dp, 4)
    r.c, r.y = c, y
    length = r.normed.shape[0]
    leading = section == 0
    pair_dp, y_dp = dp + 1 - 2 * c, dp + 2 - 4 * y
    diagonal_dp = pair_dp + y_dp - dp

    def slot_of(core, micro):
        return pl.ds(pl.multiple_of((core * 2 + micro) * length, length), length)

    def quad_rows(micro, core=c, side=y):
        return pl.ds(pl.multiple_of(((side * 2 + core) * 2 + micro) * length, length), length)

    r.quad_rows = quad_rows

    def remote(src, dst, send, recv, to_section, to_dp):
        return pltpu.make_async_remote_copy(
            src_ref=src, dst_ref=dst, send_sem=send, recv_sem=recv,
            device_id=(to_section, to_dp), device_id_type=MESH,
        )

    def local(src, dst, sem):
        return pltpu.make_async_copy(src, dst, sem)

    r.load_inward = local(r.inward_in.at[0], r.inward, r.load_sem.at[0])
    r.load_outward = local(r.outward_in.at[0], r.outward, r.load_sem.at[1])
    r.load_up = local(r.up_in.at[0], r.up, r.load_sem.at[2])
    r.load_down = local(r.down_in.at[0], r.down, r.load_sem.at[3])

    def load_rest():
        r.load_outward.start()
        r.load_up.start()
        r.load_down.start()

    r.load_rest = load_rest

    def load_x(micro):
        return local(r.x_in.at[micro, 0], r.stream.at[micro], r.source_sem.at[micro])

    def load_cot(micro):
        return local(r.cot_in.at[micro, 0], r.branch.at[quad_rows(micro)], r.source_sem.at[micro])

    def relay_up(micro):
        return remote(r.result.at[micro], r.stream.at[micro], r.relay_send.at[micro], r.relay_recv.at[micro], 1 - section, dp)

    def relay_back(micro):
        return remote(
            r.stream.at[micro], r.branch.at[quad_rows(micro)], r.relay_send.at[micro], r.relay_recv.at[micro], 1 - section, dp
        )

    def share_acts(micro, core=c):
        return remote(
            r.acts_out, r.acts.at[:, :, slot_of(core, micro)], r.acts_send.at[micro], r.acts_recv.at[micro], section, pair_dp
        )

    def branch_copy(rows, send, recv, to_dp):
        return remote(r.branch.at[rows], r.branch.at[rows], send, recv, section, to_dp)

    def share_branch(micro, core=c):
        return branch_copy(quad_rows(micro, core), r.branch_send.at[micro], r.branch_recv.at[micro], pair_dp)

    def branch_across(micro, side=y):
        return branch_copy(quad_rows(micro, c, side), r.across_send.at[micro], r.across_recv.at[micro], y_dp)

    def branch_onward(micro, core=c):
        return branch_copy(quad_rows(micro, core, 1 - y), r.onward_send.at[micro], r.onward_recv.at[micro], pair_dp)

    def share_quad(micro, peer, arriving=False):
        to_dp = (pair_dp, y_dp, diagonal_dp)[peer]
        core = 1 - c if arriving and peer != 1 else c
        side = 1 - y if arriving and peer != 0 else y
        return remote(
            r.quad_out.at[micro, peer], r.quad_acts.at[:, :, quad_rows(micro, core, side)],
            r.quad_send.at[micro, peer], r.quad_recv.at[micro, peer], section, to_dp,
        )

    def share_lifted(micro, core=c):
        rows = slot_of(core, micro)
        return remote(
            r.grads.at[0:4, rows], r.grads.at[0:4, rows], r.lifted_send.at[micro], r.lifted_recv.at[micro], section, pair_dp
        )

    def share_rest(micro, core=c):
        rows = slot_of(core, micro)
        return remote(
            r.grads.at[4:8, rows], r.grads.at[4:8, rows], r.rest_send.at[micro], r.rest_recv.at[micro], section, pair_dp
        )

    r.share_lifted = share_lifted
    r.share_acts = share_acts

    def to_y(unit):
        return remote(
            r.partial.at[unit, 0], r.y_in.at[unit - QUAD], r.y_send.at[unit - QUAD], r.y_recv.at[unit - QUAD], section, y_dp
        )

    def rows_of(place):
        return pl.ds(BLOCK * place, BLOCK)

    def near_z(unit, place, index, lane, to_dp):
        near = unit - FAR
        return remote(
            r.partial.at[unit, 1, rows_of(place)], r.z_in.at[near, index],
            r.z_send.at[near, lane], r.z_recv.at[near, index], section, to_dp,
        )

    def far_z(unit, place, index, lane, to_dp):
        return remote(
            r.partial.at[unit, :, rows_of(place)], r.far_z_in.at[unit, index],
            r.far_z_send.at[unit, lane], r.far_z_recv.at[unit, index], section, to_dp,
        )

    def far_to_y(unit, place):
        return remote(
            r.partial.at[unit, 0, rows_of(place)], r.far_y_in.at[unit], r.far_y_send.at[unit], r.far_y_recv.at[unit], section, y_dp
        )

    r.load_inward.start()

    @pl.when(leading)
    def _():
        load_x(0).start()
        load_x(1).start()

    @pl.when(jnp.logical_not(leading))
    def _():
        load_cot(0).start()
        load_cot(1).start()

    @pl.when(jnp.logical_not(leading))
    def _():
        r.load_rest()

    r.sums[...] = jnp.zeros_like(r.sums)

    barrier = pltpu.get_barrier_semaphore()
    peers = [(1 - section, dp), (section, pair_dp), (section, y_dp)]
    peers += [(section, diagonal_dp)]
    peers += [(section, lax.rem(dp + 4 * hop, 16)) for hop in (1, 2, 3)]
    for peer in peers:
        pl.semaphore_signal(barrier, inc=1, device_id=peer, device_id_type=MESH)

    def everyone_in():
        pl.semaphore_wait(barrier, len(peers))

    def arrive(micro):
        relay_back(micro).wait_recv()
        branch_across(micro).start()
        share_branch(micro).start()

    def columns_of(unit):
        return pl.ds(pl.multiple_of(lax.rem(unit, 2) * COLUMNS, 128), COLUMNS)

    def side_rows(side):
        return pl.ds(pl.multiple_of(side * 192, 64), 192)

    def near_unit(unit):
        whole = lax.div(unit, 2)
        slab = 1 + jnp.where(whole >= 8, 1, 0) + jnp.where(whole >= 9, 1, 0)
        grads = r.grads[whole - 4, :, columns_of(unit)]
        r.partial[unit, 0] = times(r.acts[slab, side_rows(1 - y), :], grads).astype(SLIM)
        to_y(unit).start()
        r.partial[unit, 1] = times(r.acts[slab, side_rows(y), :], grads).astype(SLIM)

    def far_unit(unit):
        grads = r.branch[pl.ds(pl.multiple_of(y * 4 * length, length), 4 * length), columns_of(unit)]
        r.partial[unit, 0] = times(r.acts[0, side_rows(1 - y), :], grads).astype(SLIM)
        r.partial[unit, 1] = times(r.acts[0, side_rows(y), :], grads).astype(SLIM)
        at_ends(unit, far_z, r.far_z_in)

    def quad_unit(unit):
        grads = r.branch[:, columns_of(unit)]
        r.partial[unit, 1] = times(r.quad_acts[lax.div(unit, 2) - 1], grads).astype(SLIM)
        at_ends(unit, near_z, r.z_in)

    def arrived(unit, index, copy, into):
        copy(unit, 0, index, 0, dp).wait_recv()
        return into[unit if into is r.far_z_in else unit - FAR, index].astype(WIDE)

    def pick(unit, place, copy):
        return (unit, slice(None) if copy is far_z else 1, rows_of(place))

    def go_right(unit, here, copy, into):
        for place in range(3, here, -1):
            at = pick(unit, place, copy)
            if here > 0:
                r.partial[at] = (r.partial[at].astype(WIDE) + arrived(unit, place + 1, copy, into)).astype(SLIM)
            copy(unit, place, place + 1, place - 1, dp + 4).start()

    def go_left(unit, here, copy, into):
        for place in range(here):
            at = pick(unit, place, copy)
            if here < 3:
                r.partial[at] = (r.partial[at].astype(WIDE) + arrived(unit, place, copy, into)).astype(SLIM)
            copy(unit, place, place, place, dp - 4).start()

    def at_ends(unit, copy, into):
        @pl.when(z == 0)
        def _():
            go_right(unit, 0, copy, into)

        @pl.when(z == 3)
        def _():
            go_left(unit, 3, copy, into)

    def at_middle_first(unit, copy, into):
        @pl.when(z == 1)
        def _():
            go_right(unit, 1, copy, into)

        @pl.when(z == 2)
        def _():
            go_left(unit, 2, copy, into)

    def at_middle_second(unit, copy, into):
        @pl.when(z == 1)
        def _():
            go_left(unit, 1, copy, into)

        @pl.when(z == 2)
        def _():
            go_right(unit, 2, copy, into)

    def gathered(unit, here, copy, into):
        value = r.partial[pick(unit, here, copy)].astype(WIDE)
        if here > 0:
            value = value + arrived(unit, here + 1, copy, into)
        if here < 3:
            value = value + arrived(unit, here, copy, into)
        return value

    def everywhere(action):
        for here in range(4):

            @pl.when(z == here)
            def _():
                action(here)

    def slot(t, carry):
        trailing = jnp.logical_not(leading)
        half = lax.div(t, 2)
        is_forward = (leading & (t < 2)) | (trailing & ((t == 1) | (t == 3)))
        is_backward = (leading & ((t == 3) | (t == 5))) | (trailing & ((t == 2) | (t == 4)))
        is_weights = (leading & (t == 4)) | (trailing & (t == 5))

        @pl.when(trailing & (t == 0))
        def _():
            everyone_in()
            for micro in range(2):
                load_cot(micro).wait()
                branch_across(micro).start()
                share_branch(micro).start()

        @pl.when(is_forward)
        def _():
            micro = jnp.where(leading, jnp.minimum(t, 1), jnp.minimum(half, 1))

            @pl.when(leading)
            def _():
                load_x(micro).wait()

            @pl.when(trailing)
            def _():
                relay_up(micro).wait_recv()

            forward(r, micro, pl.multiple_of((c * 2 + micro) * length, length), t == section, leading)

            @pl.when(leading & (t == 0))
            def _():
                everyone_in()

            ahead = leading & (c == 0) & (t == 0)

            @pl.when(ahead)
            def _():
                relay_up(0).start()
                relay_up(0).wait_send()
                pl.semaphore_signal(r.turn, inc=1, device_id=(section, pair_dp), device_id_type=MESH)

            @pl.when(leading & (t == 1))
            def _():
                relay_up(1).start()

            share_acts(micro).start()

            @pl.when(leading & (c == 1) & (t == 0))
            def _():
                pl.semaphore_wait(r.turn, 1)
                relay_up(0).start()

            for peer in range(3):
                share_quad(micro, peer).start()

        @pl.when(leading & (t == 3))
        def _():
            arrive(0)

        @pl.when(is_backward)
        def _():
            micro = jnp.clip(half - 1, 0, 1)
            backward(r, micro, pl.multiple_of((c * 2 + micro) * length, length))

            @pl.when(trailing)
            def _():
                relay_back(micro).start()

            share_rest(micro).start()

            @pl.when(trailing & (t == 4))
            def _():
                def body(done, carry):
                    last_output(r, done)
                    return carry

                lax.fori_loop(0, 2, body, 0)

        @pl.when(leading & (t == 4))
        def _():
            arrive(1)

        @pl.when(is_weights)
        def _():
            for micro in range(2):
                share_branch(micro, 1 - c).wait_recv()
                share_acts(micro, 1 - c).wait_recv()

            def body(unit, carry):
                far_unit(unit)
                return carry

            lax.fori_loop(0, FAR, body, 0)

        return carry

    lax.fori_loop(0, 6, slot, 0)

    def norm_copy(src, dst, index, to_dp):
        return remote(r.norms.at[src], r.norms.at[dst], r.norm_send.at[index], r.norm_recv.at[index], section, to_dp)

    def norm_to_pair():
        return norm_copy(0, 1, 0, pair_dp)

    def norm_to_y():
        return norm_copy(2, 3, 1, y_dp)

    def norm_to_z(hop):
        return norm_copy(4, 4 + hop, 1 + hop, lax.rem(dp + 4 * hop, 16))

    r.norms[0] = jnp.concatenate([jnp.sum(r.sums[...], 1), jnp.zeros((4, r.sums.shape[2]), WIDE)], 0)
    norm_to_pair().start()
    for micro in range(2):
        share_lifted(micro, 1 - c).wait_recv()

    def early_near(ahead, carry):
        near_unit(QUAD + ahead)
        return carry

    lax.fori_loop(0, EARLY_NEAR, early_near, 0)
    for micro in range(2):
        branch_across(micro, 1 - y).wait_recv()
        branch_onward(micro).start()
    for micro in range(2):
        branch_onward(micro, 1 - c).wait_recv()
        for peer in range(3):
            share_quad(micro, peer, True).wait_recv()

    def early_quad(unit, carry):
        quad_unit(unit)
        return carry

    lax.fori_loop(FAR, FAR + sum(step < 0 for step in QUAD_AT), early_quad, 0)

    def sum_y(unit):
        to_y(unit).wait_recv()
        r.partial[unit, 1] = (r.partial[unit, 1].astype(WIDE) + r.y_in[unit - QUAD].astype(WIDE)).astype(SLIM)

    def turn_of(i, steps, base):
        turn, unit = i < 0, jnp.int32(base)
        for index, step in enumerate(steps):
            if step >= 0:
                turn = turn | (i == step)
                unit = jnp.where(i == step, base + index, unit)
        return turn, unit

    def near_turn(i, lag):
        return (i >= lag) & (i < NEAR + lag), jnp.clip(i - lag, 0, NEAR - 1) + QUAD

    def end_of_line(unit):
        def action(here):
            r.staged[unit] = gathered(unit, here, near_z, r.z_in)

        everywhere(action)

    def advance(i, carry):
        issued = QUAD + EARLY_NEAR + i - HOLD

        @pl.when(issued == 16)
        def _():
            for micro in range(2):
                share_rest(micro, 1 - c).wait_recv()

        @pl.when((issued >= QUAD + EARLY_NEAR) & (issued < UNITS))
        def _():
            near_unit(issued)

        @pl.when(i < NEAR)
        def _():
            sum_y(QUAD + i)
            at_ends(QUAD + i, near_z, r.z_in)

        turn, unit = turn_of(i, QUAD_AT, FAR)

        @pl.when(turn)
        def _(unit=unit):
            quad_unit(unit)

        turn, unit = near_turn(i, LAGS[0])

        @pl.when(turn)
        def _(unit=unit):
            at_middle_first(unit, near_z, r.z_in)

        turn, unit = turn_of(i, FAR_FIRST, 0)

        @pl.when(turn)
        def _(unit=unit):
            at_middle_first(unit, far_z, r.far_z_in)

        turn, unit = turn_of(i, QUAD_FIRST, FAR)

        @pl.when(turn)
        def _(unit=unit):
            at_middle_first(unit, near_z, r.z_in)

        turn, unit = turn_of(i, FAR_SECOND, 0)

        @pl.when(turn)
        def _(unit=unit):
            at_middle_second(unit, far_z, r.far_z_in)

        turn, unit = turn_of(i, QUAD_SECOND, FAR)

        @pl.when(turn)
        def _(unit=unit):
            at_middle_second(unit, near_z, r.z_in)

        turn, unit = near_turn(i, LAGS[1])

        @pl.when(turn)
        def _(unit=unit):
            at_middle_second(unit, near_z, r.z_in)

        turn, unit = turn_of(i, QUAD_DONE, FAR)

        @pl.when(turn)
        def _(unit=unit):
            end_of_line(unit)

        turn, unit = near_turn(i, LAGS[2])

        @pl.when(turn)
        def _(unit=unit):
            end_of_line(unit)

        turn, unit = turn_of(i, FAR_ARRIVED, 0)

        @pl.when(turn)
        def _(unit=unit):
            def action(here):
                value = gathered(unit, here, far_z, r.far_z_in)
                r.partial[unit, 0, rows_of(here)] = value[0].astype(SLIM)
                far_to_y(unit, here).start()
                r.staged[unit] = value[1]

            everywhere(action)

        turn, unit = turn_of(i, FAR_DONE, 0)

        @pl.when(turn)
        def _(unit=unit):
            far_to_y(unit, 0).wait_recv()
            r.staged[unit] += r.far_y_in[unit].astype(WIDE)

        @pl.when(i == 1)
        def _():
            norm_to_pair().wait()
            r.norms[2] = r.norms[0] + r.norms[1]
            norm_to_y().start()

        @pl.when(i == 9)
        def _():
            norm_to_y().wait_recv()
            r.norms[4] = r.norms[2] + r.norms[3]
            for hop in (1, 2, 3):
                norm_to_z(hop).start()

        @pl.when(i == 15)
        def _():
            for hop in (1, 2, 3):
                norm_to_z(hop).wait_recv()
            r.out_norms[...] = (r.norms[4] + r.norms[5]) + (r.norms[6] + r.norms[7])

        return carry

    lax.fori_loop(0, NEAR + LAGS[2], advance, 0)

    norm_to_y().wait_send()
    for hop in (1, 2, 3):
        norm_to_z(hop).wait_send()
    share_acts(1).wait_send()
    for micro in range(2):
        share_branch(micro).wait_send()
        branch_across(micro).wait_send()
        branch_onward(micro).wait_send()
        for peer in range(3):
            share_quad(micro, peer).wait_send()
        share_lifted(micro).wait_send()
        share_rest(micro).wait_send()

        @pl.when(leading if micro else leading & (c == 1))
        def _():
            relay_up(micro).wait_send()

        @pl.when(jnp.logical_not(leading))
        def _():
            relay_back(micro).wait_send()

    def drain_y(near, carry):
        to_y(QUAD + near).wait_send()
        return carry

    lax.fori_loop(0, NEAR, drain_y, 0)

    def drain_z(unit, carry):
        for lane in range(3):
            near_z(unit, 0, 0, lane, dp).wait_send()
        return carry

    lax.fori_loop(FAR, UNITS, drain_z, 0)

    def drain_far(unit, carry):
        far_to_y(unit, 0).wait_send()
        for lane in range(3):
            far_z(unit, 0, 0, lane, dp).wait_send()
        return carry

    lax.fori_loop(0, FAR, drain_far, 0)


def hand_over_kernel(result, grad, staged, norms, *refs):
    out_result, out_grad, out_inward, out_outward, out_up, out_down, gain_grad, bias_grad, sem = refs
    width = result.shape[2]

    def start(source, target):
        copy = pltpu.make_async_copy(source, target, sem)
        copy.start()
        return copy

    copies = [start(result, out_result.at[0, :, 0]), start(grad, out_grad.at[0, :, 0])]
    for piece in range(UNITS):
        half = pl.ds(piece % 2 * COLUMNS, COLUMNS)
        if piece < 8:
            target = out_down.at[0, pl.ds(piece // 2 * BLOCK, BLOCK), half]
        elif piece < 16:
            target = out_up.at[0, :, pl.ds((piece - 8) * COLUMNS, COLUMNS)]
        elif piece < 18:
            target = out_outward.at[0, :, half]
        else:
            target = out_inward.at[0, :, pl.ds((piece - 18) * COLUMNS, COLUMNS)]
        copies.append(start(staged.at[piece], target))
    share = gain_grad.shape[2]
    for index in range(width // share):

        @pl.when(lax.axis_index("dp") == index)
        def _():
            gain_grad[0] = norms[0:2, index * share : (index + 1) * share]
            bias_grad[0] = norms[2:4, index * share : (index + 1) * share]

    for copy in copies:
        copy.wait()


def step_on_device(
    inputs, clip_lengths, anchor_offsets, cotangent, inward_weight, outward_weight, up_weight, down_weight, norm_gain, norm_bias
):
    _, _, length, width = inputs.shape
    wide_ff = up_weight.shape[2]
    anywhere = pl.BlockSpec(memory_space=pl.ANY)
    in_vmem = pl.BlockSpec(memory_space=pltpu.VMEM)
    in_smem = pl.BlockSpec(memory_space=pltpu.SMEM)
    dma = pltpu.SemaphoreType.DMA
    share = width // lax.axis_size("dp")
    made = pl.pallas_call(
        step_kernel,
        out_shape=(
            pltpu.VMEM((2, length, width), SLIM),
            pltpu.VMEM((2, length, width), WIDE),
            pltpu.VMEM((UNITS, BLOCK, COLUMNS), WIDE),
            pltpu.VMEM((8, width), WIDE),
        ),
        in_specs=[anywhere] * 6 + [in_vmem] * 2 + [in_smem] * 2,
        out_specs=[in_vmem] * 4,
        scratch_shapes=[
            pltpu.VMEM((2, length, width), SLIM),
            pltpu.VMEM((width, 3 * width), SLIM),
            pltpu.VMEM((width, width), SLIM),
            pltpu.VMEM((width, wide_ff), SLIM),
            pltpu.VMEM((wide_ff, width), SLIM),
            pltpu.VMEM((8, 4 * length, width), SLIM),
            pltpu.VMEM((8 * length, width), SLIM),
            pltpu.VMEM((4, 8 * BLOCK, 4 * length), SLIM),
            pltpu.VMEM((4, 8 * BLOCK, length), SLIM),
            pltpu.VMEM((3, 4 * BLOCK, 8 * length), SLIM),
            pltpu.VMEM((2, 3, 3, 4 * BLOCK, length), SLIM),
            pltpu.VMEM((2, width // HEAD, length, length), SLIM),
            pltpu.VMEM((length, width), SLIM),
            pltpu.VMEM((length, width), SLIM),
            pltpu.VMEM((width, length), SLIM),
            pltpu.VMEM((length, width), WIDE),
            pltpu.VMEM((4, 8, width), WIDE),
            pltpu.VMEM((length, length), WIDE),
            pltpu.VMEM((UNITS, 2, 4 * BLOCK, COLUMNS), SLIM),
            pltpu.VMEM((NEAR, 4 * BLOCK, COLUMNS), SLIM),
            pltpu.VMEM((UNITS - FAR, 5, BLOCK, COLUMNS), SLIM),
            pltpu.VMEM((FAR, BLOCK, COLUMNS), SLIM),
            pltpu.VMEM((FAR, 5, 2, BLOCK, COLUMNS), SLIM),
            pltpu.VMEM((8, 8, width), WIDE),
            dma((4,)), dma((2,)),
            *[dma((2,))] * 8, *[dma((2,))] * 4, dma((2, 3)), dma((2, 3)), *[dma((2,))] * 2, pltpu.SemaphoreType.REGULAR,
            dma((NEAR,)), dma((NEAR,)), dma((UNITS - FAR, 3)), dma((UNITS - FAR, 5)),
            dma((FAR,)), dma((FAR,)), dma((FAR, 3)), dma((FAR, 5)), dma((5,)), dma((5,)),
        ],
        compiler_params=pltpu.CompilerParams(
            collective_id=0, has_side_effects=True, vmem_limit_bytes=VMEM_BYTES - 4500000
        ),
    )(
        inputs, cotangent, inward_weight, outward_weight, up_weight, down_weight,
        norm_gain, norm_bias, clip_lengths, anchor_offsets,
    )
    sections = 1
    return pl.pallas_call(
        hand_over_kernel,
        out_shape=(
            jax.ShapeDtypeStruct((sections, 2, 1, length, width), SLIM),
            jax.ShapeDtypeStruct((sections, 2, 1, length, width), WIDE),
            jax.ShapeDtypeStruct((sections, BLOCK, 3 * width), WIDE),
            jax.ShapeDtypeStruct((sections, BLOCK, width), WIDE),
            jax.ShapeDtypeStruct((sections, BLOCK, wide_ff), WIDE),
            jax.ShapeDtypeStruct((sections, 4 * BLOCK, width), WIDE),
            jax.ShapeDtypeStruct((sections, 2, share), WIDE),
            jax.ShapeDtypeStruct((sections, 2, share), WIDE),
        ),
        in_specs=[in_vmem] * 4,
        out_specs=[anywhere] * 6 + [in_vmem] * 2,
        scratch_shapes=[dma],
        compiler_params=pltpu.CompilerParams(vmem_limit_bytes=1 << 20),
    )(*[pltpu.with_memory_space_constraint(one, pltpu.VMEM) for one in made])


def shifted(x, axis, by):
    size = lax.axis_size(axis)
    pairs = [(i, i + by) for i in range(size) if 0 <= i + by < size]
    return lax.ppermute(x, axis, pairs)


def norm_rows(values, norm_gain, norm_bias):
    average = jnp.mean(values, -1, keepdims=True)
    centred = values - average
    inverse = lax.rsqrt(jnp.mean(centred * centred, -1, keepdims=True) + EPSILON)
    normed = centred * inverse
    return (normed * norm_gain + norm_bias, normed, inverse)


def norm_back(norm_grad, normed, inverse, norm_gain):
    inner = norm_grad * norm_gain
    through = inverse * (
        inner
        - jnp.mean(inner, -1, keepdims=True)
        - normed * jnp.mean(inner * normed, -1, keepdims=True)
    )
    return (through, jnp.sum(norm_grad * normed, 0), jnp.sum(norm_grad, 0))


def gelu_slope(lifted):
    cumulative = 0.5 * (1.0 + lax.erf(lifted * 0.7071067811865476))
    density = jnp.exp(-0.5 * lifted * lifted) * 0.3989422804014327
    return cumulative + lifted * density


def clip_marks(lengths, offsets, length):
    positions = jnp.arange(length, dtype=jnp.int32)
    clip_ends = jnp.cumsum(lengths)
    clip_starts = clip_ends - lengths
    anchor_at = clip_starts + offsets % lengths
    clip_ids = jnp.sum((positions[:, None] >= clip_ends[None, :]).astype(jnp.int32), 1)
    anchors = jnp.any(positions[:, None] == anchor_at[None, :], 1)
    return (clip_ids, anchors)


def masked_scores(query_block, key_rows, id_block, clip_ids, anchors, scaling):
    scores = (
        jnp.einsum("qhd,khd->hqk", query_block, key_rows, preferred_element_type=jnp.float32)
        * scaling
    )
    seen = (id_block[:, None] == clip_ids[None, :]) | anchors[None, :]
    return jnp.where(seen[None], scores, -1000000000.0)


def forward_layer(source, clip_ids, anchors, params):
    inward, outward, upward, downward, norm_gain, norm_bias = params
    length, model_width = source.shape
    head_count = model_width // HEAD
    scaling = HEAD ** (-0.5)
    residual = source.astype(jnp.float32)
    first_norm, unit_one, scale_one = norm_rows(residual, norm_gain[0], norm_bias[0])
    joined = jnp.dot(
        first_norm.astype(jnp.bfloat16), inward, preferred_element_type=jnp.float32
    ).astype(jnp.bfloat16)
    heads_view = joined.reshape(length, 3, head_count, HEAD)
    queries = heads_view[:, 0]
    key_rows = heads_view[:, 1]
    values = heads_view[:, 2]
    scores = masked_scores(queries, key_rows, clip_ids, clip_ids, anchors, scaling)
    row_max = jnp.max(scores, -1, keepdims=True)
    raised = jnp.exp(scores - row_max)
    row_sum = jnp.sum(raised, -1, keepdims=True)
    weights = (raised / row_sum).astype(jnp.bfloat16)
    pieces = [jnp.einsum("hqk,khd->qhd", weights, values, preferred_element_type=jnp.float32)]
    log_sums = [(row_max + jnp.log(row_sum))[..., 0]]
    attended = jnp.concatenate(pieces, 0).reshape(length, model_width).astype(jnp.bfloat16)
    logsum = jnp.concatenate(log_sums, 1)
    middle = residual + jnp.dot(attended, outward, preferred_element_type=jnp.float32)
    second_norm, unit_two, scale_two = norm_rows(middle, norm_gain[1], norm_bias[1])
    lifted = jnp.dot(second_norm.astype(jnp.bfloat16), upward, preferred_element_type=jnp.float32)
    active = jax.nn.gelu(lifted, approximate=False).astype(jnp.bfloat16)
    result = middle + jnp.dot(active, downward, preferred_element_type=jnp.float32)
    stored = (unit_one, scale_one, joined, logsum, attended, unit_two, scale_two, lifted, active)
    return (result, stored)


def contract_rows(left, right):
    return lax.dot_general(
        left, right, (((0,), (0,)), ((), ())), preferred_element_type=jnp.float32
    )


def contract_cols(left, right):
    return lax.dot_general(
        left, right, (((1,), (1,)), ((), ())), preferred_element_type=jnp.float32
    )


def feed_backward(incoming, stored, params):
    inward, outward, upward, downward, norm_gain, norm_bias = params
    unit_one, scale_one, joined, logsum, attended, unit_two, scale_two, lifted, active = stored
    branch = incoming.astype(jnp.bfloat16)
    down_part = contract_rows(active, branch)
    hidden_grad = contract_cols(branch, downward)
    lifted_grad = (hidden_grad * gelu_slope(lifted)).astype(jnp.bfloat16)
    second_in = (unit_two * norm_gain[1] + norm_bias[1]).astype(jnp.bfloat16)
    up_part = contract_rows(second_in, lifted_grad)
    normed_grad = contract_cols(lifted_grad, upward)
    through, gain_two, bias_two = norm_back(normed_grad, unit_two, scale_two, norm_gain[1])
    return (incoming + through, (up_part, down_part, gain_two, bias_two))


def attend_backward(middle_grad, stored, clip_ids, anchors, params):
    inward, outward, upward, downward, norm_gain, norm_bias = params
    unit_one, scale_one, joined, logsum, attended, unit_two, scale_two, lifted, active = stored
    length, model_width = attended.shape
    head_count = model_width // HEAD
    scaling = HEAD ** (-0.5)
    branch = middle_grad.astype(jnp.bfloat16)
    outward_part = contract_rows(attended, branch)
    attended_grad = (
        contract_cols(branch, outward).astype(jnp.bfloat16).reshape(length, head_count, HEAD)
    )
    heads_view = joined.reshape(length, 3, head_count, HEAD)
    queries = heads_view[:, 0]
    key_rows = heads_view[:, 1]
    values = heads_view[:, 2]
    key_grad = jnp.zeros((length, head_count, HEAD), jnp.float32)
    value_grad = jnp.zeros((length, head_count, HEAD), jnp.float32)
    block_rows = min(512, length)
    scores = masked_scores(queries, key_rows, clip_ids, clip_ids, anchors, scaling)
    weights = jnp.exp(scores - logsum[:, 0:block_rows, None])
    weight_grad = jnp.einsum(
        "qhd,khd->hqk", attended_grad, values, preferred_element_type=jnp.float32
    )
    score_grad = (
        weights * (weight_grad - jnp.sum(weights * weight_grad, -1, keepdims=True))
    ).astype(jnp.bfloat16)
    query_pieces = [
        scaling
        * jnp.einsum("hqk,khd->qhd", score_grad, key_rows, preferred_element_type=jnp.float32)
    ]
    key_grad = key_grad + scaling * jnp.einsum(
        "hqk,qhd->khd", score_grad, queries, preferred_element_type=jnp.float32
    )
    value_grad = value_grad + jnp.einsum(
        "hqk,qhd->khd",
        weights.astype(jnp.bfloat16),
        attended_grad,
        preferred_element_type=jnp.float32,
    )
    query_grad = jnp.concatenate(query_pieces, 0)
    joined_grad = (
        jnp.stack([query_grad, key_grad, value_grad], 1)
        .reshape(length, 3 * model_width)
        .astype(jnp.bfloat16)
    )
    first_in = (unit_one * norm_gain[0] + norm_bias[0]).astype(jnp.bfloat16)
    inward_part = contract_rows(first_in, joined_grad)
    normed_grad = contract_cols(joined_grad, inward)
    through, gain_one, bias_one = norm_back(normed_grad, unit_one, scale_one, norm_gain[0])
    return (middle_grad + through, (inward_part, outward_part, gain_one, bias_one))


def resting(function):

    def blank(*operands):
        return jax.tree.map(jnp.zeros_like, function(*operands))

    return blank


def take_slot(holder, buffer_slot):
    return jax.tree.map(
        lambda element: lax.dynamic_index_in_dim(element, buffer_slot, 0, False), holder
    )


def place_slot(holder, item, buffer_slot, working):

    def update(element, fresh):
        former = lax.dynamic_index_in_dim(element, buffer_slot, 0, False)
        return lax.dynamic_update_index_in_dim(
            element, jnp.where(working, fresh, former), buffer_slot, 0
        )

    return jax.tree.map(update, holder, item)


def per_device(
    inputs,
    clip_lengths,
    anchor_offsets,
    cotangent,
    inward_weight,
    outward_weight,
    up_weight,
    down_weight,
    norm_gain,
    norm_bias,
):
    params = (
        inward_weight[0],
        outward_weight[0],
        up_weight[0],
        down_weight[0],
        norm_gain[0],
        norm_bias[0],
    )
    stream = inputs[:, 0]
    cot_rows = cotangent[:, 0]
    lengths_all = clip_lengths[:, 0]
    offsets_all = anchor_offsets[:, 0]
    micro_count = stream.shape[0]
    length = stream.shape[1]
    section_index = lax.axis_index("section")
    section_count = lax.axis_size("section")
    leading = section_index == 0
    trailing = section_index == section_count - 1
    periods = micro_count + section_count - 1
    arriving = jnp.zeros_like(stream[0])
    produced = jnp.zeros_like(stream)
    archive = None
    for period in range(periods):
        micro_index = period - section_index
        working = (micro_index >= 0) & (micro_index < micro_count)
        buffer_slot = jnp.clip(micro_index, 0, micro_count - 1)
        source = jnp.where(leading, stream[min(period, micro_count - 1)], arriving)
        clip_ids, anchors = clip_marks(
            take_slot(lengths_all, buffer_slot), take_slot(offsets_all, buffer_slot), length
        )
        result, stored = lax.cond(
            working, forward_layer, resting(forward_layer), source, clip_ids, anchors, params
        )
        if archive is None:
            archive = jax.tree.map(
                lambda element: jnp.zeros((micro_count,) + element.shape, element.dtype), stored
            )
        archive = place_slot(archive, stored, buffer_slot, working)
        sending = result.astype(jnp.bfloat16)
        produced = place_slot(produced, sending, buffer_slot, working)
        if period < micro_count:
            arriving = shifted(sending, "section", 1)
    inward, outward, upward, downward, gains, biases = params
    up_sum = jnp.zeros(upward.shape, jnp.float32)
    down_sum = jnp.zeros(downward.shape, jnp.float32)
    gain_two = jnp.zeros(gains.shape[1:], jnp.float32)
    bias_two = jnp.zeros(biases.shape[1:], jnp.float32)
    inward_sum = jnp.zeros(inward.shape, jnp.float32)
    outward_sum = jnp.zeros(outward.shape, jnp.float32)
    gain_one = jnp.zeros(gains.shape[1:], jnp.float32)
    bias_one = jnp.zeros(biases.shape[1:], jnp.float32)
    upstream = jnp.zeros_like(stream[0])
    returned = jnp.zeros(stream.shape, jnp.float32)
    for period in range(periods):
        micro_index = micro_count - 1 - period + (section_count - 1 - section_index)
        working = (micro_index >= 0) & (micro_index < micro_count)
        buffer_slot = jnp.clip(micro_index, 0, micro_count - 1)
        incoming = jnp.where(trailing, take_slot(cot_rows, buffer_slot), upstream).astype(
            jnp.float32
        )
        clip_ids, anchors = clip_marks(
            take_slot(lengths_all, buffer_slot), take_slot(offsets_all, buffer_slot), length
        )
        stored = take_slot(archive, buffer_slot)
        middle_grad, feed_part = lax.cond(
            working, feed_backward, resting(feed_backward), incoming, stored, params
        )
        up_sum = up_sum + feed_part[0]
        down_sum = down_sum + feed_part[1]
        gain_two = gain_two + feed_part[2]
        bias_two = bias_two + feed_part[3]
        input_grad, attend_part = lax.cond(
            working,
            attend_backward,
            resting(attend_backward),
            middle_grad,
            stored,
            clip_ids,
            anchors,
            params,
        )
        inward_sum = inward_sum + attend_part[0]
        outward_sum = outward_sum + attend_part[1]
        gain_one = gain_one + attend_part[2]
        bias_one = bias_one + attend_part[3]
        returned = place_slot(returned, input_grad, buffer_slot, working)
        if period < periods - 1:
            upstream = shifted(input_grad.astype(jnp.bfloat16), "section", -1)
    inward_sum, outward_sum, up_sum, down_sum, gain_one, gain_two, bias_one, bias_two = (
        lax.psum_scatter(inward_sum, "dp", scatter_dimension=0, tiled=True),
        lax.psum_scatter(outward_sum, "dp", scatter_dimension=0, tiled=True),
        lax.psum_scatter(up_sum, "dp", scatter_dimension=0, tiled=True),
        lax.psum_scatter(down_sum, "dp", scatter_dimension=0, tiled=True),
        lax.psum_scatter(gain_one, "dp", scatter_dimension=0, tiled=True),
        lax.psum_scatter(gain_two, "dp", scatter_dimension=0, tiled=True),
        lax.psum_scatter(bias_one, "dp", scatter_dimension=0, tiled=True),
        lax.psum_scatter(bias_two, "dp", scatter_dimension=0, tiled=True),
    )
    layer_outputs = produced[None, :, None]
    input_grads = returned[None, :, None]
    gain_grad = jnp.stack([gain_one, gain_two])[None]
    bias_grad = jnp.stack([bias_one, bias_two])[None]
    return (
        layer_outputs,
        input_grads,
        inward_sum[None],
        outward_sum[None],
        up_sum[None],
        down_sum[None],
        gain_grad,
        bias_grad,
    )


def solution(mesh):
    local = step_on_device if mesh.shape["dp"] == 16 and mesh.shape["section"] == 2 else per_device
    return jax.shard_map(
        local,
        mesh=mesh,
        in_specs=(
            P(None, "dp", None, None),
            P(None, "dp", None),
            P(None, "dp", None),
            P(None, "dp", None, None),
            P("section", None, None),
            P("section", None, None),
            P("section", None, None),
            P("section", None, None),
            P("section", None, None),
            P("section", None, None),
        ),
        out_specs=(
            P("section", None, "dp", None, None),
            P("section", None, "dp", None, None),
            P("section", "dp", None),
            P("section", "dp", None),
            P("section", "dp", None),
            P("section", "dp", None),
            P("section", None, "dp"),
            P("section", None, "dp"),
        ),
        check_vma=False,
    )
```

```python
import functools
import types

import jax
import jax.numpy as jnp
from jax import lax
from jax.experimental import pallas as pl
from jax.experimental.pallas import tpu as pltpu
from jax.sharding import PartitionSpec as P

HEAD = 64
EPSILON = 1e-06
MESH = pl.DeviceIdType.MESH
WIDE = jnp.float32
SLIM = jnp.bfloat16
VMEM_BYTES = 67043328

UNITS = 24
FAR = 2
QUAD = 8
NEAR = UNITS - QUAD
BLOCK = 48
COLUMNS = 384
EARLY_NEAR = 2
HOLD = 0
LAGS = (2, 4, 6)
FAR_FIRST = (0, 5)
FAR_SECOND = (2, 9)
FAR_ARRIVED = (3, 18)
FAR_DONE = (7, 21)
QUAD_AT = (-1, -1, 2, 4, 6, 12)
QUAD_FIRST = (3, 2, 6, 7, 9, 13)
QUAD_SECOND = (5, 7, 15, 13, 11, 16)
QUAD_DONE = (18, 13, 19, 21, 12, 20)


def times(left, right):
    return jnp.dot(left, right, preferred_element_type=WIDE)


def times_turned(left, right):
    return lax.dot_general(left, right, (((1,), (1,)), ((), ())), preferred_element_type=WIDE)


def unit_rows(values):
    centred = values - jnp.mean(values, -1, keepdims=True)
    inverse = lax.rsqrt(jnp.mean(centred * centred, -1, keepdims=True) + EPSILON)
    return centred * inverse, inverse


def norm_rows_bf16(r, values, which):
    unit, _ = unit_rows(values)
    return (unit * r.gain[0, which : which + 1, :] + r.bias[0, which : which + 1, :]).astype(SLIM)


def norm_backward(r, values, norm_grad, which):
    unit, inverse = unit_rows(values)
    width = values.shape[1]
    r.sums[which] += jnp.sum((norm_grad * unit).reshape(-1, 8, width), 0)
    r.sums[2 + which] += jnp.sum(norm_grad.reshape(-1, 8, width), 0)
    inner = norm_grad * r.gain[0, which : which + 1, :]
    return inverse * (
        inner
        - jnp.mean(inner, -1, keepdims=True)
        - unit * jnp.mean(inner * unit, -1, keepdims=True)
    )


def head_lanes():
    lane = lax.broadcasted_iota(jnp.int32, (1, 2 * HEAD), 1)
    first = jnp.where(lane < HEAD, 1.0, 0.0).astype(WIDE)
    return first, 1.0 - first


def mask_bias(r, micro):
    length = r.bias_mask.shape[0]

    def marks(positions):
        end = jnp.int32(0)
        ids = jnp.zeros(positions.shape, jnp.int32)
        anchors = jnp.zeros(positions.shape, jnp.int32)
        for clip in range(r.lengths.shape[2]):
            size = r.lengths[micro, 0, clip]
            anchor = end + lax.rem(r.offsets[micro, 0, clip], size)
            end = end + size
            ids = ids + jnp.where(positions >= end, 1, 0)
            anchors = anchors + jnp.where(positions == anchor, 1, 0)
        return ids, anchors

    key_ids, anchors = marks(lax.broadcasted_iota(jnp.int32, (length, 1), 0))
    query_ids, _ = marks(lax.broadcasted_iota(jnp.int32, (1, length), 1))
    seen = (key_ids == query_ids) | (jnp.broadcast_to(anchors, (length, length)) > 0)
    r.bias_mask[...] = jnp.where(seen, 0.0, -1000000000.0).astype(WIDE)


def place(r, slab, tokens):
    for line in range(8):
        z, y = line // 2, line % 2
        rows = pl.ds(y * 192 + z * BLOCK, BLOCK)
        own = pl.ds(pl.multiple_of(2 * BLOCK * line + r.c * BLOCK, 16), BLOCK)
        other = pl.ds(pl.multiple_of(2 * BLOCK * line + (1 - r.c) * BLOCK, 16), BLOCK)
        r.acts[slab, rows, tokens] = r.turned[own, :]
        r.acts_out[slab, rows, :] = r.turned[other, :]


def forward(r, micro, tok, first, leading):
    length, width = r.normed.shape
    tokens = pl.ds(tok, length)
    r.normed[...] = norm_rows_bf16(r, r.stream[micro].astype(WIDE), 0)

    @pl.when(first)
    def _():
        r.load_inward.wait()

        @pl.when(leading)
        def _():
            r.load_rest()

    for part in range(3):
        r.grads[5 + part, tokens, :] = times(
            r.normed[...], r.inward[:, part * width : (part + 1) * width]
        ).astype(SLIM)

    @pl.when(micro > 0)
    def _():
        r.share_acts(0).wait_send()

    r.turned[...] = r.normed[...].T
    place(r, 3, tokens)
    one, two = (lanes.astype(SLIM) for lanes in head_lanes())
    for pair in range(width // (2 * HEAD)):
        cols = pl.ds(pair * 2 * HEAD, 2 * HEAD)
        queries = r.grads[5, tokens, cols] * jnp.asarray(HEAD**-0.5, SLIM)
        keys = r.grads[6, tokens, cols]
        values_turned = r.grads[7, tokens, cols].T
        scores = times_turned(jnp.concatenate([keys * one, keys * two], 0), queries)
        pieces = []
        for head in range(2):
            masked = scores[length * head : length * (head + 1)] + r.bias_mask[...]
            raised = jnp.exp(masked - jnp.max(masked, 0, keepdims=True))
            weights = (raised * (1.0 / jnp.sum(raised, 0, keepdims=True))).astype(SLIM)
            r.weights[micro, 2 * pair + head] = weights
            pieces.append(times(values_turned[HEAD * head : HEAD * (head + 1)], weights).astype(SLIM))
        attended_turned = jnp.concatenate(pieces, 0)
        r.turned[cols, :] = attended_turned
        r.held[:, cols] = attended_turned.T
    place(r, 2, tokens)

    @pl.when(first)
    def _():
        r.load_outward.wait()

    r.middle[micro] = r.stream[micro].astype(WIDE) + times(r.held[...], r.outward[...])
    r.normed[...] = norm_rows_bf16(r, r.middle[micro], 1)
    r.turned[...] = r.normed[...].T
    place(r, 1, tokens)

    @pl.when(first)
    def _():
        r.load_up.wait()
        r.load_down.wait()

    def activate(part):
        lifted = times(r.normed[...], r.up[:, part * width : (part + 1) * width])
        cumulative = 0.5 * (1.0 + lax.erf(lifted * 0.7071067811865476))
        density = jnp.exp(-0.5 * lifted * lifted) * 0.3989422804014327
        r.grads[part, tokens, :] = (cumulative + lifted * density).astype(SLIM)
        active = (lifted * cumulative).astype(SLIM)
        r.turned[...] = active.T
        rows = pl.ds(part * BLOCK, BLOCK)
        for y in range(2):
            placed = pl.ds(y * 192 + part * BLOCK, BLOCK)
            own = pl.ds(pl.multiple_of(384 * y + r.c * 192, 16), BLOCK)
            other = pl.ds(pl.multiple_of(384 * y + (1 - r.c) * 192, 16), BLOCK)
            r.acts[0, placed, tokens] = r.turned[own, :]
            r.acts_out[0, placed, :] = r.turned[other, :]
        for piece in range(3):

            def rows_for(core, side):
                start = 384 * side + 192 * core + BLOCK * (piece + 1)
                return r.turned[pl.ds(pl.multiple_of(start, 16), BLOCK), :]

            r.quad_acts[piece, rows, r.quad_rows(micro)] = rows_for(r.c, r.y)
            r.quad_out[micro, 0, piece, rows, :] = rows_for(1 - r.c, r.y)
            r.quad_out[micro, 1, piece, rows, :] = rows_for(r.c, 1 - r.y)
            r.quad_out[micro, 2, piece, rows, :] = rows_for(1 - r.c, 1 - r.y)
        return active

    @pl.when(leading)
    def _():
        r.total[...] = r.middle[micro]
        for part in range(4):
            r.total[...] += times(activate(part), r.down[part * width : (part + 1) * width, :])
        r.result[micro] = r.total[...].astype(SLIM)

    @pl.when(jnp.logical_not(leading))
    def _():
        for part in range(4):
            set_aside(r, micro * 12 + 2 * part, activate(part))
        middle = r.middle[micro]
        upper = middle.astype(SLIM)
        set_aside(r, micro * 12 + 8, upper)
        set_aside(r, micro * 12 + 10, (middle - upper.astype(WIDE)).astype(SLIM))


def set_aside(r, slot, values):
    for half in range(2):
        columns = values[:, half * COLUMNS : (half + 1) * COLUMNS]
        r.partial[slot + half, 0] = columns[:192]
        r.partial[slot + half, 1, 0:64] = columns[192:]


def set_back(r, slot):
    halves = [
        jnp.concatenate([r.partial[slot + half, 0], r.partial[slot + half, 1, 0:64]], 0) for half in range(2)
    ]
    return jnp.concatenate(halves, 1)


def last_output(r, micro):
    width = r.normed.shape[1]
    r.total[...] = set_back(r, micro * 12 + 8).astype(WIDE) + set_back(r, micro * 12 + 10).astype(WIDE)
    for part in range(4):
        r.total[...] += times(set_back(r, micro * 12 + 2 * part), r.down[part * width : (part + 1) * width, :])
    r.result[micro] = r.total[...].astype(SLIM)


def backward(r, micro, tok):
    length, width = r.normed.shape
    tokens = pl.ds(tok, length)
    r.total[...] = jnp.zeros((length, width), WIDE)
    for part in range(4):
        cols = slice(part * width, (part + 1) * width)
        hidden = times_turned(r.branch[r.quad_rows(micro), :], r.down[cols, :])
        lifted_grad = (hidden * r.grads[part, tokens, :].astype(WIDE)).astype(SLIM)
        r.grads[part, tokens, :] = lifted_grad
        r.total[...] += times_turned(lifted_grad, r.up[:, cols])
    r.share_lifted(micro).start()
    r.between(micro)
    middle_grad = r.branch[r.quad_rows(micro), :].astype(WIDE) + norm_backward(
        r, r.middle[micro], r.total[...], 1
    )
    r.middle[micro] = middle_grad
    r.grads[4, tokens, :] = middle_grad.astype(SLIM)
    r.held[...] = times_turned(r.grads[4, tokens, :], r.outward[...]).astype(SLIM)
    first, second = head_lanes()
    one, two = first.astype(SLIM), second.astype(SLIM)
    scaling = HEAD**-0.5
    for pair in range(width // (2 * HEAD)):
        cols = pl.ds(pair * 2 * HEAD, 2 * HEAD)
        queries = r.grads[5, tokens, cols] * jnp.asarray(scaling, SLIM)
        values = r.grads[7, tokens, cols]
        keys_turned = r.grads[6, tokens, cols].T
        incoming = r.held[:, cols]
        weight_grads = times_turned(jnp.concatenate([values * one, values * two], 0), incoming)
        score_grads, query_grads, weights = [], [], []
        for head in range(2):
            kept = r.weights[micro, 2 * pair + head]
            wide = kept.astype(WIDE)
            own = weight_grads[length * head : length * (head + 1)]
            score_grad = (wide * (own - jnp.sum(wide * own, 0, keepdims=True))).astype(SLIM)
            score_grads.append(score_grad)
            weights.append(kept)
            query_grads.append(
                (times(keys_turned[HEAD * head : HEAD * (head + 1)], score_grad) * scaling).astype(SLIM)
            )
        key_grad = times(jnp.concatenate(score_grads, 0), queries)
        value_grad = times(jnp.concatenate(weights, 0), incoming)
        r.grads[5, tokens, cols] = jnp.concatenate(query_grads, 0).T
        r.grads[6, tokens, cols] = (key_grad[:length] * first + key_grad[length:] * second).astype(SLIM)
        r.grads[7, tokens, cols] = (value_grad[:length] * first + value_grad[length:] * second).astype(SLIM)
    norm_grad = times_turned(r.grads[5, tokens, :], r.inward[:, 0:width])
    for part in range(1, 3):
        norm_grad += times_turned(r.grads[5 + part, tokens, :], r.inward[:, part * width : (part + 1) * width])
    r.total[...] = norm_grad
    input_grad = r.middle[micro] + norm_backward(r, r.stream[micro].astype(WIDE), r.total[...], 0)
    r.middle[micro] = input_grad
    r.stream[micro] = input_grad.astype(SLIM)


NAMES = (
    "x_in", "cot_in", "inward_in", "outward_in", "up_in", "down_in", "gain", "bias", "lengths", "offsets",
    "result", "middle", "staged", "out_norms",
    "stream", "inward", "outward", "up", "down", "grads", "branch", "acts", "acts_out", "quad_acts", "quad_out", "weights", "normed", "held",
    "turned", "total", "sums", "bias_mask",
    "partial", "y_in", "z_in", "far_y_in", "far_z_in", "norms",
    "load_sem", "source_sem",
    "relay_send", "relay_recv", "acts_send", "acts_recv", "branch_send", "branch_recv", "lifted_send", "lifted_recv",
    "across_send", "across_recv", "onward_send", "onward_recv", "quad_send", "quad_recv",
    "rest_send", "rest_recv", "turn",
    "y_send", "y_recv", "z_send", "z_recv", "far_y_send", "far_y_recv", "far_z_send", "far_z_recv", "norm_send", "norm_recv",
)


def step_kernel(*refs):
    r = types.SimpleNamespace(**dict(zip(NAMES, refs)))
    section, dp = lax.axis_index("section"), lax.axis_index("dp")
    c, y, z = lax.rem(dp, 2), lax.rem(lax.div(dp, 2), 2), lax.div(dp, 4)
    r.c, r.y = c, y
    length = r.normed.shape[0]
    leading = section == 0
    pair_dp, y_dp = dp + 1 - 2 * c, dp + 2 - 4 * y
    diagonal_dp = pair_dp + y_dp - dp

    def slot_of(core, micro):
        return pl.ds(pl.multiple_of((core * 2 + micro) * length, length), length)

    def quad_rows(micro, core=c, side=y):
        return pl.ds(pl.multiple_of(((side * 2 + core) * 2 + micro) * length, length), length)

    r.quad_rows = quad_rows

    def remote(src, dst, send, recv, to_section, to_dp):
        return pltpu.make_async_remote_copy(
            src_ref=src, dst_ref=dst, send_sem=send, recv_sem=recv,
            device_id=(to_section, to_dp), device_id_type=MESH,
        )

    def local(src, dst, sem):
        return pltpu.make_async_copy(src, dst, sem)

    r.load_inward = local(r.inward_in.at[0], r.inward, r.load_sem.at[0])
    r.load_outward = local(r.outward_in.at[0], r.outward, r.load_sem.at[1])
    r.load_up = local(r.up_in.at[0], r.up, r.load_sem.at[2])
    r.load_down = local(r.down_in.at[0], r.down, r.load_sem.at[3])

    def load_rest():
        r.load_outward.start()
        r.load_up.start()
        r.load_down.start()

    r.load_rest = load_rest

    def load_x(micro):
        return local(r.x_in.at[micro, 0], r.stream.at[micro], r.source_sem.at[micro])

    def load_cot(micro):
        return local(r.cot_in.at[micro, 0], r.branch.at[quad_rows(micro)], r.source_sem.at[micro])

    def relay_up(micro):
        return remote(r.result.at[micro], r.stream.at[micro], r.relay_send.at[micro], r.relay_recv.at[micro], 1 - section, dp)

    def relay_back(micro):
        return remote(
            r.stream.at[micro], r.branch.at[quad_rows(micro)], r.relay_send.at[micro], r.relay_recv.at[micro], 1 - section, dp
        )

    def share_acts(micro, core=c):
        return remote(
            r.acts_out, r.acts.at[:, :, slot_of(core, micro)], r.acts_send.at[micro], r.acts_recv.at[micro], section, pair_dp
        )

    def branch_copy(rows, send, recv, to_dp):
        return remote(r.branch.at[rows], r.branch.at[rows], send, recv, section, to_dp)

    def share_branch(micro, core=c):
        return branch_copy(quad_rows(micro, core), r.branch_send.at[micro], r.branch_recv.at[micro], pair_dp)

    def branch_across(micro, side=y):
        return branch_copy(quad_rows(micro, c, side), r.across_send.at[micro], r.across_recv.at[micro], y_dp)

    def branch_onward(micro, core=c):
        return branch_copy(quad_rows(micro, core, 1 - y), r.onward_send.at[micro], r.onward_recv.at[micro], pair_dp)

    def share_quad(micro, peer, arriving=False):
        to_dp = (pair_dp, y_dp, diagonal_dp)[peer]
        core = 1 - c if arriving and peer != 1 else c
        side = 1 - y if arriving and peer != 0 else y
        return remote(
            r.quad_out.at[micro, peer], r.quad_acts.at[:, :, quad_rows(micro, core, side)],
            r.quad_send.at[micro, peer], r.quad_recv.at[micro, peer], section, to_dp,
        )

    def share_lifted(micro, core=c):
        rows = slot_of(core, micro)
        return remote(
            r.grads.at[0:4, rows], r.grads.at[0:4, rows], r.lifted_send.at[micro], r.lifted_recv.at[micro], section, pair_dp
        )

    def share_rest(micro, core=c):
        rows = slot_of(core, micro)
        return remote(
            r.grads.at[4:8, rows], r.grads.at[4:8, rows], r.rest_send.at[micro], r.rest_recv.at[micro], section, pair_dp
        )

    r.share_lifted = share_lifted
    r.share_acts = share_acts

    def to_y(unit):
        return remote(
            r.partial.at[unit, 0], r.y_in.at[unit - QUAD], r.y_send.at[unit - QUAD], r.y_recv.at[unit - QUAD], section, y_dp
        )

    def rows_of(place):
        return pl.ds(BLOCK * place, BLOCK)

    def near_z(unit, place, index, lane, to_dp):
        near = unit - FAR
        return remote(
            r.partial.at[unit, 1, rows_of(place)], r.z_in.at[near, index],
            r.z_send.at[near, lane], r.z_recv.at[near, index], section, to_dp,
        )

    def far_z(unit, place, index, lane, to_dp):
        return remote(
            r.partial.at[unit, :, rows_of(place)], r.far_z_in.at[unit, index],
            r.far_z_send.at[unit, lane], r.far_z_recv.at[unit, index], section, to_dp,
        )

    def far_to_y(unit, place):
        return remote(
            r.partial.at[unit, 0, rows_of(place)], r.far_y_in.at[unit], r.far_y_send.at[unit], r.far_y_recv.at[unit], section, y_dp
        )

    r.load_inward.start()

    @pl.when(leading)
    def _():
        load_x(0).start()
        load_x(1).start()

    @pl.when(jnp.logical_not(leading))
    def _():
        load_cot(0).start()
        load_cot(1).start()

    @pl.when(jnp.logical_not(leading))
    def _():
        r.load_rest()

    r.sums[...] = jnp.zeros_like(r.sums)

    barrier = pltpu.get_barrier_semaphore()
    peers = [(1 - section, dp), (section, pair_dp), (section, y_dp)]
    peers += [(section, diagonal_dp)]
    peers += [(section, lax.rem(dp + 4 * hop, 16)) for hop in (1, 2, 3)]
    for peer in peers:
        pl.semaphore_signal(barrier, inc=1, device_id=peer, device_id_type=MESH)

    def everyone_in():
        pl.semaphore_wait(barrier, len(peers))

    def arrive(micro):
        relay_back(micro).wait_recv()
        branch_across(micro).start()
        share_branch(micro).start()

    def columns_of(unit):
        return pl.ds(pl.multiple_of(lax.rem(unit, 2) * COLUMNS, 128), COLUMNS)

    def side_rows(side):
        return pl.ds(pl.multiple_of(side * 192, 64), 192)

    def near_unit(unit):
        whole = lax.div(unit, 2)
        slab = 1 + jnp.where(whole >= 8, 1, 0) + jnp.where(whole >= 9, 1, 0)
        grads = r.grads[whole - 4, :, columns_of(unit)]
        r.partial[unit, 0] = times(r.acts[slab, side_rows(1 - y), :], grads).astype(SLIM)
        to_y(unit).start()
        r.partial[unit, 1] = times(r.acts[slab, side_rows(y), :], grads).astype(SLIM)

    def far_unit(unit):
        grads = r.branch[pl.ds(pl.multiple_of(y * 4 * length, length), 4 * length), columns_of(unit)]
        r.partial[unit, 0] = times(r.acts[0, side_rows(1 - y), :], grads).astype(SLIM)
        r.partial[unit, 1] = times(r.acts[0, side_rows(y), :], grads).astype(SLIM)
        at_ends(unit, far_z, r.far_z_in)

    def quad_unit(unit):
        grads = r.branch[:, columns_of(unit)]
        r.partial[unit, 1] = times(r.quad_acts[lax.div(unit, 2) - 1], grads).astype(SLIM)
        at_ends(unit, near_z, r.z_in)

    def arrived(unit, index, copy, into):
        copy(unit, 0, index, 0, dp).wait_recv()
        return into[unit if into is r.far_z_in else unit - FAR, index].astype(WIDE)

    def pick(unit, place, copy):
        return (unit, slice(None) if copy is far_z else 1, rows_of(place))

    def go_right(unit, here, copy, into):
        for place in range(3, here, -1):
            at = pick(unit, place, copy)
            if here > 0:
                r.partial[at] = (r.partial[at].astype(WIDE) + arrived(unit, place + 1, copy, into)).astype(SLIM)
            copy(unit, place, place + 1, place - 1, dp + 4).start()

    def go_left(unit, here, copy, into):
        for place in range(here):
            at = pick(unit, place, copy)
            if here < 3:
                r.partial[at] = (r.partial[at].astype(WIDE) + arrived(unit, place, copy, into)).astype(SLIM)
            copy(unit, place, place, place, dp - 4).start()

    def at_ends(unit, copy, into):
        @pl.when(z == 0)
        def _():
            go_right(unit, 0, copy, into)

        @pl.when(z == 3)
        def _():
            go_left(unit, 3, copy, into)

    def at_middle_first(unit, copy, into):
        @pl.when(z == 1)
        def _():
            go_right(unit, 1, copy, into)

        @pl.when(z == 2)
        def _():
            go_left(unit, 2, copy, into)

    def at_middle_second(unit, copy, into):
        @pl.when(z == 1)
        def _():
            go_left(unit, 1, copy, into)

        @pl.when(z == 2)
        def _():
            go_right(unit, 2, copy, into)

    def gathered(unit, here, copy, into):
        value = r.partial[pick(unit, here, copy)].astype(WIDE)
        if here > 0:
            value = value + arrived(unit, here + 1, copy, into)
        if here < 3:
            value = value + arrived(unit, here, copy, into)
        return value

    def everywhere(action):
        for here in range(4):

            @pl.when(z == here)
            def _():
                action(here)

    def far_units():
        for micro in range(2):
            share_branch(micro, 1 - c).wait_recv()
            share_acts(micro, 1 - c).wait_recv()

        def body(unit, carry):
            far_unit(unit)
            return carry

        lax.fori_loop(0, FAR, body, 0)
        branch_across(0, 1 - y).wait_recv()
        branch_onward(0).start()

    r.between = lambda micro: pl.when(leading & (micro == 1))(far_units)

    def slot(t, carry):
        trailing = jnp.logical_not(leading)
        half = lax.div(t, 2)
        is_forward = (leading & (t < 2)) | (trailing & ((t == 1) | (t == 3)))
        is_backward = (leading & ((t == 3) | (t == 5))) | (trailing & ((t == 2) | (t == 4)))

        @pl.when(trailing & (t == 0))
        def _():
            everyone_in()
            for micro in range(2):
                load_cot(micro).wait()
                branch_across(micro).start()
                share_branch(micro).start()

        @pl.when(is_forward)
        def _():
            micro = jnp.where(leading, jnp.minimum(t, 1), jnp.minimum(half, 1))

            mask_bias(r, micro)

            @pl.when(leading)
            def _():
                load_x(micro).wait()

            @pl.when(trailing)
            def _():
                relay_up(micro).wait_recv()

            forward(r, micro, pl.multiple_of((c * 2 + micro) * length, length), t == section, leading)

            @pl.when(leading & (t == 0))
            def _():
                everyone_in()

            ahead = leading & (c == 0) & (t == 0)

            @pl.when(ahead)
            def _():
                relay_up(0).start()
                relay_up(0).wait_send()
                pl.semaphore_signal(r.turn, inc=1, device_id=(section, pair_dp), device_id_type=MESH)

            @pl.when(leading & (t == 1))
            def _():
                relay_up(1).start()

            share_acts(micro).start()

            @pl.when(leading & (c == 1) & (t == 0))
            def _():
                pl.semaphore_wait(r.turn, 1)
                relay_up(0).start()

            for peer in range(3):
                share_quad(micro, peer).start()

        @pl.when(leading & (t == 3))
        def _():
            arrive(0)

        @pl.when(is_backward)
        def _():
            micro = jnp.clip(half - 1, 0, 1)
            backward(r, micro, pl.multiple_of((c * 2 + micro) * length, length))

            @pl.when(trailing)
            def _():
                relay_back(micro).start()

            share_rest(micro).start()

            @pl.when(trailing & (t == 4))
            def _():
                def body(done, carry):
                    last_output(r, done)
                    return carry

                lax.fori_loop(0, 2, body, 0)

        @pl.when(leading & (t == 4))
        def _():
            arrive(1)

        pl.when(trailing & (t == 5))(far_units)
        return carry

    lax.fori_loop(0, 6, slot, 0)

    def norm_copy(src, dst, index, to_dp):
        return remote(r.norms.at[src], r.norms.at[dst], r.norm_send.at[index], r.norm_recv.at[index], section, to_dp)

    def norm_to_pair():
        return norm_copy(0, 1, 0, pair_dp)

    def norm_to_y():
        return norm_copy(2, 3, 1, y_dp)

    def norm_to_z(hop):
        return norm_copy(4, 4 + hop, 1 + hop, lax.rem(dp + 4 * hop, 16))

    r.norms[0] = jnp.concatenate([jnp.sum(r.sums[...], 1), jnp.zeros((4, r.sums.shape[2]), WIDE)], 0)
    norm_to_pair().start()
    for micro in range(2):
        share_lifted(micro, 1 - c).wait_recv()

    def early_near(ahead, carry):
        near_unit(QUAD + ahead)
        return carry

    lax.fori_loop(0, EARLY_NEAR, early_near, 0)
    branch_across(1, 1 - y).wait_recv()
    branch_onward(1).start()
    for micro in range(2):
        branch_onward(micro, 1 - c).wait_recv()
        for peer in range(3):
            share_quad(micro, peer, True).wait_recv()

    def early_quad(unit, carry):
        quad_unit(unit)
        return carry

    lax.fori_loop(FAR, FAR + sum(step < 0 for step in QUAD_AT), early_quad, 0)

    def sum_y(unit):
        to_y(unit).wait_recv()
        r.partial[unit, 1] = (r.partial[unit, 1].astype(WIDE) + r.y_in[unit - QUAD].astype(WIDE)).astype(SLIM)

    def turn_of(i, steps, base):
        turn, unit = i < 0, jnp.int32(base)
        for index, step in enumerate(steps):
            if step >= 0:
                turn = turn | (i == step)
                unit = jnp.where(i == step, base + index, unit)
        return turn, unit

    def near_turn(i, lag):
        return (i >= lag) & (i < NEAR + lag), jnp.clip(i - lag, 0, NEAR - 1) + QUAD

    def end_of_line(unit):
        def action(here):
            r.staged[unit] = gathered(unit, here, near_z, r.z_in)

        everywhere(action)

    def advance(i, carry):
        issued = QUAD + EARLY_NEAR + i - HOLD

        @pl.when(issued == 16)
        def _():
            for micro in range(2):
                share_rest(micro, 1 - c).wait_recv()

        @pl.when((issued >= QUAD + EARLY_NEAR) & (issued < UNITS))
        def _():
            near_unit(issued)

        @pl.when(i < NEAR)
        def _():
            sum_y(QUAD + i)
            at_ends(QUAD + i, near_z, r.z_in)

        turn, unit = turn_of(i, QUAD_AT, FAR)

        @pl.when(turn)
        def _(unit=unit):
            quad_unit(unit)

        turn, unit = near_turn(i, LAGS[0])

        @pl.when(turn)
        def _(unit=unit):
            at_middle_first(unit, near_z, r.z_in)

        turn, unit = turn_of(i, FAR_FIRST, 0)

        @pl.when(turn)
        def _(unit=unit):
            at_middle_first(unit, far_z, r.far_z_in)

        turn, unit = turn_of(i, QUAD_FIRST, FAR)

        @pl.when(turn)
        def _(unit=unit):
            at_middle_first(unit, near_z, r.z_in)

        turn, unit = turn_of(i, FAR_SECOND, 0)

        @pl.when(turn)
        def _(unit=unit):
            at_middle_second(unit, far_z, r.far_z_in)

        turn, unit = turn_of(i, QUAD_SECOND, FAR)

        @pl.when(turn)
        def _(unit=unit):
            at_middle_second(unit, near_z, r.z_in)

        turn, unit = near_turn(i, LAGS[1])

        @pl.when(turn)
        def _(unit=unit):
            at_middle_second(unit, near_z, r.z_in)

        turn, unit = turn_of(i, QUAD_DONE, FAR)

        @pl.when(turn)
        def _(unit=unit):
            end_of_line(unit)

        turn, unit = near_turn(i, LAGS[2])

        @pl.when(turn)
        def _(unit=unit):
            end_of_line(unit)

        turn, unit = turn_of(i, FAR_ARRIVED, 0)

        @pl.when(turn)
        def _(unit=unit):
            def action(here):
                value = gathered(unit, here, far_z, r.far_z_in)
                r.partial[unit, 0, rows_of(here)] = value[0].astype(SLIM)
                far_to_y(unit, here).start()
                r.staged[unit] = value[1]

            everywhere(action)

        turn, unit = turn_of(i, FAR_DONE, 0)

        @pl.when(turn)
        def _(unit=unit):
            far_to_y(unit, 0).wait_recv()
            r.staged[unit] += r.far_y_in[unit].astype(WIDE)

        @pl.when(i == 1)
        def _():
            norm_to_pair().wait()
            r.norms[2] = r.norms[0] + r.norms[1]
            norm_to_y().start()

        @pl.when(i == 9)
        def _():
            norm_to_y().wait_recv()
            r.norms[4] = r.norms[2] + r.norms[3]
            for hop in (1, 2, 3):
                norm_to_z(hop).start()

        @pl.when(i == 15)
        def _():
            for hop in (1, 2, 3):
                norm_to_z(hop).wait_recv()
            r.out_norms[...] = (r.norms[4] + r.norms[5]) + (r.norms[6] + r.norms[7])

        return carry

    lax.fori_loop(0, NEAR + LAGS[2], advance, 0)

    norm_to_y().wait_send()
    for hop in (1, 2, 3):
        norm_to_z(hop).wait_send()
    share_acts(1).wait_send()
    for micro in range(2):
        share_branch(micro).wait_send()
        branch_across(micro).wait_send()
        branch_onward(micro).wait_send()
        for peer in range(3):
            share_quad(micro, peer).wait_send()
        share_lifted(micro).wait_send()
        share_rest(micro).wait_send()

        @pl.when(leading if micro else leading & (c == 1))
        def _():
            relay_up(micro).wait_send()

        @pl.when(jnp.logical_not(leading))
        def _():
            relay_back(micro).wait_send()

    def drain_y(near, carry):
        to_y(QUAD + near).wait_send()
        return carry

    lax.fori_loop(0, NEAR, drain_y, 0)

    def drain_z(unit, carry):
        for lane in range(3):
            near_z(unit, 0, 0, lane, dp).wait_send()
        return carry

    lax.fori_loop(FAR, UNITS, drain_z, 0)

    def drain_far(unit, carry):
        far_to_y(unit, 0).wait_send()
        for lane in range(3):
            far_z(unit, 0, 0, lane, dp).wait_send()
        return carry

    lax.fori_loop(0, FAR, drain_far, 0)


def hand_over_kernel(result, grad, staged, norms, *refs):
    out_result, out_grad, out_inward, out_outward, out_up, out_down, gain_grad, bias_grad, sem = refs
    width = result.shape[2]

    def start(source, target):
        copy = pltpu.make_async_copy(source, target, sem)
        copy.start()
        return copy

    copies = [start(result, out_result.at[0, :, 0]), start(grad, out_grad.at[0, :, 0])]
    for piece in range(UNITS):
        half = pl.ds(piece % 2 * COLUMNS, COLUMNS)
        if piece < 8:
            target = out_down.at[0, pl.ds(piece // 2 * BLOCK, BLOCK), half]
        elif piece < 16:
            target = out_up.at[0, :, pl.ds((piece - 8) * COLUMNS, COLUMNS)]
        elif piece < 18:
            target = out_outward.at[0, :, half]
        else:
            target = out_inward.at[0, :, pl.ds((piece - 18) * COLUMNS, COLUMNS)]
        copies.append(start(staged.at[piece], target))
    share = gain_grad.shape[2]
    for index in range(width // share):

        @pl.when(lax.axis_index("dp") == index)
        def _():
            gain_grad[0] = norms[0:2, index * share : (index + 1) * share]
            bias_grad[0] = norms[2:4, index * share : (index + 1) * share]

    for copy in copies:
        copy.wait()


def step_on_device(
    inputs, clip_lengths, anchor_offsets, cotangent, inward_weight, outward_weight, up_weight, down_weight, norm_gain, norm_bias
):
    _, _, length, width = inputs.shape
    wide_ff = up_weight.shape[2]
    anywhere = pl.BlockSpec(memory_space=pl.ANY)
    in_vmem = pl.BlockSpec(memory_space=pltpu.VMEM)
    in_smem = pl.BlockSpec(memory_space=pltpu.SMEM)
    dma = pltpu.SemaphoreType.DMA
    share = width // lax.axis_size("dp")
    made = pl.pallas_call(
        step_kernel,
        out_shape=(
            pltpu.VMEM((2, length, width), SLIM),
            pltpu.VMEM((2, length, width), WIDE),
            pltpu.VMEM((UNITS, BLOCK, COLUMNS), WIDE),
            pltpu.VMEM((8, width), WIDE),
        ),
        in_specs=[anywhere] * 6 + [in_vmem] * 2 + [in_smem] * 2,
        out_specs=[in_vmem] * 4,
        scratch_shapes=[
            pltpu.VMEM((2, length, width), SLIM),
            pltpu.VMEM((width, 3 * width), SLIM),
            pltpu.VMEM((width, width), SLIM),
            pltpu.VMEM((width, wide_ff), SLIM),
            pltpu.VMEM((wide_ff, width), SLIM),
            pltpu.VMEM((8, 4 * length, width), SLIM),
            pltpu.VMEM((8 * length, width), SLIM),
            pltpu.VMEM((4, 8 * BLOCK, 4 * length), SLIM),
            pltpu.VMEM((4, 8 * BLOCK, length), SLIM),
            pltpu.VMEM((3, 4 * BLOCK, 8 * length), SLIM),
            pltpu.VMEM((2, 3, 3, 4 * BLOCK, length), SLIM),
            pltpu.VMEM((2, width // HEAD, length, length), SLIM),
            pltpu.VMEM((length, width), SLIM),
            pltpu.VMEM((length, width), SLIM),
            pltpu.VMEM((width, length), SLIM),
            pltpu.VMEM((length, width), WIDE),
            pltpu.VMEM((4, 8, width), WIDE),
            pltpu.VMEM((length, length), WIDE),
            pltpu.VMEM((UNITS, 2, 4 * BLOCK, COLUMNS), SLIM),
            pltpu.VMEM((NEAR, 4 * BLOCK, COLUMNS), SLIM),
            pltpu.VMEM((UNITS - FAR, 5, BLOCK, COLUMNS), SLIM),
            pltpu.VMEM((FAR, BLOCK, COLUMNS), SLIM),
            pltpu.VMEM((FAR, 5, 2, BLOCK, COLUMNS), SLIM),
            pltpu.VMEM((8, 8, width), WIDE),
            dma((4,)), dma((2,)),
            *[dma((2,))] * 8, *[dma((2,))] * 4, dma((2, 3)), dma((2, 3)), *[dma((2,))] * 2, pltpu.SemaphoreType.REGULAR,
            dma((NEAR,)), dma((NEAR,)), dma((UNITS - FAR, 3)), dma((UNITS - FAR, 5)),
            dma((FAR,)), dma((FAR,)), dma((FAR, 3)), dma((FAR, 5)), dma((5,)), dma((5,)),
        ],
        compiler_params=pltpu.CompilerParams(
            collective_id=0, has_side_effects=True, vmem_limit_bytes=VMEM_BYTES - 4500000
        ),
    )(
        inputs, cotangent, inward_weight, outward_weight, up_weight, down_weight,
        norm_gain, norm_bias, clip_lengths, anchor_offsets,
    )
    sections = 1
    return pl.pallas_call(
        hand_over_kernel,
        out_shape=(
            jax.ShapeDtypeStruct((sections, 2, 1, length, width), SLIM),
            jax.ShapeDtypeStruct((sections, 2, 1, length, width), WIDE),
            jax.ShapeDtypeStruct((sections, BLOCK, 3 * width), WIDE),
            jax.ShapeDtypeStruct((sections, BLOCK, width), WIDE),
            jax.ShapeDtypeStruct((sections, BLOCK, wide_ff), WIDE),
            jax.ShapeDtypeStruct((sections, 4 * BLOCK, width), WIDE),
            jax.ShapeDtypeStruct((sections, 2, share), WIDE),
            jax.ShapeDtypeStruct((sections, 2, share), WIDE),
        ),
        in_specs=[in_vmem] * 4,
        out_specs=[anywhere] * 6 + [in_vmem] * 2,
        scratch_shapes=[dma],
        compiler_params=pltpu.CompilerParams(vmem_limit_bytes=1 << 20),
    )(*[pltpu.with_memory_space_constraint(one, pltpu.VMEM) for one in made])


def shifted(x, axis, by):
    size = lax.axis_size(axis)
    pairs = [(i, i + by) for i in range(size) if 0 <= i + by < size]
    return lax.ppermute(x, axis, pairs)


def norm_rows(values, norm_gain, norm_bias):
    average = jnp.mean(values, -1, keepdims=True)
    centred = values - average
    inverse = lax.rsqrt(jnp.mean(centred * centred, -1, keepdims=True) + EPSILON)
    normed = centred * inverse
    return (normed * norm_gain + norm_bias, normed, inverse)


def norm_back(norm_grad, normed, inverse, norm_gain):
    inner = norm_grad * norm_gain
    through = inverse * (
        inner
        - jnp.mean(inner, -1, keepdims=True)
        - normed * jnp.mean(inner * normed, -1, keepdims=True)
    )
    return (through, jnp.sum(norm_grad * normed, 0), jnp.sum(norm_grad, 0))


def gelu_slope(lifted):
    cumulative = 0.5 * (1.0 + lax.erf(lifted * 0.7071067811865476))
    density = jnp.exp(-0.5 * lifted * lifted) * 0.3989422804014327
    return cumulative + lifted * density


def clip_marks(lengths, offsets, length):
    positions = jnp.arange(length, dtype=jnp.int32)
    clip_ends = jnp.cumsum(lengths)
    clip_starts = clip_ends - lengths
    anchor_at = clip_starts + offsets % lengths
    clip_ids = jnp.sum((positions[:, None] >= clip_ends[None, :]).astype(jnp.int32), 1)
    anchors = jnp.any(positions[:, None] == anchor_at[None, :], 1)
    return (clip_ids, anchors)


def masked_scores(query_block, key_rows, id_block, clip_ids, anchors, scaling):
    scores = (
        jnp.einsum("qhd,khd->hqk", query_block, key_rows, preferred_element_type=jnp.float32)
        * scaling
    )
    seen = (id_block[:, None] == clip_ids[None, :]) | anchors[None, :]
    return jnp.where(seen[None], scores, -1000000000.0)


def forward_layer(source, clip_ids, anchors, params):
    inward, outward, upward, downward, norm_gain, norm_bias = params
    length, model_width = source.shape
    head_count = model_width // HEAD
    scaling = HEAD ** (-0.5)
    residual = source.astype(jnp.float32)
    first_norm, unit_one, scale_one = norm_rows(residual, norm_gain[0], norm_bias[0])
    joined = jnp.dot(
        first_norm.astype(jnp.bfloat16), inward, preferred_element_type=jnp.float32
    ).astype(jnp.bfloat16)
    heads_view = joined.reshape(length, 3, head_count, HEAD)
    queries = heads_view[:, 0]
    key_rows = heads_view[:, 1]
    values = heads_view[:, 2]
    scores = masked_scores(queries, key_rows, clip_ids, clip_ids, anchors, scaling)
    row_max = jnp.max(scores, -1, keepdims=True)
    raised = jnp.exp(scores - row_max)
    row_sum = jnp.sum(raised, -1, keepdims=True)
    weights = (raised / row_sum).astype(jnp.bfloat16)
    pieces = [jnp.einsum("hqk,khd->qhd", weights, values, preferred_element_type=jnp.float32)]
    log_sums = [(row_max + jnp.log(row_sum))[..., 0]]
    attended = jnp.concatenate(pieces, 0).reshape(length, model_width).astype(jnp.bfloat16)
    logsum = jnp.concatenate(log_sums, 1)
    middle = residual + jnp.dot(attended, outward, preferred_element_type=jnp.float32)
    second_norm, unit_two, scale_two = norm_rows(middle, norm_gain[1], norm_bias[1])
    lifted = jnp.dot(second_norm.astype(jnp.bfloat16), upward, preferred_element_type=jnp.float32)
    active = jax.nn.gelu(lifted, approximate=False).astype(jnp.bfloat16)
    result = middle + jnp.dot(active, downward, preferred_element_type=jnp.float32)
    stored = (unit_one, scale_one, joined, logsum, attended, unit_two, scale_two, lifted, active)
    return (result, stored)


def contract_rows(left, right):
    return lax.dot_general(
        left, right, (((0,), (0,)), ((), ())), preferred_element_type=jnp.float32
    )


def contract_cols(left, right):
    return lax.dot_general(
        left, right, (((1,), (1,)), ((), ())), preferred_element_type=jnp.float32
    )


def feed_backward(incoming, stored, params):
    inward, outward, upward, downward, norm_gain, norm_bias = params
    unit_one, scale_one, joined, logsum, attended, unit_two, scale_two, lifted, active = stored
    branch = incoming.astype(jnp.bfloat16)
    down_part = contract_rows(active, branch)
    hidden_grad = contract_cols(branch, downward)
    lifted_grad = (hidden_grad * gelu_slope(lifted)).astype(jnp.bfloat16)
    second_in = (unit_two * norm_gain[1] + norm_bias[1]).astype(jnp.bfloat16)
    up_part = contract_rows(second_in, lifted_grad)
    normed_grad = contract_cols(lifted_grad, upward)
    through, gain_two, bias_two = norm_back(normed_grad, unit_two, scale_two, norm_gain[1])
    return (incoming + through, (up_part, down_part, gain_two, bias_two))


def attend_backward(middle_grad, stored, clip_ids, anchors, params):
    inward, outward, upward, downward, norm_gain, norm_bias = params
    unit_one, scale_one, joined, logsum, attended, unit_two, scale_two, lifted, active = stored
    length, model_width = attended.shape
    head_count = model_width // HEAD
    scaling = HEAD ** (-0.5)
    branch = middle_grad.astype(jnp.bfloat16)
    outward_part = contract_rows(attended, branch)
    attended_grad = (
        contract_cols(branch, outward).astype(jnp.bfloat16).reshape(length, head_count, HEAD)
    )
    heads_view = joined.reshape(length, 3, head_count, HEAD)
    queries = heads_view[:, 0]
    key_rows = heads_view[:, 1]
    values = heads_view[:, 2]
    key_grad = jnp.zeros((length, head_count, HEAD), jnp.float32)
    value_grad = jnp.zeros((length, head_count, HEAD), jnp.float32)
    block_rows = min(512, length)
    scores = masked_scores(queries, key_rows, clip_ids, clip_ids, anchors, scaling)
    weights = jnp.exp(scores - logsum[:, 0:block_rows, None])
    weight_grad = jnp.einsum(
        "qhd,khd->hqk", attended_grad, values, preferred_element_type=jnp.float32
    )
    score_grad = (
        weights * (weight_grad - jnp.sum(weights * weight_grad, -1, keepdims=True))
    ).astype(jnp.bfloat16)
    query_pieces = [
        scaling
        * jnp.einsum("hqk,khd->qhd", score_grad, key_rows, preferred_element_type=jnp.float32)
    ]
    key_grad = key_grad + scaling * jnp.einsum(
        "hqk,qhd->khd", score_grad, queries, preferred_element_type=jnp.float32
    )
    value_grad = value_grad + jnp.einsum(
        "hqk,qhd->khd",
        weights.astype(jnp.bfloat16),
        attended_grad,
        preferred_element_type=jnp.float32,
    )
    query_grad = jnp.concatenate(query_pieces, 0)
    joined_grad = (
        jnp.stack([query_grad, key_grad, value_grad], 1)
        .reshape(length, 3 * model_width)
        .astype(jnp.bfloat16)
    )
    first_in = (unit_one * norm_gain[0] + norm_bias[0]).astype(jnp.bfloat16)
    inward_part = contract_rows(first_in, joined_grad)
    normed_grad = contract_cols(joined_grad, inward)
    through, gain_one, bias_one = norm_back(normed_grad, unit_one, scale_one, norm_gain[0])
    return (middle_grad + through, (inward_part, outward_part, gain_one, bias_one))


def resting(function):

    def blank(*operands):
        return jax.tree.map(jnp.zeros_like, function(*operands))

    return blank


def take_slot(holder, buffer_slot):
    return jax.tree.map(
        lambda element: lax.dynamic_index_in_dim(element, buffer_slot, 0, False), holder
    )


def place_slot(holder, item, buffer_slot, working):

    def update(element, fresh):
        former = lax.dynamic_index_in_dim(element, buffer_slot, 0, False)
        return lax.dynamic_update_index_in_dim(
            element, jnp.where(working, fresh, former), buffer_slot, 0
        )

    return jax.tree.map(update, holder, item)


def per_device(
    inputs,
    clip_lengths,
    anchor_offsets,
    cotangent,
    inward_weight,
    outward_weight,
    up_weight,
    down_weight,
    norm_gain,
    norm_bias,
):
    params = (
        inward_weight[0],
        outward_weight[0],
        up_weight[0],
        down_weight[0],
        norm_gain[0],
        norm_bias[0],
    )
    stream = inputs[:, 0]
    cot_rows = cotangent[:, 0]
    lengths_all = clip_lengths[:, 0]
    offsets_all = anchor_offsets[:, 0]
    micro_count = stream.shape[0]
    length = stream.shape[1]
    section_index = lax.axis_index("section")
    section_count = lax.axis_size("section")
    leading = section_index == 0
    trailing = section_index == section_count - 1
    periods = micro_count + section_count - 1
    arriving = jnp.zeros_like(stream[0])
    produced = jnp.zeros_like(stream)
    archive = None
    for period in range(periods):
        micro_index = period - section_index
        working = (micro_index >= 0) & (micro_index < micro_count)
        buffer_slot = jnp.clip(micro_index, 0, micro_count - 1)
        source = jnp.where(leading, stream[min(period, micro_count - 1)], arriving)
        clip_ids, anchors = clip_marks(
            take_slot(lengths_all, buffer_slot), take_slot(offsets_all, buffer_slot), length
        )
        result, stored = lax.cond(
            working, forward_layer, resting(forward_layer), source, clip_ids, anchors, params
        )
        if archive is None:
            archive = jax.tree.map(
                lambda element: jnp.zeros((micro_count,) + element.shape, element.dtype), stored
            )
        archive = place_slot(archive, stored, buffer_slot, working)
        sending = result.astype(jnp.bfloat16)
        produced = place_slot(produced, sending, buffer_slot, working)
        if period < micro_count:
            arriving = shifted(sending, "section", 1)
    inward, outward, upward, downward, gains, biases = params
    up_sum = jnp.zeros(upward.shape, jnp.float32)
    down_sum = jnp.zeros(downward.shape, jnp.float32)
    gain_two = jnp.zeros(gains.shape[1:], jnp.float32)
    bias_two = jnp.zeros(biases.shape[1:], jnp.float32)
    inward_sum = jnp.zeros(inward.shape, jnp.float32)
    outward_sum = jnp.zeros(outward.shape, jnp.float32)
    gain_one = jnp.zeros(gains.shape[1:], jnp.float32)
    bias_one = jnp.zeros(biases.shape[1:], jnp.float32)
    upstream = jnp.zeros_like(stream[0])
    returned = jnp.zeros(stream.shape, jnp.float32)
    for period in range(periods):
        micro_index = micro_count - 1 - period + (section_count - 1 - section_index)
        working = (micro_index >= 0) & (micro_index < micro_count)
        buffer_slot = jnp.clip(micro_index, 0, micro_count - 1)
        incoming = jnp.where(trailing, take_slot(cot_rows, buffer_slot), upstream).astype(
            jnp.float32
        )
        clip_ids, anchors = clip_marks(
            take_slot(lengths_all, buffer_slot), take_slot(offsets_all, buffer_slot), length
        )
        stored = take_slot(archive, buffer_slot)
        middle_grad, feed_part = lax.cond(
            working, feed_backward, resting(feed_backward), incoming, stored, params
        )
        up_sum = up_sum + feed_part[0]
        down_sum = down_sum + feed_part[1]
        gain_two = gain_two + feed_part[2]
        bias_two = bias_two + feed_part[3]
        input_grad, attend_part = lax.cond(
            working,
            attend_backward,
            resting(attend_backward),
            middle_grad,
            stored,
            clip_ids,
            anchors,
            params,
        )
        inward_sum = inward_sum + attend_part[0]
        outward_sum = outward_sum + attend_part[1]
        gain_one = gain_one + attend_part[2]
        bias_one = bias_one + attend_part[3]
        returned = place_slot(returned, input_grad, buffer_slot, working)
        if period < periods - 1:
            upstream = shifted(input_grad.astype(jnp.bfloat16), "section", -1)
    inward_sum, outward_sum, up_sum, down_sum, gain_one, gain_two, bias_one, bias_two = (
        lax.psum_scatter(inward_sum, "dp", scatter_dimension=0, tiled=True),
        lax.psum_scatter(outward_sum, "dp", scatter_dimension=0, tiled=True),
        lax.psum_scatter(up_sum, "dp", scatter_dimension=0, tiled=True),
        lax.psum_scatter(down_sum, "dp", scatter_dimension=0, tiled=True),
        lax.psum_scatter(gain_one, "dp", scatter_dimension=0, tiled=True),
        lax.psum_scatter(gain_two, "dp", scatter_dimension=0, tiled=True),
        lax.psum_scatter(bias_one, "dp", scatter_dimension=0, tiled=True),
        lax.psum_scatter(bias_two, "dp", scatter_dimension=0, tiled=True),
    )
    layer_outputs = produced[None, :, None]
    input_grads = returned[None, :, None]
    gain_grad = jnp.stack([gain_one, gain_two])[None]
    bias_grad = jnp.stack([bias_one, bias_two])[None]
    return (
        layer_outputs,
        input_grads,
        inward_sum[None],
        outward_sum[None],
        up_sum[None],
        down_sum[None],
        gain_grad,
        bias_grad,
    )


def solution(mesh):
    local = step_on_device if mesh.shape["dp"] == 16 and mesh.shape["section"] == 2 else per_device
    return jax.shard_map(
        local,
        mesh=mesh,
        in_specs=(
            P(None, "dp", None, None),
            P(None, "dp", None),
            P(None, "dp", None),
            P(None, "dp", None, None),
            P("section", None, None),
            P("section", None, None),
            P("section", None, None),
            P("section", None, None),
            P("section", None, None),
            P("section", None, None),
        ),
        out_specs=(
            P("section", None, "dp", None, None),
            P("section", None, "dp", None, None),
            P("section", "dp", None),
            P("section", "dp", None),
            P("section", "dp", None),
            P("section", "dp", None),
            P("section", None, "dp"),
            P("section", None, "dp"),
        ),
        check_vma=False,
    )
```

```python
import functools
import types

import jax
import jax.numpy as jnp
from jax import lax
from jax.experimental import pallas as pl
from jax.experimental.pallas import tpu as pltpu
from jax.sharding import PartitionSpec as P

HEAD = 64
EPSILON = 1e-06
MESH = pl.DeviceIdType.MESH
WIDE = jnp.float32
SLIM = jnp.bfloat16
VMEM_BYTES = 67043328

UNITS = 24
FAR = 2
QUAD = 8
NEAR = UNITS - QUAD
BLOCK = 48
COLUMNS = 384
EARLY_NEAR = 3
HOLD = 1
LAGS = (2, 4, 6)
FAR_FIRST = (0, 5)
FAR_SECOND = (2, 9)
FAR_ARRIVED = (3, 18)
FAR_DONE = (7, 21)
QUAD_AT = (-1, -1, 2, 4, 6, 12)
QUAD_FIRST = (3, 2, 6, 7, 9, 13)
QUAD_SECOND = (5, 7, 15, 13, 11, 16)
QUAD_DONE = (18, 13, 19, 21, 12, 20)


def times(left, right):
    return jnp.dot(left, right, preferred_element_type=WIDE)


def times_turned(left, right):
    return lax.dot_general(left, right, (((1,), (1,)), ((), ())), preferred_element_type=WIDE)


def unit_rows(values):
    centred = values - jnp.mean(values, -1, keepdims=True)
    inverse = lax.rsqrt(jnp.mean(centred * centred, -1, keepdims=True) + EPSILON)
    return centred * inverse, inverse


def norm_rows_bf16(r, values, which):
    unit, _ = unit_rows(values)
    return (unit * r.gain[0, which : which + 1, :] + r.bias[0, which : which + 1, :]).astype(SLIM)


def norm_backward(r, values, norm_grad, which):
    unit, inverse = unit_rows(values)
    width = values.shape[1]
    r.sums[which] += jnp.sum((norm_grad * unit).reshape(-1, 8, width), 0)
    r.sums[2 + which] += jnp.sum(norm_grad.reshape(-1, 8, width), 0)
    inner = norm_grad * r.gain[0, which : which + 1, :]
    return inverse * (
        inner
        - jnp.mean(inner, -1, keepdims=True)
        - unit * jnp.mean(inner * unit, -1, keepdims=True)
    )


def head_lanes():
    lane = lax.broadcasted_iota(jnp.int32, (1, 2 * HEAD), 1)
    first = jnp.where(lane < HEAD, 1.0, 0.0).astype(WIDE)
    return first, 1.0 - first


def mask_bias(r, micro):
    length = r.bias_mask.shape[0]

    def marks(positions):
        end = jnp.int32(0)
        ids = jnp.zeros(positions.shape, jnp.int32)
        anchors = jnp.zeros(positions.shape, jnp.int32)
        for clip in range(r.lengths.shape[2]):
            size = r.lengths[micro, 0, clip]
            anchor = end + lax.rem(r.offsets[micro, 0, clip], size)
            end = end + size
            ids = ids + jnp.where(positions >= end, 1, 0)
            anchors = anchors + jnp.where(positions == anchor, 1, 0)
        return ids, anchors

    key_ids, anchors = marks(lax.broadcasted_iota(jnp.int32, (length, 1), 0))
    query_ids, _ = marks(lax.broadcasted_iota(jnp.int32, (1, length), 1))
    seen = (key_ids == query_ids) | (jnp.broadcast_to(anchors, (length, length)) > 0)
    r.bias_mask[...] = jnp.where(seen, 0.0, -1000000000.0).astype(WIDE)


def place(r, slab, tokens):
    for line in range(8):
        z, y = line // 2, line % 2
        rows = pl.ds(y * 192 + z * BLOCK, BLOCK)
        own = pl.ds(pl.multiple_of(2 * BLOCK * line + r.c * BLOCK, 16), BLOCK)
        other = pl.ds(pl.multiple_of(2 * BLOCK * line + (1 - r.c) * BLOCK, 16), BLOCK)
        r.acts[slab, rows, tokens] = r.turned[own, :]
        r.acts_out[slab, rows, :] = r.turned[other, :]


def forward(r, micro, tok, first, leading):
    length, width = r.normed.shape
    tokens = pl.ds(tok, length)
    r.normed[...] = norm_rows_bf16(r, r.stream[micro].astype(WIDE), 0)

    @pl.when(first)
    def _():
        r.load_inward.wait()

        @pl.when(leading)
        def _():
            r.load_rest()

    for part in range(3):
        r.grads[5 + part, tokens, :] = times(
            r.normed[...], r.inward[:, part * width : (part + 1) * width]
        ).astype(SLIM)

    @pl.when(micro > 0)
    def _():
        r.share_acts(0).wait_send()

    r.turned[...] = r.normed[...].T
    place(r, 3, tokens)
    one, two = (lanes.astype(SLIM) for lanes in head_lanes())
    for pair in range(width // (2 * HEAD)):
        cols = pl.ds(pair * 2 * HEAD, 2 * HEAD)
        queries = r.grads[5, tokens, cols] * jnp.asarray(HEAD**-0.5, SLIM)
        keys = r.grads[6, tokens, cols]
        values_turned = r.grads[7, tokens, cols].T
        scores = times_turned(jnp.concatenate([keys * one, keys * two], 0), queries)
        pieces = []
        for head in range(2):
            masked = scores[length * head : length * (head + 1)] + r.bias_mask[...]
            raised = jnp.exp(masked - jnp.max(masked, 0, keepdims=True))
            weights = (raised * (1.0 / jnp.sum(raised, 0, keepdims=True))).astype(SLIM)
            r.weights[micro, 2 * pair + head] = weights
            pieces.append(times(values_turned[HEAD * head : HEAD * (head + 1)], weights).astype(SLIM))
        attended_turned = jnp.concatenate(pieces, 0)
        r.turned[cols, :] = attended_turned
        r.held[:, cols] = attended_turned.T
    place(r, 2, tokens)

    @pl.when(first)
    def _():
        r.load_outward.wait()

    r.middle[micro] = r.stream[micro].astype(WIDE) + times(r.held[...], r.outward[...])
    r.normed[...] = norm_rows_bf16(r, r.middle[micro], 1)
    r.turned[...] = r.normed[...].T
    place(r, 1, tokens)

    @pl.when(first)
    def _():
        r.load_up.wait()
        r.load_down.wait()

    def activate(part):
        lifted = times(r.normed[...], r.up[:, part * width : (part + 1) * width])
        cumulative = 0.5 * (1.0 + lax.erf(lifted * 0.7071067811865476))
        density = jnp.exp(-0.5 * lifted * lifted) * 0.3989422804014327
        r.grads[part, tokens, :] = (cumulative + lifted * density).astype(SLIM)
        active = (lifted * cumulative).astype(SLIM)
        r.turned[...] = active.T
        rows = pl.ds(part * BLOCK, BLOCK)
        for y in range(2):
            placed = pl.ds(y * 192 + part * BLOCK, BLOCK)
            own = pl.ds(pl.multiple_of(384 * y + r.c * 192, 16), BLOCK)
            other = pl.ds(pl.multiple_of(384 * y + (1 - r.c) * 192, 16), BLOCK)
            r.acts[0, placed, tokens] = r.turned[own, :]
            r.acts_out[0, placed, :] = r.turned[other, :]
        for piece in range(3):

            def rows_for(core, side):
                start = 384 * side + 192 * core + BLOCK * (piece + 1)
                return r.turned[pl.ds(pl.multiple_of(start, 16), BLOCK), :]

            r.quad_acts[piece, rows, r.quad_rows(micro)] = rows_for(r.c, r.y)
            r.quad_out[micro, 0, piece, rows, :] = rows_for(1 - r.c, r.y)
            r.quad_out[micro, 1, piece, rows, :] = rows_for(r.c, 1 - r.y)
            r.quad_out[micro, 2, piece, rows, :] = rows_for(1 - r.c, 1 - r.y)
        return active

    @pl.when(leading)
    def _():
        r.total[...] = r.middle[micro]
        for part in range(4):
            r.total[...] += times(activate(part), r.down[part * width : (part + 1) * width, :])
        r.result[micro] = r.total[...].astype(SLIM)

    @pl.when(jnp.logical_not(leading))
    def _():
        for part in range(4):
            set_aside(r, micro * 12 + 2 * part, activate(part))
        middle = r.middle[micro]
        upper = middle.astype(SLIM)
        set_aside(r, micro * 12 + 8, upper)
        set_aside(r, micro * 12 + 10, (middle - upper.astype(WIDE)).astype(SLIM))


def set_aside(r, slot, values):
    for half in range(2):
        columns = values[:, half * COLUMNS : (half + 1) * COLUMNS]
        r.partial[slot + half, 0] = columns[:192]
        r.partial[slot + half, 1, 0:64] = columns[192:]


def set_back(r, slot):
    halves = [
        jnp.concatenate([r.partial[slot + half, 0], r.partial[slot + half, 1, 0:64]], 0) for half in range(2)
    ]
    return jnp.concatenate(halves, 1)


def last_output(r, micro):
    width = r.normed.shape[1]
    r.total[...] = set_back(r, micro * 12 + 8).astype(WIDE) + set_back(r, micro * 12 + 10).astype(WIDE)
    for part in range(4):
        r.total[...] += times(set_back(r, micro * 12 + 2 * part), r.down[part * width : (part + 1) * width, :])
    r.result[micro] = r.total[...].astype(SLIM)


def backward(r, micro, tok):
    length, width = r.normed.shape
    tokens = pl.ds(tok, length)
    r.total[...] = jnp.zeros((length, width), WIDE)
    for part in range(4):
        cols = slice(part * width, (part + 1) * width)
        hidden = times_turned(r.branch[r.quad_rows(micro), :], r.down[cols, :])
        lifted_grad = (hidden * r.grads[part, tokens, :].astype(WIDE)).astype(SLIM)
        r.grads[part, tokens, :] = lifted_grad
        r.total[...] += times_turned(lifted_grad, r.up[:, cols])
    r.share_lifted(micro).start()
    r.between(micro)
    middle_grad = r.branch[r.quad_rows(micro), :].astype(WIDE) + norm_backward(
        r, r.middle[micro], r.total[...], 1
    )
    r.middle[micro] = middle_grad
    r.grads[4, tokens, :] = middle_grad.astype(SLIM)
    r.held[...] = times_turned(r.grads[4, tokens, :], r.outward[...]).astype(SLIM)
    first, second = head_lanes()
    one, two = first.astype(SLIM), second.astype(SLIM)
    scaling = HEAD**-0.5
    for pair in range(width // (2 * HEAD)):
        cols = pl.ds(pair * 2 * HEAD, 2 * HEAD)
        queries = r.grads[5, tokens, cols] * jnp.asarray(scaling, SLIM)
        values = r.grads[7, tokens, cols]
        keys_turned = r.grads[6, tokens, cols].T
        incoming = r.held[:, cols]
        weight_grads = times_turned(jnp.concatenate([values * one, values * two], 0), incoming)
        score_grads, query_grads, weights = [], [], []
        for head in range(2):
            kept = r.weights[micro, 2 * pair + head]
            wide = kept.astype(WIDE)
            own = weight_grads[length * head : length * (head + 1)]
            score_grad = (wide * (own - jnp.sum(wide * own, 0, keepdims=True))).astype(SLIM)
            score_grads.append(score_grad)
            weights.append(kept)
            query_grads.append(
                (times(keys_turned[HEAD * head : HEAD * (head + 1)], score_grad) * scaling).astype(SLIM)
            )
        key_grad = times(jnp.concatenate(score_grads, 0), queries)
        value_grad = times(jnp.concatenate(weights, 0), incoming)
        r.grads[5, tokens, cols] = jnp.concatenate(query_grads, 0).T
        r.grads[6, tokens, cols] = (key_grad[:length] * first + key_grad[length:] * second).astype(SLIM)
        r.grads[7, tokens, cols] = (value_grad[:length] * first + value_grad[length:] * second).astype(SLIM)
    norm_grad = times_turned(r.grads[5, tokens, :], r.inward[:, 0:width])
    for part in range(1, 3):
        norm_grad += times_turned(r.grads[5 + part, tokens, :], r.inward[:, part * width : (part + 1) * width])
    r.total[...] = norm_grad
    input_grad = r.middle[micro] + norm_backward(r, r.stream[micro].astype(WIDE), r.total[...], 0)
    r.middle[micro] = input_grad
    r.stream[micro] = input_grad.astype(SLIM)


NAMES = (
    "x_in", "cot_in", "inward_in", "outward_in", "up_in", "down_in", "gain", "bias", "lengths", "offsets",
    "result", "middle", "staged", "out_norms",
    "stream", "inward", "outward", "up", "down", "grads", "branch", "acts", "acts_out", "quad_acts", "quad_out", "weights", "normed", "held",
    "turned", "total", "sums", "bias_mask",
    "partial", "y_in", "z_in", "far_y_in", "far_z_in", "norms",
    "load_sem", "source_sem",
    "relay_send", "relay_recv", "acts_send", "acts_recv", "branch_send", "branch_recv", "lifted_send", "lifted_recv",
    "across_send", "across_recv", "onward_send", "onward_recv", "quad_send", "quad_recv",
    "rest_send", "rest_recv", "turn",
    "y_send", "y_recv", "z_send", "z_recv", "far_y_send", "far_y_recv", "far_z_send", "far_z_recv", "norm_send", "norm_recv",
)


def step_kernel(*refs):
    r = types.SimpleNamespace(**dict(zip(NAMES, refs)))
    section, dp = lax.axis_index("section"), lax.axis_index("dp")
    c, y, z = lax.rem(dp, 2), lax.rem(lax.div(dp, 2), 2), lax.div(dp, 4)
    r.c, r.y = c, y
    length = r.normed.shape[0]
    leading = section == 0
    pair_dp, y_dp = dp + 1 - 2 * c, dp + 2 - 4 * y
    diagonal_dp = pair_dp + y_dp - dp

    def slot_of(core, micro):
        return pl.ds(pl.multiple_of((core * 2 + micro) * length, length), length)

    def quad_rows(micro, core=c, side=y):
        return pl.ds(pl.multiple_of(((side * 2 + core) * 2 + micro) * length, length), length)

    r.quad_rows = quad_rows

    def remote(src, dst, send, recv, to_section, to_dp):
        return pltpu.make_async_remote_copy(
            src_ref=src, dst_ref=dst, send_sem=send, recv_sem=recv,
            device_id=(to_section, to_dp), device_id_type=MESH,
        )

    def local(src, dst, sem):
        return pltpu.make_async_copy(src, dst, sem)

    r.load_inward = local(r.inward_in.at[0], r.inward, r.load_sem.at[0])
    r.load_outward = local(r.outward_in.at[0], r.outward, r.load_sem.at[1])
    r.load_up = local(r.up_in.at[0], r.up, r.load_sem.at[2])
    r.load_down = local(r.down_in.at[0], r.down, r.load_sem.at[3])

    def load_rest():
        r.load_outward.start()
        r.load_up.start()
        r.load_down.start()

    r.load_rest = load_rest

    def load_x(micro):
        return local(r.x_in.at[micro, 0], r.stream.at[micro], r.source_sem.at[micro])

    def load_cot(micro):
        return local(r.cot_in.at[micro, 0], r.branch.at[quad_rows(micro)], r.source_sem.at[micro])

    def relay_up(micro):
        return remote(r.result.at[micro], r.stream.at[micro], r.relay_send.at[micro], r.relay_recv.at[micro], 1 - section, dp)

    def relay_back(micro):
        return remote(
            r.stream.at[micro], r.branch.at[quad_rows(micro)], r.relay_send.at[micro], r.relay_recv.at[micro], 1 - section, dp
        )

    def share_acts(micro, core=c):
        return remote(
            r.acts_out, r.acts.at[:, :, slot_of(core, micro)], r.acts_send.at[micro], r.acts_recv.at[micro], section, pair_dp
        )

    def branch_copy(rows, send, recv, to_dp):
        return remote(r.branch.at[rows], r.branch.at[rows], send, recv, section, to_dp)

    def share_branch(micro, core=c):
        return branch_copy(quad_rows(micro, core), r.branch_send.at[micro], r.branch_recv.at[micro], pair_dp)

    def branch_across(micro, side=y):
        return branch_copy(quad_rows(micro, c, side), r.across_send.at[micro], r.across_recv.at[micro], y_dp)

    def branch_onward(micro, core=c):
        return branch_copy(quad_rows(micro, core, 1 - y), r.onward_send.at[micro], r.onward_recv.at[micro], pair_dp)

    def share_quad(micro, peer, arriving=False):
        to_dp = (pair_dp, y_dp, diagonal_dp)[peer]
        core = 1 - c if arriving and peer != 1 else c
        side = 1 - y if arriving and peer != 0 else y
        return remote(
            r.quad_out.at[micro, peer], r.quad_acts.at[:, :, quad_rows(micro, core, side)],
            r.quad_send.at[micro, peer], r.quad_recv.at[micro, peer], section, to_dp,
        )

    def share_lifted(micro, core=c):
        rows = slot_of(core, micro)
        return remote(
            r.grads.at[0:4, rows], r.grads.at[0:4, rows], r.lifted_send.at[micro], r.lifted_recv.at[micro], section, pair_dp
        )

    def share_rest(micro, core=c):
        rows = slot_of(core, micro)
        return remote(
            r.grads.at[4:8, rows], r.grads.at[4:8, rows], r.rest_send.at[micro], r.rest_recv.at[micro], section, pair_dp
        )

    r.share_lifted = share_lifted
    r.share_acts = share_acts

    def to_y(unit):
        return remote(
            r.partial.at[unit, 0], r.y_in.at[unit - QUAD], r.y_send.at[unit - QUAD], r.y_recv.at[unit - QUAD], section, y_dp
        )

    def rows_of(place):
        return pl.ds(BLOCK * place, BLOCK)

    def near_z(unit, place, index, lane, to_dp):
        near = unit - FAR
        return remote(
            r.partial.at[unit, 1, rows_of(place)], r.z_in.at[near, index],
            r.z_send.at[near, lane], r.z_recv.at[near, index], section, to_dp,
        )

    def far_z(unit, place, index, lane, to_dp):
        return remote(
            r.partial.at[unit, :, rows_of(place)], r.far_z_in.at[unit, index],
            r.far_z_send.at[unit, lane], r.far_z_recv.at[unit, index], section, to_dp,
        )

    def far_to_y(unit, place):
        return remote(
            r.partial.at[unit, 0, rows_of(place)], r.far_y_in.at[unit], r.far_y_send.at[unit], r.far_y_recv.at[unit], section, y_dp
        )

    r.load_inward.start()

    @pl.when(leading)
    def _():
        load_x(0).start()
        load_x(1).start()

    @pl.when(jnp.logical_not(leading))
    def _():
        load_cot(0).start()
        load_cot(1).start()

    @pl.when(jnp.logical_not(leading))
    def _():
        r.load_rest()

    r.sums[...] = jnp.zeros_like(r.sums)

    barrier = pltpu.get_barrier_semaphore()
    peers = [(1 - section, dp), (section, pair_dp), (section, y_dp)]
    peers += [(section, diagonal_dp)]
    peers += [(section, lax.rem(dp + 4 * hop, 16)) for hop in (1, 2, 3)]
    for peer in peers:
        pl.semaphore_signal(barrier, inc=1, device_id=peer, device_id_type=MESH)

    def everyone_in():
        pl.semaphore_wait(barrier, len(peers))

    def arrive(micro):
        relay_back(micro).wait_recv()
        branch_across(micro).start()
        share_branch(micro).start()

    def columns_of(unit):
        return pl.ds(pl.multiple_of(lax.rem(unit, 2) * COLUMNS, 128), COLUMNS)

    def side_rows(side):
        return pl.ds(pl.multiple_of(side * 192, 64), 192)

    def near_unit(unit):
        whole = lax.div(unit, 2)
        slab = 1 + jnp.where(whole >= 8, 1, 0) + jnp.where(whole >= 9, 1, 0)
        grads = r.grads[whole - 4, :, columns_of(unit)]
        r.partial[unit, 0] = times(r.acts[slab, side_rows(1 - y), :], grads).astype(SLIM)
        to_y(unit).start()
        r.partial[unit, 1] = times(r.acts[slab, side_rows(y), :], grads).astype(SLIM)

    def far_unit(unit):
        grads = r.branch[pl.ds(pl.multiple_of(y * 4 * length, length), 4 * length), columns_of(unit)]
        r.partial[unit, 0] = times(r.acts[0, side_rows(1 - y), :], grads).astype(SLIM)
        r.partial[unit, 1] = times(r.acts[0, side_rows(y), :], grads).astype(SLIM)
        at_ends(unit, far_z, r.far_z_in)

    def quad_unit(unit):
        grads = r.branch[:, columns_of(unit)]
        r.partial[unit, 1] = times(r.quad_acts[lax.div(unit, 2) - 1], grads).astype(SLIM)
        at_ends(unit, near_z, r.z_in)

    def arrived(unit, index, copy, into):
        copy(unit, 0, index, 0, dp).wait_recv()
        return into[unit if into is r.far_z_in else unit - FAR, index].astype(WIDE)

    def pick(unit, place, copy):
        return (unit, slice(None) if copy is far_z else 1, rows_of(place))

    def go_right(unit, here, copy, into):
        for place in range(3, here, -1):
            at = pick(unit, place, copy)
            if here > 0:
                r.partial[at] = (r.partial[at].astype(WIDE) + arrived(unit, place + 1, copy, into)).astype(SLIM)
            copy(unit, place, place + 1, place - 1, dp + 4).start()

    def go_left(unit, here, copy, into):
        for place in range(here):
            at = pick(unit, place, copy)
            if here < 3:
                r.partial[at] = (r.partial[at].astype(WIDE) + arrived(unit, place, copy, into)).astype(SLIM)
            copy(unit, place, place, place, dp - 4).start()

    def at_ends(unit, copy, into):
        @pl.when(z == 0)
        def _():
            go_right(unit, 0, copy, into)

        @pl.when(z == 3)
        def _():
            go_left(unit, 3, copy, into)

    def at_middle_first(unit, copy, into):
        @pl.when(z == 1)
        def _():
            go_right(unit, 1, copy, into)

        @pl.when(z == 2)
        def _():
            go_left(unit, 2, copy, into)

    def at_middle_second(unit, copy, into):
        @pl.when(z == 1)
        def _():
            go_left(unit, 1, copy, into)

        @pl.when(z == 2)
        def _():
            go_right(unit, 2, copy, into)

    def gathered(unit, here, copy, into):
        value = r.partial[pick(unit, here, copy)].astype(WIDE)
        if here > 0:
            value = value + arrived(unit, here + 1, copy, into)
        if here < 3:
            value = value + arrived(unit, here, copy, into)
        return value

    def everywhere(action):
        for here in range(4):

            @pl.when(z == here)
            def _():
                action(here)

    def far_units():
        for micro in range(2):
            share_branch(micro, 1 - c).wait_recv()
            share_acts(micro, 1 - c).wait_recv()

        def body(unit, carry):
            far_unit(unit)
            return carry

        lax.fori_loop(0, FAR, body, 0)
        branch_across(0, 1 - y).wait_recv()
        branch_onward(0).start()

    r.between = lambda micro: pl.when(leading & (micro == 1))(far_units)

    def slot(t, carry):
        trailing = jnp.logical_not(leading)
        half = lax.div(t, 2)
        is_forward = (leading & (t < 2)) | (trailing & ((t == 1) | (t == 3)))
        is_backward = (leading & ((t == 3) | (t == 5))) | (trailing & ((t == 2) | (t == 4)))

        @pl.when(trailing & (t == 0))
        def _():
            everyone_in()
            for micro in range(2):
                load_cot(micro).wait()
                branch_across(micro).start()
                share_branch(micro).start()

        @pl.when(is_forward)
        def _():
            micro = jnp.where(leading, jnp.minimum(t, 1), jnp.minimum(half, 1))

            mask_bias(r, micro)

            @pl.when(leading)
            def _():
                load_x(micro).wait()

            @pl.when(trailing)
            def _():
                relay_up(micro).wait_recv()

            forward(r, micro, pl.multiple_of((c * 2 + micro) * length, length), t == section, leading)

            @pl.when(leading & (t == 0))
            def _():
                everyone_in()

            ahead = leading & (c == 0) & (t == 0)

            @pl.when(ahead)
            def _():
                relay_up(0).start()
                relay_up(0).wait_send()
                pl.semaphore_signal(r.turn, inc=1, device_id=(section, pair_dp), device_id_type=MESH)

            @pl.when(leading & (t == 1))
            def _():
                relay_up(1).start()

            share_acts(micro).start()

            @pl.when(leading & (c == 1) & (t == 0))
            def _():
                pl.semaphore_wait(r.turn, 1)
                relay_up(0).start()

            for peer in range(3):
                share_quad(micro, peer).start()

        @pl.when(leading & (t == 3))
        def _():
            arrive(0)

        @pl.when(is_backward)
        def _():
            micro = jnp.clip(half - 1, 0, 1)
            backward(r, micro, pl.multiple_of((c * 2 + micro) * length, length))

            @pl.when(trailing)
            def _():
                relay_back(micro).start()

            share_rest(micro).start()

            @pl.when(trailing & (t == 4))
            def _():
                def body(done, carry):
                    last_output(r, done)
                    return carry

                lax.fori_loop(0, 2, body, 0)

        @pl.when(leading & (t == 4))
        def _():
            arrive(1)

        pl.when(trailing & (t == 5))(far_units)
        return carry

    lax.fori_loop(0, 6, slot, 0)

    def norm_copy(src, dst, index, to_dp):
        return remote(r.norms.at[src], r.norms.at[dst], r.norm_send.at[index], r.norm_recv.at[index], section, to_dp)

    def norm_to_pair():
        return norm_copy(0, 1, 0, pair_dp)

    def norm_to_y():
        return norm_copy(2, 3, 1, y_dp)

    def norm_to_z(hop):
        return norm_copy(4, 4 + hop, 1 + hop, lax.rem(dp + 4 * hop, 16))

    r.norms[0] = jnp.concatenate([jnp.sum(r.sums[...], 1), jnp.zeros((4, r.sums.shape[2]), WIDE)], 0)
    norm_to_pair().start()
    for micro in range(2):
        share_lifted(micro, 1 - c).wait_recv()

    def early_near(ahead, carry):
        near_unit(QUAD + ahead)
        return carry

    lax.fori_loop(0, EARLY_NEAR, early_near, 0)
    branch_across(1, 1 - y).wait_recv()
    branch_onward(1).start()
    for micro in range(2):
        branch_onward(micro, 1 - c).wait_recv()
        for peer in range(3):
            share_quad(micro, peer, True).wait_recv()

    def early_quad(unit, carry):
        quad_unit(unit)
        return carry

    lax.fori_loop(FAR, FAR + sum(step < 0 for step in QUAD_AT), early_quad, 0)

    def sum_y(unit):
        to_y(unit).wait_recv()
        r.partial[unit, 1] = (r.partial[unit, 1].astype(WIDE) + r.y_in[unit - QUAD].astype(WIDE)).astype(SLIM)

    def turn_of(i, steps, base):
        turn, unit = i < 0, jnp.int32(base)
        for index, step in enumerate(steps):
            if step >= 0:
                turn = turn | (i == step)
                unit = jnp.where(i == step, base + index, unit)
        return turn, unit

    def near_turn(i, lag):
        return (i >= lag) & (i < NEAR + lag), jnp.clip(i - lag, 0, NEAR - 1) + QUAD

    def end_of_line(unit):
        def action(here):
            r.staged[unit] = gathered(unit, here, near_z, r.z_in)

        everywhere(action)

    def advance(i, carry):
        issued = QUAD + EARLY_NEAR + i - HOLD

        @pl.when(issued == 16)
        def _():
            for micro in range(2):
                share_rest(micro, 1 - c).wait_recv()

        @pl.when((issued >= QUAD + EARLY_NEAR) & (issued < UNITS))
        def _():
            near_unit(issued)

        @pl.when(i < NEAR)
        def _():
            sum_y(QUAD + i)
            at_ends(QUAD + i, near_z, r.z_in)

        turn, unit = turn_of(i, QUAD_AT, FAR)

        @pl.when(turn)
        def _(unit=unit):
            quad_unit(unit)

        turn, unit = near_turn(i, LAGS[0])

        @pl.when(turn)
        def _(unit=unit):
            at_middle_first(unit, near_z, r.z_in)

        turn, unit = turn_of(i, FAR_FIRST, 0)

        @pl.when(turn)
        def _(unit=unit):
            at_middle_first(unit, far_z, r.far_z_in)

        turn, unit = turn_of(i, QUAD_FIRST, FAR)

        @pl.when(turn)
        def _(unit=unit):
            at_middle_first(unit, near_z, r.z_in)

        turn, unit = turn_of(i, FAR_SECOND, 0)

        @pl.when(turn)
        def _(unit=unit):
            at_middle_second(unit, far_z, r.far_z_in)

        turn, unit = turn_of(i, QUAD_SECOND, FAR)

        @pl.when(turn)
        def _(unit=unit):
            at_middle_second(unit, near_z, r.z_in)

        turn, unit = near_turn(i, LAGS[1])

        @pl.when(turn)
        def _(unit=unit):
            at_middle_second(unit, near_z, r.z_in)

        turn, unit = turn_of(i, QUAD_DONE, FAR)

        @pl.when(turn)
        def _(unit=unit):
            end_of_line(unit)

        turn, unit = near_turn(i, LAGS[2])

        @pl.when(turn)
        def _(unit=unit):
            end_of_line(unit)

        turn, unit = turn_of(i, FAR_ARRIVED, 0)

        @pl.when(turn)
        def _(unit=unit):
            def action(here):
                value = gathered(unit, here, far_z, r.far_z_in)
                r.partial[unit, 0, rows_of(here)] = value[0].astype(SLIM)
                far_to_y(unit, here).start()
                r.staged[unit] = value[1]

            everywhere(action)

        turn, unit = turn_of(i, FAR_DONE, 0)

        @pl.when(turn)
        def _(unit=unit):
            far_to_y(unit, 0).wait_recv()
            r.staged[unit] += r.far_y_in[unit].astype(WIDE)

        @pl.when(i == 1)
        def _():
            norm_to_pair().wait()
            r.norms[2] = r.norms[0] + r.norms[1]
            norm_to_y().start()

        @pl.when(i == 9)
        def _():
            norm_to_y().wait_recv()
            r.norms[4] = r.norms[2] + r.norms[3]
            for hop in (1, 2, 3):
                norm_to_z(hop).start()

        @pl.when(i == 15)
        def _():
            for hop in (1, 2, 3):
                norm_to_z(hop).wait_recv()
            r.out_norms[...] = (r.norms[4] + r.norms[5]) + (r.norms[6] + r.norms[7])

        return carry

    lax.fori_loop(0, NEAR + LAGS[2], advance, 0)

    norm_to_y().wait_send()
    for hop in (1, 2, 3):
        norm_to_z(hop).wait_send()
    share_acts(1).wait_send()
    for micro in range(2):
        share_branch(micro).wait_send()
        branch_across(micro).wait_send()
        branch_onward(micro).wait_send()
        for peer in range(3):
            share_quad(micro, peer).wait_send()
        share_lifted(micro).wait_send()
        share_rest(micro).wait_send()

        @pl.when(leading if micro else leading & (c == 1))
        def _():
            relay_up(micro).wait_send()

        @pl.when(jnp.logical_not(leading))
        def _():
            relay_back(micro).wait_send()

    def drain_y(near, carry):
        to_y(QUAD + near).wait_send()
        return carry

    lax.fori_loop(0, NEAR, drain_y, 0)

    def drain_z(unit, carry):
        for lane in range(3):
            near_z(unit, 0, 0, lane, dp).wait_send()
        return carry

    lax.fori_loop(FAR, UNITS, drain_z, 0)

    def drain_far(unit, carry):
        far_to_y(unit, 0).wait_send()
        for lane in range(3):
            far_z(unit, 0, 0, lane, dp).wait_send()
        return carry

    lax.fori_loop(0, FAR, drain_far, 0)


def hand_over_kernel(result, grad, staged, norms, *refs):
    out_result, out_grad, out_inward, out_outward, out_up, out_down, gain_grad, bias_grad, sem = refs
    width = result.shape[2]

    def start(source, target):
        copy = pltpu.make_async_copy(source, target, sem)
        copy.start()
        return copy

    copies = [start(result, out_result.at[0, :, 0]), start(grad, out_grad.at[0, :, 0])]
    for piece in range(UNITS):
        half = pl.ds(piece % 2 * COLUMNS, COLUMNS)
        if piece < 8:
            target = out_down.at[0, pl.ds(piece // 2 * BLOCK, BLOCK), half]
        elif piece < 16:
            target = out_up.at[0, :, pl.ds((piece - 8) * COLUMNS, COLUMNS)]
        elif piece < 18:
            target = out_outward.at[0, :, half]
        else:
            target = out_inward.at[0, :, pl.ds((piece - 18) * COLUMNS, COLUMNS)]
        copies.append(start(staged.at[piece], target))
    share = gain_grad.shape[2]
    for index in range(width // share):

        @pl.when(lax.axis_index("dp") == index)
        def _():
            gain_grad[0] = norms[0:2, index * share : (index + 1) * share]
            bias_grad[0] = norms[2:4, index * share : (index + 1) * share]

    for copy in copies:
        copy.wait()


def step_on_device(
    inputs, clip_lengths, anchor_offsets, cotangent, inward_weight, outward_weight, up_weight, down_weight, norm_gain, norm_bias
):
    _, _, length, width = inputs.shape
    wide_ff = up_weight.shape[2]
    anywhere = pl.BlockSpec(memory_space=pl.ANY)
    in_vmem = pl.BlockSpec(memory_space=pltpu.VMEM)
    in_smem = pl.BlockSpec(memory_space=pltpu.SMEM)
    dma = pltpu.SemaphoreType.DMA
    share = width // lax.axis_size("dp")
    made = pl.pallas_call(
        step_kernel,
        out_shape=(
            pltpu.VMEM((2, length, width), SLIM),
            pltpu.VMEM((2, length, width), WIDE),
            pltpu.VMEM((UNITS, BLOCK, COLUMNS), WIDE),
            pltpu.VMEM((8, width), WIDE),
        ),
        in_specs=[anywhere] * 6 + [in_vmem] * 2 + [in_smem] * 2,
        out_specs=[in_vmem] * 4,
        scratch_shapes=[
            pltpu.VMEM((2, length, width), SLIM),
            pltpu.VMEM((width, 3 * width), SLIM),
            pltpu.VMEM((width, width), SLIM),
            pltpu.VMEM((width, wide_ff), SLIM),
            pltpu.VMEM((wide_ff, width), SLIM),
            pltpu.VMEM((8, 4 * length, width), SLIM),
            pltpu.VMEM((8 * length, width), SLIM),
            pltpu.VMEM((4, 8 * BLOCK, 4 * length), SLIM),
            pltpu.VMEM((4, 8 * BLOCK, length), SLIM),
            pltpu.VMEM((3, 4 * BLOCK, 8 * length), SLIM),
            pltpu.VMEM((2, 3, 3, 4 * BLOCK, length), SLIM),
            pltpu.VMEM((2, width // HEAD, length, length), SLIM),
            pltpu.VMEM((length, width), SLIM),
            pltpu.VMEM((length, width), SLIM),
            pltpu.VMEM((width, length), SLIM),
            pltpu.VMEM((length, width), WIDE),
            pltpu.VMEM((4, 8, width), WIDE),
            pltpu.VMEM((length, length), WIDE),
            pltpu.VMEM((UNITS, 2, 4 * BLOCK, COLUMNS), SLIM),
            pltpu.VMEM((NEAR, 4 * BLOCK, COLUMNS), SLIM),
            pltpu.VMEM((UNITS - FAR, 5, BLOCK, COLUMNS), SLIM),
            pltpu.VMEM((FAR, BLOCK, COLUMNS), SLIM),
            pltpu.VMEM((FAR, 5, 2, BLOCK, COLUMNS), SLIM),
            pltpu.VMEM((8, 8, width), WIDE),
            dma((4,)), dma((2,)),
            *[dma((2,))] * 8, *[dma((2,))] * 4, dma((2, 3)), dma((2, 3)), *[dma((2,))] * 2, pltpu.SemaphoreType.REGULAR,
            dma((NEAR,)), dma((NEAR,)), dma((UNITS - FAR, 3)), dma((UNITS - FAR, 5)),
            dma((FAR,)), dma((FAR,)), dma((FAR, 3)), dma((FAR, 5)), dma((5,)), dma((5,)),
        ],
        compiler_params=pltpu.CompilerParams(
            collective_id=0, has_side_effects=True, vmem_limit_bytes=VMEM_BYTES - 4500000
        ),
    )(
        inputs, cotangent, inward_weight, outward_weight, up_weight, down_weight,
        norm_gain, norm_bias, clip_lengths, anchor_offsets,
    )
    sections = 1
    return pl.pallas_call(
        hand_over_kernel,
        out_shape=(
            jax.ShapeDtypeStruct((sections, 2, 1, length, width), SLIM),
            jax.ShapeDtypeStruct((sections, 2, 1, length, width), WIDE),
            jax.ShapeDtypeStruct((sections, BLOCK, 3 * width), WIDE),
            jax.ShapeDtypeStruct((sections, BLOCK, width), WIDE),
            jax.ShapeDtypeStruct((sections, BLOCK, wide_ff), WIDE),
            jax.ShapeDtypeStruct((sections, 4 * BLOCK, width), WIDE),
            jax.ShapeDtypeStruct((sections, 2, share), WIDE),
            jax.ShapeDtypeStruct((sections, 2, share), WIDE),
        ),
        in_specs=[in_vmem] * 4,
        out_specs=[anywhere] * 6 + [in_vmem] * 2,
        scratch_shapes=[dma],
        compiler_params=pltpu.CompilerParams(vmem_limit_bytes=1 << 20),
    )(*[pltpu.with_memory_space_constraint(one, pltpu.VMEM) for one in made])


def shifted(x, axis, by):
    size = lax.axis_size(axis)
    pairs = [(i, i + by) for i in range(size) if 0 <= i + by < size]
    return lax.ppermute(x, axis, pairs)


def norm_rows(values, norm_gain, norm_bias):
    average = jnp.mean(values, -1, keepdims=True)
    centred = values - average
    inverse = lax.rsqrt(jnp.mean(centred * centred, -1, keepdims=True) + EPSILON)
    normed = centred * inverse
    return (normed * norm_gain + norm_bias, normed, inverse)


def norm_back(norm_grad, normed, inverse, norm_gain):
    inner = norm_grad * norm_gain
    through = inverse * (
        inner
        - jnp.mean(inner, -1, keepdims=True)
        - normed * jnp.mean(inner * normed, -1, keepdims=True)
    )
    return (through, jnp.sum(norm_grad * normed, 0), jnp.sum(norm_grad, 0))


def gelu_slope(lifted):
    cumulative = 0.5 * (1.0 + lax.erf(lifted * 0.7071067811865476))
    density = jnp.exp(-0.5 * lifted * lifted) * 0.3989422804014327
    return cumulative + lifted * density


def clip_marks(lengths, offsets, length):
    positions = jnp.arange(length, dtype=jnp.int32)
    clip_ends = jnp.cumsum(lengths)
    clip_starts = clip_ends - lengths
    anchor_at = clip_starts + offsets % lengths
    clip_ids = jnp.sum((positions[:, None] >= clip_ends[None, :]).astype(jnp.int32), 1)
    anchors = jnp.any(positions[:, None] == anchor_at[None, :], 1)
    return (clip_ids, anchors)


def masked_scores(query_block, key_rows, id_block, clip_ids, anchors, scaling):
    scores = (
        jnp.einsum("qhd,khd->hqk", query_block, key_rows, preferred_element_type=jnp.float32)
        * scaling
    )
    seen = (id_block[:, None] == clip_ids[None, :]) | anchors[None, :]
    return jnp.where(seen[None], scores, -1000000000.0)


def forward_layer(source, clip_ids, anchors, params):
    inward, outward, upward, downward, norm_gain, norm_bias = params
    length, model_width = source.shape
    head_count = model_width // HEAD
    scaling = HEAD ** (-0.5)
    residual = source.astype(jnp.float32)
    first_norm, unit_one, scale_one = norm_rows(residual, norm_gain[0], norm_bias[0])
    joined = jnp.dot(
        first_norm.astype(jnp.bfloat16), inward, preferred_element_type=jnp.float32
    ).astype(jnp.bfloat16)
    heads_view = joined.reshape(length, 3, head_count, HEAD)
    queries = heads_view[:, 0]
    key_rows = heads_view[:, 1]
    values = heads_view[:, 2]
    scores = masked_scores(queries, key_rows, clip_ids, clip_ids, anchors, scaling)
    row_max = jnp.max(scores, -1, keepdims=True)
    raised = jnp.exp(scores - row_max)
    row_sum = jnp.sum(raised, -1, keepdims=True)
    weights = (raised / row_sum).astype(jnp.bfloat16)
    pieces = [jnp.einsum("hqk,khd->qhd", weights, values, preferred_element_type=jnp.float32)]
    log_sums = [(row_max + jnp.log(row_sum))[..., 0]]
    attended = jnp.concatenate(pieces, 0).reshape(length, model_width).astype(jnp.bfloat16)
    logsum = jnp.concatenate(log_sums, 1)
    middle = residual + jnp.dot(attended, outward, preferred_element_type=jnp.float32)
    second_norm, unit_two, scale_two = norm_rows(middle, norm_gain[1], norm_bias[1])
    lifted = jnp.dot(second_norm.astype(jnp.bfloat16), upward, preferred_element_type=jnp.float32)
    active = jax.nn.gelu(lifted, approximate=False).astype(jnp.bfloat16)
    result = middle + jnp.dot(active, downward, preferred_element_type=jnp.float32)
    stored = (unit_one, scale_one, joined, logsum, attended, unit_two, scale_two, lifted, active)
    return (result, stored)


def contract_rows(left, right):
    return lax.dot_general(
        left, right, (((0,), (0,)), ((), ())), preferred_element_type=jnp.float32
    )


def contract_cols(left, right):
    return lax.dot_general(
        left, right, (((1,), (1,)), ((), ())), preferred_element_type=jnp.float32
    )


def feed_backward(incoming, stored, params):
    inward, outward, upward, downward, norm_gain, norm_bias = params
    unit_one, scale_one, joined, logsum, attended, unit_two, scale_two, lifted, active = stored
    branch = incoming.astype(jnp.bfloat16)
    down_part = contract_rows(active, branch)
    hidden_grad = contract_cols(branch, downward)
    lifted_grad = (hidden_grad * gelu_slope(lifted)).astype(jnp.bfloat16)
    second_in = (unit_two * norm_gain[1] + norm_bias[1]).astype(jnp.bfloat16)
    up_part = contract_rows(second_in, lifted_grad)
    normed_grad = contract_cols(lifted_grad, upward)
    through, gain_two, bias_two = norm_back(normed_grad, unit_two, scale_two, norm_gain[1])
    return (incoming + through, (up_part, down_part, gain_two, bias_two))


def attend_backward(middle_grad, stored, clip_ids, anchors, params):
    inward, outward, upward, downward, norm_gain, norm_bias = params
    unit_one, scale_one, joined, logsum, attended, unit_two, scale_two, lifted, active = stored
    length, model_width = attended.shape
    head_count = model_width // HEAD
    scaling = HEAD ** (-0.5)
    branch = middle_grad.astype(jnp.bfloat16)
    outward_part = contract_rows(attended, branch)
    attended_grad = (
        contract_cols(branch, outward).astype(jnp.bfloat16).reshape(length, head_count, HEAD)
    )
    heads_view = joined.reshape(length, 3, head_count, HEAD)
    queries = heads_view[:, 0]
    key_rows = heads_view[:, 1]
    values = heads_view[:, 2]
    key_grad = jnp.zeros((length, head_count, HEAD), jnp.float32)
    value_grad = jnp.zeros((length, head_count, HEAD), jnp.float32)
    block_rows = min(512, length)
    scores = masked_scores(queries, key_rows, clip_ids, clip_ids, anchors, scaling)
    weights = jnp.exp(scores - logsum[:, 0:block_rows, None])
    weight_grad = jnp.einsum(
        "qhd,khd->hqk", attended_grad, values, preferred_element_type=jnp.float32
    )
    score_grad = (
        weights * (weight_grad - jnp.sum(weights * weight_grad, -1, keepdims=True))
    ).astype(jnp.bfloat16)
    query_pieces = [
        scaling
        * jnp.einsum("hqk,khd->qhd", score_grad, key_rows, preferred_element_type=jnp.float32)
    ]
    key_grad = key_grad + scaling * jnp.einsum(
        "hqk,qhd->khd", score_grad, queries, preferred_element_type=jnp.float32
    )
    value_grad = value_grad + jnp.einsum(
        "hqk,qhd->khd",
        weights.astype(jnp.bfloat16),
        attended_grad,
        preferred_element_type=jnp.float32,
    )
    query_grad = jnp.concatenate(query_pieces, 0)
    joined_grad = (
        jnp.stack([query_grad, key_grad, value_grad], 1)
        .reshape(length, 3 * model_width)
        .astype(jnp.bfloat16)
    )
    first_in = (unit_one * norm_gain[0] + norm_bias[0]).astype(jnp.bfloat16)
    inward_part = contract_rows(first_in, joined_grad)
    normed_grad = contract_cols(joined_grad, inward)
    through, gain_one, bias_one = norm_back(normed_grad, unit_one, scale_one, norm_gain[0])
    return (middle_grad + through, (inward_part, outward_part, gain_one, bias_one))


def resting(function):

    def blank(*operands):
        return jax.tree.map(jnp.zeros_like, function(*operands))

    return blank


def take_slot(holder, buffer_slot):
    return jax.tree.map(
        lambda element: lax.dynamic_index_in_dim(element, buffer_slot, 0, False), holder
    )


def place_slot(holder, item, buffer_slot, working):

    def update(element, fresh):
        former = lax.dynamic_index_in_dim(element, buffer_slot, 0, False)
        return lax.dynamic_update_index_in_dim(
            element, jnp.where(working, fresh, former), buffer_slot, 0
        )

    return jax.tree.map(update, holder, item)


def per_device(
    inputs,
    clip_lengths,
    anchor_offsets,
    cotangent,
    inward_weight,
    outward_weight,
    up_weight,
    down_weight,
    norm_gain,
    norm_bias,
):
    params = (
        inward_weight[0],
        outward_weight[0],
        up_weight[0],
        down_weight[0],
        norm_gain[0],
        norm_bias[0],
    )
    stream = inputs[:, 0]
    cot_rows = cotangent[:, 0]
    lengths_all = clip_lengths[:, 0]
    offsets_all = anchor_offsets[:, 0]
    micro_count = stream.shape[0]
    length = stream.shape[1]
    section_index = lax.axis_index("section")
    section_count = lax.axis_size("section")
    leading = section_index == 0
    trailing = section_index == section_count - 1
    periods = micro_count + section_count - 1
    arriving = jnp.zeros_like(stream[0])
    produced = jnp.zeros_like(stream)
    archive = None
    for period in range(periods):
        micro_index = period - section_index
        working = (micro_index >= 0) & (micro_index < micro_count)
        buffer_slot = jnp.clip(micro_index, 0, micro_count - 1)
        source = jnp.where(leading, stream[min(period, micro_count - 1)], arriving)
        clip_ids, anchors = clip_marks(
            take_slot(lengths_all, buffer_slot), take_slot(offsets_all, buffer_slot), length
        )
        result, stored = lax.cond(
            working, forward_layer, resting(forward_layer), source, clip_ids, anchors, params
        )
        if archive is None:
            archive = jax.tree.map(
                lambda element: jnp.zeros((micro_count,) + element.shape, element.dtype), stored
            )
        archive = place_slot(archive, stored, buffer_slot, working)
        sending = result.astype(jnp.bfloat16)
        produced = place_slot(produced, sending, buffer_slot, working)
        if period < micro_count:
            arriving = shifted(sending, "section", 1)
    inward, outward, upward, downward, gains, biases = params
    up_sum = jnp.zeros(upward.shape, jnp.float32)
    down_sum = jnp.zeros(downward.shape, jnp.float32)
    gain_two = jnp.zeros(gains.shape[1:], jnp.float32)
    bias_two = jnp.zeros(biases.shape[1:], jnp.float32)
    inward_sum = jnp.zeros(inward.shape, jnp.float32)
    outward_sum = jnp.zeros(outward.shape, jnp.float32)
    gain_one = jnp.zeros(gains.shape[1:], jnp.float32)
    bias_one = jnp.zeros(biases.shape[1:], jnp.float32)
    upstream = jnp.zeros_like(stream[0])
    returned = jnp.zeros(stream.shape, jnp.float32)
    for period in range(periods):
        micro_index = micro_count - 1 - period + (section_count - 1 - section_index)
        working = (micro_index >= 0) & (micro_index < micro_count)
        buffer_slot = jnp.clip(micro_index, 0, micro_count - 1)
        incoming = jnp.where(trailing, take_slot(cot_rows, buffer_slot), upstream).astype(
            jnp.float32
        )
        clip_ids, anchors = clip_marks(
            take_slot(lengths_all, buffer_slot), take_slot(offsets_all, buffer_slot), length
        )
        stored = take_slot(archive, buffer_slot)
        middle_grad, feed_part = lax.cond(
            working, feed_backward, resting(feed_backward), incoming, stored, params
        )
        up_sum = up_sum + feed_part[0]
        down_sum = down_sum + feed_part[1]
        gain_two = gain_two + feed_part[2]
        bias_two = bias_two + feed_part[3]
        input_grad, attend_part = lax.cond(
            working,
            attend_backward,
            resting(attend_backward),
            middle_grad,
            stored,
            clip_ids,
            anchors,
            params,
        )
        inward_sum = inward_sum + attend_part[0]
        outward_sum = outward_sum + attend_part[1]
        gain_one = gain_one + attend_part[2]
        bias_one = bias_one + attend_part[3]
        returned = place_slot(returned, input_grad, buffer_slot, working)
        if period < periods - 1:
            upstream = shifted(input_grad.astype(jnp.bfloat16), "section", -1)
    inward_sum, outward_sum, up_sum, down_sum, gain_one, gain_two, bias_one, bias_two = (
        lax.psum_scatter(inward_sum, "dp", scatter_dimension=0, tiled=True),
        lax.psum_scatter(outward_sum, "dp", scatter_dimension=0, tiled=True),
        lax.psum_scatter(up_sum, "dp", scatter_dimension=0, tiled=True),
        lax.psum_scatter(down_sum, "dp", scatter_dimension=0, tiled=True),
        lax.psum_scatter(gain_one, "dp", scatter_dimension=0, tiled=True),
        lax.psum_scatter(gain_two, "dp", scatter_dimension=0, tiled=True),
        lax.psum_scatter(bias_one, "dp", scatter_dimension=0, tiled=True),
        lax.psum_scatter(bias_two, "dp", scatter_dimension=0, tiled=True),
    )
    layer_outputs = produced[None, :, None]
    input_grads = returned[None, :, None]
    gain_grad = jnp.stack([gain_one, gain_two])[None]
    bias_grad = jnp.stack([bias_one, bias_two])[None]
    return (
        layer_outputs,
        input_grads,
        inward_sum[None],
        outward_sum[None],
        up_sum[None],
        down_sum[None],
        gain_grad,
        bias_grad,
    )


def solution(mesh):
    local = step_on_device if mesh.shape["dp"] == 16 and mesh.shape["section"] == 2 else per_device
    return jax.shard_map(
        local,
        mesh=mesh,
        in_specs=(
            P(None, "dp", None, None),
            P(None, "dp", None),
            P(None, "dp", None),
            P(None, "dp", None, None),
            P("section", None, None),
            P("section", None, None),
            P("section", None, None),
            P("section", None, None),
            P("section", None, None),
            P("section", None, None),
        ),
        out_specs=(
            P("section", None, "dp", None, None),
            P("section", None, "dp", None, None),
            P("section", "dp", None),
            P("section", "dp", None),
            P("section", "dp", None),
            P("section", "dp", None),
            P("section", None, "dp"),
            P("section", None, "dp"),
        ),
        check_vma=False,
    )
```

```python
import functools
import types

import jax
import jax.numpy as jnp
from jax import lax
from jax.experimental import pallas as pl
from jax.experimental.pallas import tpu as pltpu
from jax.sharding import PartitionSpec as P

HEAD = 64
EPSILON = 1e-06
MESH = pl.DeviceIdType.MESH
WIDE = jnp.float32
SLIM = jnp.bfloat16
VMEM_BYTES = 67043328

UNITS = 24
FAR = 2
QUAD = 8
NEAR = UNITS - QUAD
BLOCK = 48
COLUMNS = 384
EARLY_NEAR = 3
HOLD = 0
LAGS = (2, 4, 6)
FAR_FIRST = (0, 5)
FAR_SECOND = (2, 9)
FAR_ARRIVED = (3, 18)
FAR_DONE = (7, 21)
QUAD_AT = (-1, -1, 2, 4, 6, 12)
QUAD_FIRST = (3, 2, 6, 7, 9, 13)
QUAD_SECOND = (5, 7, 15, 13, 11, 16)
QUAD_DONE = (18, 13, 19, 21, 12, 20)


def times(left, right):
    return jnp.dot(left, right, preferred_element_type=WIDE)


def times_turned(left, right):
    return lax.dot_general(left, right, (((1,), (1,)), ((), ())), preferred_element_type=WIDE)


def unit_rows(values):
    centred = values - jnp.mean(values, -1, keepdims=True)
    inverse = lax.rsqrt(jnp.mean(centred * centred, -1, keepdims=True) + EPSILON)
    return centred * inverse, inverse


def norm_rows_bf16(r, values, which):
    unit, _ = unit_rows(values)
    return (unit * r.gain[0, which : which + 1, :] + r.bias[0, which : which + 1, :]).astype(SLIM)


def norm_backward(r, values, norm_grad, which):
    unit, inverse = unit_rows(values)
    width = values.shape[1]
    r.sums[which] += jnp.sum((norm_grad * unit).reshape(-1, 8, width), 0)
    r.sums[2 + which] += jnp.sum(norm_grad.reshape(-1, 8, width), 0)
    inner = norm_grad * r.gain[0, which : which + 1, :]
    return inverse * (
        inner
        - jnp.mean(inner, -1, keepdims=True)
        - unit * jnp.mean(inner * unit, -1, keepdims=True)
    )


def head_lanes():
    lane = lax.broadcasted_iota(jnp.int32, (1, 2 * HEAD), 1)
    first = jnp.where(lane < HEAD, 1.0, 0.0).astype(WIDE)
    return first, 1.0 - first


def mask_bias(r, micro):
    length = r.bias_mask.shape[0]

    def marks(positions):
        end = jnp.int32(0)
        ids = jnp.zeros(positions.shape, jnp.int32)
        anchors = jnp.zeros(positions.shape, jnp.int32)
        for clip in range(r.lengths.shape[2]):
            size = r.lengths[micro, 0, clip]
            anchor = end + lax.rem(r.offsets[micro, 0, clip], size)
            end = end + size
            ids = ids + jnp.where(positions >= end, 1, 0)
            anchors = anchors + jnp.where(positions == anchor, 1, 0)
        return ids, anchors

    key_ids, anchors = marks(lax.broadcasted_iota(jnp.int32, (length, 1), 0))
    query_ids, _ = marks(lax.broadcasted_iota(jnp.int32, (1, length), 1))
    seen = (key_ids == query_ids) | (jnp.broadcast_to(anchors, (length, length)) > 0)
    r.bias_mask[...] = jnp.where(seen, 0.0, -1000000000.0).astype(WIDE)


def place(r, slab, tokens):
    for line in range(8):
        z, y = line // 2, line % 2
        rows = pl.ds(y * 192 + z * BLOCK, BLOCK)
        own = pl.ds(pl.multiple_of(2 * BLOCK * line + r.c * BLOCK, 16), BLOCK)
        other = pl.ds(pl.multiple_of(2 * BLOCK * line + (1 - r.c) * BLOCK, 16), BLOCK)
        r.acts[slab, rows, tokens] = r.turned[own, :]
        r.acts_out[slab, rows, :] = r.turned[other, :]


def forward(r, micro, tok, first, leading):
    length, width = r.normed.shape
    tokens = pl.ds(tok, length)
    r.normed[...] = norm_rows_bf16(r, r.stream[micro].astype(WIDE), 0)

    @pl.when(first)
    def _():
        r.load_inward.wait()

        @pl.when(leading)
        def _():
            r.load_rest()

    for part in range(3):
        r.grads[5 + part, tokens, :] = times(
            r.normed[...], r.inward[:, part * width : (part + 1) * width]
        ).astype(SLIM)

    @pl.when(micro > 0)
    def _():
        r.share_acts(0).wait_send()

    r.turned[...] = r.normed[...].T
    place(r, 3, tokens)
    one, two = (lanes.astype(SLIM) for lanes in head_lanes())
    for pair in range(width // (2 * HEAD)):
        cols = pl.ds(pair * 2 * HEAD, 2 * HEAD)
        queries = r.grads[5, tokens, cols] * jnp.asarray(HEAD**-0.5, SLIM)
        keys = r.grads[6, tokens, cols]
        values_turned = r.grads[7, tokens, cols].T
        scores = times_turned(jnp.concatenate([keys * one, keys * two], 0), queries)
        pieces = []
        for head in range(2):
            masked = scores[length * head : length * (head + 1)] + r.bias_mask[...]
            raised = jnp.exp(masked - jnp.max(masked, 0, keepdims=True))
            weights = (raised * (1.0 / jnp.sum(raised, 0, keepdims=True))).astype(SLIM)
            r.weights[micro, 2 * pair + head] = weights
            pieces.append(times(values_turned[HEAD * head : HEAD * (head + 1)], weights).astype(SLIM))
        attended_turned = jnp.concatenate(pieces, 0)
        r.turned[cols, :] = attended_turned
        r.held[:, cols] = attended_turned.T
    place(r, 2, tokens)

    @pl.when(first)
    def _():
        r.load_outward.wait()

    r.middle[micro] = r.stream[micro].astype(WIDE) + times(r.held[...], r.outward[...])
    r.normed[...] = norm_rows_bf16(r, r.middle[micro], 1)
    r.turned[...] = r.normed[...].T
    place(r, 1, tokens)

    @pl.when(first)
    def _():
        r.load_up.wait()
        r.load_down.wait()

    def activate(part):
        lifted = times(r.normed[...], r.up[:, part * width : (part + 1) * width])
        cumulative = 0.5 * (1.0 + lax.erf(lifted * 0.7071067811865476))
        density = jnp.exp(-0.5 * lifted * lifted) * 0.3989422804014327
        r.grads[part, tokens, :] = (cumulative + lifted * density).astype(SLIM)
        active = (lifted * cumulative).astype(SLIM)
        r.turned[...] = active.T
        rows = pl.ds(part * BLOCK, BLOCK)
        for y in range(2):
            placed = pl.ds(y * 192 + part * BLOCK, BLOCK)
            own = pl.ds(pl.multiple_of(384 * y + r.c * 192, 16), BLOCK)
            other = pl.ds(pl.multiple_of(384 * y + (1 - r.c) * 192, 16), BLOCK)
            r.acts[0, placed, tokens] = r.turned[own, :]
            r.acts_out[0, placed, :] = r.turned[other, :]
        for piece in range(3):

            def rows_for(core, side):
                start = 384 * side + 192 * core + BLOCK * (piece + 1)
                return r.turned[pl.ds(pl.multiple_of(start, 16), BLOCK), :]

            r.quad_acts[piece, rows, r.quad_rows(micro)] = rows_for(r.c, r.y)
            r.quad_out[micro, 0, piece, rows, :] = rows_for(1 - r.c, r.y)
            r.quad_out[micro, 1, piece, rows, :] = rows_for(r.c, 1 - r.y)
            r.quad_out[micro, 2, piece, rows, :] = rows_for(1 - r.c, 1 - r.y)
        return active

    @pl.when(leading)
    def _():
        r.total[...] = r.middle[micro]
        for part in range(4):
            r.total[...] += times(activate(part), r.down[part * width : (part + 1) * width, :])
        r.result[micro] = r.total[...].astype(SLIM)

    @pl.when(jnp.logical_not(leading))
    def _():
        for part in range(4):
            set_aside(r, micro * 12 + 2 * part, activate(part))
        middle = r.middle[micro]
        upper = middle.astype(SLIM)
        set_aside(r, micro * 12 + 8, upper)
        set_aside(r, micro * 12 + 10, (middle - upper.astype(WIDE)).astype(SLIM))


def set_aside(r, slot, values):
    for half in range(2):
        columns = values[:, half * COLUMNS : (half + 1) * COLUMNS]
        r.partial[slot + half, 0] = columns[:192]
        r.partial[slot + half, 1, 0:64] = columns[192:]


def set_back(r, slot):
    halves = [
        jnp.concatenate([r.partial[slot + half, 0], r.partial[slot + half, 1, 0:64]], 0) for half in range(2)
    ]
    return jnp.concatenate(halves, 1)


def last_output(r, micro):
    width = r.normed.shape[1]
    r.total[...] = set_back(r, micro * 12 + 8).astype(WIDE) + set_back(r, micro * 12 + 10).astype(WIDE)
    for part in range(4):
        r.total[...] += times(set_back(r, micro * 12 + 2 * part), r.down[part * width : (part + 1) * width, :])
    r.result[micro] = r.total[...].astype(SLIM)


def backward(r, micro, tok):
    length, width = r.normed.shape
    tokens = pl.ds(tok, length)
    r.total[...] = jnp.zeros((length, width), WIDE)
    for part in range(4):
        cols = slice(part * width, (part + 1) * width)
        hidden = times_turned(r.branch[r.quad_rows(micro), :], r.down[cols, :])
        lifted_grad = (hidden * r.grads[part, tokens, :].astype(WIDE)).astype(SLIM)
        r.grads[part, tokens, :] = lifted_grad
        r.total[...] += times_turned(lifted_grad, r.up[:, cols])
    r.share_lifted(micro).start()
    r.between(micro)
    middle_grad = r.branch[r.quad_rows(micro), :].astype(WIDE) + norm_backward(
        r, r.middle[micro], r.total[...], 1
    )
    r.middle[micro] = middle_grad
    r.grads[4, tokens, :] = middle_grad.astype(SLIM)
    r.held[...] = times_turned(r.grads[4, tokens, :], r.outward[...]).astype(SLIM)
    first, second = head_lanes()
    one, two = first.astype(SLIM), second.astype(SLIM)
    scaling = HEAD**-0.5
    for pair in range(width // (2 * HEAD)):
        cols = pl.ds(pair * 2 * HEAD, 2 * HEAD)
        queries = r.grads[5, tokens, cols] * jnp.asarray(scaling, SLIM)
        values = r.grads[7, tokens, cols]
        keys_turned = r.grads[6, tokens, cols].T
        incoming = r.held[:, cols]
        weight_grads = times_turned(jnp.concatenate([values * one, values * two], 0), incoming)
        score_grads, query_grads, weights = [], [], []
        for head in range(2):
            kept = r.weights[micro, 2 * pair + head]
            wide = kept.astype(WIDE)
            own = weight_grads[length * head : length * (head + 1)]
            score_grad = (wide * (own - jnp.sum(wide * own, 0, keepdims=True))).astype(SLIM)
            score_grads.append(score_grad)
            weights.append(kept)
            query_grads.append(
                (times(keys_turned[HEAD * head : HEAD * (head + 1)], score_grad) * scaling).astype(SLIM)
            )
        key_grad = times(jnp.concatenate(score_grads, 0), queries)
        value_grad = times(jnp.concatenate(weights, 0), incoming)
        r.grads[5, tokens, cols] = jnp.concatenate(query_grads, 0).T
        r.grads[6, tokens, cols] = (key_grad[:length] * first + key_grad[length:] * second).astype(SLIM)
        r.grads[7, tokens, cols] = (value_grad[:length] * first + value_grad[length:] * second).astype(SLIM)
    norm_grad = times_turned(r.grads[5, tokens, :], r.inward[:, 0:width])
    for part in range(1, 3):
        norm_grad += times_turned(r.grads[5 + part, tokens, :], r.inward[:, part * width : (part + 1) * width])
    r.total[...] = norm_grad
    input_grad = r.middle[micro] + norm_backward(r, r.stream[micro].astype(WIDE), r.total[...], 0)
    r.middle[micro] = input_grad
    r.stream[micro] = input_grad.astype(SLIM)


NAMES = (
    "x_in", "cot_in", "inward_in", "outward_in", "up_in", "down_in", "gain", "bias", "lengths", "offsets",
    "result", "middle", "staged", "out_norms",
    "stream", "inward", "outward", "up", "down", "grads", "branch", "acts", "acts_out", "quad_acts", "quad_out", "weights", "normed", "held",
    "turned", "total", "sums", "bias_mask",
    "partial", "y_in", "z_in", "far_y_in", "far_z_in", "norms",
    "load_sem", "source_sem",
    "relay_send", "relay_recv", "acts_send", "acts_recv", "branch_send", "branch_recv", "lifted_send", "lifted_recv",
    "across_send", "across_recv", "onward_send", "onward_recv", "quad_send", "quad_recv",
    "rest_send", "rest_recv", "turn",
    "y_send", "y_recv", "z_send", "z_recv", "far_y_send", "far_y_recv", "far_z_send", "far_z_recv", "norm_send", "norm_recv",
)


def step_kernel(*refs):
    r = types.SimpleNamespace(**dict(zip(NAMES, refs)))
    section, dp = lax.axis_index("section"), lax.axis_index("dp")
    c, y, z = lax.rem(dp, 2), lax.rem(lax.div(dp, 2), 2), lax.div(dp, 4)
    r.c, r.y = c, y
    length = r.normed.shape[0]
    leading = section == 0
    pair_dp, y_dp = dp + 1 - 2 * c, dp + 2 - 4 * y
    diagonal_dp = pair_dp + y_dp - dp

    def slot_of(core, micro):
        return pl.ds(pl.multiple_of((core * 2 + micro) * length, length), length)

    def quad_rows(micro, core=c, side=y):
        return pl.ds(pl.multiple_of(((side * 2 + core) * 2 + micro) * length, length), length)

    r.quad_rows = quad_rows

    def remote(src, dst, send, recv, to_section, to_dp):
        return pltpu.make_async_remote_copy(
            src_ref=src, dst_ref=dst, send_sem=send, recv_sem=recv,
            device_id=(to_section, to_dp), device_id_type=MESH,
        )

    def local(src, dst, sem):
        return pltpu.make_async_copy(src, dst, sem)

    r.load_inward = local(r.inward_in.at[0], r.inward, r.load_sem.at[0])
    r.load_outward = local(r.outward_in.at[0], r.outward, r.load_sem.at[1])
    r.load_up = local(r.up_in.at[0], r.up, r.load_sem.at[2])
    r.load_down = local(r.down_in.at[0], r.down, r.load_sem.at[3])

    def load_rest():
        r.load_outward.start()
        r.load_up.start()
        r.load_down.start()

    r.load_rest = load_rest

    def load_x(micro):
        return local(r.x_in.at[micro, 0], r.stream.at[micro], r.source_sem.at[micro])

    def load_cot(micro):
        return local(r.cot_in.at[micro, 0], r.branch.at[quad_rows(micro)], r.source_sem.at[micro])

    def relay_up(micro):
        return remote(r.result.at[micro], r.stream.at[micro], r.relay_send.at[micro], r.relay_recv.at[micro], 1 - section, dp)

    def relay_back(micro):
        return remote(
            r.stream.at[micro], r.branch.at[quad_rows(micro)], r.relay_send.at[micro], r.relay_recv.at[micro], 1 - section, dp
        )

    def share_acts(micro, core=c):
        return remote(
            r.acts_out, r.acts.at[:, :, slot_of(core, micro)], r.acts_send.at[micro], r.acts_recv.at[micro], section, pair_dp
        )

    def branch_copy(rows, send, recv, to_dp):
        return remote(r.branch.at[rows], r.branch.at[rows], send, recv, section, to_dp)

    def share_branch(micro, core=c):
        return branch_copy(quad_rows(micro, core), r.branch_send.at[micro], r.branch_recv.at[micro], pair_dp)

    def branch_across(micro, side=y):
        return branch_copy(quad_rows(micro, c, side), r.across_send.at[micro], r.across_recv.at[micro], y_dp)

    def branch_onward(micro, core=c):
        return branch_copy(quad_rows(micro, core, 1 - y), r.onward_send.at[micro], r.onward_recv.at[micro], pair_dp)

    def share_quad(micro, peer, arriving=False):
        to_dp = (pair_dp, y_dp, diagonal_dp)[peer]
        core = 1 - c if arriving and peer != 1 else c
        side = 1 - y if arriving and peer != 0 else y
        return remote(
            r.quad_out.at[micro, peer], r.quad_acts.at[:, :, quad_rows(micro, core, side)],
            r.quad_send.at[micro, peer], r.quad_recv.at[micro, peer], section, to_dp,
        )

    def share_lifted(micro, core=c):
        rows = slot_of(core, micro)
        return remote(
            r.grads.at[0:4, rows], r.grads.at[0:4, rows], r.lifted_send.at[micro], r.lifted_recv.at[micro], section, pair_dp
        )

    def share_rest(micro, core=c):
        rows = slot_of(core, micro)
        return remote(
            r.grads.at[4:8, rows], r.grads.at[4:8, rows], r.rest_send.at[micro], r.rest_recv.at[micro], section, pair_dp
        )

    r.share_lifted = share_lifted
    r.share_acts = share_acts

    def to_y(unit):
        return remote(
            r.partial.at[unit, 0], r.y_in.at[unit - QUAD], r.y_send.at[unit - QUAD], r.y_recv.at[unit - QUAD], section, y_dp
        )

    def rows_of(place):
        return pl.ds(BLOCK * place, BLOCK)

    def near_z(unit, place, index, lane, to_dp):
        near = unit - FAR
        return remote(
            r.partial.at[unit, 1, rows_of(place)], r.z_in.at[near, index],
            r.z_send.at[near, lane], r.z_recv.at[near, index], section, to_dp,
        )

    def far_z(unit, place, index, lane, to_dp):
        return remote(
            r.partial.at[unit, :, rows_of(place)], r.far_z_in.at[unit, index],
            r.far_z_send.at[unit, lane], r.far_z_recv.at[unit, index], section, to_dp,
        )

    def far_to_y(unit, place):
        return remote(
            r.partial.at[unit, 0, rows_of(place)], r.far_y_in.at[unit], r.far_y_send.at[unit], r.far_y_recv.at[unit], section, y_dp
        )

    r.load_inward.start()

    @pl.when(leading)
    def _():
        load_x(0).start()
        load_x(1).start()

    @pl.when(jnp.logical_not(leading))
    def _():
        load_cot(0).start()
        load_cot(1).start()

    @pl.when(jnp.logical_not(leading))
    def _():
        r.load_rest()

    r.sums[...] = jnp.zeros_like(r.sums)

    barrier = pltpu.get_barrier_semaphore()
    peers = [(1 - section, dp), (section, pair_dp), (section, y_dp)]
    peers += [(section, diagonal_dp)]
    peers += [(section, lax.rem(dp + 4 * hop, 16)) for hop in (1, 2, 3)]
    for peer in peers:
        pl.semaphore_signal(barrier, inc=1, device_id=peer, device_id_type=MESH)

    def everyone_in():
        pl.semaphore_wait(barrier, len(peers))

    def arrive(micro):
        relay_back(micro).wait_recv()
        branch_across(micro).start()
        share_branch(micro).start()

    def columns_of(unit):
        return pl.ds(pl.multiple_of(lax.rem(unit, 2) * COLUMNS, 128), COLUMNS)

    def side_rows(side):
        return pl.ds(pl.multiple_of(side * 192, 64), 192)

    def near_unit(unit):
        whole = lax.div(unit, 2)
        slab = 1 + jnp.where(whole >= 8, 1, 0) + jnp.where(whole >= 9, 1, 0)
        grads = r.grads[whole - 4, :, columns_of(unit)]
        r.partial[unit, 0] = times(r.acts[slab, side_rows(1 - y), :], grads).astype(SLIM)
        to_y(unit).start()
        r.partial[unit, 1] = times(r.acts[slab, side_rows(y), :], grads).astype(SLIM)

    def far_unit(unit):
        grads = r.branch[pl.ds(pl.multiple_of(y * 4 * length, length), 4 * length), columns_of(unit)]
        r.partial[unit, 0] = times(r.acts[0, side_rows(1 - y), :], grads).astype(SLIM)
        r.partial[unit, 1] = times(r.acts[0, side_rows(y), :], grads).astype(SLIM)
        at_ends(unit, far_z, r.far_z_in)

    def quad_unit(unit):
        grads = r.branch[:, columns_of(unit)]
        r.partial[unit, 1] = times(r.quad_acts[lax.div(unit, 2) - 1], grads).astype(SLIM)
        at_ends(unit, near_z, r.z_in)

    def arrived(unit, index, copy, into):
        copy(unit, 0, index, 0, dp).wait_recv()
        return into[unit if into is r.far_z_in else unit - FAR, index].astype(WIDE)

    def pick(unit, place, copy):
        return (unit, slice(None) if copy is far_z else 1, rows_of(place))

    def go_right(unit, here, copy, into):
        for place in range(3, here, -1):
            at = pick(unit, place, copy)
            if here > 0:
                r.partial[at] = (r.partial[at].astype(WIDE) + arrived(unit, place + 1, copy, into)).astype(SLIM)
            copy(unit, place, place + 1, place - 1, dp + 4).start()

    def go_left(unit, here, copy, into):
        for place in range(here):
            at = pick(unit, place, copy)
            if here < 3:
                r.partial[at] = (r.partial[at].astype(WIDE) + arrived(unit, place, copy, into)).astype(SLIM)
            copy(unit, place, place, place, dp - 4).start()

    def at_ends(unit, copy, into):
        @pl.when(z == 0)
        def _():
            go_right(unit, 0, copy, into)

        @pl.when(z == 3)
        def _():
            go_left(unit, 3, copy, into)

    def at_middle_first(unit, copy, into):
        @pl.when(z == 1)
        def _():
            go_right(unit, 1, copy, into)

        @pl.when(z == 2)
        def _():
            go_left(unit, 2, copy, into)

    def at_middle_second(unit, copy, into):
        @pl.when(z == 1)
        def _():
            go_left(unit, 1, copy, into)

        @pl.when(z == 2)
        def _():
            go_right(unit, 2, copy, into)

    def gathered(unit, here, copy, into):
        value = r.partial[pick(unit, here, copy)].astype(WIDE)
        if here > 0:
            value = value + arrived(unit, here + 1, copy, into)
        if here < 3:
            value = value + arrived(unit, here, copy, into)
        return value

    def everywhere(action):
        for here in range(4):

            @pl.when(z == here)
            def _():
                action(here)

    def far_units():
        for micro in range(2):
            share_branch(micro, 1 - c).wait_recv()
            share_acts(micro, 1 - c).wait_recv()

        def body(unit, carry):
            far_unit(unit)
            return carry

        lax.fori_loop(0, FAR, body, 0)
        branch_across(0, 1 - y).wait_recv()
        branch_onward(0).start()

    r.between = lambda micro: pl.when(leading & (micro == 1))(far_units)

    def slot(t, carry):
        trailing = jnp.logical_not(leading)
        half = lax.div(t, 2)
        is_forward = (leading & (t < 2)) | (trailing & ((t == 1) | (t == 3)))
        is_backward = (leading & ((t == 3) | (t == 5))) | (trailing & ((t == 2) | (t == 4)))

        @pl.when(trailing & (t == 0))
        def _():
            everyone_in()
            for micro in range(2):
                load_cot(micro).wait()
                branch_across(micro).start()
                share_branch(micro).start()

        @pl.when(is_forward)
        def _():
            micro = jnp.where(leading, jnp.minimum(t, 1), jnp.minimum(half, 1))

            mask_bias(r, micro)

            @pl.when(leading)
            def _():
                load_x(micro).wait()

            @pl.when(trailing)
            def _():
                relay_up(micro).wait_recv()

            forward(r, micro, pl.multiple_of((c * 2 + micro) * length, length), t == section, leading)

            @pl.when(leading & (t == 0))
            def _():
                everyone_in()

            ahead = leading & (c == 0) & (t == 0)

            @pl.when(ahead)
            def _():
                relay_up(0).start()
                relay_up(0).wait_send()
                pl.semaphore_signal(r.turn, inc=1, device_id=(section, pair_dp), device_id_type=MESH)

            @pl.when(leading & (t == 1))
            def _():
                relay_up(1).start()

            share_acts(micro).start()

            @pl.when(leading & (c == 1) & (t == 0))
            def _():
                pl.semaphore_wait(r.turn, 1)
                relay_up(0).start()

            for peer in range(3):
                share_quad(micro, peer).start()

        @pl.when(leading & (t == 3))
        def _():
            arrive(0)

        @pl.when(is_backward)
        def _():
            micro = jnp.clip(half - 1, 0, 1)
            backward(r, micro, pl.multiple_of((c * 2 + micro) * length, length))

            @pl.when(trailing)
            def _():
                relay_back(micro).start()

            share_rest(micro).start()

            @pl.when(trailing & (t == 4))
            def _():
                def body(done, carry):
                    last_output(r, done)
                    return carry

                lax.fori_loop(0, 2, body, 0)

        @pl.when(leading & (t == 4))
        def _():
            arrive(1)

        pl.when(trailing & (t == 5))(far_units)
        return carry

    lax.fori_loop(0, 6, slot, 0)

    def norm_copy(src, dst, index, to_dp):
        return remote(r.norms.at[src], r.norms.at[dst], r.norm_send.at[index], r.norm_recv.at[index], section, to_dp)

    def norm_to_pair():
        return norm_copy(0, 1, 0, pair_dp)

    def norm_to_y():
        return norm_copy(2, 3, 1, y_dp)

    def norm_to_z(hop):
        return norm_copy(4, 4 + hop, 1 + hop, lax.rem(dp + 4 * hop, 16))

    r.norms[0] = jnp.concatenate([jnp.sum(r.sums[...], 1), jnp.zeros((4, r.sums.shape[2]), WIDE)], 0)
    norm_to_pair().start()
    for micro in range(2):
        share_lifted(micro, 1 - c).wait_recv()

    def early_near(ahead, carry):
        near_unit(QUAD + ahead)
        return carry

    lax.fori_loop(0, EARLY_NEAR, early_near, 0)
    branch_across(1, 1 - y).wait_recv()
    branch_onward(1).start()
    for micro in range(2):
        branch_onward(micro, 1 - c).wait_recv()
        for peer in range(3):
            share_quad(micro, peer, True).wait_recv()

    def early_quad(unit, carry):
        quad_unit(unit)
        return carry

    lax.fori_loop(FAR, FAR + sum(step < 0 for step in QUAD_AT), early_quad, 0)

    def sum_y(unit):
        to_y(unit).wait_recv()
        r.partial[unit, 1] = (r.partial[unit, 1].astype(WIDE) + r.y_in[unit - QUAD].astype(WIDE)).astype(SLIM)

    def turn_of(i, steps, base):
        turn, unit = i < 0, jnp.int32(base)
        for index, step in enumerate(steps):
            if step >= 0:
                turn = turn | (i == step)
                unit = jnp.where(i == step, base + index, unit)
        return turn, unit

    def near_turn(i, lag):
        return (i >= lag) & (i < NEAR + lag), jnp.clip(i - lag, 0, NEAR - 1) + QUAD

    def end_of_line(unit):
        def action(here):
            r.staged[unit] = gathered(unit, here, near_z, r.z_in)

        everywhere(action)

    def advance(i, carry):
        issued = QUAD + EARLY_NEAR + i - HOLD

        @pl.when(issued == 16)
        def _():
            for micro in range(2):
                share_rest(micro, 1 - c).wait_recv()

        @pl.when((issued >= QUAD + EARLY_NEAR) & (issued < UNITS))
        def _():
            near_unit(issued)

        @pl.when(i < NEAR)
        def _():
            sum_y(QUAD + i)
            at_ends(QUAD + i, near_z, r.z_in)

        turn, unit = turn_of(i, QUAD_AT, FAR)

        @pl.when(turn)
        def _(unit=unit):
            quad_unit(unit)

        turn, unit = near_turn(i, LAGS[0])

        @pl.when(turn)
        def _(unit=unit):
            at_middle_first(unit, near_z, r.z_in)

        turn, unit = turn_of(i, FAR_FIRST, 0)

        @pl.when(turn)
        def _(unit=unit):
            at_middle_first(unit, far_z, r.far_z_in)

        turn, unit = turn_of(i, QUAD_FIRST, FAR)

        @pl.when(turn)
        def _(unit=unit):
            at_middle_first(unit, near_z, r.z_in)

        turn, unit = turn_of(i, FAR_SECOND, 0)

        @pl.when(turn)
        def _(unit=unit):
            at_middle_second(unit, far_z, r.far_z_in)

        turn, unit = turn_of(i, QUAD_SECOND, FAR)

        @pl.when(turn)
        def _(unit=unit):
            at_middle_second(unit, near_z, r.z_in)

        turn, unit = near_turn(i, LAGS[1])

        @pl.when(turn)
        def _(unit=unit):
            at_middle_second(unit, near_z, r.z_in)

        turn, unit = turn_of(i, QUAD_DONE, FAR)

        @pl.when(turn)
        def _(unit=unit):
            end_of_line(unit)

        turn, unit = near_turn(i, LAGS[2])

        @pl.when(turn)
        def _(unit=unit):
            end_of_line(unit)

        turn, unit = turn_of(i, FAR_ARRIVED, 0)

        @pl.when(turn)
        def _(unit=unit):
            def action(here):
                value = gathered(unit, here, far_z, r.far_z_in)
                r.partial[unit, 0, rows_of(here)] = value[0].astype(SLIM)
                far_to_y(unit, here).start()
                r.staged[unit] = value[1]

            everywhere(action)

        turn, unit = turn_of(i, FAR_DONE, 0)

        @pl.when(turn)
        def _(unit=unit):
            far_to_y(unit, 0).wait_recv()
            r.staged[unit] += r.far_y_in[unit].astype(WIDE)

        @pl.when(i == 1)
        def _():
            norm_to_pair().wait()
            r.norms[2] = r.norms[0] + r.norms[1]
            norm_to_y().start()

        @pl.when(i == 9)
        def _():
            norm_to_y().wait_recv()
            r.norms[4] = r.norms[2] + r.norms[3]
            for hop in (1, 2, 3):
                norm_to_z(hop).start()

        @pl.when(i == 15)
        def _():
            for hop in (1, 2, 3):
                norm_to_z(hop).wait_recv()
            r.out_norms[...] = (r.norms[4] + r.norms[5]) + (r.norms[6] + r.norms[7])

        return carry

    lax.fori_loop(0, NEAR + LAGS[2], advance, 0)

    norm_to_y().wait_send()
    for hop in (1, 2, 3):
        norm_to_z(hop).wait_send()
    share_acts(1).wait_send()
    for micro in range(2):
        share_branch(micro).wait_send()
        branch_across(micro).wait_send()
        branch_onward(micro).wait_send()
        for peer in range(3):
            share_quad(micro, peer).wait_send()
        share_lifted(micro).wait_send()
        share_rest(micro).wait_send()

        @pl.when(leading if micro else leading & (c == 1))
        def _():
            relay_up(micro).wait_send()

        @pl.when(jnp.logical_not(leading))
        def _():
            relay_back(micro).wait_send()

    def drain_y(near, carry):
        to_y(QUAD + near).wait_send()
        return carry

    lax.fori_loop(0, NEAR, drain_y, 0)

    def drain_z(unit, carry):
        for lane in range(3):
            near_z(unit, 0, 0, lane, dp).wait_send()
        return carry

    lax.fori_loop(FAR, UNITS, drain_z, 0)

    def drain_far(unit, carry):
        far_to_y(unit, 0).wait_send()
        for lane in range(3):
            far_z(unit, 0, 0, lane, dp).wait_send()
        return carry

    lax.fori_loop(0, FAR, drain_far, 0)


def hand_over_kernel(result, grad, staged, norms, *refs):
    out_result, out_grad, out_inward, out_outward, out_up, out_down, gain_grad, bias_grad, sem = refs
    width = result.shape[2]

    def start(source, target):
        copy = pltpu.make_async_copy(source, target, sem)
        copy.start()
        return copy

    copies = [start(result, out_result.at[0, :, 0]), start(grad, out_grad.at[0, :, 0])]
    for piece in range(UNITS):
        half = pl.ds(piece % 2 * COLUMNS, COLUMNS)
        if piece < 8:
            target = out_down.at[0, pl.ds(piece // 2 * BLOCK, BLOCK), half]
        elif piece < 16:
            target = out_up.at[0, :, pl.ds((piece - 8) * COLUMNS, COLUMNS)]
        elif piece < 18:
            target = out_outward.at[0, :, half]
        else:
            target = out_inward.at[0, :, pl.ds((piece - 18) * COLUMNS, COLUMNS)]
        copies.append(start(staged.at[piece], target))
    share = gain_grad.shape[2]
    for index in range(width // share):

        @pl.when(lax.axis_index("dp") == index)
        def _():
            gain_grad[0] = norms[0:2, index * share : (index + 1) * share]
            bias_grad[0] = norms[2:4, index * share : (index + 1) * share]

    for copy in copies:
        copy.wait()


def step_on_device(
    inputs, clip_lengths, anchor_offsets, cotangent, inward_weight, outward_weight, up_weight, down_weight, norm_gain, norm_bias
):
    _, _, length, width = inputs.shape
    wide_ff = up_weight.shape[2]
    anywhere = pl.BlockSpec(memory_space=pl.ANY)
    in_vmem = pl.BlockSpec(memory_space=pltpu.VMEM)
    in_smem = pl.BlockSpec(memory_space=pltpu.SMEM)
    dma = pltpu.SemaphoreType.DMA
    share = width // lax.axis_size("dp")
    made = pl.pallas_call(
        step_kernel,
        out_shape=(
            pltpu.VMEM((2, length, width), SLIM),
            pltpu.VMEM((2, length, width), WIDE),
            pltpu.VMEM((UNITS, BLOCK, COLUMNS), WIDE),
            pltpu.VMEM((8, width), WIDE),
        ),
        in_specs=[anywhere] * 6 + [in_vmem] * 2 + [in_smem] * 2,
        out_specs=[in_vmem] * 4,
        scratch_shapes=[
            pltpu.VMEM((2, length, width), SLIM),
            pltpu.VMEM((width, 3 * width), SLIM),
            pltpu.VMEM((width, width), SLIM),
            pltpu.VMEM((width, wide_ff), SLIM),
            pltpu.VMEM((wide_ff, width), SLIM),
            pltpu.VMEM((8, 4 * length, width), SLIM),
            pltpu.VMEM((8 * length, width), SLIM),
            pltpu.VMEM((4, 8 * BLOCK, 4 * length), SLIM),
            pltpu.VMEM((4, 8 * BLOCK, length), SLIM),
            pltpu.VMEM((3, 4 * BLOCK, 8 * length), SLIM),
            pltpu.VMEM((2, 3, 3, 4 * BLOCK, length), SLIM),
            pltpu.VMEM((2, width // HEAD, length, length), SLIM),
            pltpu.VMEM((length, width), SLIM),
            pltpu.VMEM((length, width), SLIM),
            pltpu.VMEM((width, length), SLIM),
            pltpu.VMEM((length, width), WIDE),
            pltpu.VMEM((4, 8, width), WIDE),
            pltpu.VMEM((length, length), WIDE),
            pltpu.VMEM((UNITS, 2, 4 * BLOCK, COLUMNS), SLIM),
            pltpu.VMEM((NEAR, 4 * BLOCK, COLUMNS), SLIM),
            pltpu.VMEM((UNITS - FAR, 5, BLOCK, COLUMNS), SLIM),
            pltpu.VMEM((FAR, BLOCK, COLUMNS), SLIM),
            pltpu.VMEM((FAR, 5, 2, BLOCK, COLUMNS), SLIM),
            pltpu.VMEM((8, 8, width), WIDE),
            dma((4,)), dma((2,)),
            *[dma((2,))] * 8, *[dma((2,))] * 4, dma((2, 3)), dma((2, 3)), *[dma((2,))] * 2, pltpu.SemaphoreType.REGULAR,
            dma((NEAR,)), dma((NEAR,)), dma((UNITS - FAR, 3)), dma((UNITS - FAR, 5)),
            dma((FAR,)), dma((FAR,)), dma((FAR, 3)), dma((FAR, 5)), dma((5,)), dma((5,)),
        ],
        compiler_params=pltpu.CompilerParams(
            collective_id=0, has_side_effects=True, vmem_limit_bytes=VMEM_BYTES - 4500000
        ),
    )(
        inputs, cotangent, inward_weight, outward_weight, up_weight, down_weight,
        norm_gain, norm_bias, clip_lengths, anchor_offsets,
    )
    sections = 1
    return pl.pallas_call(
        hand_over_kernel,
        out_shape=(
            jax.ShapeDtypeStruct((sections, 2, 1, length, width), SLIM),
            jax.ShapeDtypeStruct((sections, 2, 1, length, width), WIDE),
            jax.ShapeDtypeStruct((sections, BLOCK, 3 * width), WIDE),
            jax.ShapeDtypeStruct((sections, BLOCK, width), WIDE),
            jax.ShapeDtypeStruct((sections, BLOCK, wide_ff), WIDE),
            jax.ShapeDtypeStruct((sections, 4 * BLOCK, width), WIDE),
            jax.ShapeDtypeStruct((sections, 2, share), WIDE),
            jax.ShapeDtypeStruct((sections, 2, share), WIDE),
        ),
        in_specs=[in_vmem] * 4,
        out_specs=[anywhere] * 6 + [in_vmem] * 2,
        scratch_shapes=[dma],
        compiler_params=pltpu.CompilerParams(vmem_limit_bytes=1 << 20),
    )(*[pltpu.with_memory_space_constraint(one, pltpu.VMEM) for one in made])


def shifted(x, axis, by):
    size = lax.axis_size(axis)
    pairs = [(i, i + by) for i in range(size) if 0 <= i + by < size]
    return lax.ppermute(x, axis, pairs)


def norm_rows(values, norm_gain, norm_bias):
    average = jnp.mean(values, -1, keepdims=True)
    centred = values - average
    inverse = lax.rsqrt(jnp.mean(centred * centred, -1, keepdims=True) + EPSILON)
    normed = centred * inverse
    return (normed * norm_gain + norm_bias, normed, inverse)


def norm_back(norm_grad, normed, inverse, norm_gain):
    inner = norm_grad * norm_gain
    through = inverse * (
        inner
        - jnp.mean(inner, -1, keepdims=True)
        - normed * jnp.mean(inner * normed, -1, keepdims=True)
    )
    return (through, jnp.sum(norm_grad * normed, 0), jnp.sum(norm_grad, 0))


def gelu_slope(lifted):
    cumulative = 0.5 * (1.0 + lax.erf(lifted * 0.7071067811865476))
    density = jnp.exp(-0.5 * lifted * lifted) * 0.3989422804014327
    return cumulative + lifted * density


def clip_marks(lengths, offsets, length):
    positions = jnp.arange(length, dtype=jnp.int32)
    clip_ends = jnp.cumsum(lengths)
    clip_starts = clip_ends - lengths
    anchor_at = clip_starts + offsets % lengths
    clip_ids = jnp.sum((positions[:, None] >= clip_ends[None, :]).astype(jnp.int32), 1)
    anchors = jnp.any(positions[:, None] == anchor_at[None, :], 1)
    return (clip_ids, anchors)


def masked_scores(query_block, key_rows, id_block, clip_ids, anchors, scaling):
    scores = (
        jnp.einsum("qhd,khd->hqk", query_block, key_rows, preferred_element_type=jnp.float32)
        * scaling
    )
    seen = (id_block[:, None] == clip_ids[None, :]) | anchors[None, :]
    return jnp.where(seen[None], scores, -1000000000.0)


def forward_layer(source, clip_ids, anchors, params):
    inward, outward, upward, downward, norm_gain, norm_bias = params
    length, model_width = source.shape
    head_count = model_width // HEAD
    scaling = HEAD ** (-0.5)
    residual = source.astype(jnp.float32)
    first_norm, unit_one, scale_one = norm_rows(residual, norm_gain[0], norm_bias[0])
    joined = jnp.dot(
        first_norm.astype(jnp.bfloat16), inward, preferred_element_type=jnp.float32
    ).astype(jnp.bfloat16)
    heads_view = joined.reshape(length, 3, head_count, HEAD)
    queries = heads_view[:, 0]
    key_rows = heads_view[:, 1]
    values = heads_view[:, 2]
    scores = masked_scores(queries, key_rows, clip_ids, clip_ids, anchors, scaling)
    row_max = jnp.max(scores, -1, keepdims=True)
    raised = jnp.exp(scores - row_max)
    row_sum = jnp.sum(raised, -1, keepdims=True)
    weights = (raised / row_sum).astype(jnp.bfloat16)
    pieces = [jnp.einsum("hqk,khd->qhd", weights, values, preferred_element_type=jnp.float32)]
    log_sums = [(row_max + jnp.log(row_sum))[..., 0]]
    attended = jnp.concatenate(pieces, 0).reshape(length, model_width).astype(jnp.bfloat16)
    logsum = jnp.concatenate(log_sums, 1)
    middle = residual + jnp.dot(attended, outward, preferred_element_type=jnp.float32)
    second_norm, unit_two, scale_two = norm_rows(middle, norm_gain[1], norm_bias[1])
    lifted = jnp.dot(second_norm.astype(jnp.bfloat16), upward, preferred_element_type=jnp.float32)
    active = jax.nn.gelu(lifted, approximate=False).astype(jnp.bfloat16)
    result = middle + jnp.dot(active, downward, preferred_element_type=jnp.float32)
    stored = (unit_one, scale_one, joined, logsum, attended, unit_two, scale_two, lifted, active)
    return (result, stored)


def contract_rows(left, right):
    return lax.dot_general(
        left, right, (((0,), (0,)), ((), ())), preferred_element_type=jnp.float32
    )


def contract_cols(left, right):
    return lax.dot_general(
        left, right, (((1,), (1,)), ((), ())), preferred_element_type=jnp.float32
    )


def feed_backward(incoming, stored, params):
    inward, outward, upward, downward, norm_gain, norm_bias = params
    unit_one, scale_one, joined, logsum, attended, unit_two, scale_two, lifted, active = stored
    branch = incoming.astype(jnp.bfloat16)
    down_part = contract_rows(active, branch)
    hidden_grad = contract_cols(branch, downward)
    lifted_grad = (hidden_grad * gelu_slope(lifted)).astype(jnp.bfloat16)
    second_in = (unit_two * norm_gain[1] + norm_bias[1]).astype(jnp.bfloat16)
    up_part = contract_rows(second_in, lifted_grad)
    normed_grad = contract_cols(lifted_grad, upward)
    through, gain_two, bias_two = norm_back(normed_grad, unit_two, scale_two, norm_gain[1])
    return (incoming + through, (up_part, down_part, gain_two, bias_two))


def attend_backward(middle_grad, stored, clip_ids, anchors, params):
    inward, outward, upward, downward, norm_gain, norm_bias = params
    unit_one, scale_one, joined, logsum, attended, unit_two, scale_two, lifted, active = stored
    length, model_width = attended.shape
    head_count = model_width // HEAD
    scaling = HEAD ** (-0.5)
    branch = middle_grad.astype(jnp.bfloat16)
    outward_part = contract_rows(attended, branch)
    attended_grad = (
        contract_cols(branch, outward).astype(jnp.bfloat16).reshape(length, head_count, HEAD)
    )
    heads_view = joined.reshape(length, 3, head_count, HEAD)
    queries = heads_view[:, 0]
    key_rows = heads_view[:, 1]
    values = heads_view[:, 2]
    key_grad = jnp.zeros((length, head_count, HEAD), jnp.float32)
    value_grad = jnp.zeros((length, head_count, HEAD), jnp.float32)
    block_rows = min(512, length)
    scores = masked_scores(queries, key_rows, clip_ids, clip_ids, anchors, scaling)
    weights = jnp.exp(scores - logsum[:, 0:block_rows, None])
    weight_grad = jnp.einsum(
        "qhd,khd->hqk", attended_grad, values, preferred_element_type=jnp.float32
    )
    score_grad = (
        weights * (weight_grad - jnp.sum(weights * weight_grad, -1, keepdims=True))
    ).astype(jnp.bfloat16)
    query_pieces = [
        scaling
        * jnp.einsum("hqk,khd->qhd", score_grad, key_rows, preferred_element_type=jnp.float32)
    ]
    key_grad = key_grad + scaling * jnp.einsum(
        "hqk,qhd->khd", score_grad, queries, preferred_element_type=jnp.float32
    )
    value_grad = value_grad + jnp.einsum(
        "hqk,qhd->khd",
        weights.astype(jnp.bfloat16),
        attended_grad,
        preferred_element_type=jnp.float32,
    )
    query_grad = jnp.concatenate(query_pieces, 0)
    joined_grad = (
        jnp.stack([query_grad, key_grad, value_grad], 1)
        .reshape(length, 3 * model_width)
        .astype(jnp.bfloat16)
    )
    first_in = (unit_one * norm_gain[0] + norm_bias[0]).astype(jnp.bfloat16)
    inward_part = contract_rows(first_in, joined_grad)
    normed_grad = contract_cols(joined_grad, inward)
    through, gain_one, bias_one = norm_back(normed_grad, unit_one, scale_one, norm_gain[0])
    return (middle_grad + through, (inward_part, outward_part, gain_one, bias_one))


def resting(function):

    def blank(*operands):
        return jax.tree.map(jnp.zeros_like, function(*operands))

    return blank


def take_slot(holder, buffer_slot):
    return jax.tree.map(
        lambda element: lax.dynamic_index_in_dim(element, buffer_slot, 0, False), holder
    )


def place_slot(holder, item, buffer_slot, working):

    def update(element, fresh):
        former = lax.dynamic_index_in_dim(element, buffer_slot, 0, False)
        return lax.dynamic_update_index_in_dim(
            element, jnp.where(working, fresh, former), buffer_slot, 0
        )

    return jax.tree.map(update, holder, item)


def per_device(
    inputs,
    clip_lengths,
    anchor_offsets,
    cotangent,
    inward_weight,
    outward_weight,
    up_weight,
    down_weight,
    norm_gain,
    norm_bias,
):
    params = (
        inward_weight[0],
        outward_weight[0],
        up_weight[0],
        down_weight[0],
        norm_gain[0],
        norm_bias[0],
    )
    stream = inputs[:, 0]
    cot_rows = cotangent[:, 0]
    lengths_all = clip_lengths[:, 0]
    offsets_all = anchor_offsets[:, 0]
    micro_count = stream.shape[0]
    length = stream.shape[1]
    section_index = lax.axis_index("section")
    section_count = lax.axis_size("section")
    leading = section_index == 0
    trailing = section_index == section_count - 1
    periods = micro_count + section_count - 1
    arriving = jnp.zeros_like(stream[0])
    produced = jnp.zeros_like(stream)
    archive = None
    for period in range(periods):
        micro_index = period - section_index
        working = (micro_index >= 0) & (micro_index < micro_count)
        buffer_slot = jnp.clip(micro_index, 0, micro_count - 1)
        source = jnp.where(leading, stream[min(period, micro_count - 1)], arriving)
        clip_ids, anchors = clip_marks(
            take_slot(lengths_all, buffer_slot), take_slot(offsets_all, buffer_slot), length
        )
        result, stored = lax.cond(
            working, forward_layer, resting(forward_layer), source, clip_ids, anchors, params
        )
        if archive is None:
            archive = jax.tree.map(
                lambda element: jnp.zeros((micro_count,) + element.shape, element.dtype), stored
            )
        archive = place_slot(archive, stored, buffer_slot, working)
        sending = result.astype(jnp.bfloat16)
        produced = place_slot(produced, sending, buffer_slot, working)
        if period < micro_count:
            arriving = shifted(sending, "section", 1)
    inward, outward, upward, downward, gains, biases = params
    up_sum = jnp.zeros(upward.shape, jnp.float32)
    down_sum = jnp.zeros(downward.shape, jnp.float32)
    gain_two = jnp.zeros(gains.shape[1:], jnp.float32)
    bias_two = jnp.zeros(biases.shape[1:], jnp.float32)
    inward_sum = jnp.zeros(inward.shape, jnp.float32)
    outward_sum = jnp.zeros(outward.shape, jnp.float32)
    gain_one = jnp.zeros(gains.shape[1:], jnp.float32)
    bias_one = jnp.zeros(biases.shape[1:], jnp.float32)
    upstream = jnp.zeros_like(stream[0])
    returned = jnp.zeros(stream.shape, jnp.float32)
    for period in range(periods):
        micro_index = micro_count - 1 - period + (section_count - 1 - section_index)
        working = (micro_index >= 0) & (micro_index < micro_count)
        buffer_slot = jnp.clip(micro_index, 0, micro_count - 1)
        incoming = jnp.where(trailing, take_slot(cot_rows, buffer_slot), upstream).astype(
            jnp.float32
        )
        clip_ids, anchors = clip_marks(
            take_slot(lengths_all, buffer_slot), take_slot(offsets_all, buffer_slot), length
        )
        stored = take_slot(archive, buffer_slot)
        middle_grad, feed_part = lax.cond(
            working, feed_backward, resting(feed_backward), incoming, stored, params
        )
        up_sum = up_sum + feed_part[0]
        down_sum = down_sum + feed_part[1]
        gain_two = gain_two + feed_part[2]
        bias_two = bias_two + feed_part[3]
        input_grad, attend_part = lax.cond(
            working,
            attend_backward,
            resting(attend_backward),
            middle_grad,
            stored,
            clip_ids,
            anchors,
            params,
        )
        inward_sum = inward_sum + attend_part[0]
        outward_sum = outward_sum + attend_part[1]
        gain_one = gain_one + attend_part[2]
        bias_one = bias_one + attend_part[3]
        returned = place_slot(returned, input_grad, buffer_slot, working)
        if period < periods - 1:
            upstream = shifted(input_grad.astype(jnp.bfloat16), "section", -1)
    inward_sum, outward_sum, up_sum, down_sum, gain_one, gain_two, bias_one, bias_two = (
        lax.psum_scatter(inward_sum, "dp", scatter_dimension=0, tiled=True),
        lax.psum_scatter(outward_sum, "dp", scatter_dimension=0, tiled=True),
        lax.psum_scatter(up_sum, "dp", scatter_dimension=0, tiled=True),
        lax.psum_scatter(down_sum, "dp", scatter_dimension=0, tiled=True),
        lax.psum_scatter(gain_one, "dp", scatter_dimension=0, tiled=True),
        lax.psum_scatter(gain_two, "dp", scatter_dimension=0, tiled=True),
        lax.psum_scatter(bias_one, "dp", scatter_dimension=0, tiled=True),
        lax.psum_scatter(bias_two, "dp", scatter_dimension=0, tiled=True),
    )
    layer_outputs = produced[None, :, None]
    input_grads = returned[None, :, None]
    gain_grad = jnp.stack([gain_one, gain_two])[None]
    bias_grad = jnp.stack([bias_one, bias_two])[None]
    return (
        layer_outputs,
        input_grads,
        inward_sum[None],
        outward_sum[None],
        up_sum[None],
        down_sum[None],
        gain_grad,
        bias_grad,
    )


def solution(mesh):
    local = step_on_device if mesh.shape["dp"] == 16 and mesh.shape["section"] == 2 else per_device
    return jax.shard_map(
        local,
        mesh=mesh,
        in_specs=(
            P(None, "dp", None, None),
            P(None, "dp", None),
            P(None, "dp", None),
            P(None, "dp", None, None),
            P("section", None, None),
            P("section", None, None),
            P("section", None, None),
            P("section", None, None),
            P("section", None, None),
            P("section", None, None),
        ),
        out_specs=(
            P("section", None, "dp", None, None),
            P("section", None, "dp", None, None),
            P("section", "dp", None),
            P("section", "dp", None),
            P("section", "dp", None),
            P("section", "dp", None),
            P("section", None, "dp"),
            P("section", None, "dp"),
        ),
        check_vma=False,
    )
```
